32 devices in a mesh: seq: 16 (over z, y, x), head: 2 (over core).
Axes of the slice: x: 2, y: 2, z: 4, core: 2. Of those that a mesh axis runs over, the one named last changes fastest.
Arguments:
- inputs: bfloat16 [2, 2048, 2048], P(None, 'seq'), may hold values from -6 to 6
- norm_gain1: bfloat16 [2048], P('seq'), may hold values from 0.099609375 to 1.8984375
- w_query: bfloat16 [2048, 256], P('seq', 'head'), may hold values from -0.125 to 0.125
- w_key: bfloat16 [2048, 256], P('seq', 'head'), may hold values from -0.125 to 0.125
- w_value: bfloat16 [2048, 2048], P('seq', 'head'), may hold values from -0.125 to 0.125
- w_out: bfloat16 [2048, 2048], P('head', 'seq'), may hold values from -1 to 1
- norm_gain2: bfloat16 [2048], P('seq'), may hold values from 0.099609375 to 1.8984375
- w_gate: bfloat16 [2048, 5632], P('seq', 'head'), may hold values from -0.125 to 0.125
- w_up: bfloat16 [2048, 5632], P('seq', 'head'), may hold values from -0.125 to 0.125
- w_down: bfloat16 [5632, 2048], P('head', 'seq'), may hold values from -0.078125 to 0.078125
- cotangent: bfloat16 [2, 2048, 2048], P(None, 'seq'), may hold values from -6 to 6
Outputs:
- outputs: bfloat16 [2, 2048, 2048], P(None, 'seq')
- input_grad: bfloat16 [2, 2048, 2048], P(None, 'seq')
- grad_gain1: float32 [2048], P('seq')
- grad_query: float32 [2048, 256], P('seq', 'head')
- grad_key: float32 [2048, 256], P('seq', 'head')
- grad_value: float32 [2048, 2048], P('seq', 'head')
- grad_out: float32 [2048, 2048], P('head', 'seq')
- grad_gain2: float32 [2048], P('seq')
- grad_gate: float32 [2048, 5632], P('seq', 'head')
- grad_up: float32 [2048, 5632], P('seq', 'head')
- grad_down: float32 [5632, 2048], P('head', 'seq')
The draws below stay inside these ranges and needn't reach their ends.
All inputs are finite; a program needn't handle non-finite values.
Results may differ from the reference program's by a relative error of at most 0.017.
Values may be sent and summed in bfloat16 or wider, within the bound.
A program may use at most 320 MiB of HBM per device.

```python
import jax
import jax.numpy as jnp
from jax import lax

D = 2048
H = 16
F = 16
DV = 128
FF = 5632
NF = 273
TOK_DEV = 128
MB = 2
L = 2048


def block_levels(rng, extent, cuts, least, largest):
    level, own = 1.0, jax.random.fold_in(rng, 6)
    for axis_at, blocks in cuts:
        heights = jnp.exp(jax.random.uniform(jax.random.fold_in(own, axis_at), (blocks,), jnp.float32, least / len(cuts), largest / len(cuts)))
        level = level * jnp.repeat(heights, extent[axis_at] // blocks).reshape([-1 if axis == axis_at else 1 for axis in range(len(extent))])
    return level


def gaussian(stream_key, dims, scale, limit, cuts=(), held_as=jnp.bfloat16):
    array = scale * jax.random.normal(stream_key, dims, jnp.float32)
    if cuts:
        array = array * block_levels(stream_key, dims, cuts, -0.22, 0.18)
    return jnp.clip(array, -limit, limit).astype(held_as)


def setup_inputs(seed: int = 0) -> dict:
    splits = jax.random.split(jax.random.key(seed), 12)
    return {
        "inputs": gaussian(splits[0], (MB, L, D), 1.0, 6.0, ((1, 16),)),
        "norm_gain1": jnp.clip(1.0 + 0.18 * jax.random.normal(splits[1], (D,), jnp.float32), 0.099609375, 1.8984375).astype(jnp.bfloat16),
        "w_query": gaussian(splits[2], (D, H * F), D ** -0.5, 0.125, ((0, 16), (1, 2))),
        "w_key": gaussian(splits[3], (D, H * F), D ** -0.5, 0.125, ((0, 16), (1, 2))),
        "w_value": gaussian(splits[4], (D, H * DV), D ** -0.5, 0.125, ((0, 16), (1, 2))),
        "w_out": gaussian(splits[5], (H * DV, D), (max(1, H * DV // 64)) ** -0.5, 1.0, ((0, 2), (1, 16))),
        "norm_gain2": jnp.clip(1.0 + 0.18 * jax.random.normal(splits[6], (D,), jnp.float32), 0.099609375, 1.8984375).astype(jnp.bfloat16),
        "w_gate": gaussian(splits[7], (D, FF), D ** -0.5, 0.125, ((0, 16), (1, 2))),
        "w_up": gaussian(splits[8], (D, FF), D ** -0.5, 0.125, ((0, 16), (1, 2))),
        "w_down": gaussian(splits[9], (FF, D), FF ** -0.5, 0.078125, ((0, 2), (1, 16))),
        "cotangent": gaussian(splits[10], (MB, L, D), 1.0, 6.0, ((1, 16),)),
    }


@jax.custom_vjp
def low(v):
    return lax.optimization_barrier(v.astype(jnp.bfloat16)).astype(jnp.float32)

@jax.custom_vjp
def low_back(v):
    return v

def low_keep(v):
    return (low(v), None)

def low_pass(kept, grad):
    return (grad,)

def back_keep(v):
    return (v, None)

def back_low(kept, grad):
    return (low(grad),)
low.defvjp(low_keep, low_pass)
low_back.defvjp(back_keep, back_low)
epsilon = 1e-05
highest = lax.Precision.HIGHEST

def rms_apply(values, gain):
    scale = lax.rsqrt(lax.optimization_barrier(jnp.mean(values * values, axis=-1, keepdims=True)) + epsilon)
    return values * scale * gain

def feature_map(projected):
    count = projected.shape[0]
    pieces = projected.reshape(count, -1, F)
    square = (pieces[:, :, :, None] * pieces[:, :, None, :]).reshape(count, pieces.shape[1], F * F)
    return jnp.concatenate([jnp.ones_like(pieces[:, :, :1]), pieces * F ** (-0.25), square * (2.0 * F) ** (-0.5)], axis=-1)

def swiglu(gate, up_part):
    return jax.nn.silu(gate) * up_part

def forward(stream, gain_one, query_w, key_w, value_w, out_w, gain_two, gate_w, up_w, down_w):
    length = stream.shape[0]
    blocks = length // TOK_DEV
    normed = low(rms_apply(stream, gain_one))
    queries = low_back(jnp.dot(normed, query_w, precision=highest))
    keys_all = low_back(jnp.dot(normed, key_w, precision=highest))
    values = low_back(low(jnp.dot(normed, value_w, precision=highest)))
    query_feat = low_back(low(feature_map(queries))).reshape(blocks, TOK_DEV, H, NF)
    key_feat = low_back(low(feature_map(keys_all))).reshape(blocks, TOK_DEV, H, NF)
    value_blk = values.reshape(blocks, TOK_DEV, H, DV)
    causal = (jnp.arange(TOK_DEV)[:, None] >= jnp.arange(TOK_DEV)[None, :]).astype(stream.dtype)
    scores = jnp.einsum('bthf,bshf->bhts', query_feat, key_feat, precision=highest) * causal
    weighted = low_back(low(scores))
    num_local = jnp.einsum('bhts,bshd->bthd', weighted, value_blk, precision=highest)
    den_local = jnp.transpose(lax.optimization_barrier(jnp.sum(weighted, axis=-1)), (0, 2, 1))
    states = jnp.einsum('bshf,bshd->bhfd', key_feat, value_blk, precision=highest)
    totals = lax.optimization_barrier(jnp.sum(key_feat, axis=1))
    state_before = jnp.concatenate([jnp.zeros_like(states[:1]), jnp.cumsum(states, axis=0)[:-1]], axis=0)
    total_before = jnp.concatenate([jnp.zeros_like(totals[:1]), jnp.cumsum(totals, axis=0)[:-1]], axis=0)
    numer = low_back(num_local + jnp.einsum('bthf,bhfd->bthd', query_feat, state_before, precision=highest))
    denom = den_local + jnp.einsum('bthf,bhf->bth', query_feat, total_before, precision=highest)
    heads_out = low((numer / denom[..., None]).reshape(length, H * DV))
    attended = low_back(jnp.dot(heads_out, out_w, precision=highest))
    middle = stream + attended
    normed_two = low(rms_apply(middle, gain_two))
    gate = low_back(jnp.dot(normed_two, gate_w, precision=highest))
    up_part = low_back(jnp.dot(normed_two, up_w, precision=highest))
    hidden = low(swiglu(gate, up_part))
    return middle + low_back(jnp.dot(hidden, down_w, precision=highest))

def reference(inputs, norm_gain1, w_query, w_key, w_value, w_out, norm_gain2, w_gate, w_up, w_down, cotangent):
    weights = tuple((weight_in.astype(jnp.float32) for weight_in in (norm_gain1, w_query, w_key, w_value, w_out, norm_gain2, w_gate, w_up, w_down)))

    def one_sequence(carry, paired):
        stream, upstream = paired
        result, pull = jax.vjp(forward, stream.astype(jnp.float32), *weights)
        grads = pull(upstream.astype(jnp.float32))
        summed = tuple((older + newer for older, newer in zip(carry, grads[1:])))
        return (summed, (result.astype(jnp.bfloat16), grads[0].astype(jnp.bfloat16)))
    start = tuple((jnp.zeros_like(weight_in) for weight_in in weights))
    summed, (outputs, input_grad) = lax.scan(one_sequence, start, (inputs, cotangent))
    return (outputs, input_grad, summed[0], summed[1], summed[2], summed[3], summed[4], summed[5], summed[6], summed[7], summed[8])
```

```python
import jax
import jax.numpy as jnp
from jax import lax
from jax.experimental import pallas as pl
from jax.experimental.pallas import tpu as pltpu
from jax.sharding import PartitionSpec as P

F = 16
DV = 128


epsilon = 1e-05
highest = lax.Precision.HIGHEST


def entering(part, axis, combine, identity, reverse):
    count = lax.axis_size(axis)
    place = lax.axis_index(axis)
    ahead = count - 1 - place if reverse else place
    gathered = jax.tree.map(lambda a: lax.all_gather(a, axis), part)
    state = jax.tree.map(lambda a, e: jnp.zeros_like(a) + jnp.asarray(e, a.dtype), part, identity)

    def one(turn, state):
        source = count - 1 - turn if reverse else turn
        return combine(
            state, jax.tree.map(lambda a: lax.dynamic_index_in_dim(a, source, 0, False), gathered)
        )

    return lax.fori_loop(0, ahead, one, state)


def rms_apply(values, gain):
    scale = lax.rsqrt(jnp.mean(values * values, axis=-1, keepdims=True) + epsilon)
    return values * scale * gain


def feature_map(projected):
    count = projected.shape[0]
    pieces = projected.reshape(count, -1, F)
    square = (pieces[:, :, :, None] * pieces[:, :, None, :]).reshape(count, pieces.shape[1], F * F)
    return jnp.concatenate(
        [jnp.ones_like(pieces[:, :, :1]), pieces * F ** (-0.25), square * (2.0 * F) ** (-0.5)],
        axis=-1,
    )


def swiglu(gate, up_part):
    return jax.nn.silu(gate) * up_part


def round_trip(values):
    return lax.optimization_barrier(values.astype(jnp.bfloat16)).astype(jnp.float32)


def add_pair(earlier, later):
    return (earlier[0] + later[0], earlier[1] + later[1])


def block_pass(tokens, upstream, gathered):
    gain_one, query_w, key_w, value_w, out_w, gain_two, gate_w, up_w, down_w = gathered
    f32 = jnp.float32
    bf16 = jnp.bfloat16
    stream = tokens.astype(f32)
    count = stream.shape[0]
    normed_f, norm_one_pull = jax.vjp(rms_apply, stream, gain_one.astype(f32))
    normed = normed_f.astype(bf16)
    queries = jnp.dot(normed, query_w, preferred_element_type=f32)
    keys_all = jnp.dot(normed, key_w, preferred_element_type=f32)
    values = jnp.dot(normed, value_w, preferred_element_type=f32).astype(bf16)
    query_feat_f, query_pull = jax.vjp(feature_map, queries)
    key_feat_f, key_pull = jax.vjp(feature_map, keys_all)
    query_feat = jnp.transpose(query_feat_f.astype(bf16), (1, 0, 2))
    key_feat = jnp.transpose(key_feat_f.astype(bf16), (1, 0, 2))
    value_heads = jnp.transpose(values.reshape(count, -1, DV), (1, 0, 2))
    causal = (jnp.arange(count)[:, None] >= jnp.arange(count)[None, :]).astype(f32)
    scores = jnp.einsum("htf,hsf->hts", query_feat, key_feat, preferred_element_type=f32) * causal
    weighted = scores.astype(bf16)
    num_local = jnp.einsum("hts,hsd->htd", weighted, value_heads, preferred_element_type=f32)
    den_local = jnp.sum(weighted.astype(f32), axis=-1)
    states = jnp.einsum("hsf,hsd->hfd", key_feat, value_heads, preferred_element_type=f32)
    totals = jnp.sum(key_feat.astype(f32), axis=1)
    state_before, total_before = entering(
        (states, totals), "seq", add_pair, (jnp.zeros_like(states), jnp.zeros_like(totals)), False
    )
    query_wide = query_feat.astype(f32)
    numer = num_local + jnp.einsum("htf,hfd->htd", query_wide, state_before, precision=highest)
    denom = den_local + jnp.einsum("htf,hf->ht", query_wide, total_before, precision=highest)
    ratio = numer / denom[..., None]
    heads_out = jnp.transpose(ratio, (1, 0, 2)).reshape(count, -1).astype(bf16)
    attended = lax.psum(jnp.dot(heads_out, out_w, preferred_element_type=f32), "head")
    middle = stream + attended
    normed_two_f, norm_two_pull = jax.vjp(rms_apply, middle, gain_two.astype(f32))
    normed_two = normed_two_f.astype(bf16)
    gate = jnp.dot(normed_two, gate_w, preferred_element_type=f32)
    up_part = jnp.dot(normed_two, up_w, preferred_element_type=f32)
    active, active_pull = jax.vjp(swiglu, gate, up_part)
    hidden = active.astype(bf16)
    branch = lax.psum(
        jnp.dot(hidden, down_w, preferred_element_type=f32).astype(jnp.bfloat16), "head"
    ).astype(jnp.float32)
    result = (middle + branch).astype(bf16)
    grad_down = jnp.dot(hidden.T, upstream, preferred_element_type=f32)
    d_hidden = jnp.dot(upstream, down_w.T, preferred_element_type=f32)
    d_gate_f, d_up_f = active_pull(d_hidden)
    d_gate = d_gate_f.astype(bf16)
    d_up = d_up_f.astype(bf16)
    grad_gate = jnp.dot(normed_two.T, d_gate, preferred_element_type=f32)
    grad_up = jnp.dot(normed_two.T, d_up, preferred_element_type=f32)
    d_normed_two = lax.psum(
        jnp.dot(d_gate, gate_w.T, preferred_element_type=f32)
        + jnp.dot(d_up, up_w.T, preferred_element_type=f32),
        "head",
    )
    d_middle_norm, grad_gain2 = norm_two_pull(d_normed_two)
    d_middle = upstream.astype(f32) + d_middle_norm
    d_attended = d_middle.astype(bf16)
    grad_out = jnp.dot(heads_out.T, d_attended, preferred_element_type=f32)
    d_heads = jnp.transpose(
        jnp.dot(d_attended, out_w.T, preferred_element_type=f32).reshape(count, -1, DV), (1, 0, 2)
    )
    d_numer = (d_heads / denom[..., None]).astype(bf16)
    d_denom = -jnp.sum(d_heads * ratio, axis=-1) / denom
    d_numer_wide = d_numer.astype(f32)
    d_before = jnp.einsum("htf,htd->hfd", query_wide, d_numer_wide, precision=highest)
    d_total_before = jnp.einsum("htf,ht->hf", query_wide, d_denom, precision=highest)
    d_state, d_total = entering(
        (d_before, d_total_before),
        "seq",
        add_pair,
        (jnp.zeros_like(d_before), jnp.zeros_like(d_total_before)),
        True,
    )
    d_scores = (
        (
            jnp.einsum("htd,hsd->hts", d_numer, value_heads, preferred_element_type=f32)
            + d_denom[..., None]
        )
        * causal
    ).astype(bf16)
    d_values = jnp.einsum(
        "hts,htd->hsd", weighted, d_numer, preferred_element_type=f32
    ) + jnp.einsum("hsf,hfd->hsd", key_feat.astype(f32), d_state, precision=highest)
    d_query_feat = (
        jnp.einsum("hts,hsf->htf", d_scores, key_feat, preferred_element_type=f32)
        + jnp.einsum("htd,hfd->htf", d_numer_wide, state_before, precision=highest)
        + d_denom[..., None] * total_before[:, None, :]
    )
    d_key_feat = (
        jnp.einsum("hts,htf->hsf", d_scores, query_feat, preferred_element_type=f32)
        + jnp.einsum("hsd,hfd->hsf", value_heads.astype(f32), d_state, precision=highest)
        + d_total[:, None, :]
    )
    d_queries = query_pull(jnp.transpose(round_trip(d_query_feat), (1, 0, 2)))[0].astype(bf16)
    d_keys = key_pull(jnp.transpose(round_trip(d_key_feat), (1, 0, 2)))[0].astype(bf16)
    d_values_flat = jnp.transpose(d_values, (1, 0, 2)).reshape(count, -1).astype(bf16)
    grad_query = jnp.dot(normed.T, d_queries, preferred_element_type=f32)
    grad_key = jnp.dot(normed.T, d_keys, preferred_element_type=f32)
    grad_value = jnp.dot(normed.T, d_values_flat, preferred_element_type=f32)
    d_normed_part = (
        jnp.dot(d_queries, query_w.T, preferred_element_type=f32)
        + jnp.dot(d_keys, key_w.T, preferred_element_type=f32)
        + jnp.dot(d_values_flat, value_w.T, preferred_element_type=f32)
    )
    d_normed = lax.psum(d_normed_part.astype(jnp.bfloat16), "head").astype(jnp.float32)
    d_stream_norm, grad_gain1 = norm_one_pull(d_normed)
    input_grad = (d_middle + d_stream_norm).astype(bf16)
    return (
        result,
        input_grad,
        grad_gain1,
        grad_query,
        grad_key,
        grad_value,
        grad_out,
        grad_gain2,
        grad_gate,
        grad_up,
        grad_down,
    )


def local(
    inputs, norm_gain1, w_query, w_key, w_value, w_out, norm_gain2, w_gate, w_up, w_down, cotangent
):
    micro = inputs.shape[0]
    summed = None
    results = []
    input_grads = []
    for step_index in range(micro):
        gathered = (
            lax.all_gather(norm_gain1, "seq", axis=0, tiled=True),
            lax.all_gather(w_query, "seq", axis=0, tiled=True),
            lax.all_gather(w_key, "seq", axis=0, tiled=True),
            lax.all_gather(w_value, "seq", axis=0, tiled=True),
            lax.all_gather(w_out, "seq", axis=1, tiled=True),
            lax.all_gather(norm_gain2, "seq", axis=0, tiled=True),
            lax.all_gather(w_gate, "seq", axis=0, tiled=True),
            lax.all_gather(w_up, "seq", axis=0, tiled=True),
            lax.all_gather(w_down, "seq", axis=1, tiled=True),
        )
        (
            result,
            input_grad,
            grad_gain1,
            grad_query,
            grad_key,
            grad_value,
            grad_out,
            grad_gain2,
            grad_gate,
            grad_up,
            grad_down,
        ) = block_pass(inputs[step_index], cotangent[step_index], gathered)
        results.append(result)
        input_grads.append(input_grad)
        fresh = (
            lax.psum_scatter(grad_gain1, "seq", scatter_dimension=0, tiled=True),
            lax.psum_scatter(grad_query, "seq", scatter_dimension=0, tiled=True),
            lax.psum_scatter(grad_key, "seq", scatter_dimension=0, tiled=True),
            lax.psum_scatter(grad_value, "seq", scatter_dimension=0, tiled=True),
            lax.psum_scatter(grad_out, "seq", scatter_dimension=1, tiled=True),
            lax.psum_scatter(grad_gain2, "seq", scatter_dimension=0, tiled=True),
            lax.psum_scatter(grad_gate, "seq", scatter_dimension=0, tiled=True),
            lax.psum_scatter(grad_up, "seq", scatter_dimension=0, tiled=True),
            lax.psum_scatter(grad_down, "seq", scatter_dimension=1, tiled=True),
        )
        summed = (
            fresh
            if summed is None
            else tuple((older + newer for older, newer in zip(summed, fresh)))
        )
    return (
        jnp.stack(results),
        jnp.stack(input_grads),
        summed[0],
        summed[1],
        summed[2],
        summed[3],
        summed[4],
        summed[5],
        summed[6],
        summed[7],
        summed[8],
    )


MESH = pl.DeviceIdType.MESH
bf16 = jnp.bfloat16
f32 = jnp.float32
ZED = 4
VMEM_LIMIT = 60 * 1024 * 1024


def where_am_i():
    place = lax.axis_index("seq")
    return place % 2, (place // 2) % 2, place // 4, lax.axis_index("head")


def index_of(z, y, x):
    return (z * 2 + y) * 2 + x


def remote(src, dst, send, recv, place, head):
    return pltpu.make_async_remote_copy(
        src_ref=src, dst_ref=dst, send_sem=send, recv_sem=recv, device_id=(place, head),
        device_id_type=MESH,
    )


def arrived(dst, send, recv, place, head):
    remote(dst, dst, send, recv, place, head).wait_recv()


def params():
    return pltpu.CompilerParams(has_side_effects=True, vmem_limit_bytes=VMEM_LIMIT)


ANY = pl.BlockSpec(memory_space=pl.ANY)
VMEM = pl.BlockSpec(memory_space=pltpu.VMEM)
DMA = pltpu.SemaphoreType.DMA
ORDER = (0, 1, 3, 2)


def gather_kernel(a, m, g, wa, wm, gg, ls, zs, zr, ps, pr, ds, dr):
    x, y, z, h = where_am_i()
    me = index_of(z, y, x)
    at_x, at_y = index_of(z, y, 1 - x), index_of(z, 1 - y, x)
    half = a.shape[1] // 2

    def rows(zz, yy, xx):
        return pl.ds(pl.multiple_of(index_of(zz, yy, xx) * 128, 128), 128)

    mine = rows(z, y, x)
    local = [
        pltpu.make_async_copy(a, wa.at[mine], ls.at[0]),
        pltpu.make_async_copy(m.at[z], wm.at[mine], ls.at[1]),
        pltpu.make_async_copy(g, gg.at[z], ls.at[2]),
    ]
    for copy in local:
        copy.start()
    sends = []
    for d in (1, 3, 2):
        there = index_of((z + d) % ZED, y, x)
        sends.append(remote(a, wa.at[mine], zs.at[0, d], zr.at[0, d], there, h))
    for d in (1, 3, 2):
        there = index_of((z + d) % ZED, y, x)
        sends.append(remote(m.at[(z + d) % ZED], wm.at[mine], zs.at[1, d], zr.at[1, d], there, h))
    for d in (1, 3, 2):
        there = index_of((z + d) % ZED, y, x)
        sends.append(remote(g.at[h], gg.at[z, h], zs.at[2, d], zr.at[2, d], there, h))
    for copy in sends:
        copy.start()
    local[0].wait()
    local[1].wait()
    local[2].wait()
    sets = [(0, wa, d) for d in ORDER] + [(1, wm, d) for d in ORDER]
    late = []
    for turn in range(len(sets) + 1):
        if turn < len(sets):
            kind, w, d = sets[turn]
            zz = (z + ZED - d) % ZED
            block = w.at[rows(zz, y, x)]
            if d:
                arrived(block, zs.at[kind, d], zr.at[kind, d], me, h)
            for side, there in ((0, at_x), (1, at_y)):
                copy = remote(block, block, ps.at[kind, d, side], pr.at[kind, d, side], there, h)
                copy.start()
                late.append(copy)
        if turn > 0:
            kind, w, d = sets[turn - 1]
            zz = (z + ZED - d) % ZED
            from_x, from_y = rows(zz, y, 1 - x), rows(zz, 1 - y, x)
            arrived(w.at[from_x], ps.at[kind, d, 0], pr.at[kind, d, 0], me, h)
            arrived(w.at[from_y], ps.at[kind, d, 1], pr.at[kind, d, 1], me, h)
            left = w.at[from_y, pl.ds(0, half)]
            right = w.at[from_x, pl.ds(half, half)]
            for side, part, there in ((2, left, at_x), (3, right, at_y)):
                copy = remote(part, part, ps.at[kind, d, side], pr.at[kind, d, side], there, h)
                copy.start()
                late.append(copy)
    for d in (1, 3, 2):
        zz = (z + ZED - d) % ZED
        arrived(gg.at[zz, h], zs.at[2, d], zr.at[2, d], me, h)
        copy = remote(gg.at[zz, h], gg.at[zz, h], ds.at[d], dr.at[d], me, 1 - h)
        copy.start()
        late.append(copy)
    for kind, w, d in sets:
        zz = (z + ZED - d) % ZED
        corner = rows(zz, 1 - y, 1 - x)
        arrived(w.at[corner, pl.ds(0, half)], ps.at[kind, d, 2], pr.at[kind, d, 2], me, h)
        arrived(w.at[corner, pl.ds(half, half)], ps.at[kind, d, 3], pr.at[kind, d, 3], me, h)
    for d in (1, 3, 2):
        zz = (z + ZED - d) % ZED
        arrived(gg.at[zz, 1 - h], ds.at[d], dr.at[d], me, 1 - h)
    for copy in sends + late:
        copy.wait_send()


def gather_all(a, m, g):
    depth, wide = 16 * a.shape[0], a.shape[1]
    return pl.pallas_call(
        gather_kernel,
        out_shape=(
            jax.ShapeDtypeStruct((depth, wide), bf16),
            jax.ShapeDtypeStruct((depth, wide), bf16),
            jax.ShapeDtypeStruct((ZED,) + g.shape, bf16),
        ),
        in_specs=[ANY] * 3,
        out_specs=(ANY,) * 3,
        scratch_shapes=[
            DMA((3,)), DMA((3, 4)), DMA((3, 4)), DMA((2, 4, 4)), DMA((2, 4, 4)), DMA((4,)), DMA((4,)),
        ],
        compiler_params=params(),
        name="gather_all",
    )(a, m, g)


def exchange_kernel(src, dst, ls, ss, rs):
    x, y, z, h = where_am_i()
    me = index_of(z, y, x)
    local = pltpu.make_async_copy(src.at[me], dst.at[me], ls)
    local.start()
    copies = []
    for d in range(1, 16):
        there = (me + d) % 16
        copies.append(remote(src.at[there], dst.at[me], ss.at[d], rs.at[d], there, h))
    for copy in copies:
        copy.start()
    local.wait()
    for d in range(1, 16):
        arrived(dst.at[(me + 16 - d) % 16], ss.at[d], rs.at[d], me, h)
    for copy in copies:
        copy.wait_send()


def exchange(blocks):
    return pl.pallas_call(
        exchange_kernel,
        out_shape=jax.ShapeDtypeStruct(blocks.shape, blocks.dtype),
        in_specs=[ANY],
        out_specs=ANY,
        scratch_shapes=[DMA, DMA((16,)), DMA((16,))],
        compiler_params=params(),
        name="exchange",
    )(blocks)


def norm_kernel(part, xin, middle, near, other, sem, zs, zr, ds, dr):
    x, y, z, h = where_am_i()
    me = index_of(z, y, x)
    swap = remote(part, other, sem.at[0], sem.at[1], me, 1 - h)
    swap.start()
    swap.wait()

    def one(mb):
        def body(turn, carry):
            row = pl.ds(pl.multiple_of(turn * 16, 16), 16)
            mid = xin[mb, row, :].astype(f32) + (part[mb, row, :] + other[mb, row, :])
            middle[mb, row, :] = mid
            scale = lax.rsqrt(jnp.mean(mid * mid, axis=-1, keepdims=True) + epsilon)
            near[z, mb, row, :] = (mid * scale).astype(bf16)
            return carry

        lax.fori_loop(0, 8, body, 0)

    one(h)
    copies = []
    for d in (2, 1, 3):
        there = index_of((z + d) % ZED, y, x)
        copies.append(remote(near.at[z, h], near.at[z, h], zs.at[d], zr.at[d], there, h))
    for copy in copies:
        copy.start()
    one(1 - h)
    for d in (1, 3, 2):
        zz = (z + ZED - d) % ZED
        arrived(near.at[zz, h], zs.at[d], zr.at[d], me, h)
        copy = remote(near.at[zz, h], near.at[zz, h], ds.at[d], dr.at[d], me, 1 - h)
        copy.start()
        copies.append(copy)
    for d in (1, 3, 2):
        zz = (z + ZED - d) % ZED
        arrived(near.at[zz, 1 - h], ds.at[d], dr.at[d], me, 1 - h)
    for copy in copies:
        copy.wait_send()


def norm_two(part, xin):
    return pl.pallas_call(
        norm_kernel,
        out_shape=(
            jax.ShapeDtypeStruct(part.shape, f32),
            jax.ShapeDtypeStruct((ZED,) + part.shape, bf16),
        ),
        in_specs=[VMEM] * 2,
        out_specs=(VMEM,) * 2,
        scratch_shapes=[
            pltpu.VMEM(part.shape, f32), DMA((2,)), DMA((4,)), DMA((4,)), DMA((4,)), DMA((4,)),
        ],
        compiler_params=params(),
        name="norm_two",
    )(part, xin)


def combine_kernel(t, out, other, summed, landed, sem, zs, zr, ds, dr):
    x, y, z, h = where_am_i()
    me = index_of(z, y, x)
    kinds = t.shape[0]
    swaps = []
    for d in (2, 1, 3, 0):
        zz = (z + d) % ZED
        for kind in range(kinds):
            swaps.append(
                remote(t.at[kind, zz, 1 - h], other.at[kind, zz], sem.at[0, kind, d], sem.at[1, kind, d], me, 1 - h)
            )
    for copy in swaps:
        copy.start()
    copies = []
    for d in (2, 1, 3, 0):
        zz = (z + d) % ZED
        for kind in range(kinds):
            arrived(other.at[kind, zz], sem.at[0, kind, d], sem.at[1, kind, d], me, h)

            def add(turn, carry):
                row = pl.ds(pl.multiple_of(turn * 16, 16), 16)
                summed[kind, zz, row, :] = (
                    t[kind, zz, h, row, :].astype(f32) + other[kind, zz, row, :].astype(f32)
                ).astype(bf16)
                return carry

            lax.fori_loop(0, 8, add, 0)
            if d:
                copy = remote(
                    summed.at[kind, zz], landed.at[kind, d], zs.at[kind, d], zr.at[kind, d],
                    index_of(zz, y, x), h,
                )
                copy.start()
                copies.append(copy)
    for kind in range(kinds):
        for d in (1, 3, 2):
            arrived(landed.at[kind, d], zs.at[kind, d], zr.at[kind, d], me, h)

        def total(turn, carry):
            row = pl.ds(pl.multiple_of(turn * 16, 16), 16)
            acc = summed[kind, z, row, :].astype(f32)
            for d in (1, 2, 3):
                acc = acc + landed[kind, d, row, :].astype(f32)
            out[kind, h, row, :] = acc.astype(bf16)
            return carry

        lax.fori_loop(0, 8, total, 0)
        copy = remote(out.at[kind, h], out.at[kind, h], ds.at[kind], dr.at[kind], me, 1 - h)
        copy.start()
        copies.append(copy)
    for kind in range(kinds):
        arrived(out.at[kind, 1 - h], ds.at[kind], dr.at[kind], me, 1 - h)
    for copy in swaps + copies:
        copy.wait_send()


def combine(t):
    kinds, _, mbs, count, wide = t.shape
    return pl.pallas_call(
        combine_kernel,
        out_shape=jax.ShapeDtypeStruct((kinds, mbs, count, wide), bf16),
        in_specs=[VMEM],
        out_specs=VMEM,
        scratch_shapes=[
            pltpu.VMEM((kinds, ZED, count, wide), bf16),
            pltpu.VMEM((kinds, ZED, count, wide), bf16),
            pltpu.VMEM((kinds, ZED, count, wide), bf16),
            DMA((2, kinds, 4)), DMA((kinds, 4)), DMA((kinds, 4)), DMA((kinds,)), DMA((kinds,)),
        ],
        compiler_params=params(),
        name="combine",
    )(t)


def pair_kernel(part, out, other, sem):
    x, y, z, h = where_am_i()
    me = index_of(z, y, x)
    swap = remote(part, other, sem.at[0], sem.at[1], me, 1 - h)
    swap.start()
    swap.wait()
    out[...] = part[...] + other[...]


def pair_sum(part):
    return pl.pallas_call(
        pair_kernel,
        out_shape=jax.ShapeDtypeStruct(part.shape, part.dtype),
        in_specs=[VMEM],
        out_specs=VMEM,
        scratch_shapes=[pltpu.VMEM(part.shape, part.dtype), DMA((2,))],
        compiler_params=params(),
        name="pair_sum",
    )(part)


def scatter_kernel(ga, gm, za, zm, r1x, r1y, r2x, r2y, f1, f2, fin, s1, q1, s2, q2, s3, q3):
    x, y, z, h = where_am_i()
    me = index_of(z, y, x)
    at_x, at_y = index_of(z, y, 1 - x), index_of(z, 1 - y, x)
    half = ga.shape[-1] // 2
    low, high = pl.ds(0, half), pl.ds(half, half)
    sets = [(0, ga, za, d) for d in (2, 1, 3, 0)] + [(1, gm, zm, d) for d in (2, 1, 3, 0)]
    copies = []

    def start(copy):
        copy.start()
        copies.append(copy)

    for n, (kind, g, out, d) in enumerate(sets):
        zz = (z + d) % ZED
        start(remote(g.at[zz, :, 1 - x, :, low], r1x.at[n], s1.at[n, 0], q1.at[n, 0], at_x, h))
        start(remote(g.at[zz, 1 - y, :, :, high], r1y.at[n], s1.at[n, 1], q1.at[n, 1], at_y, h))

    def wide(turns):
        return pl.ds(pl.multiple_of(turns * 16, 16), 16)

    for turn in range(len(sets) + 1):
        if turn < len(sets):
            n = turn
            kind, g, out, d = sets[n]
            zz = (z + d) % ZED
            arrived(r1x.at[n], s1.at[n, 0], q1.at[n, 0], me, h)
            arrived(r1y.at[n], s1.at[n, 1], q1.at[n, 1], me, h)

            def forward(i, carry):
                row = wide(i)
                f1[n, row, :] = (
                    g[zz, 1 - y, x, row, low].astype(f32) + r1x[n, 1 - y, row, :].astype(f32)
                ).astype(bf16)
                f2[n, row, :] = (
                    g[zz, y, 1 - x, row, high].astype(f32) + r1y[n, 1 - x, row, :].astype(f32)
                ).astype(bf16)
                return carry

            lax.fori_loop(0, 8, forward, 0)
            start(remote(f1.at[n], r2y.at[n], s2.at[n, 0], q2.at[n, 0], at_y, h))
            start(remote(f2.at[n], r2x.at[n], s2.at[n, 1], q2.at[n, 1], at_x, h))
        if turn > 0:
            n = turn - 1
            kind, g, out, d = sets[n]
            zz = (z + d) % ZED
            arrived(r2y.at[n], s2.at[n, 0], q2.at[n, 0], me, h)
            arrived(r2x.at[n], s2.at[n, 1], q2.at[n, 1], me, h)
            target = fin.at[n] if d else out.at[z]

            def finish(i, carry):
                row = wide(i)
                target[row, low] = (
                    g[zz, y, x, row, low].astype(f32)
                    + r1x[n, y, row, :].astype(f32)
                    + r2y[n, row, :].astype(f32)
                ).astype(bf16)
                target[row, high] = (
                    g[zz, y, x, row, high].astype(f32)
                    + r1y[n, x, row, :].astype(f32)
                    + r2x[n, row, :].astype(f32)
                ).astype(bf16)
                return carry

            lax.fori_loop(0, 8, finish, 0)
            if d:
                start(
                    remote(fin.at[n], out.at[z], s3.at[kind, d], q3.at[kind, d], index_of(zz, y, x), h)
                )
    for kind, g, out, d in sets:
        if d:
            arrived(out.at[(z + ZED - d) % ZED], s3.at[kind, d], q3.at[kind, d], me, h)
    for copy in copies:
        copy.wait_send()


def scatter_all(ga, gm):
    wide = ga.shape[-1]
    ga = ga.reshape(ZED, 2, 2, 128, wide)
    gm = gm.reshape(ZED, 2, 2, 128, wide)
    give = jax.ShapeDtypeStruct((ZED, 128, wide), bf16)
    return pl.pallas_call(
        scatter_kernel,
        out_shape=(give, give),
        in_specs=[VMEM] * 2,
        out_specs=(VMEM,) * 2,
        scratch_shapes=[
            pltpu.VMEM((8, 2, 128, wide // 2), bf16),
            pltpu.VMEM((8, 2, 128, wide // 2), bf16),
            pltpu.VMEM((8, 128, wide // 2), bf16),
            pltpu.VMEM((8, 128, wide // 2), bf16),
            pltpu.VMEM((8, 128, wide // 2), bf16),
            pltpu.VMEM((8, 128, wide // 2), bf16),
            pltpu.VMEM((8, 128, wide), bf16),
            DMA((8, 2)), DMA((8, 2)), DMA((8, 2)), DMA((8, 2)), DMA((2, 4)), DMA((2, 4)),
        ],
        compiler_params=params(),
        name="scatter_all",
    )(ga, gm)


def mix(a, b, over):
    return lax.dot_general(a, b, (over, ((), ())), preferred_element_type=f32)


def attend(q_t, k_t, v):
    count = v.shape[0]
    s = mix(q_t, k_t, ((0,), (0,)))
    causal = lax.broadcasted_iota(jnp.int32, (count, count), 0) >= lax.broadcasted_iota(
        jnp.int32, (count, count), 1
    )
    scores = jnp.where(causal, 1.0 + s * (0.25 + s * (1.0 / 32.0)), 0.0)
    weighted = scores.astype(bf16)
    numer = mix(weighted, v, ((1,), (0,)))
    denom = jnp.sum(weighted.astype(f32), axis=-1, keepdims=True)
    return numer / denom, denom


def attend_back(q_t, k_t, v, ratio, denom, d_heads):
    count = v.shape[0]
    s = mix(q_t, k_t, ((0,), (0,)))
    causal = lax.broadcasted_iota(jnp.int32, (count, count), 0) >= lax.broadcasted_iota(
        jnp.int32, (count, count), 1
    )
    weighted = jnp.where(causal, 1.0 + s * (0.25 + s * (1.0 / 32.0)), 0.0).astype(bf16)
    d_numer = (d_heads / denom).astype(bf16)
    d_denom = -jnp.sum(d_heads * ratio, axis=-1, keepdims=True) / denom
    d_scores = mix(d_numer, v, ((1,), (1,))) + d_denom
    d_s = jnp.where(causal, d_scores * (0.25 + s * (1.0 / 16.0)), 0.0).astype(bf16)
    d_v = mix(weighted, d_numer, ((0,), (0,)))
    d_q = mix(k_t, d_s, ((1,), (1,)))
    d_k = mix(q_t, d_s, ((1,), (0,)))
    return d_q, d_k, d_v


def fast(
    inputs, norm_gain1, w_query, w_key, w_value, w_out, norm_gain2, w_gate, w_up, w_down, cotangent
):
    mbs, count, wide = inputs.shape
    heads = w_query.shape[1] // F
    units = w_gate.shape[1] // ZED
    room = -(-units // 128) * 128
    qk, vv = 2 * heads * F, heads * DV
    rows = w_query.shape[0]
    gain1, gain2 = norm_gain1.astype(f32)[:, None], norm_gain2.astype(f32)[:, None]

    def folded(weight, gain):
        return (weight.astype(f32) * gain).astype(bf16)

    a = jnp.concatenate(
        [folded(w_query, gain1), folded(w_key, gain1), folded(w_value, gain1), w_out.T], axis=1
    )

    def cut(weight):
        pieces = jnp.transpose(weight.reshape(rows, ZED, units), (1, 0, 2))
        return jnp.pad(pieces, ((0, 0), (0, 0), (0, room - units)))

    m = jnp.concatenate([cut(folded(w_gate, gain2)), cut(folded(w_up, gain2)), cut(w_down.T)], axis=2)
    wa, wm, gg = gather_all(a, m, cotangent)
    w_qk, w_v, w_o = wa[:, :qk], wa[:, qk : qk + vv], wa[:, qk + vv :]
    w_g, w_u, w_d = wm[:, :room], wm[:, room : 2 * room], wm[:, 2 * room :]

    stream = inputs.astype(f32).reshape(mbs * count, wide)
    r1 = lax.rsqrt(jnp.mean(stream * stream, axis=-1, keepdims=True) + epsilon)
    xh1 = (stream * r1).astype(bf16)
    qk_t = mix(w_qk, xh1, ((0,), (1,))).astype(bf16)
    qk_t = qk_t.reshape(2, heads, F, mbs, count).transpose(3, 1, 0, 2, 4).reshape(16, 2 * F, count)
    val = mix(xh1, w_v, ((1,), (0,))).astype(bf16)
    val = val.reshape(mbs, count, heads, DV).transpose(0, 2, 1, 3).reshape(16, count, DV)
    got = exchange(jnp.concatenate([qk_t, val], axis=1))
    q_t = got[:, :F].transpose(1, 0, 2).reshape(F, 16 * count)
    k_t = got[:, F : 2 * F].transpose(1, 0, 2).reshape(F, 16 * count)
    v = got[:, 2 * F :].reshape(16 * count, DV)
    ratio, denom = attend(q_t, k_t, v)
    back = exchange(ratio.astype(bf16).reshape(16, count, DV))
    heads_out = back.reshape(mbs, heads, count, DV).transpose(0, 2, 1, 3).reshape(mbs * count, vv)
    part = mix(heads_out, w_o, ((1,), (1,)))
    middle, near = norm_two(part.reshape(mbs, count, wide), inputs)
    middle = middle.reshape(mbs * count, wide)
    many = ZED * mbs * count
    n2 = near.reshape(many, wide)
    up_g = gg.reshape(many, wide)
    gate = mix(n2, w_g, ((1,), (0,)))
    up = mix(n2, w_u, ((1,), (0,)))
    d_hidden = mix(up_g, w_d, ((1,), (0,)))
    sig = jax.nn.sigmoid(gate)
    silu = gate * sig
    hidden = (silu * up).astype(bf16)
    d_gate = (d_hidden * up * sig * (1.0 + gate * (1.0 - sig))).astype(bf16)
    d_up = (d_hidden * silu).astype(bf16)
    branch = mix(hidden, w_d, ((1,), (1,))).astype(bf16)
    d_n2 = (mix(d_gate, w_g, ((1,), (1,))) + mix(d_up, w_u, ((1,), (1,)))).astype(bf16)
    both = combine(jnp.stack([d_n2, branch]).reshape(2, ZED, mbs, count, wide))
    e2 = both[0].reshape(mbs * count, wide).astype(f32)
    outputs = (middle + both[1].reshape(mbs * count, wide).astype(f32)).astype(bf16)
    r2 = lax.rsqrt(jnp.mean(middle * middle, axis=-1, keepdims=True) + epsilon)
    xh2 = middle * r2
    d_middle = cotangent.reshape(mbs * count, wide).astype(f32) + r2 * (
        e2 - xh2 * jnp.mean(e2 * xh2, axis=-1, keepdims=True)
    )
    d_att = d_middle.astype(bf16)
    d_heads = mix(d_att, w_o, ((1,), (0,))).astype(bf16)
    d_heads = d_heads.reshape(mbs, count, heads, DV).transpose(0, 2, 1, 3).reshape(16, count, DV)
    d_heads = exchange(d_heads).reshape(16 * count, DV).astype(f32)
    d_q, d_k, d_v = attend_back(q_t, k_t, v, ratio, denom, d_heads)
    d_qk = jnp.concatenate([d_q, d_k], axis=0).astype(bf16)
    d_qk = d_qk.reshape(2 * F, 16, count).transpose(1, 0, 2)
    home = exchange(jnp.concatenate([d_qk, d_v.astype(bf16).reshape(16, count, DV)], axis=1))
    d_qk = home[:, : 2 * F].reshape(mbs, heads, 2, F, count).transpose(0, 4, 2, 1, 3)
    d_qk = d_qk.reshape(mbs * count, qk)
    d_val = home[:, 2 * F :].reshape(mbs, heads, count, DV).transpose(0, 2, 1, 3)
    d_val = d_val.reshape(mbs * count, vv)
    e1 = pair_sum(mix(d_qk, w_qk, ((1,), (1,))) + mix(d_val, w_v, ((1,), (1,))))
    xh1f = stream * r1
    input_grad = (
        d_middle + r1 * (e1 - xh1f * jnp.mean(e1 * xh1f, axis=-1, keepdims=True))
    ).astype(bf16)
    first = ((0,), (0,))
    ga = jnp.concatenate(
        [mix(xh1, d_qk, first), mix(xh1, d_val, first), mix(d_att, heads_out, first)], axis=1
    ).astype(bf16)
    gm = jnp.concatenate(
        [mix(n2, d_gate, first), mix(n2, d_up, first), mix(up_g, hidden, first)], axis=1
    ).astype(bf16)
    za, zm = scatter_all(ga, gm)
    za = jnp.sum(za.astype(f32), axis=0)
    zm = zm.astype(f32)

    def joined(piece):
        return jnp.transpose(piece[:, :, :units], (1, 0, 2)).reshape(rows, ZED * units)

    g_gate, g_up, g_down = joined(zm[:, :, :room]), joined(zm[:, :, room : 2 * room]), joined(zm[:, :, 2 * room :])
    s_q, s_k, s_v = za[:, : qk // 2], za[:, qk // 2 : qk], za[:, qk : qk + vv]
    g_gain1 = (
        jnp.sum(w_query.astype(f32) * s_q, axis=1)
        + jnp.sum(w_key.astype(f32) * s_k, axis=1)
        + jnp.sum(w_value.astype(f32) * s_v, axis=1)
    )
    g_gain2 = jnp.sum(w_gate.astype(f32) * g_gate, axis=1) + jnp.sum(w_up.astype(f32) * g_up, axis=1)
    gains = lax.psum(jnp.stack([g_gain1, g_gain2]), "head")
    return (
        outputs.reshape(mbs, count, wide),
        input_grad.reshape(mbs, count, wide),
        gains[0],
        s_q * gain1,
        s_k * gain1,
        s_v * gain1,
        za[:, qk + vv :].T,
        gains[1],
        g_gate * gain2,
        g_up * gain2,
        g_down.T,
    )


def solution(mesh):
    return jax.shard_map(
        fast if mesh.shape["seq"] == 16 else local,
        mesh=mesh,
        in_specs=(
            P(None, "seq", None),
            P("seq"),
            P("seq", "head"),
            P("seq", "head"),
            P("seq", "head"),
            P("head", "seq"),
            P("seq"),
            P("seq", "head"),
            P("seq", "head"),
            P("head", "seq"),
            P(None, "seq", None),
        ),
        out_specs=(
            P(None, "seq", None),
            P(None, "seq", None),
            P("seq"),
            P("seq", "head"),
            P("seq", "head"),
            P("seq", "head"),
            P("head", "seq"),
            P("seq"),
            P("seq", "head"),
            P("seq", "head"),
            P("head", "seq"),
        ),
        check_vma=False,
    )
```

```python
import jax
import jax.numpy as jnp
from jax import lax
from jax.experimental import pallas as pl
from jax.experimental.pallas import tpu as pltpu
from jax.sharding import PartitionSpec as P

F = 16
DV = 128


epsilon = 1e-05
highest = lax.Precision.HIGHEST


def entering(part, axis, combine, identity, reverse):
    count = lax.axis_size(axis)
    place = lax.axis_index(axis)
    ahead = count - 1 - place if reverse else place
    gathered = jax.tree.map(lambda a: lax.all_gather(a, axis), part)
    state = jax.tree.map(lambda a, e: jnp.zeros_like(a) + jnp.asarray(e, a.dtype), part, identity)

    def one(turn, state):
        source = count - 1 - turn if reverse else turn
        return combine(
            state, jax.tree.map(lambda a: lax.dynamic_index_in_dim(a, source, 0, False), gathered)
        )

    return lax.fori_loop(0, ahead, one, state)


def rms_apply(values, gain):
    scale = lax.rsqrt(jnp.mean(values * values, axis=-1, keepdims=True) + epsilon)
    return values * scale * gain


def feature_map(projected):
    count = projected.shape[0]
    pieces = projected.reshape(count, -1, F)
    square = (pieces[:, :, :, None] * pieces[:, :, None, :]).reshape(count, pieces.shape[1], F * F)
    return jnp.concatenate(
        [jnp.ones_like(pieces[:, :, :1]), pieces * F ** (-0.25), square * (2.0 * F) ** (-0.5)],
        axis=-1,
    )


def swiglu(gate, up_part):
    return jax.nn.silu(gate) * up_part


def round_trip(values):
    return lax.optimization_barrier(values.astype(jnp.bfloat16)).astype(jnp.float32)


def add_pair(earlier, later):
    return (earlier[0] + later[0], earlier[1] + later[1])


def block_pass(tokens, upstream, gathered):
    gain_one, query_w, key_w, value_w, out_w, gain_two, gate_w, up_w, down_w = gathered
    f32 = jnp.float32
    bf16 = jnp.bfloat16
    stream = tokens.astype(f32)
    count = stream.shape[0]
    normed_f, norm_one_pull = jax.vjp(rms_apply, stream, gain_one.astype(f32))
    normed = normed_f.astype(bf16)
    queries = jnp.dot(normed, query_w, preferred_element_type=f32)
    keys_all = jnp.dot(normed, key_w, preferred_element_type=f32)
    values = jnp.dot(normed, value_w, preferred_element_type=f32).astype(bf16)
    query_feat_f, query_pull = jax.vjp(feature_map, queries)
    key_feat_f, key_pull = jax.vjp(feature_map, keys_all)
    query_feat = jnp.transpose(query_feat_f.astype(bf16), (1, 0, 2))
    key_feat = jnp.transpose(key_feat_f.astype(bf16), (1, 0, 2))
    value_heads = jnp.transpose(values.reshape(count, -1, DV), (1, 0, 2))
    causal = (jnp.arange(count)[:, None] >= jnp.arange(count)[None, :]).astype(f32)
    scores = jnp.einsum("htf,hsf->hts", query_feat, key_feat, preferred_element_type=f32) * causal
    weighted = scores.astype(bf16)
    num_local = jnp.einsum("hts,hsd->htd", weighted, value_heads, preferred_element_type=f32)
    den_local = jnp.sum(weighted.astype(f32), axis=-1)
    states = jnp.einsum("hsf,hsd->hfd", key_feat, value_heads, preferred_element_type=f32)
    totals = jnp.sum(key_feat.astype(f32), axis=1)
    state_before, total_before = entering(
        (states, totals), "seq", add_pair, (jnp.zeros_like(states), jnp.zeros_like(totals)), False
    )
    query_wide = query_feat.astype(f32)
    numer = num_local + jnp.einsum("htf,hfd->htd", query_wide, state_before, precision=highest)
    denom = den_local + jnp.einsum("htf,hf->ht", query_wide, total_before, precision=highest)
    ratio = numer / denom[..., None]
    heads_out = jnp.transpose(ratio, (1, 0, 2)).reshape(count, -1).astype(bf16)
    attended = lax.psum(jnp.dot(heads_out, out_w, preferred_element_type=f32), "head")
    middle = stream + attended
    normed_two_f, norm_two_pull = jax.vjp(rms_apply, middle, gain_two.astype(f32))
    normed_two = normed_two_f.astype(bf16)
    gate = jnp.dot(normed_two, gate_w, preferred_element_type=f32)
    up_part = jnp.dot(normed_two, up_w, preferred_element_type=f32)
    active, active_pull = jax.vjp(swiglu, gate, up_part)
    hidden = active.astype(bf16)
    branch = lax.psum(
        jnp.dot(hidden, down_w, preferred_element_type=f32).astype(jnp.bfloat16), "head"
    ).astype(jnp.float32)
    result = (middle + branch).astype(bf16)
    grad_down = jnp.dot(hidden.T, upstream, preferred_element_type=f32)
    d_hidden = jnp.dot(upstream, down_w.T, preferred_element_type=f32)
    d_gate_f, d_up_f = active_pull(d_hidden)
    d_gate = d_gate_f.astype(bf16)
    d_up = d_up_f.astype(bf16)
    grad_gate = jnp.dot(normed_two.T, d_gate, preferred_element_type=f32)
    grad_up = jnp.dot(normed_two.T, d_up, preferred_element_type=f32)
    d_normed_two = lax.psum(
        jnp.dot(d_gate, gate_w.T, preferred_element_type=f32)
        + jnp.dot(d_up, up_w.T, preferred_element_type=f32),
        "head",
    )
    d_middle_norm, grad_gain2 = norm_two_pull(d_normed_two)
    d_middle = upstream.astype(f32) + d_middle_norm
    d_attended = d_middle.astype(bf16)
    grad_out = jnp.dot(heads_out.T, d_attended, preferred_element_type=f32)
    d_heads = jnp.transpose(
        jnp.dot(d_attended, out_w.T, preferred_element_type=f32).reshape(count, -1, DV), (1, 0, 2)
    )
    d_numer = (d_heads / denom[..., None]).astype(bf16)
    d_denom = -jnp.sum(d_heads * ratio, axis=-1) / denom
    d_numer_wide = d_numer.astype(f32)
    d_before = jnp.einsum("htf,htd->hfd", query_wide, d_numer_wide, precision=highest)
    d_total_before = jnp.einsum("htf,ht->hf", query_wide, d_denom, precision=highest)
    d_state, d_total = entering(
        (d_before, d_total_before),
        "seq",
        add_pair,
        (jnp.zeros_like(d_before), jnp.zeros_like(d_total_before)),
        True,
    )
    d_scores = (
        (
            jnp.einsum("htd,hsd->hts", d_numer, value_heads, preferred_element_type=f32)
            + d_denom[..., None]
        )
        * causal
    ).astype(bf16)
    d_values = jnp.einsum(
        "hts,htd->hsd", weighted, d_numer, preferred_element_type=f32
    ) + jnp.einsum("hsf,hfd->hsd", key_feat.astype(f32), d_state, precision=highest)
    d_query_feat = (
        jnp.einsum("hts,hsf->htf", d_scores, key_feat, preferred_element_type=f32)
        + jnp.einsum("htd,hfd->htf", d_numer_wide, state_before, precision=highest)
        + d_denom[..., None] * total_before[:, None, :]
    )
    d_key_feat = (
        jnp.einsum("hts,htf->hsf", d_scores, query_feat, preferred_element_type=f32)
        + jnp.einsum("hsd,hfd->hsf", value_heads.astype(f32), d_state, precision=highest)
        + d_total[:, None, :]
    )
    d_queries = query_pull(jnp.transpose(round_trip(d_query_feat), (1, 0, 2)))[0].astype(bf16)
    d_keys = key_pull(jnp.transpose(round_trip(d_key_feat), (1, 0, 2)))[0].astype(bf16)
    d_values_flat = jnp.transpose(d_values, (1, 0, 2)).reshape(count, -1).astype(bf16)
    grad_query = jnp.dot(normed.T, d_queries, preferred_element_type=f32)
    grad_key = jnp.dot(normed.T, d_keys, preferred_element_type=f32)
    grad_value = jnp.dot(normed.T, d_values_flat, preferred_element_type=f32)
    d_normed_part = (
        jnp.dot(d_queries, query_w.T, preferred_element_type=f32)
        + jnp.dot(d_keys, key_w.T, preferred_element_type=f32)
        + jnp.dot(d_values_flat, value_w.T, preferred_element_type=f32)
    )
    d_normed = lax.psum(d_normed_part.astype(jnp.bfloat16), "head").astype(jnp.float32)
    d_stream_norm, grad_gain1 = norm_one_pull(d_normed)
    input_grad = (d_middle + d_stream_norm).astype(bf16)
    return (
        result,
        input_grad,
        grad_gain1,
        grad_query,
        grad_key,
        grad_value,
        grad_out,
        grad_gain2,
        grad_gate,
        grad_up,
        grad_down,
    )


def local(
    inputs, norm_gain1, w_query, w_key, w_value, w_out, norm_gain2, w_gate, w_up, w_down, cotangent
):
    micro = inputs.shape[0]
    summed = None
    results = []
    input_grads = []
    for step_index in range(micro):
        gathered = (
            lax.all_gather(norm_gain1, "seq", axis=0, tiled=True),
            lax.all_gather(w_query, "seq", axis=0, tiled=True),
            lax.all_gather(w_key, "seq", axis=0, tiled=True),
            lax.all_gather(w_value, "seq", axis=0, tiled=True),
            lax.all_gather(w_out, "seq", axis=1, tiled=True),
            lax.all_gather(norm_gain2, "seq", axis=0, tiled=True),
            lax.all_gather(w_gate, "seq", axis=0, tiled=True),
            lax.all_gather(w_up, "seq", axis=0, tiled=True),
            lax.all_gather(w_down, "seq", axis=1, tiled=True),
        )
        (
            result,
            input_grad,
            grad_gain1,
            grad_query,
            grad_key,
            grad_value,
            grad_out,
            grad_gain2,
            grad_gate,
            grad_up,
            grad_down,
        ) = block_pass(inputs[step_index], cotangent[step_index], gathered)
        results.append(result)
        input_grads.append(input_grad)
        fresh = (
            lax.psum_scatter(grad_gain1, "seq", scatter_dimension=0, tiled=True),
            lax.psum_scatter(grad_query, "seq", scatter_dimension=0, tiled=True),
            lax.psum_scatter(grad_key, "seq", scatter_dimension=0, tiled=True),
            lax.psum_scatter(grad_value, "seq", scatter_dimension=0, tiled=True),
            lax.psum_scatter(grad_out, "seq", scatter_dimension=1, tiled=True),
            lax.psum_scatter(grad_gain2, "seq", scatter_dimension=0, tiled=True),
            lax.psum_scatter(grad_gate, "seq", scatter_dimension=0, tiled=True),
            lax.psum_scatter(grad_up, "seq", scatter_dimension=0, tiled=True),
            lax.psum_scatter(grad_down, "seq", scatter_dimension=1, tiled=True),
        )
        summed = (
            fresh
            if summed is None
            else tuple((older + newer for older, newer in zip(summed, fresh)))
        )
    return (
        jnp.stack(results),
        jnp.stack(input_grads),
        summed[0],
        summed[1],
        summed[2],
        summed[3],
        summed[4],
        summed[5],
        summed[6],
        summed[7],
        summed[8],
    )


MESH = pl.DeviceIdType.MESH
bf16 = jnp.bfloat16
f32 = jnp.float32
ZED = 4
VMEM_LIMIT = 60 * 1024 * 1024


def where_am_i():
    place = lax.axis_index("seq")
    return place % 2, (place // 2) % 2, place // 4, lax.axis_index("head")


def index_of(z, y, x):
    return (z * 2 + y) * 2 + x


def remote(src, dst, send, recv, place, head):
    return pltpu.make_async_remote_copy(
        src_ref=src, dst_ref=dst, send_sem=send, recv_sem=recv, device_id=(place, head),
        device_id_type=MESH,
    )


def arrived(dst, send, recv, place, head):
    remote(dst, dst, send, recv, place, head).wait_recv()


def params():
    return pltpu.CompilerParams(has_side_effects=True, vmem_limit_bytes=VMEM_LIMIT)


ANY = pl.BlockSpec(memory_space=pl.ANY)
VMEM = pl.BlockSpec(memory_space=pltpu.VMEM)
DMA = pltpu.SemaphoreType.DMA
ORDER = (0, 1, 3, 2)


def exchange_kernel(src, dst, ls, ss, rs):
    x, y, z, h = where_am_i()
    me = index_of(z, y, x)
    local = pltpu.make_async_copy(src.at[me], dst.at[me], ls)
    local.start()
    copies = []
    for d in range(1, 16):
        there = (me + d) % 16
        copies.append(remote(src.at[there], dst.at[me], ss.at[d], rs.at[d], there, h))
    for copy in copies:
        copy.start()
    local.wait()
    for d in range(1, 16):
        arrived(dst.at[(me + 16 - d) % 16], ss.at[d], rs.at[d], me, h)
    for copy in copies:
        copy.wait_send()


def exchange(blocks):
    return pl.pallas_call(
        exchange_kernel,
        out_shape=jax.ShapeDtypeStruct(blocks.shape, blocks.dtype),
        in_specs=[ANY],
        out_specs=ANY,
        scratch_shapes=[DMA, DMA((16,)), DMA((16,))],
        compiler_params=params(),
        name="exchange",
    )(blocks)


def combine_kernel(t, out, other, summed, landed, sem, zs, zr, ds, dr):
    x, y, z, h = where_am_i()
    me = index_of(z, y, x)
    kinds = t.shape[0]
    swaps = []
    for d in (2, 1, 3, 0):
        zz = (z + d) % ZED
        for kind in range(kinds):
            swaps.append(
                remote(t.at[kind, zz, 1 - h], other.at[kind, zz], sem.at[0, kind, d], sem.at[1, kind, d], me, 1 - h)
            )
    for copy in swaps:
        copy.start()
    copies = []
    for d in (2, 1, 3, 0):
        zz = (z + d) % ZED
        for kind in range(kinds):
            arrived(other.at[kind, zz], sem.at[0, kind, d], sem.at[1, kind, d], me, h)

            def add(turn, carry):
                row = pl.ds(pl.multiple_of(turn * 16, 16), 16)
                summed[kind, zz, row, :] = (
                    t[kind, zz, h, row, :].astype(f32) + other[kind, zz, row, :].astype(f32)
                ).astype(bf16)
                return carry

            lax.fori_loop(0, 8, add, 0)
            if d:
                copy = remote(
                    summed.at[kind, zz], landed.at[kind, d], zs.at[kind, d], zr.at[kind, d],
                    index_of(zz, y, x), h,
                )
                copy.start()
                copies.append(copy)
    for kind in range(kinds):
        for d in (1, 3, 2):
            arrived(landed.at[kind, d], zs.at[kind, d], zr.at[kind, d], me, h)

        def total(turn, carry):
            row = pl.ds(pl.multiple_of(turn * 16, 16), 16)
            acc = summed[kind, z, row, :].astype(f32)
            for d in (1, 2, 3):
                acc = acc + landed[kind, d, row, :].astype(f32)
            out[kind, h, row, :] = acc.astype(bf16)
            return carry

        lax.fori_loop(0, 8, total, 0)
        copy = remote(out.at[kind, h], out.at[kind, h], ds.at[kind], dr.at[kind], me, 1 - h)
        copy.start()
        copies.append(copy)
    for kind in range(kinds):
        arrived(out.at[kind, 1 - h], ds.at[kind], dr.at[kind], me, 1 - h)
    for copy in swaps + copies:
        copy.wait_send()


def combine(t):
    kinds, _, mbs, count, wide = t.shape
    return pl.pallas_call(
        combine_kernel,
        out_shape=jax.ShapeDtypeStruct((kinds, mbs, count, wide), bf16),
        in_specs=[VMEM],
        out_specs=VMEM,
        scratch_shapes=[
            pltpu.VMEM((kinds, ZED, count, wide), bf16),
            pltpu.VMEM((kinds, ZED, count, wide), bf16),
            pltpu.VMEM((kinds, ZED, count, wide), bf16),
            DMA((2, kinds, 4)), DMA((kinds, 4)), DMA((kinds, 4)), DMA((kinds,)), DMA((kinds,)),
        ],
        compiler_params=params(),
        name="combine",
    )(t)


def pair_kernel(part, out, other, sem):
    x, y, z, h = where_am_i()
    me = index_of(z, y, x)
    swap = remote(part, other, sem.at[0], sem.at[1], me, 1 - h)
    swap.start()
    swap.wait()
    out[...] = part[...] + other[...]


def pair_sum(part):
    return pl.pallas_call(
        pair_kernel,
        out_shape=jax.ShapeDtypeStruct(part.shape, part.dtype),
        in_specs=[VMEM],
        out_specs=VMEM,
        scratch_shapes=[pltpu.VMEM(part.shape, part.dtype), DMA((2,))],
        compiler_params=params(),
        name="pair_sum",
    )(part)


def scatter_kernel(ga, gm, za, zm, r1x, r1y, r2x, r2y, f1, f2, fin, s1, q1, s2, q2, s3, q3):
    x, y, z, h = where_am_i()
    me = index_of(z, y, x)
    at_x, at_y = index_of(z, y, 1 - x), index_of(z, 1 - y, x)
    half = ga.shape[-1] // 2
    low, high = pl.ds(0, half), pl.ds(half, half)
    sets = [(0, ga, za, d) for d in (2, 1, 3, 0)] + [(1, gm, zm, d) for d in (2, 1, 3, 0)]
    copies = []

    def start(copy):
        copy.start()
        copies.append(copy)

    for n, (kind, g, out, d) in enumerate(sets):
        zz = (z + d) % ZED
        start(remote(g.at[zz, :, 1 - x, :, low], r1x.at[n], s1.at[n, 0], q1.at[n, 0], at_x, h))
        start(remote(g.at[zz, 1 - y, :, :, high], r1y.at[n], s1.at[n, 1], q1.at[n, 1], at_y, h))

    def wide(turns):
        return pl.ds(pl.multiple_of(turns * 16, 16), 16)

    for turn in range(len(sets) + 1):
        if turn < len(sets):
            n = turn
            kind, g, out, d = sets[n]
            zz = (z + d) % ZED
            arrived(r1x.at[n], s1.at[n, 0], q1.at[n, 0], me, h)
            arrived(r1y.at[n], s1.at[n, 1], q1.at[n, 1], me, h)

            def forward(i, carry):
                row = wide(i)
                f1[n, row, :] = (
                    g[zz, 1 - y, x, row, low].astype(f32) + r1x[n, 1 - y, row, :].astype(f32)
                ).astype(bf16)
                f2[n, row, :] = (
                    g[zz, y, 1 - x, row, high].astype(f32) + r1y[n, 1 - x, row, :].astype(f32)
                ).astype(bf16)
                return carry

            lax.fori_loop(0, 8, forward, 0)
            start(remote(f1.at[n], r2y.at[n], s2.at[n, 0], q2.at[n, 0], at_y, h))
            start(remote(f2.at[n], r2x.at[n], s2.at[n, 1], q2.at[n, 1], at_x, h))
        if turn > 0:
            n = turn - 1
            kind, g, out, d = sets[n]
            zz = (z + d) % ZED
            arrived(r2y.at[n], s2.at[n, 0], q2.at[n, 0], me, h)
            arrived(r2x.at[n], s2.at[n, 1], q2.at[n, 1], me, h)
            target = fin.at[n] if d else out.at[z]

            def finish(i, carry):
                row = wide(i)
                target[row, low] = (
                    g[zz, y, x, row, low].astype(f32)
                    + r1x[n, y, row, :].astype(f32)
                    + r2y[n, row, :].astype(f32)
                ).astype(bf16)
                target[row, high] = (
                    g[zz, y, x, row, high].astype(f32)
                    + r1y[n, x, row, :].astype(f32)
                    + r2x[n, row, :].astype(f32)
                ).astype(bf16)
                return carry

            lax.fori_loop(0, 8, finish, 0)
            if d:
                start(
                    remote(fin.at[n], out.at[z], s3.at[kind, d], q3.at[kind, d], index_of(zz, y, x), h)
                )
    for kind, g, out, d in sets:
        if d:
            arrived(out.at[(z + ZED - d) % ZED], s3.at[kind, d], q3.at[kind, d], me, h)
    for copy in copies:
        copy.wait_send()


def scatter_all(ga, gm):
    wide = ga.shape[-1]
    ga = ga.reshape(ZED, 2, 2, 128, wide)
    gm = gm.reshape(ZED, 2, 2, 128, wide)
    give = jax.ShapeDtypeStruct((ZED, 128, wide), bf16)
    return pl.pallas_call(
        scatter_kernel,
        out_shape=(give, give),
        in_specs=[VMEM] * 2,
        out_specs=(VMEM,) * 2,
        scratch_shapes=[
            pltpu.VMEM((8, 2, 128, wide // 2), bf16),
            pltpu.VMEM((8, 2, 128, wide // 2), bf16),
            pltpu.VMEM((8, 128, wide // 2), bf16),
            pltpu.VMEM((8, 128, wide // 2), bf16),
            pltpu.VMEM((8, 128, wide // 2), bf16),
            pltpu.VMEM((8, 128, wide // 2), bf16),
            pltpu.VMEM((8, 128, wide), bf16),
            DMA((8, 2)), DMA((8, 2)), DMA((8, 2)), DMA((8, 2)), DMA((2, 4)), DMA((2, 4)),
        ],
        compiler_params=params(),
        name="scatter_all",
    )(ga, gm)


def mix(a, b, over):
    return lax.dot_general(a, b, (over, ((), ())), preferred_element_type=f32)


CHUNK = 512
COLS = 256


def spread(got, q_t, k_t, va):
    count = got.shape[2]
    for b in range(got.shape[0]):
        q_t[:, b * count : (b + 1) * count] = got[b, 0:F, :]
        k_t[:, b * count : (b + 1) * count] = got[b, F : 2 * F, :]
        va[b * count : (b + 1) * count, 0:DV] = got[b, 2 * F :, :]
    va[:, DV:] = jnp.ones((va.shape[0], va.shape[1] - DV), bf16)


def lower(count):
    return lax.broadcasted_iota(jnp.int32, (count, count), 0) >= lax.broadcasted_iota(
        jnp.int32, (count, count), 1
    )


def attend_rows(qi, q_t, k_t, va, ratio, den, causal):
    qs = slice(qi * CHUNK, (qi + 1) * CHUNK)
    acc = jnp.zeros((CHUNK, va.shape[1]), f32)
    for kj in range(qi + 1):
        ks = slice(kj * CHUNK, (kj + 1) * CHUNK)
        s = mix(q_t[:, qs], k_t[:, ks], ((0,), (0,)))
        p = 1.0 + s * (0.25 + s * (1.0 / 32.0))
        if kj == qi:
            p = jnp.where(causal, p, 0.0)
        acc = acc + mix(p.astype(bf16), va[ks, :], ((1,), (0,)))
    ratio[qs, :] = acc[:, :DV] / acc[:, DV:]
    den[qs, :] = acc[:, DV:]


def front_kernel(
    a1, a2, m, xh, xin,
    wa1, wa2, wm, got, ratio, den, heads_out, middle, near,
    w1, w2, pack, q_t, k_t, va, ob, part, other,
    ls, zs, zr, ps, pr, e1s, e1r, e2s, e2r, ws, wr, ns, nr, ds, dr,
):
    x, y, z, h = where_am_i()
    me = index_of(z, y, x)
    at_x, at_y = index_of(z, y, 1 - x), index_of(z, 1 - y, x)
    count = xin.shape[1]
    heads = 16 // xin.shape[0]
    late = []

    def go(copy):
        copy.start()
        late.append(copy)

    def rows(zz, yy, xx):
        return pl.ds(pl.multiple_of(index_of(zz, yy, xx) * 128, 128), 128)

    mine = rows(z, y, x)
    kept = [
        pltpu.make_async_copy(a1, w1.at[mine], ls.at[0]),
        pltpu.make_async_copy(a2, w2.at[mine], ls.at[1]),
        pltpu.make_async_copy(m.at[z], wm.at[mine], ls.at[2]),
    ]
    for copy in kept:
        copy.start()
    dest = (w1, w2, wm)

    def line(kind):
        for d in (1, 3, 2):
            zz = (z + d) % ZED
            src = (a1, a2, m.at[zz])[kind]
            go(remote(src, dest[kind].at[mine], zs.at[kind, d], zr.at[kind, d], index_of(zz, y, x), h))

    def plane(kind, d):
        block = dest[kind].at[rows((z + ZED - d) % ZED, y, x)]
        if d:
            arrived(block, zs.at[kind, d], zr.at[kind, d], me, h)
        else:
            kept[kind].wait()
        go(remote(block, block, ps.at[kind, d, 0], pr.at[kind, d, 0], at_x, h))
        go(remote(block, block, ps.at[kind, d, 1], pr.at[kind, d, 1], at_y, h))

    def onward(kind, d):
        w = dest[kind]
        zz = (z + ZED - d) % ZED
        half = w.shape[1] // 2
        from_x, from_y = rows(zz, y, 1 - x), rows(zz, 1 - y, x)
        arrived(w.at[from_x], ps.at[kind, d, 0], pr.at[kind, d, 0], me, h)
        arrived(w.at[from_y], ps.at[kind, d, 1], pr.at[kind, d, 1], me, h)
        left = w.at[from_y, pl.ds(0, half)]
        right = w.at[from_x, pl.ds(half, half)]
        go(remote(left, left, ps.at[kind, d, 2], pr.at[kind, d, 2], at_x, h))
        go(remote(right, right, ps.at[kind, d, 3], pr.at[kind, d, 3], at_y, h))

    def corner(kind):
        w = dest[kind]
        half = w.shape[1] // 2
        for d in ORDER:
            far = rows((z + ZED - d) % ZED, 1 - y, 1 - x)
            arrived(w.at[far, pl.ds(0, half)], ps.at[kind, d, 2], pr.at[kind, d, 2], me, h)
            arrived(w.at[far, pl.ds(half, half)], ps.at[kind, d, 3], pr.at[kind, d, 3], me, h)

    line(0)
    plane(0, 0)
    plane(0, 1)
    onward(0, 0)
    plane(0, 3)
    line(1)
    onward(0, 1)
    plane(0, 2)
    onward(0, 3)
    plane(1, 0)
    onward(0, 2)
    corner(0)
    out1 = pltpu.make_async_copy(w1, wa1, ls.at[3])
    out1.start()
    kq = mix(xh[...], w1[:, 0 : 2 * heads * F], ((1,), (0,)))
    qk = jnp.transpose(kq).astype(bf16)
    for mb in range(16 // heads):
        for k in range(heads):
            t = k + heads * mb
            cols = slice(mb * count, (mb + 1) * count)
            pack[t, 0:F, :] = qk[k * F : (k + 1) * F, cols]
            pack[t, F : 2 * F, :] = qk[(heads + k) * F : (heads + k + 1) * F, cols]
    for c in range(heads * DV // COLS):
        at = 2 * heads * F + c * COLS
        val = mix(xh[...], w1[:, at : at + COLS], ((1,), (0,))).astype(bf16)
        for mb in range(16 // heads):
            for i in range(COLS // DV):
                t = c * (COLS // DV) + i + heads * mb
                pack[t, 2 * F :, :] = val[mb * count : (mb + 1) * count, i * DV : (i + 1) * DV]
    keep = pltpu.make_async_copy(pack.at[me], got.at[me], ls.at[4])
    keep.start()
    for d in range(1, 16):
        there = (me + d) % 16
        go(remote(pack.at[there], got.at[me], e1s.at[d], e1r.at[d], there, h))
    plane(1, 1)
    onward(1, 0)
    plane(1, 3)
    onward(1, 1)
    plane(1, 2)
    onward(1, 3)
    keep.wait()
    for d in range(1, 16):
        arrived(got.at[(me + 16 - d) % 16], e1s.at[d], e1r.at[d], me, h)
    line(2)
    plane(2, 0)
    onward(1, 2)
    spread(got, q_t, k_t, va)
    causal = lower(CHUNK)
    for qi in range(va.shape[0] // CHUNK):
        attend_rows(qi, q_t, k_t, va, ratio, den, causal)
    for b in range(16):
        ob[b, :, :] = ratio[b * count : (b + 1) * count, :].astype(bf16)

    def window(source):
        return heads_out.at[
            pl.ds(pl.multiple_of((source // heads) * count, count), count),
            pl.ds(pl.multiple_of((source % heads) * DV, DV), DV),
        ]

    keep = pltpu.make_async_copy(ob.at[me], window(me), ls.at[4])
    keep.start()
    for d in range(1, 16):
        there = (me + d) % 16
        go(remote(ob.at[there], window(me), e2s.at[d], e2r.at[d], there, h))
    onward(2, 0)
    corner(1)
    out2 = pltpu.make_async_copy(w2, wa2, ls.at[5])
    out2.start()
    keep.wait()
    for d in range(1, 16):
        arrived(window((me + 16 - d) % 16), e2s.at[d], e2r.at[d], me, h)
    wide = part.shape[1]
    swaps = []
    for c in range(wide // COLS):
        cols = pl.ds(c * COLS, COLS)
        part[:, c * COLS : (c + 1) * COLS] = mix(
            heads_out[...], w2[c * COLS : (c + 1) * COLS, :], ((1,), (1,))
        )
        go(remote(part.at[:, cols], other.at[:, cols], ws.at[c], wr.at[c], me, 1 - h))
    for c in range(wide // COLS):
        cols = pl.ds(c * COLS, COLS)
        arrived(other.at[:, cols], ws.at[c], wr.at[c], me, 1 - h)

    def one(mb):
        def body(turn, carry):
            row = pl.ds(pl.multiple_of(turn * 16, 16), 16)
            flat = pl.ds(pl.multiple_of(mb * count + turn * 16, 16), 16)
            mid = xin[mb, row, :].astype(f32) + (part[flat, :] + other[flat, :])
            middle[mb, row, :] = mid
            scale = lax.rsqrt(jnp.mean(mid * mid, axis=-1, keepdims=True) + epsilon)
            near[z, mb, row, :] = (mid * scale).astype(bf16)
            return carry

        lax.fori_loop(0, count // 16, body, 0)

    one(h)
    for d in (2, 1, 3):
        there = index_of((z + d) % ZED, y, x)
        go(remote(near.at[z, h], near.at[z, h], ns.at[d], nr.at[d], there, h))
    one(1 - h)
    plane(2, 1)
    plane(2, 3)
    onward(2, 1)
    plane(2, 2)
    onward(2, 3)
    for d in (1, 3, 2):
        zz = (z + ZED - d) % ZED
        arrived(near.at[zz, h], ns.at[d], nr.at[d], me, h)
        go(remote(near.at[zz, h], near.at[zz, h], ds.at[d], dr.at[d], me, 1 - h))
    onward(2, 2)
    corner(2)
    for d in (1, 3, 2):
        zz = (z + ZED - d) % ZED
        arrived(near.at[zz, 1 - h], ds.at[d], dr.at[d], me, 1 - h)
    out1.wait()
    out2.wait()
    for copy in late:
        copy.wait_send()


def front(a1, a2, m, xh, xin):
    mbs, count, wide = xin.shape
    depth = 16 * count
    wide1, wide2 = a1.shape[1], a2.shape[1]
    shape = jax.ShapeDtypeStruct
    return pl.pallas_call(
        front_kernel,
        out_shape=(
            shape((wide, wide1), bf16),
            shape((wide, wide2), bf16),
            shape((wide, m.shape[2]), bf16),
            shape((16, 2 * F + DV, count), bf16),
            shape((depth, DV), f32),
            shape((depth, DV), f32),
            shape((mbs * count, wide2), bf16),
            shape(xin.shape, f32),
            shape((ZED,) + xin.shape, bf16),
        ),
        in_specs=[ANY] * 3 + [VMEM] * 2,
        out_specs=(ANY,) * 3 + (VMEM,) * 6,
        scratch_shapes=[
            pltpu.VMEM((wide, wide1), bf16),
            pltpu.VMEM((wide, wide2), bf16),
            pltpu.VMEM((16, 2 * F + DV, count), bf16),
            pltpu.VMEM((F, depth), bf16),
            pltpu.VMEM((F, depth), bf16),
            pltpu.VMEM((depth, 2 * DV), bf16),
            pltpu.VMEM((16, count, DV), bf16),
            pltpu.VMEM((mbs * count, wide), f32),
            pltpu.VMEM((mbs * count, wide), f32),
            DMA((6,)), DMA((3, 4)), DMA((3, 4)), DMA((3, 4, 4)), DMA((3, 4, 4)),
            DMA((16,)), DMA((16,)), DMA((16,)), DMA((16,)),
            DMA((wide // COLS,)), DMA((wide // COLS,)), DMA((4,)), DMA((4,)), DMA((4,)), DMA((4,)),
        ],
        compiler_params=params(),
        name="front",
    )(a1, a2, m, xh, xin)


def back_rows_kernel(got, ratio, den, d_o, d_qk, d_v, q_t, k_t, va, da, dn_t):
    attend_back_body(got, ratio, den, d_o, d_qk, d_v, q_t, k_t, va, da, dn_t)


def attend_back_body(got, ratio, den, d_o, d_qk, d_v, q_t, k_t, va, da, dn_t):
    spread(got, q_t, k_t, va)
    depth = va.shape[0]
    lane = lax.broadcasted_iota(jnp.int32, (CHUNK, DV), 1)
    for qi in range(depth // CHUNK):
        qs = slice(qi * CHUNK, (qi + 1) * CHUNK)
        dn = d_o[qs, :].astype(f32) / den[qs, :]
        dd = -jnp.sum(dn * ratio[qs, :], axis=-1, keepdims=True)
        big = dd.astype(bf16).astype(f32)
        da[qs, 0:DV] = dn.astype(bf16)
        da[qs, DV:] = jnp.where(lane == 0, big, jnp.where(lane == 1, dd - big, 0.0)).astype(bf16)
        dn_t[:, qs] = jnp.transpose(dn).astype(bf16)
    causal = lower(CHUNK)
    for kj in range(depth // CHUNK):
        ks = slice(kj * CHUNK, (kj + 1) * CHUNK)
        acc_k = jnp.zeros((F, CHUNK), f32)
        acc_v = jnp.zeros((DV, CHUNK), f32)
        for qi in range(kj, depth // CHUNK):
            qs = slice(qi * CHUNK, (qi + 1) * CHUNK)
            s = mix(q_t[:, qs], k_t[:, ks], ((0,), (0,)))
            p = 1.0 + s * (0.25 + s * (1.0 / 32.0))
            d_s = mix(da[qs, :], va[ks, :], ((1,), (1,))) * (0.25 + s * (1.0 / 16.0))
            if kj == qi:
                p = jnp.where(causal, p, 0.0)
                d_s = jnp.where(causal, d_s, 0.0)
            d_s = d_s.astype(bf16)
            acc_v = acc_v + mix(dn_t[:, qs], p.astype(bf16), ((1,), (0,)))
            acc_k = acc_k + mix(q_t[:, qs], d_s, ((1,), (0,)))
            d_q = mix(k_t[:, ks], d_s, ((1,), (1,)))
            d_qk[0:F, qs] = d_q if kj == 0 else d_qk[0:F, qs] + d_q
        d_qk[F : 2 * F, ks] = acc_k
        d_v[ks, :] = jnp.transpose(acc_v)


def attend_back(got, ratio, den, d_o):
    depth = d_o.shape[0]
    shape = jax.ShapeDtypeStruct
    return pl.pallas_call(
        back_rows_kernel,
        out_shape=(shape((2 * F, depth), f32), shape((depth, DV), f32)),
        in_specs=[VMEM] * 4,
        out_specs=(VMEM,) * 2,
        scratch_shapes=[
            pltpu.VMEM((F, depth), bf16),
            pltpu.VMEM((F, depth), bf16),
            pltpu.VMEM((depth, 2 * DV), bf16),
            pltpu.VMEM((depth, 2 * DV), bf16),
            pltpu.VMEM((DV, depth), bf16),
        ],
        compiler_params=pltpu.CompilerParams(vmem_limit_bytes=VMEM_LIMIT),
        name="attend_back",
    )(got, ratio, den, d_o)


def share_kernel(g, gg, ls, zs, zr, ds, dr):
    x, y, z, h = where_am_i()
    me = index_of(z, y, x)
    local = pltpu.make_async_copy(g, gg.at[z], ls)
    local.start()
    copies = []
    for d in (2, 1, 3):
        there = index_of((z + d) % ZED, y, x)
        copies.append(remote(g.at[h], gg.at[z, h], zs.at[d], zr.at[d], there, h))
    for copy in copies:
        copy.start()
    for d in (1, 3, 2):
        zz = (z + ZED - d) % ZED
        arrived(gg.at[zz, h], zs.at[d], zr.at[d], me, h)
        copy = remote(gg.at[zz, h], gg.at[zz, h], ds.at[d], dr.at[d], me, 1 - h)
        copy.start()
        copies.append(copy)
    for d in (1, 3, 2):
        zz = (z + ZED - d) % ZED
        arrived(gg.at[zz, 1 - h], ds.at[d], dr.at[d], me, 1 - h)
    local.wait()
    for copy in copies:
        copy.wait_send()


def share(g):
    return pl.pallas_call(
        share_kernel,
        out_shape=jax.ShapeDtypeStruct((ZED,) + g.shape, bf16),
        in_specs=[ANY],
        out_specs=ANY,
        scratch_shapes=[DMA, DMA((4,)), DMA((4,)), DMA((4,)), DMA((4,))],
        compiler_params=params(),
        name="share",
    )(g)


def fast(
    inputs, norm_gain1, w_query, w_key, w_value, w_out, norm_gain2, w_gate, w_up, w_down, cotangent
):
    mbs, count, wide = inputs.shape
    heads = w_query.shape[1] // F
    units = w_gate.shape[1] // ZED
    room = -(-units // 128) * 128
    qk, vv = 2 * heads * F, heads * DV
    rows = w_query.shape[0]
    gain1, gain2 = norm_gain1.astype(f32)[:, None], norm_gain2.astype(f32)[:, None]

    def folded(weight, gain):
        return (weight.astype(f32) * gain).astype(bf16)

    a1 = jnp.concatenate([folded(w_query, gain1), folded(w_key, gain1), folded(w_value, gain1)], axis=1)

    def cut(weight):
        pieces = jnp.transpose(weight.reshape(rows, ZED, units), (1, 0, 2))
        return jnp.pad(pieces, ((0, 0), (0, 0), (0, room - units)))

    m = jnp.concatenate([cut(folded(w_gate, gain2)), cut(folded(w_up, gain2)), cut(w_down.T)], axis=2)
    stream = inputs.astype(f32).reshape(mbs * count, wide)
    r1 = lax.rsqrt(jnp.mean(stream * stream, axis=-1, keepdims=True) + epsilon)
    xh1 = (stream * r1).astype(bf16)
    wa1, w_o, wm, got, ratio, den, heads_out, middle, near = front(a1, w_out.T, m, xh1, inputs)
    gg = share(cotangent)
    w_qk, w_v = wa1[:, :qk], wa1[:, qk:]
    w_g, w_u, w_d = wm[:, :room], wm[:, room : 2 * room], wm[:, 2 * room :]
    middle = middle.reshape(mbs * count, wide)
    many = ZED * mbs * count
    n2 = near.reshape(many, wide)
    up_g = gg.reshape(many, wide)
    gate = mix(n2, w_g, ((1,), (0,)))
    up = mix(n2, w_u, ((1,), (0,)))
    d_hidden = mix(up_g, w_d, ((1,), (0,)))
    sig = jax.nn.sigmoid(gate)
    silu = gate * sig
    hidden = (silu * up).astype(bf16)
    d_gate = (d_hidden * up * sig * (1.0 + gate * (1.0 - sig))).astype(bf16)
    d_up = (d_hidden * silu).astype(bf16)
    branch = mix(hidden, w_d, ((1,), (1,))).astype(bf16)
    d_n2 = (mix(d_gate, w_g, ((1,), (1,))) + mix(d_up, w_u, ((1,), (1,)))).astype(bf16)
    both = combine(jnp.stack([d_n2, branch]).reshape(2, ZED, mbs, count, wide))
    e2 = both[0].reshape(mbs * count, wide).astype(f32)
    outputs = (middle + both[1].reshape(mbs * count, wide).astype(f32)).astype(bf16)
    r2 = lax.rsqrt(jnp.mean(middle * middle, axis=-1, keepdims=True) + epsilon)
    xh2 = middle * r2
    d_middle = cotangent.reshape(mbs * count, wide).astype(f32) + r2 * (
        e2 - xh2 * jnp.mean(e2 * xh2, axis=-1, keepdims=True)
    )
    d_att = d_middle.astype(bf16)
    d_heads = mix(d_att, w_o, ((1,), (0,))).astype(bf16)
    d_heads = d_heads.reshape(mbs, count, heads, DV).transpose(0, 2, 1, 3).reshape(16, count, DV)
    d_heads = exchange(d_heads).reshape(16 * count, DV)
    d_qk, d_v = attend_back(got, ratio, den, d_heads)
    d_qk = d_qk.astype(bf16).reshape(2 * F, 16, count).transpose(1, 0, 2)
    home = exchange(jnp.concatenate([d_qk, d_v.astype(bf16).reshape(16, count, DV)], axis=1))
    d_qk = home[:, : 2 * F].reshape(mbs, heads, 2, F, count).transpose(0, 4, 2, 1, 3)
    d_qk = d_qk.reshape(mbs * count, qk)
    d_val = home[:, 2 * F :].reshape(mbs, heads, count, DV).transpose(0, 2, 1, 3)
    d_val = d_val.reshape(mbs * count, vv)
    e1 = pair_sum(mix(d_qk, w_qk, ((1,), (1,))) + mix(d_val, w_v, ((1,), (1,))))
    xh1f = stream * r1
    input_grad = (
        d_middle + r1 * (e1 - xh1f * jnp.mean(e1 * xh1f, axis=-1, keepdims=True))
    ).astype(bf16)
    first = ((0,), (0,))
    ga = jnp.concatenate(
        [mix(xh1, d_qk, first), mix(xh1, d_val, first), mix(d_att, heads_out, first)], axis=1
    ).astype(bf16)
    gm = jnp.concatenate(
        [mix(n2, d_gate, first), mix(n2, d_up, first), mix(up_g, hidden, first)], axis=1
    ).astype(bf16)
    za, zm = scatter_all(ga, gm)
    za = jnp.sum(za.astype(f32), axis=0)
    zm = zm.astype(f32)

    def joined(piece):
        return jnp.transpose(piece[:, :, :units], (1, 0, 2)).reshape(rows, ZED * units)

    g_gate, g_up, g_down = joined(zm[:, :, :room]), joined(zm[:, :, room : 2 * room]), joined(zm[:, :, 2 * room :])
    s_q, s_k, s_v = za[:, : qk // 2], za[:, qk // 2 : qk], za[:, qk : qk + vv]
    g_gain1 = (
        jnp.sum(w_query.astype(f32) * s_q, axis=1)
        + jnp.sum(w_key.astype(f32) * s_k, axis=1)
        + jnp.sum(w_value.astype(f32) * s_v, axis=1)
    )
    g_gain2 = jnp.sum(w_gate.astype(f32) * g_gate, axis=1) + jnp.sum(w_up.astype(f32) * g_up, axis=1)
    gains = lax.psum(jnp.stack([g_gain1, g_gain2]), "head")
    return (
        outputs.reshape(mbs, count, wide),
        input_grad.reshape(mbs, count, wide),
        gains[0],
        s_q * gain1,
        s_k * gain1,
        s_v * gain1,
        za[:, qk + vv :].T,
        gains[1],
        g_gate * gain2,
        g_up * gain2,
        g_down.T,
    )


def solution(mesh):
    return jax.shard_map(
        fast if mesh.shape["seq"] == 16 else local,
        mesh=mesh,
        in_specs=(
            P(None, "seq", None),
            P("seq"),
            P("seq", "head"),
            P("seq", "head"),
            P("seq", "head"),
            P("head", "seq"),
            P("seq"),
            P("seq", "head"),
            P("seq", "head"),
            P("head", "seq"),
            P(None, "seq", None),
        ),
        out_specs=(
            P(None, "seq", None),
            P(None, "seq", None),
            P("seq"),
            P("seq", "head"),
            P("seq", "head"),
            P("seq", "head"),
            P("head", "seq"),
            P("seq"),
            P("seq", "head"),
            P("seq", "head"),
            P("head", "seq"),
        ),
        check_vma=False,
    )
```

```python
import jax
import jax.numpy as jnp
from jax import lax
from jax.experimental import pallas as pl
from jax.experimental.pallas import tpu as pltpu
from jax.sharding import PartitionSpec as P

F = 16
DV = 128


epsilon = 1e-05
highest = lax.Precision.HIGHEST


def entering(part, axis, combine, identity, reverse):
    count = lax.axis_size(axis)
    place = lax.axis_index(axis)
    ahead = count - 1 - place if reverse else place
    gathered = jax.tree.map(lambda a: lax.all_gather(a, axis), part)
    state = jax.tree.map(lambda a, e: jnp.zeros_like(a) + jnp.asarray(e, a.dtype), part, identity)

    def one(turn, state):
        source = count - 1 - turn if reverse else turn
        return combine(
            state, jax.tree.map(lambda a: lax.dynamic_index_in_dim(a, source, 0, False), gathered)
        )

    return lax.fori_loop(0, ahead, one, state)


def rms_apply(values, gain):
    scale = lax.rsqrt(jnp.mean(values * values, axis=-1, keepdims=True) + epsilon)
    return values * scale * gain


def feature_map(projected):
    count = projected.shape[0]
    pieces = projected.reshape(count, -1, F)
    square = (pieces[:, :, :, None] * pieces[:, :, None, :]).reshape(count, pieces.shape[1], F * F)
    return jnp.concatenate(
        [jnp.ones_like(pieces[:, :, :1]), pieces * F ** (-0.25), square * (2.0 * F) ** (-0.5)],
        axis=-1,
    )


def swiglu(gate, up_part):
    return jax.nn.silu(gate) * up_part


def round_trip(values):
    return lax.optimization_barrier(values.astype(jnp.bfloat16)).astype(jnp.float32)


def add_pair(earlier, later):
    return (earlier[0] + later[0], earlier[1] + later[1])


def block_pass(tokens, upstream, gathered):
    gain_one, query_w, key_w, value_w, out_w, gain_two, gate_w, up_w, down_w = gathered
    f32 = jnp.float32
    bf16 = jnp.bfloat16
    stream = tokens.astype(f32)
    count = stream.shape[0]
    normed_f, norm_one_pull = jax.vjp(rms_apply, stream, gain_one.astype(f32))
    normed = normed_f.astype(bf16)
    queries = jnp.dot(normed, query_w, preferred_element_type=f32)
    keys_all = jnp.dot(normed, key_w, preferred_element_type=f32)
    values = jnp.dot(normed, value_w, preferred_element_type=f32).astype(bf16)
    query_feat_f, query_pull = jax.vjp(feature_map, queries)
    key_feat_f, key_pull = jax.vjp(feature_map, keys_all)
    query_feat = jnp.transpose(query_feat_f.astype(bf16), (1, 0, 2))
    key_feat = jnp.transpose(key_feat_f.astype(bf16), (1, 0, 2))
    value_heads = jnp.transpose(values.reshape(count, -1, DV), (1, 0, 2))
    causal = (jnp.arange(count)[:, None] >= jnp.arange(count)[None, :]).astype(f32)
    scores = jnp.einsum("htf,hsf->hts", query_feat, key_feat, preferred_element_type=f32) * causal
    weighted = scores.astype(bf16)
    num_local = jnp.einsum("hts,hsd->htd", weighted, value_heads, preferred_element_type=f32)
    den_local = jnp.sum(weighted.astype(f32), axis=-1)
    states = jnp.einsum("hsf,hsd->hfd", key_feat, value_heads, preferred_element_type=f32)
    totals = jnp.sum(key_feat.astype(f32), axis=1)
    state_before, total_before = entering(
        (states, totals), "seq", add_pair, (jnp.zeros_like(states), jnp.zeros_like(totals)), False
    )
    query_wide = query_feat.astype(f32)
    numer = num_local + jnp.einsum("htf,hfd->htd", query_wide, state_before, precision=highest)
    denom = den_local + jnp.einsum("htf,hf->ht", query_wide, total_before, precision=highest)
    ratio = numer / denom[..., None]
    heads_out = jnp.transpose(ratio, (1, 0, 2)).reshape(count, -1).astype(bf16)
    attended = lax.psum(jnp.dot(heads_out, out_w, preferred_element_type=f32), "head")
    middle = stream + attended
    normed_two_f, norm_two_pull = jax.vjp(rms_apply, middle, gain_two.astype(f32))
    normed_two = normed_two_f.astype(bf16)
    gate = jnp.dot(normed_two, gate_w, preferred_element_type=f32)
    up_part = jnp.dot(normed_two, up_w, preferred_element_type=f32)
    active, active_pull = jax.vjp(swiglu, gate, up_part)
    hidden = active.astype(bf16)
    branch = lax.psum(
        jnp.dot(hidden, down_w, preferred_element_type=f32).astype(jnp.bfloat16), "head"
    ).astype(jnp.float32)
    result = (middle + branch).astype(bf16)
    grad_down = jnp.dot(hidden.T, upstream, preferred_element_type=f32)
    d_hidden = jnp.dot(upstream, down_w.T, preferred_element_type=f32)
    d_gate_f, d_up_f = active_pull(d_hidden)
    d_gate = d_gate_f.astype(bf16)
    d_up = d_up_f.astype(bf16)
    grad_gate = jnp.dot(normed_two.T, d_gate, preferred_element_type=f32)
    grad_up = jnp.dot(normed_two.T, d_up, preferred_element_type=f32)
    d_normed_two = lax.psum(
        jnp.dot(d_gate, gate_w.T, preferred_element_type=f32)
        + jnp.dot(d_up, up_w.T, preferred_element_type=f32),
        "head",
    )
    d_middle_norm, grad_gain2 = norm_two_pull(d_normed_two)
    d_middle = upstream.astype(f32) + d_middle_norm
    d_attended = d_middle.astype(bf16)
    grad_out = jnp.dot(heads_out.T, d_attended, preferred_element_type=f32)
    d_heads = jnp.transpose(
        jnp.dot(d_attended, out_w.T, preferred_element_type=f32).reshape(count, -1, DV), (1, 0, 2)
    )
    d_numer = (d_heads / denom[..., None]).astype(bf16)
    d_denom = -jnp.sum(d_heads * ratio, axis=-1) / denom
    d_numer_wide = d_numer.astype(f32)
    d_before = jnp.einsum("htf,htd->hfd", query_wide, d_numer_wide, precision=highest)
    d_total_before = jnp.einsum("htf,ht->hf", query_wide, d_denom, precision=highest)
    d_state, d_total = entering(
        (d_before, d_total_before),
        "seq",
        add_pair,
        (jnp.zeros_like(d_before), jnp.zeros_like(d_total_before)),
        True,
    )
    d_scores = (
        (
            jnp.einsum("htd,hsd->hts", d_numer, value_heads, preferred_element_type=f32)
            + d_denom[..., None]
        )
        * causal
    ).astype(bf16)
    d_values = jnp.einsum(
        "hts,htd->hsd", weighted, d_numer, preferred_element_type=f32
    ) + jnp.einsum("hsf,hfd->hsd", key_feat.astype(f32), d_state, precision=highest)
    d_query_feat = (
        jnp.einsum("hts,hsf->htf", d_scores, key_feat, preferred_element_type=f32)
        + jnp.einsum("htd,hfd->htf", d_numer_wide, state_before, precision=highest)
        + d_denom[..., None] * total_before[:, None, :]
    )
    d_key_feat = (
        jnp.einsum("hts,htf->hsf", d_scores, query_feat, preferred_element_type=f32)
        + jnp.einsum("hsd,hfd->hsf", value_heads.astype(f32), d_state, precision=highest)
        + d_total[:, None, :]
    )
    d_queries = query_pull(jnp.transpose(round_trip(d_query_feat), (1, 0, 2)))[0].astype(bf16)
    d_keys = key_pull(jnp.transpose(round_trip(d_key_feat), (1, 0, 2)))[0].astype(bf16)
    d_values_flat = jnp.transpose(d_values, (1, 0, 2)).reshape(count, -1).astype(bf16)
    grad_query = jnp.dot(normed.T, d_queries, preferred_element_type=f32)
    grad_key = jnp.dot(normed.T, d_keys, preferred_element_type=f32)
    grad_value = jnp.dot(normed.T, d_values_flat, preferred_element_type=f32)
    d_normed_part = (
        jnp.dot(d_queries, query_w.T, preferred_element_type=f32)
        + jnp.dot(d_keys, key_w.T, preferred_element_type=f32)
        + jnp.dot(d_values_flat, value_w.T, preferred_element_type=f32)
    )
    d_normed = lax.psum(d_normed_part.astype(jnp.bfloat16), "head").astype(jnp.float32)
    d_stream_norm, grad_gain1 = norm_one_pull(d_normed)
    input_grad = (d_middle + d_stream_norm).astype(bf16)
    return (
        result,
        input_grad,
        grad_gain1,
        grad_query,
        grad_key,
        grad_value,
        grad_out,
        grad_gain2,
        grad_gate,
        grad_up,
        grad_down,
    )


def local(
    inputs, norm_gain1, w_query, w_key, w_value, w_out, norm_gain2, w_gate, w_up, w_down, cotangent
):
    micro = inputs.shape[0]
    summed = None
    results = []
    input_grads = []
    for step_index in range(micro):
        gathered = (
            lax.all_gather(norm_gain1, "seq", axis=0, tiled=True),
            lax.all_gather(w_query, "seq", axis=0, tiled=True),
            lax.all_gather(w_key, "seq", axis=0, tiled=True),
            lax.all_gather(w_value, "seq", axis=0, tiled=True),
            lax.all_gather(w_out, "seq", axis=1, tiled=True),
            lax.all_gather(norm_gain2, "seq", axis=0, tiled=True),
            lax.all_gather(w_gate, "seq", axis=0, tiled=True),
            lax.all_gather(w_up, "seq", axis=0, tiled=True),
            lax.all_gather(w_down, "seq", axis=1, tiled=True),
        )
        (
            result,
            input_grad,
            grad_gain1,
            grad_query,
            grad_key,
            grad_value,
            grad_out,
            grad_gain2,
            grad_gate,
            grad_up,
            grad_down,
        ) = block_pass(inputs[step_index], cotangent[step_index], gathered)
        results.append(result)
        input_grads.append(input_grad)
        fresh = (
            lax.psum_scatter(grad_gain1, "seq", scatter_dimension=0, tiled=True),
            lax.psum_scatter(grad_query, "seq", scatter_dimension=0, tiled=True),
            lax.psum_scatter(grad_key, "seq", scatter_dimension=0, tiled=True),
            lax.psum_scatter(grad_value, "seq", scatter_dimension=0, tiled=True),
            lax.psum_scatter(grad_out, "seq", scatter_dimension=1, tiled=True),
            lax.psum_scatter(grad_gain2, "seq", scatter_dimension=0, tiled=True),
            lax.psum_scatter(grad_gate, "seq", scatter_dimension=0, tiled=True),
            lax.psum_scatter(grad_up, "seq", scatter_dimension=0, tiled=True),
            lax.psum_scatter(grad_down, "seq", scatter_dimension=1, tiled=True),
        )
        summed = (
            fresh
            if summed is None
            else tuple((older + newer for older, newer in zip(summed, fresh)))
        )
    return (
        jnp.stack(results),
        jnp.stack(input_grads),
        summed[0],
        summed[1],
        summed[2],
        summed[3],
        summed[4],
        summed[5],
        summed[6],
        summed[7],
        summed[8],
    )


MESH = pl.DeviceIdType.MESH
bf16 = jnp.bfloat16
f32 = jnp.float32
ZED = 4
VMEM_LIMIT = 60 * 1024 * 1024


def where_am_i():
    place = lax.axis_index("seq")
    return place % 2, (place // 2) % 2, place // 4, lax.axis_index("head")


def index_of(z, y, x):
    return (z * 2 + y) * 2 + x


def remote(src, dst, send, recv, place, head):
    return pltpu.make_async_remote_copy(
        src_ref=src, dst_ref=dst, send_sem=send, recv_sem=recv, device_id=(place, head),
        device_id_type=MESH,
    )


def arrived(dst, send, recv, place, head):
    remote(dst, dst, send, recv, place, head).wait_recv()


def params():
    return pltpu.CompilerParams(has_side_effects=True, vmem_limit_bytes=VMEM_LIMIT)


ANY = pl.BlockSpec(memory_space=pl.ANY)
VMEM = pl.BlockSpec(memory_space=pltpu.VMEM)
DMA = pltpu.SemaphoreType.DMA
ORDER = (0, 1, 3, 2)


def mix(a, b, over):
    return lax.dot_general(a, b, (over, ((), ())), preferred_element_type=f32)


CHUNK = 512
COLS = 256


def spread(got, q_t, k_t, va):
    count = got.shape[2]
    for b in range(got.shape[0]):
        q_t[:, b * count : (b + 1) * count] = got[b, 0:F, :]
        k_t[:, b * count : (b + 1) * count] = got[b, F : 2 * F, :]
        va[b * count : (b + 1) * count, 0:DV] = got[b, 2 * F :, :]
    va[:, DV:] = jnp.ones((va.shape[0], va.shape[1] - DV), bf16)


def lower(count):
    return lax.broadcasted_iota(jnp.int32, (count, count), 0) >= lax.broadcasted_iota(
        jnp.int32, (count, count), 1
    )


def attend_rows(qi, q_t, k_t, va, ratio, den, causal):
    qs = slice(qi * CHUNK, (qi + 1) * CHUNK)
    acc = jnp.zeros((CHUNK, va.shape[1]), f32)
    for kj in range(qi + 1):
        ks = slice(kj * CHUNK, (kj + 1) * CHUNK)
        s = mix(q_t[:, qs], k_t[:, ks], ((0,), (0,)))
        p = 1.0 + s * (0.25 + s * (1.0 / 32.0))
        if kj == qi:
            p = jnp.where(causal, p, 0.0)
        acc = acc + mix(p.astype(bf16), va[ks, :], ((1,), (0,)))
    ratio[qs, :] = acc[:, :DV] / acc[:, DV:]
    den[qs, :] = acc[:, DV:]


def front_kernel(
    a1, a2, m, xh, xin,
    wa1, wa2, wm, got, ratio, den, heads_out, middle, near,
    w1, w2, pack, q_t, k_t, va, ob, part, other,
    ls, zs, zr, ps, pr, e1s, e1r, e2s, e2r, ws, wr, ns, nr, ds, dr,
):
    x, y, z, h = where_am_i()
    me = index_of(z, y, x)
    at_x, at_y = index_of(z, y, 1 - x), index_of(z, 1 - y, x)
    count = xin.shape[1]
    heads = 16 // xin.shape[0]
    late = []

    def go(copy):
        copy.start()
        late.append(copy)

    def rows(zz, yy, xx):
        return pl.ds(pl.multiple_of(index_of(zz, yy, xx) * 128, 128), 128)

    mine = rows(z, y, x)
    kept = [
        pltpu.make_async_copy(a1, w1.at[mine], ls.at[0]),
        pltpu.make_async_copy(a2, w2.at[mine], ls.at[1]),
        pltpu.make_async_copy(m.at[z], wm.at[mine], ls.at[2]),
    ]
    for copy in kept:
        copy.start()
    dest = (w1, w2, wm)

    def line(kind):
        for d in (1, 3, 2):
            zz = (z + d) % ZED
            src = (a1, a2, m.at[zz])[kind]
            go(remote(src, dest[kind].at[mine], zs.at[kind, d], zr.at[kind, d], index_of(zz, y, x), h))

    def plane(kind, d):
        block = dest[kind].at[rows((z + ZED - d) % ZED, y, x)]
        if d:
            arrived(block, zs.at[kind, d], zr.at[kind, d], me, h)
        else:
            kept[kind].wait()
        go(remote(block, block, ps.at[kind, d, 0], pr.at[kind, d, 0], at_x, h))
        go(remote(block, block, ps.at[kind, d, 1], pr.at[kind, d, 1], at_y, h))

    def onward(kind, d):
        w = dest[kind]
        zz = (z + ZED - d) % ZED
        half = w.shape[1] // 2
        from_x, from_y = rows(zz, y, 1 - x), rows(zz, 1 - y, x)
        arrived(w.at[from_x], ps.at[kind, d, 0], pr.at[kind, d, 0], me, h)
        arrived(w.at[from_y], ps.at[kind, d, 1], pr.at[kind, d, 1], me, h)
        left = w.at[from_y, pl.ds(0, half)]
        right = w.at[from_x, pl.ds(half, half)]
        go(remote(left, left, ps.at[kind, d, 2], pr.at[kind, d, 2], at_x, h))
        go(remote(right, right, ps.at[kind, d, 3], pr.at[kind, d, 3], at_y, h))

    def corner(kind):
        w = dest[kind]
        half = w.shape[1] // 2
        for d in ORDER:
            far = rows((z + ZED - d) % ZED, 1 - y, 1 - x)
            arrived(w.at[far, pl.ds(0, half)], ps.at[kind, d, 2], pr.at[kind, d, 2], me, h)
            arrived(w.at[far, pl.ds(half, half)], ps.at[kind, d, 3], pr.at[kind, d, 3], me, h)

    line(0)
    plane(0, 0)
    plane(0, 1)
    onward(0, 0)
    plane(0, 3)
    line(1)
    onward(0, 1)
    plane(0, 2)
    onward(0, 3)
    plane(1, 0)
    onward(0, 2)
    corner(0)
    out1 = pltpu.make_async_copy(w1, wa1, ls.at[3])
    out1.start()
    kq = mix(xh[...], w1[:, 0 : 2 * heads * F], ((1,), (0,)))
    qk = jnp.transpose(kq).astype(bf16)
    for mb in range(16 // heads):
        for k in range(heads):
            t = k + heads * mb
            cols = slice(mb * count, (mb + 1) * count)
            pack[t, 0:F, :] = qk[k * F : (k + 1) * F, cols]
            pack[t, F : 2 * F, :] = qk[(heads + k) * F : (heads + k + 1) * F, cols]
    for c in range(heads * DV // COLS):
        at = 2 * heads * F + c * COLS
        val = mix(xh[...], w1[:, at : at + COLS], ((1,), (0,))).astype(bf16)
        for mb in range(16 // heads):
            for i in range(COLS // DV):
                t = c * (COLS // DV) + i + heads * mb
                pack[t, 2 * F :, :] = val[mb * count : (mb + 1) * count, i * DV : (i + 1) * DV]
    keep = pltpu.make_async_copy(pack.at[me], got.at[me], ls.at[4])
    keep.start()
    for d in range(1, 16):
        there = (me + d) % 16
        go(remote(pack.at[there], got.at[me], e1s.at[d], e1r.at[d], there, h))
    plane(1, 1)
    onward(1, 0)
    plane(1, 3)
    onward(1, 1)
    plane(1, 2)
    onward(1, 3)
    keep.wait()
    for d in range(1, 16):
        arrived(got.at[(me + 16 - d) % 16], e1s.at[d], e1r.at[d], me, h)
    line(2)
    plane(2, 0)
    onward(1, 2)
    spread(got, q_t, k_t, va)
    causal = lower(CHUNK)
    for qi in range(va.shape[0] // CHUNK):
        attend_rows(qi, q_t, k_t, va, ratio, den, causal)
    for b in range(16):
        ob[b, :, :] = ratio[b * count : (b + 1) * count, :].astype(bf16)

    def window(source):
        return heads_out.at[
            pl.ds(pl.multiple_of((source // heads) * count, count), count),
            pl.ds(pl.multiple_of((source % heads) * DV, DV), DV),
        ]

    keep = pltpu.make_async_copy(ob.at[me], window(me), ls.at[4])
    keep.start()
    for d in range(1, 16):
        there = (me + d) % 16
        go(remote(ob.at[there], window(me), e2s.at[d], e2r.at[d], there, h))
    onward(2, 0)
    corner(1)
    out2 = pltpu.make_async_copy(w2, wa2, ls.at[5])
    out2.start()
    keep.wait()
    for d in range(1, 16):
        arrived(window((me + 16 - d) % 16), e2s.at[d], e2r.at[d], me, h)
    wide = part.shape[1]
    swaps = []
    for c in range(wide // COLS):
        cols = pl.ds(c * COLS, COLS)
        part[:, c * COLS : (c + 1) * COLS] = mix(
            heads_out[...], w2[c * COLS : (c + 1) * COLS, :], ((1,), (1,))
        )
        go(remote(part.at[:, cols], other.at[:, cols], ws.at[c], wr.at[c], me, 1 - h))
    for c in range(wide // COLS):
        cols = pl.ds(c * COLS, COLS)
        arrived(other.at[:, cols], ws.at[c], wr.at[c], me, 1 - h)

    def one(mb):
        def body(turn, carry):
            row = pl.ds(pl.multiple_of(turn * 16, 16), 16)
            flat = pl.ds(pl.multiple_of(mb * count + turn * 16, 16), 16)
            mid = xin[mb, row, :].astype(f32) + (part[flat, :] + other[flat, :])
            middle[mb, row, :] = mid
            scale = lax.rsqrt(jnp.mean(mid * mid, axis=-1, keepdims=True) + epsilon)
            near[z, mb, row, :] = (mid * scale).astype(bf16)
            return carry

        lax.fori_loop(0, count // 16, body, 0)

    one(h)
    for d in (2, 1, 3):
        there = index_of((z + d) % ZED, y, x)
        go(remote(near.at[z, h], near.at[z, h], ns.at[d], nr.at[d], there, h))
    one(1 - h)
    plane(2, 1)
    plane(2, 3)
    onward(2, 1)
    plane(2, 2)
    onward(2, 3)
    for d in (1, 3, 2):
        zz = (z + ZED - d) % ZED
        arrived(near.at[zz, h], ns.at[d], nr.at[d], me, h)
        go(remote(near.at[zz, h], near.at[zz, h], ds.at[d], dr.at[d], me, 1 - h))
    onward(2, 2)
    corner(2)
    for d in (1, 3, 2):
        zz = (z + ZED - d) % ZED
        arrived(near.at[zz, 1 - h], ds.at[d], dr.at[d], me, 1 - h)
    out1.wait()
    out2.wait()
    for copy in late:
        copy.wait_send()


def front(a1, a2, m, xh, xin):
    mbs, count, wide = xin.shape
    depth = 16 * count
    wide1, wide2 = a1.shape[1], a2.shape[1]
    shape = jax.ShapeDtypeStruct
    return pl.pallas_call(
        front_kernel,
        out_shape=(
            shape((wide, wide1), bf16),
            shape((wide, wide2), bf16),
            shape((wide, m.shape[2]), bf16),
            shape((16, 2 * F + DV, count), bf16),
            shape((depth, DV), f32),
            shape((depth, DV), f32),
            shape((mbs * count, wide2), bf16),
            shape(xin.shape, f32),
            shape((ZED,) + xin.shape, bf16),
        ),
        in_specs=[ANY] * 3 + [VMEM] * 2,
        out_specs=(ANY,) * 3 + (VMEM,) * 6,
        scratch_shapes=[
            pltpu.VMEM((wide, wide1), bf16),
            pltpu.VMEM((wide, wide2), bf16),
            pltpu.VMEM((16, 2 * F + DV, count), bf16),
            pltpu.VMEM((F, depth), bf16),
            pltpu.VMEM((F, depth), bf16),
            pltpu.VMEM((depth, 2 * DV), bf16),
            pltpu.VMEM((16, count, DV), bf16),
            pltpu.VMEM((mbs * count, wide), f32),
            pltpu.VMEM((mbs * count, wide), f32),
            DMA((6,)), DMA((3, 4)), DMA((3, 4)), DMA((3, 4, 4)), DMA((3, 4, 4)),
            DMA((16,)), DMA((16,)), DMA((16,)), DMA((16,)),
            DMA((wide // COLS,)), DMA((wide // COLS,)), DMA((4,)), DMA((4,)), DMA((4,)), DMA((4,)),
        ],
        compiler_params=params(),
        name="front",
    )(a1, a2, m, xh, xin)


def attend_back_body(got, ratio, den, d_o, d_qk, d_v, q_t, k_t, va, da, dn_t):
    spread(got, q_t, k_t, va)
    depth = va.shape[0]
    lane = lax.broadcasted_iota(jnp.int32, (CHUNK, DV), 1)
    for qi in range(depth // CHUNK):
        qs = slice(qi * CHUNK, (qi + 1) * CHUNK)
        dn = d_o[qs, :].astype(f32) / den[qs, :]
        dd = -jnp.sum(dn * ratio[qs, :], axis=-1, keepdims=True)
        big = dd.astype(bf16).astype(f32)
        da[qs, 0:DV] = dn.astype(bf16)
        da[qs, DV:] = jnp.where(lane == 0, big, jnp.where(lane == 1, dd - big, 0.0)).astype(bf16)
        dn_t[:, qs] = jnp.transpose(dn).astype(bf16)
    causal = lower(CHUNK)
    for kj in range(depth // CHUNK):
        ks = slice(kj * CHUNK, (kj + 1) * CHUNK)
        acc_k = jnp.zeros((F, CHUNK), f32)
        acc_v = jnp.zeros((DV, CHUNK), f32)
        for qi in range(kj, depth // CHUNK):
            qs = slice(qi * CHUNK, (qi + 1) * CHUNK)
            s = mix(q_t[:, qs], k_t[:, ks], ((0,), (0,)))
            p = 1.0 + s * (0.25 + s * (1.0 / 32.0))
            d_s = mix(da[qs, :], va[ks, :], ((1,), (1,))) * (0.25 + s * (1.0 / 16.0))
            if kj == qi:
                p = jnp.where(causal, p, 0.0)
                d_s = jnp.where(causal, d_s, 0.0)
            d_s = d_s.astype(bf16)
            acc_v = acc_v + mix(dn_t[:, qs], p.astype(bf16), ((1,), (0,)))
            acc_k = acc_k + mix(q_t[:, qs], d_s, ((1,), (0,)))
            d_q = mix(k_t[:, ks], d_s, ((1,), (1,)))
            d_qk[0:F, qs] = d_q if kj == 0 else d_qk[0:F, qs] + d_q
        d_qk[F : 2 * F, ks] = acc_k
        d_v[ks, :] = jnp.transpose(acc_v)


def share_kernel(g, gg, ls, zs, zr, ds, dr):
    x, y, z, h = where_am_i()
    me = index_of(z, y, x)
    local = pltpu.make_async_copy(g, gg.at[z], ls)
    local.start()
    copies = []
    for d in (2, 1, 3):
        there = index_of((z + d) % ZED, y, x)
        copies.append(remote(g.at[h], gg.at[z, h], zs.at[d], zr.at[d], there, h))
    for copy in copies:
        copy.start()
    for d in (1, 3, 2):
        zz = (z + ZED - d) % ZED
        arrived(gg.at[zz, h], zs.at[d], zr.at[d], me, h)
        copy = remote(gg.at[zz, h], gg.at[zz, h], ds.at[d], dr.at[d], me, 1 - h)
        copy.start()
        copies.append(copy)
    for d in (1, 3, 2):
        zz = (z + ZED - d) % ZED
        arrived(gg.at[zz, 1 - h], ds.at[d], dr.at[d], me, 1 - h)
    local.wait()
    for copy in copies:
        copy.wait_send()


def share(g):
    return pl.pallas_call(
        share_kernel,
        out_shape=jax.ShapeDtypeStruct((ZED,) + g.shape, bf16),
        in_specs=[ANY],
        out_specs=ANY,
        scratch_shapes=[DMA, DMA((4,)), DMA((4,)), DMA((4,)), DMA((4,))],
        compiler_params=params(),
        name="share",
    )(g)


FAR = (2, 1, 3, 0)


def chunk(turn):
    return pl.ds(pl.multiple_of(turn * 16, 16), 16)


class Scatter:
    def __init__(self, g, low_acc, high_acc, fin, out, r1x, r1y, r2x, r2y, s, q, go):
        self.g, self.low_acc, self.high_acc, self.fin, self.out = g, low_acc, high_acc, fin, out
        self.r1x, self.r1y, self.r2x, self.r2y, self.s, self.q = r1x, r1y, r2x, r2y, s, q
        self.go = go
        self.x, self.y, self.z, self.h = where_am_i()
        self.me = index_of(self.z, self.y, self.x)
        self.at_x = index_of(self.z, self.y, 1 - self.x)
        self.at_y = index_of(self.z, 1 - self.y, self.x)
        self.half = r1x.shape[-1]
        self.low, self.high = pl.ds(0, self.half), pl.ds(self.half, self.half)

    def first(self, d):
        zz, x, y, g = (self.z + d) % ZED, self.x, self.y, self.g
        self.go(remote(g.at[zz, :, 1 - x, :, self.low], self.r1x.at[d], self.s.at[d, 0], self.q.at[d, 0], self.at_x, self.h))
        self.go(remote(g.at[zz, 1 - y, :, :, self.high], self.r1y.at[d], self.s.at[d, 1], self.q.at[d, 1], self.at_y, self.h))

    def second(self, d):
        x, y, me, h, r1x, r1y = self.x, self.y, self.me, self.h, self.r1x, self.r1y
        arrived(r1x.at[d], self.s.at[d, 0], self.q.at[d, 0], me, h)
        arrived(r1y.at[d], self.s.at[d, 1], self.q.at[d, 1], me, h)
        low_acc, high_acc = self.low_acc(d), self.high_acc(d)

        def body(i, carry):
            row = chunk(i)
            low_acc[row, :] = (
                low_acc[row, :].astype(f32) + r1x[d, 1 - y, row, :].astype(f32)
            ).astype(bf16)
            high_acc[row, :] = (
                high_acc[row, :].astype(f32) + r1y[d, 1 - x, row, :].astype(f32)
            ).astype(bf16)
            return carry

        lax.fori_loop(0, 8, body, 0)
        self.go(remote(low_acc, self.r2y.at[d], self.s.at[d, 2], self.q.at[d, 2], self.at_y, h))
        self.go(remote(high_acc, self.r2x.at[d], self.s.at[d, 3], self.q.at[d, 3], self.at_x, h))

    def third(self, d):
        x, y, me, h, z = self.x, self.y, self.me, self.h, self.z
        arrived(self.r2y.at[d], self.s.at[d, 2], self.q.at[d, 2], me, h)
        arrived(self.r2x.at[d], self.s.at[d, 3], self.q.at[d, 3], me, h)
        fin, low, high = self.fin(d), self.low, self.high
        target = fin if d else self.out.at[z]

        def body(i, carry):
            row = chunk(i)
            target[row, low] = (
                fin[row, low].astype(f32)
                + self.r1x[d, y, row, :].astype(f32)
                + self.r2y[d, row, :].astype(f32)
            ).astype(bf16)
            target[row, high] = (
                fin[row, high].astype(f32)
                + self.r1y[d, x, row, :].astype(f32)
                + self.r2x[d, row, :].astype(f32)
            ).astype(bf16)
            return carry

        lax.fori_loop(0, 8, body, 0)
        if d:
            there = index_of((z + d) % ZED, y, x)
            self.go(remote(fin, self.out.at[z], self.s.at[d, 4], self.q.at[d, 4], there, h))

    def last(self):
        for d in (1, 3, 2):
            arrived(
                self.out.at[(self.z + ZED - d) % ZED], self.s.at[d, 4], self.q.at[d, 4], self.me, self.h
            )


class Combine:
    def __init__(self, t, out, other, summed, landed, ls, s, q, go):
        self.t, self.out, self.other, self.summed, self.landed = t, out, other, summed, landed
        self.ls, self.s, self.q, self.go = ls, s, q, go
        self.x, self.y, self.z, self.h = where_am_i()
        self.me = index_of(self.z, self.y, self.x)

    def begin(self):
        t, h, other = self.t, self.h, self.other
        self.own = {}
        for d in FAR:
            zz = (self.z + d) % ZED
            self.own[d] = pltpu.make_async_copy(t.at[zz, h], self.summed.at[d], self.ls.at[d])
            self.own[d].start()
            self.go(remote(t.at[zz, 1 - h], other.at[d], self.s.at[d, 0], self.q.at[d, 0], self.me, 1 - h))

    def spread(self):
        summed, other = self.summed, self.other
        for d in FAR:
            zz = (self.z + d) % ZED
            self.own[d].wait()
            arrived(other.at[d], self.s.at[d, 0], self.q.at[d, 0], self.me, 1 - self.h)

            def add(turn, carry):
                row = chunk(turn)
                summed[d, row, :] = (
                    summed[d, row, :].astype(f32) + other[d, row, :].astype(f32)
                ).astype(bf16)
                return carry

            lax.fori_loop(0, 8, add, 0)
            if d:
                there = index_of(zz, self.y, self.x)
                self.go(remote(summed.at[d], self.landed.at[d], self.s.at[d, 1], self.q.at[d, 1], there, self.h))

    def total(self):
        summed, landed, out, h = self.summed, self.landed, self.out, self.h
        for d in (1, 3, 2):
            arrived(landed.at[d], self.s.at[d, 1], self.q.at[d, 1], self.me, h)

        def body(turn, carry):
            row = chunk(turn)
            acc = summed[0, row, :].astype(f32)
            for d in (1, 2, 3):
                acc = acc + landed[d, row, :].astype(f32)
            out[h, row, :] = acc.astype(bf16)
            return carry

        lax.fori_loop(0, 8, body, 0)
        self.go(remote(out.at[h], out.at[h], self.s.at[0, 1], self.q.at[0, 1], self.me, 1 - h))

    def done(self):
        arrived(self.out.at[1 - self.h], self.s.at[0, 1], self.q.at[0, 1], self.me, 1 - self.h)


def back_kernel(
    gm, t, wo, mid, cot, got, ratio, den,
    zm, d_mid, d_att, home,
    r1x, r1y, r2x, r2y, f1, f2, fin, e2, other, summed, landed, w2, pack, d_o, d_qk, d_v,
    q_t, k_t, va, da, dn_t, pack2,
    ls, fs, gs, gq, cs, cq, e1s, e1r, e2s, e2r,
):
    x, y, z, h = where_am_i()
    me = index_of(z, y, x)
    count = mid.shape[1]
    heads = 16 // mid.shape[0]
    late = []

    def go(copy):
        copy.start()
        late.append(copy)

    combine = Combine(t, e2, other, summed, landed, ls, cs, cq, go)
    scatter = Scatter(
        gm, lambda d: f1.at[d], lambda d: f2.at[d], lambda d: fin.at[d], zm,
        r1x, r1y, r2x, r2y, gs, gq, go,
    )
    combine.begin()
    for d in FAR:
        scatter.first(d)
    keep = {}
    for d in FAR:
        zz = (z + d) % ZED
        keep[d] = [
            pltpu.make_async_copy(gm.at[zz, 1 - y, x, :, scatter.low], f1.at[d], fs.at[d, 0]),
            pltpu.make_async_copy(gm.at[zz, y, 1 - x, :, scatter.high], f2.at[d], fs.at[d, 1]),
            pltpu.make_async_copy(gm.at[zz, y, x], fin.at[d], fs.at[d, 2]),
        ]
        for copy in keep[d]:
            copy.start()
    weight = pltpu.make_async_copy(wo, w2, ls.at[4])
    weight.start()
    combine.spread()
    for d in FAR:
        for copy in keep[d]:
            copy.wait()
    weight.wait()
    scatter.second(2)
    scatter.second(1)
    combine.total()
    combine.done()

    for mb in range(mid.shape[0]):

        def body(turn, carry):
            row = chunk(turn)
            m = mid[mb, row, :]
            scale = lax.rsqrt(jnp.mean(m * m, axis=-1, keepdims=True) + epsilon)
            hat = m * scale
            e = e2[mb, row, :].astype(f32)
            d_m = cot[mb, row, :].astype(f32) + scale * (
                e - hat * jnp.mean(e * hat, axis=-1, keepdims=True)
            )
            d_mid[mb, row, :] = d_m
            d_att[pl.ds(pl.multiple_of(mb * count + turn * 16, 16), 16), :] = d_m.astype(bf16)
            return carry

        lax.fori_loop(0, count // 16, body, 0)
    for c in range(heads * DV // COLS):
        val = mix(d_att[...], w2[:, c * COLS : (c + 1) * COLS], ((1,), (0,))).astype(bf16)
        for mb in range(16 // heads):
            for i in range(COLS // DV):
                pack[c * (COLS // DV) + i + heads * mb, :, :] = val[
                    mb * count : (mb + 1) * count, i * DV : (i + 1) * DV
                ]

    def window(source):
        return d_o.at[pl.ds(pl.multiple_of(source * count, count), count)]

    own = pltpu.make_async_copy(pack.at[me], window(me), ls.at[5])
    own.start()
    for d in range(1, 16):
        there = (me + d) % 16
        go(remote(pack.at[there], window(me), e1s.at[d], e1r.at[d], there, h))
    scatter.second(3)
    own.wait()
    for d in range(1, 16):
        arrived(window((me + 16 - d) % 16), e1s.at[d], e1r.at[d], me, h)
    scatter.second(0)
    scatter.third(2)
    attend_back_body(got, ratio, den, d_o, d_qk, d_v, q_t, k_t, va, da, dn_t)
    for b in range(16):
        pack2[b, 0 : 2 * F, :] = d_qk[:, b * count : (b + 1) * count].astype(bf16)
        pack2[b, 2 * F :, :] = d_v[b * count : (b + 1) * count, :].astype(bf16)
    own = pltpu.make_async_copy(pack2.at[me], home.at[me], ls.at[5])
    own.start()
    for d in range(1, 16):
        there = (me + d) % 16
        go(remote(pack2.at[there], home.at[me], e2s.at[d], e2r.at[d], there, h))
    scatter.third(1)
    scatter.third(3)
    scatter.third(0)
    own.wait()
    for d in range(1, 16):
        arrived(home.at[(me + 16 - d) % 16], e2s.at[d], e2r.at[d], me, h)
    scatter.last()
    for copy in late:
        copy.wait_send()


def scatter_room(wide):
    return [
        pltpu.VMEM((4, 2, 128, wide // 2), bf16),
        pltpu.VMEM((4, 2, 128, wide // 2), bf16),
        pltpu.VMEM((4, 128, wide // 2), bf16),
        pltpu.VMEM((4, 128, wide // 2), bf16),
    ]


def back(gm, t, wo, mid, cot, got, ratio, den):
    mbs, count, wide = cot.shape
    depth = 16 * count
    shape = jax.ShapeDtypeStruct
    cols = gm.shape[-1]
    line = pltpu.VMEM((ZED, count, wide), bf16)
    return pl.pallas_call(
        back_kernel,
        out_shape=(
            shape((ZED, 128, cols), bf16),
            shape(cot.shape, f32),
            shape((mbs * count, wide), bf16),
            shape((16, 2 * F + DV, count), bf16),
        ),
        in_specs=[ANY] * 3 + [VMEM] * 5,
        out_specs=(VMEM,) * 4,
        scratch_shapes=scatter_room(cols) + [
            pltpu.VMEM((4, 128, cols // 2), bf16),
            pltpu.VMEM((4, 128, cols // 2), bf16),
            pltpu.VMEM((4, 128, cols), bf16),
            pltpu.VMEM(cot.shape, bf16), line, line, line,
            pltpu.VMEM(wo.shape, bf16),
            pltpu.VMEM((16, count, DV), bf16),
            pltpu.VMEM((depth, DV), bf16),
            pltpu.VMEM((2 * F, depth), f32),
            pltpu.VMEM((depth, DV), f32),
            pltpu.VMEM((F, depth), bf16),
            pltpu.VMEM((F, depth), bf16),
            pltpu.VMEM((depth, 2 * DV), bf16),
            pltpu.VMEM((depth, 2 * DV), bf16),
            pltpu.VMEM((DV, depth), bf16),
            pltpu.VMEM((16, 2 * F + DV, count), bf16),
            DMA((6,)), DMA((4, 3)), DMA((4, 5)), DMA((4, 5)), DMA((4, 2)), DMA((4, 2)),
            DMA((16,)), DMA((16,)), DMA((16,)), DMA((16,)),
        ],
        compiler_params=params(),
        name="back",
    )(gm.reshape(ZED, 2, 2, 128, cols), t, wo, mid, cot, got, ratio, den)


def end_kernel(
    t, home, xh, d_att, heads_out, wa1, d_mid, xin, mid,
    za, d_in, outputs,
    g, r1x, r1y, r2x, r2y, branch, other, summed, landed, w1, dqk_t, dqkv, part, swap,
    ls, gs, gq, cs, cq, ws, wr,
):
    x, y, z, h = where_am_i()
    me = index_of(z, y, x)
    mbs, count, wide = xin.shape
    heads = 16 // mbs
    qk, vv = 2 * heads * F, heads * DV
    late = []

    def go(copy):
        copy.start()
        late.append(copy)

    combine = Combine(t, branch, other, summed, landed, ls, cs, cq, go)
    scatter = Scatter(
        g,
        lambda d: g.at[(z + d) % ZED, 1 - y, x, :, pl.ds(0, g.shape[-1] // 2)],
        lambda d: g.at[(z + d) % ZED, y, 1 - x, :, pl.ds(g.shape[-1] // 2, g.shape[-1] // 2)],
        lambda d: g.at[(z + d) % ZED, y, x],
        za, r1x, r1y, r2x, r2y, gs, gq, go,
    )
    combine.begin()
    weight = pltpu.make_async_copy(wa1, w1, ls.at[4])
    weight.start()
    for mb in range(mbs):
        cols = slice(mb * count, (mb + 1) * count)
        for k in range(heads):
            block = home.at[k + heads * mb]
            dqk_t[k * F : (k + 1) * F, cols] = block[0:F, :].astype(f32)
            dqk_t[(heads + k) * F : (heads + k + 1) * F, cols] = block[F : 2 * F, :].astype(f32)
            dqkv[cols, qk + k * DV : qk + (k + 1) * DV] = block[2 * F :, :]
    dqkv[:, 0:qk] = jnp.transpose(dqk_t[...]).astype(bf16)
    for n, d in enumerate(FAR):
        zz = (z + d) % ZED
        for yy in range(2):
            for xx in range(2):
                at = pl.ds(pl.multiple_of(index_of(zz, yy, xx) * 128, 128), 128)
                g[zz, yy, xx, :, 0 : qk + vv] = mix(xh[:, at], dqkv[...], ((0,), (0,))).astype(bf16)
                g[zz, yy, xx, :, qk + vv :] = mix(d_att[:, at], heads_out[...], ((0,), (0,))).astype(bf16)
        scatter.first(d)
        if n == 0:
            combine.spread()
    weight.wait()
    for c in range(wide // COLS):
        cols = pl.ds(c * COLS, COLS)
        part[:, c * COLS : (c + 1) * COLS] = mix(dqkv[...], w1[c * COLS : (c + 1) * COLS, :], ((1,), (1,)))
        go(remote(part.at[:, cols], swap.at[:, cols], ws.at[c], wr.at[c], me, 1 - h))
    scatter.second(2)
    for c in range(wide // COLS):
        cols = pl.ds(c * COLS, COLS)
        arrived(swap.at[:, cols], ws.at[c], wr.at[c], me, 1 - h)
    for mb in range(mbs):

        def body(turn, carry):
            row = chunk(turn)
            flat = pl.ds(pl.multiple_of(mb * count + turn * 16, 16), 16)
            v = xin[mb, row, :].astype(f32)
            scale = lax.rsqrt(jnp.mean(v * v, axis=-1, keepdims=True) + epsilon)
            hat = v * scale
            e = part[flat, :] + swap[flat, :]
            d_in[mb, row, :] = (
                d_mid[mb, row, :] + scale * (e - hat * jnp.mean(e * hat, axis=-1, keepdims=True))
            ).astype(bf16)
            return carry

        lax.fori_loop(0, count // 16, body, 0)
    scatter.second(1)
    scatter.third(2)
    scatter.second(3)
    scatter.third(1)
    scatter.second(0)
    scatter.third(3)
    combine.total()
    scatter.third(0)
    combine.done()
    for mb in range(mbs):

        def body(turn, carry):
            row = chunk(turn)
            outputs[mb, row, :] = (mid[mb, row, :] + branch[mb, row, :].astype(f32)).astype(bf16)
            return carry

        lax.fori_loop(0, count // 16, body, 0)
    scatter.last()
    for copy in late:
        copy.wait_send()


def end(t, home, xh, d_att, heads_out, wa1, d_mid, xin, mid):
    mbs, count, wide = xin.shape
    shape = jax.ShapeDtypeStruct
    cols = wa1.shape[1] + heads_out.shape[1]
    line = pltpu.VMEM((ZED, count, wide), bf16)
    return pl.pallas_call(
        end_kernel,
        out_shape=(shape((ZED, 128, cols), bf16), shape(xin.shape, bf16), shape(xin.shape, bf16)),
        in_specs=[ANY] + [VMEM] * 4 + [ANY] + [VMEM] * 3,
        out_specs=(VMEM,) * 3,
        scratch_shapes=[pltpu.VMEM((ZED, 2, 2, 128, cols), bf16)] + scatter_room(cols) + [
            pltpu.VMEM(xin.shape, bf16), line, line, line,
            pltpu.VMEM(wa1.shape, bf16),
            pltpu.VMEM((mbs * count, mbs * count), f32),
            pltpu.VMEM((mbs * count, wa1.shape[1]), bf16),
            pltpu.VMEM((mbs * count, wide), f32),
            pltpu.VMEM((mbs * count, wide), f32),
            DMA((6,)), DMA((4, 5)), DMA((4, 5)), DMA((4, 2)), DMA((4, 2)),
            DMA((wide // COLS,)), DMA((wide // COLS,)),
        ],
        compiler_params=params(),
        name="end",
    )(t, home, xh, d_att, heads_out, wa1, d_mid, xin, mid)


def fast(
    inputs, norm_gain1, w_query, w_key, w_value, w_out, norm_gain2, w_gate, w_up, w_down, cotangent
):
    mbs, count, wide = inputs.shape
    heads = w_query.shape[1] // F
    units = w_gate.shape[1] // ZED
    room = -(-units // 128) * 128
    qk, vv = 2 * heads * F, heads * DV
    rows = w_query.shape[0]
    gain1, gain2 = norm_gain1.astype(f32)[:, None], norm_gain2.astype(f32)[:, None]

    def folded(weight, gain):
        return (weight.astype(f32) * gain).astype(bf16)

    a1 = jnp.concatenate([folded(w_query, gain1), folded(w_key, gain1), folded(w_value, gain1)], axis=1)

    def cut(weight):
        pieces = jnp.transpose(weight.reshape(rows, ZED, units), (1, 0, 2))
        return jnp.pad(pieces, ((0, 0), (0, 0), (0, room - units)))

    m = jnp.concatenate([cut(folded(w_gate, gain2)), cut(folded(w_up, gain2)), cut(w_down.T)], axis=2)
    stream = inputs.astype(f32).reshape(mbs * count, wide)
    r1 = lax.rsqrt(jnp.mean(stream * stream, axis=-1, keepdims=True) + epsilon)
    xh1 = (stream * r1).astype(bf16)
    wa1, w_o, wm, got, ratio, den, heads_out, middle, near = front(a1, w_out.T, m, xh1, inputs)
    gg = share(cotangent)
    w_g, w_u, w_d = wm[:, :room], wm[:, room : 2 * room], wm[:, 2 * room :]
    many = ZED * mbs * count
    n2 = near.reshape(many, wide)
    up_g = gg.reshape(many, wide)
    gate = mix(n2, w_g, ((1,), (0,)))
    up = mix(n2, w_u, ((1,), (0,)))
    d_hidden = mix(up_g, w_d, ((1,), (0,)))
    sig = jax.nn.sigmoid(gate)
    silu = gate * sig
    hidden = (silu * up).astype(bf16)
    d_gate = (d_hidden * up * sig * (1.0 + gate * (1.0 - sig))).astype(bf16)
    d_up = (d_hidden * silu).astype(bf16)
    branch = mix(hidden, w_d, ((1,), (1,))).astype(bf16)
    d_n2 = (mix(d_gate, w_g, ((1,), (1,))) + mix(d_up, w_u, ((1,), (1,)))).astype(bf16)
    first = ((0,), (0,))
    gm = jnp.concatenate(
        [mix(n2, d_gate, first), mix(n2, d_up, first), mix(up_g, hidden, first)], axis=1
    ).astype(bf16)
    lines = (ZED, mbs, count, wide)
    zm, d_mid, d_att, home = back(
        gm, d_n2.reshape(lines), w_o, middle, cotangent, got, ratio, den
    )
    za, input_grad, outputs = end(
        branch.reshape(lines), home, xh1, d_att, heads_out, wa1, d_mid, inputs, middle
    )
    za = jnp.sum(za.astype(f32), axis=0)
    zm = zm.astype(f32)

    def joined(piece):
        return jnp.transpose(piece[:, :, :units], (1, 0, 2)).reshape(rows, ZED * units)

    g_gate, g_up, g_down = joined(zm[:, :, :room]), joined(zm[:, :, room : 2 * room]), joined(zm[:, :, 2 * room :])
    s_q, s_k, s_v = za[:, : qk // 2], za[:, qk // 2 : qk], za[:, qk : qk + vv]
    g_gain1 = (
        jnp.sum(w_query.astype(f32) * s_q, axis=1)
        + jnp.sum(w_key.astype(f32) * s_k, axis=1)
        + jnp.sum(w_value.astype(f32) * s_v, axis=1)
    )
    g_gain2 = jnp.sum(w_gate.astype(f32) * g_gate, axis=1) + jnp.sum(w_up.astype(f32) * g_up, axis=1)
    gains = lax.psum(jnp.stack([g_gain1, g_gain2]), "head")
    return (
        outputs,
        input_grad,
        gains[0],
        s_q * gain1,
        s_k * gain1,
        s_v * gain1,
        za[:, qk + vv :].T,
        gains[1],
        g_gate * gain2,
        g_up * gain2,
        g_down.T,
    )


def solution(mesh):
    return jax.shard_map(
        fast if mesh.shape["seq"] == 16 else local,
        mesh=mesh,
        in_specs=(
            P(None, "seq", None),
            P("seq"),
            P("seq", "head"),
            P("seq", "head"),
            P("seq", "head"),
            P("head", "seq"),
            P("seq"),
            P("seq", "head"),
            P("seq", "head"),
            P("head", "seq"),
            P(None, "seq", None),
        ),
        out_specs=(
            P(None, "seq", None),
            P(None, "seq", None),
            P("seq"),
            P("seq", "head"),
            P("seq", "head"),
            P("seq", "head"),
            P("head", "seq"),
            P("seq"),
            P("seq", "head"),
            P("seq", "head"),
            P("head", "seq"),
        ),
        check_vma=False,
    )
```

```python
import jax
import jax.numpy as jnp
from jax import lax
from jax.experimental import pallas as pl
from jax.experimental.pallas import tpu as pltpu
from jax.sharding import PartitionSpec as P

F = 16
DV = 128


epsilon = 1e-05
highest = lax.Precision.HIGHEST


def entering(part, axis, combine, identity, reverse):
    count = lax.axis_size(axis)
    place = lax.axis_index(axis)
    ahead = count - 1 - place if reverse else place
    gathered = jax.tree.map(lambda a: lax.all_gather(a, axis), part)
    state = jax.tree.map(lambda a, e: jnp.zeros_like(a) + jnp.asarray(e, a.dtype), part, identity)

    def one(turn, state):
        source = count - 1 - turn if reverse else turn
        return combine(
            state, jax.tree.map(lambda a: lax.dynamic_index_in_dim(a, source, 0, False), gathered)
        )

    return lax.fori_loop(0, ahead, one, state)


def rms_apply(values, gain):
    scale = lax.rsqrt(jnp.mean(values * values, axis=-1, keepdims=True) + epsilon)
    return values * scale * gain


def feature_map(projected):
    count = projected.shape[0]
    pieces = projected.reshape(count, -1, F)
    square = (pieces[:, :, :, None] * pieces[:, :, None, :]).reshape(count, pieces.shape[1], F * F)
    return jnp.concatenate(
        [jnp.ones_like(pieces[:, :, :1]), pieces * F ** (-0.25), square * (2.0 * F) ** (-0.5)],
        axis=-1,
    )


def swiglu(gate, up_part):
    return jax.nn.silu(gate) * up_part


def round_trip(values):
    return lax.optimization_barrier(values.astype(jnp.bfloat16)).astype(jnp.float32)


def add_pair(earlier, later):
    return (earlier[0] + later[0], earlier[1] + later[1])


def block_pass(tokens, upstream, gathered):
    gain_one, query_w, key_w, value_w, out_w, gain_two, gate_w, up_w, down_w = gathered
    f32 = jnp.float32
    bf16 = jnp.bfloat16
    stream = tokens.astype(f32)
    count = stream.shape[0]
    normed_f, norm_one_pull = jax.vjp(rms_apply, stream, gain_one.astype(f32))
    normed = normed_f.astype(bf16)
    queries = jnp.dot(normed, query_w, preferred_element_type=f32)
    keys_all = jnp.dot(normed, key_w, preferred_element_type=f32)
    values = jnp.dot(normed, value_w, preferred_element_type=f32).astype(bf16)
    query_feat_f, query_pull = jax.vjp(feature_map, queries)
    key_feat_f, key_pull = jax.vjp(feature_map, keys_all)
    query_feat = jnp.transpose(query_feat_f.astype(bf16), (1, 0, 2))
    key_feat = jnp.transpose(key_feat_f.astype(bf16), (1, 0, 2))
    value_heads = jnp.transpose(values.reshape(count, -1, DV), (1, 0, 2))
    causal = (jnp.arange(count)[:, None] >= jnp.arange(count)[None, :]).astype(f32)
    scores = jnp.einsum("htf,hsf->hts", query_feat, key_feat, preferred_element_type=f32) * causal
    weighted = scores.astype(bf16)
    num_local = jnp.einsum("hts,hsd->htd", weighted, value_heads, preferred_element_type=f32)
    den_local = jnp.sum(weighted.astype(f32), axis=-1)
    states = jnp.einsum("hsf,hsd->hfd", key_feat, value_heads, preferred_element_type=f32)
    totals = jnp.sum(key_feat.astype(f32), axis=1)
    state_before, total_before = entering(
        (states, totals), "seq", add_pair, (jnp.zeros_like(states), jnp.zeros_like(totals)), False
    )
    query_wide = query_feat.astype(f32)
    numer = num_local + jnp.einsum("htf,hfd->htd", query_wide, state_before, precision=highest)
    denom = den_local + jnp.einsum("htf,hf->ht", query_wide, total_before, precision=highest)
    ratio = numer / denom[..., None]
    heads_out = jnp.transpose(ratio, (1, 0, 2)).reshape(count, -1).astype(bf16)
    attended = lax.psum(jnp.dot(heads_out, out_w, preferred_element_type=f32), "head")
    middle = stream + attended
    normed_two_f, norm_two_pull = jax.vjp(rms_apply, middle, gain_two.astype(f32))
    normed_two = normed_two_f.astype(bf16)
    gate = jnp.dot(normed_two, gate_w, preferred_element_type=f32)
    up_part = jnp.dot(normed_two, up_w, preferred_element_type=f32)
    active, active_pull = jax.vjp(swiglu, gate, up_part)
    hidden = active.astype(bf16)
    branch = lax.psum(
        jnp.dot(hidden, down_w, preferred_element_type=f32).astype(jnp.bfloat16), "head"
    ).astype(jnp.float32)
    result = (middle + branch).astype(bf16)
    grad_down = jnp.dot(hidden.T, upstream, preferred_element_type=f32)
    d_hidden = jnp.dot(upstream, down_w.T, preferred_element_type=f32)
    d_gate_f, d_up_f = active_pull(d_hidden)
    d_gate = d_gate_f.astype(bf16)
    d_up = d_up_f.astype(bf16)
    grad_gate = jnp.dot(normed_two.T, d_gate, preferred_element_type=f32)
    grad_up = jnp.dot(normed_two.T, d_up, preferred_element_type=f32)
    d_normed_two = lax.psum(
        jnp.dot(d_gate, gate_w.T, preferred_element_type=f32)
        + jnp.dot(d_up, up_w.T, preferred_element_type=f32),
        "head",
    )
    d_middle_norm, grad_gain2 = norm_two_pull(d_normed_two)
    d_middle = upstream.astype(f32) + d_middle_norm
    d_attended = d_middle.astype(bf16)
    grad_out = jnp.dot(heads_out.T, d_attended, preferred_element_type=f32)
    d_heads = jnp.transpose(
        jnp.dot(d_attended, out_w.T, preferred_element_type=f32).reshape(count, -1, DV), (1, 0, 2)
    )
    d_numer = (d_heads / denom[..., None]).astype(bf16)
    d_denom = -jnp.sum(d_heads * ratio, axis=-1) / denom
    d_numer_wide = d_numer.astype(f32)
    d_before = jnp.einsum("htf,htd->hfd", query_wide, d_numer_wide, precision=highest)
    d_total_before = jnp.einsum("htf,ht->hf", query_wide, d_denom, precision=highest)
    d_state, d_total = entering(
        (d_before, d_total_before),
        "seq",
        add_pair,
        (jnp.zeros_like(d_before), jnp.zeros_like(d_total_before)),
        True,
    )
    d_scores = (
        (
            jnp.einsum("htd,hsd->hts", d_numer, value_heads, preferred_element_type=f32)
            + d_denom[..., None]
        )
        * causal
    ).astype(bf16)
    d_values = jnp.einsum(
        "hts,htd->hsd", weighted, d_numer, preferred_element_type=f32
    ) + jnp.einsum("hsf,hfd->hsd", key_feat.astype(f32), d_state, precision=highest)
    d_query_feat = (
        jnp.einsum("hts,hsf->htf", d_scores, key_feat, preferred_element_type=f32)
        + jnp.einsum("htd,hfd->htf", d_numer_wide, state_before, precision=highest)
        + d_denom[..., None] * total_before[:, None, :]
    )
    d_key_feat = (
        jnp.einsum("hts,htf->hsf", d_scores, query_feat, preferred_element_type=f32)
        + jnp.einsum("hsd,hfd->hsf", value_heads.astype(f32), d_state, precision=highest)
        + d_total[:, None, :]
    )
    d_queries = query_pull(jnp.transpose(round_trip(d_query_feat), (1, 0, 2)))[0].astype(bf16)
    d_keys = key_pull(jnp.transpose(round_trip(d_key_feat), (1, 0, 2)))[0].astype(bf16)
    d_values_flat = jnp.transpose(d_values, (1, 0, 2)).reshape(count, -1).astype(bf16)
    grad_query = jnp.dot(normed.T, d_queries, preferred_element_type=f32)
    grad_key = jnp.dot(normed.T, d_keys, preferred_element_type=f32)
    grad_value = jnp.dot(normed.T, d_values_flat, preferred_element_type=f32)
    d_normed_part = (
        jnp.dot(d_queries, query_w.T, preferred_element_type=f32)
        + jnp.dot(d_keys, key_w.T, preferred_element_type=f32)
        + jnp.dot(d_values_flat, value_w.T, preferred_element_type=f32)
    )
    d_normed = lax.psum(d_normed_part.astype(jnp.bfloat16), "head").astype(jnp.float32)
    d_stream_norm, grad_gain1 = norm_one_pull(d_normed)
    input_grad = (d_middle + d_stream_norm).astype(bf16)
    return (
        result,
        input_grad,
        grad_gain1,
        grad_query,
        grad_key,
        grad_value,
        grad_out,
        grad_gain2,
        grad_gate,
        grad_up,
        grad_down,
    )


def local(
    inputs, norm_gain1, w_query, w_key, w_value, w_out, norm_gain2, w_gate, w_up, w_down, cotangent
):
    micro = inputs.shape[0]
    summed = None
    results = []
    input_grads = []
    for step_index in range(micro):
        gathered = (
            lax.all_gather(norm_gain1, "seq", axis=0, tiled=True),
            lax.all_gather(w_query, "seq", axis=0, tiled=True),
            lax.all_gather(w_key, "seq", axis=0, tiled=True),
            lax.all_gather(w_value, "seq", axis=0, tiled=True),
            lax.all_gather(w_out, "seq", axis=1, tiled=True),
            lax.all_gather(norm_gain2, "seq", axis=0, tiled=True),
            lax.all_gather(w_gate, "seq", axis=0, tiled=True),
            lax.all_gather(w_up, "seq", axis=0, tiled=True),
            lax.all_gather(w_down, "seq", axis=1, tiled=True),
        )
        (
            result,
            input_grad,
            grad_gain1,
            grad_query,
            grad_key,
            grad_value,
            grad_out,
            grad_gain2,
            grad_gate,
            grad_up,
            grad_down,
        ) = block_pass(inputs[step_index], cotangent[step_index], gathered)
        results.append(result)
        input_grads.append(input_grad)
        fresh = (
            lax.psum_scatter(grad_gain1, "seq", scatter_dimension=0, tiled=True),
            lax.psum_scatter(grad_query, "seq", scatter_dimension=0, tiled=True),
            lax.psum_scatter(grad_key, "seq", scatter_dimension=0, tiled=True),
            lax.psum_scatter(grad_value, "seq", scatter_dimension=0, tiled=True),
            lax.psum_scatter(grad_out, "seq", scatter_dimension=1, tiled=True),
            lax.psum_scatter(grad_gain2, "seq", scatter_dimension=0, tiled=True),
            lax.psum_scatter(grad_gate, "seq", scatter_dimension=0, tiled=True),
            lax.psum_scatter(grad_up, "seq", scatter_dimension=0, tiled=True),
            lax.psum_scatter(grad_down, "seq", scatter_dimension=1, tiled=True),
        )
        summed = (
            fresh
            if summed is None
            else tuple((older + newer for older, newer in zip(summed, fresh)))
        )
    return (
        jnp.stack(results),
        jnp.stack(input_grads),
        summed[0],
        summed[1],
        summed[2],
        summed[3],
        summed[4],
        summed[5],
        summed[6],
        summed[7],
        summed[8],
    )


MESH = pl.DeviceIdType.MESH
bf16 = jnp.bfloat16
f32 = jnp.float32
ZED = 4
VMEM_LIMIT = 60 * 1024 * 1024


def where_am_i():
    place = lax.axis_index("seq")
    return place % 2, (place // 2) % 2, place // 4, lax.axis_index("head")


def index_of(z, y, x):
    return (z * 2 + y) * 2 + x


def remote(src, dst, send, recv, place, head):
    return pltpu.make_async_remote_copy(
        src_ref=src, dst_ref=dst, send_sem=send, recv_sem=recv, device_id=(place, head),
        device_id_type=MESH,
    )


def arrived(dst, send, recv, place, head):
    remote(dst, dst, send, recv, place, head).wait_recv()


def params():
    return pltpu.CompilerParams(has_side_effects=True, vmem_limit_bytes=VMEM_LIMIT)


ANY = pl.BlockSpec(memory_space=pl.ANY)
VMEM = pl.BlockSpec(memory_space=pltpu.VMEM)
DMA = pltpu.SemaphoreType.DMA
ORDER = (0, 1, 3, 2)


def mix(a, b, over):
    return lax.dot_general(a, b, (over, ((), ())), preferred_element_type=f32)


CHUNK = 512
COLS = 256


def spread(got, q_t, k_t, va):
    count = got.shape[2]
    for b in range(got.shape[0]):
        q_t[:, b * count : (b + 1) * count] = got[b, 0:F, :]
        k_t[:, b * count : (b + 1) * count] = got[b, F : 2 * F, :]
        va[b * count : (b + 1) * count, 0:DV] = got[b, 2 * F :, :]
    va[:, DV:] = jnp.ones((va.shape[0], va.shape[1] - DV), bf16)


def lower(count):
    return lax.broadcasted_iota(jnp.int32, (count, count), 0) >= lax.broadcasted_iota(
        jnp.int32, (count, count), 1
    )


def attend_rows(qi, q_t, k_t, va, ratio, den, causal):
    qs = slice(qi * CHUNK, (qi + 1) * CHUNK)
    acc = jnp.zeros((CHUNK, va.shape[1]), f32)
    for kj in range(qi + 1):
        ks = slice(kj * CHUNK, (kj + 1) * CHUNK)
        s = mix(q_t[:, qs], k_t[:, ks], ((0,), (0,)))
        p = 1.0 + s * (0.25 + s * (1.0 / 32.0))
        if kj == qi:
            p = jnp.where(causal, p, 0.0)
        acc = acc + mix(p.astype(bf16), va[ks, :], ((1,), (0,)))
    ratio[qs, :] = acc[:, :DV] / acc[:, DV:]
    den[qs, :] = acc[:, DV:]


def front_kernel(
    a1, a2, m, cot, xh, xin,
    wa1, wa2, wm, gg, got, ratio, den, heads_out, middle, near,
    w1, w2, pack, q_t, k_t, va, ob, part, other,
    ls, zs, zr, us, ur, ps, pr, e1s, e1r, e2s, e2r, ws, wr, ds, dr,
):
    x, y, z, h = where_am_i()
    me = index_of(z, y, x)
    at_x, at_y = index_of(z, y, 1 - x), index_of(z, 1 - y, x)
    count = xin.shape[1]
    heads = 16 // xin.shape[0]
    late = []

    def when(true, do):
        if true is None:
            do()
        else:
            pl.when(true)(do)

    def go(copy, true=None):
        when(true, copy.start)
        late.append((true, copy))

    def rows(zz, yy, xx):
        return pl.ds(pl.multiple_of(index_of(zz, yy, xx) * 128, 128), 128)

    mine = rows(z, y, x)
    kept = [
        pltpu.make_async_copy(a1, w1.at[mine], ls.at[0]),
        pltpu.make_async_copy(a2, w2.at[mine], ls.at[1]),
        pltpu.make_async_copy(m.at[z], wm.at[mine], ls.at[2]),
        pltpu.make_async_copy(cot, gg.at[z], ls.at[6]),
    ]
    for copy in kept:
        copy.start()
    dest = (w1, w2, wm)
    UP, DOWN = 0, 1
    COT, NEAR = 2, 3

    def held(kind, zz):
        return (lambda: w1.at[rows(zz, y, x)], lambda: w2.at[rows(zz, y, x)],
                lambda: gg.at[zz, h], lambda: near.at[zz, h])[kind]()

    def origin(way, step):
        return (z + ZED - step) % ZED if way == UP else (z + step) % ZED

    def valid(way, step):
        return z >= step if way == UP else z <= ZED - 1 - step

    def pass_on(kind, way, step, src, true):
        there = index_of((z + 1) % ZED if way == UP else (z + ZED - 1) % ZED, y, x)
        block = held(kind, origin(way, step))
        go(remote(block if src is None else src, block, us.at[kind, way, step], ur.at[kind, way, step + 1], there, h), true)

    def offer(kind, src=None):
        pass_on(kind, UP, 0, src, z < ZED - 1)
        pass_on(kind, DOWN, 0, src, z > 0)

    def hop(kind, way, step):
        block = held(kind, origin(way, step))
        when(
            valid(way, step),
            lambda: arrived(block, us.at[kind, way, step], ur.at[kind, way, step], me, h),
        )
        if step < ZED - 1:
            more = z < ZED - 1 if way == UP else z > 0
            pass_on(kind, way, step, None, valid(way, step) & more)

    def across(kind, way, step):
        zz = origin(way, step)
        block = held(kind, zz)
        go(remote(block, block, ds.at[kind, way, step], dr.at[kind, way, step], me, 1 - h), valid(way, step))

    def across_done(kind, way, step):
        zz = origin(way, step)
        block = (gg if kind == COT else near).at[zz, 1 - h]
        when(
            valid(way, step),
            lambda: arrived(block, ds.at[kind, way, step], dr.at[kind, way, step], me, 1 - h),
        )

    def both(do, kind, step):
        do(kind, UP, step)
        do(kind, DOWN, step)

    def line():
        for d in (1, 3, 2):
            zz = (z + d) % ZED
            go(remote(m.at[zz], wm.at[mine], zs.at[d], zr.at[d], index_of(zz, y, x), h))

    def slot_of(way, step):
        return step if way == UP else 3 + step if step else 0

    def plane_set(kind, slot, zz, true):
        block = dest[kind].at[rows(zz, y, x)]
        go(remote(block, block, ps.at[kind, slot, 0], pr.at[kind, slot, 0], at_x, h), true)
        go(remote(block, block, ps.at[kind, slot, 1], pr.at[kind, slot, 1], at_y, h), true)

    def onward_set(kind, slot, zz, true):
        w = dest[kind]
        half = w.shape[1] // 2
        from_x, from_y = rows(zz, y, 1 - x), rows(zz, 1 - y, x)

        def wait():
            arrived(w.at[from_x], ps.at[kind, slot, 0], pr.at[kind, slot, 0], me, h)
            arrived(w.at[from_y], ps.at[kind, slot, 1], pr.at[kind, slot, 1], me, h)

        when(true, wait)
        left = w.at[from_y, pl.ds(0, half)]
        right = w.at[from_x, pl.ds(half, half)]
        go(remote(left, left, ps.at[kind, slot, 2], pr.at[kind, slot, 2], at_x, h), true)
        go(remote(right, right, ps.at[kind, slot, 3], pr.at[kind, slot, 3], at_y, h), true)

    def corner_set(kind, slot, zz, true):
        w = dest[kind]
        half = w.shape[1] // 2
        far = rows(zz, 1 - y, 1 - x)

        def wait():
            arrived(w.at[far, pl.ds(0, half)], ps.at[kind, slot, 2], pr.at[kind, slot, 2], me, h)
            arrived(w.at[far, pl.ds(half, half)], ps.at[kind, slot, 3], pr.at[kind, slot, 3], me, h)

        when(true, wait)

    def plane(kind, way, step):
        if step == 0:
            kept[kind].wait()
        plane_set(kind, slot_of(way, step), origin(way, step), valid(way, step) if step else None)

    def onward(kind, way, step):
        onward_set(kind, slot_of(way, step), origin(way, step), valid(way, step) if step else None)

    def corner(kind):
        corner_set(kind, 0, z, None)
        for step in (1, 2, 3):
            for way in (UP, DOWN):
                corner_set(kind, slot_of(way, step), origin(way, step), valid(way, step))

    def m_plane(d):
        zz = (z + ZED - d) % ZED
        if d:
            arrived(wm.at[rows(zz, y, x)], zs.at[d], zr.at[d], me, h)
        else:
            kept[2].wait()
        plane_set(2, d, zz, None)

    def m_onward(d):
        onward_set(2, d, (z + ZED - d) % ZED, None)

    offer(0, a1)
    plane(0, UP, 0)
    for way in (UP, DOWN):
        hop(0, way, 1)
        plane(0, way, 1)
    offer(1, a2)
    onward(0, UP, 0)
    for way in (UP, DOWN):
        hop(0, way, 2)
        plane(0, way, 2)
    both(onward, 0, 1)
    both(hop, 1, 1)
    for way in (UP, DOWN):
        hop(0, way, 3)
        plane(0, way, 3)
    both(onward, 0, 2)
    both(hop, 1, 2)
    plane(1, UP, 0)
    both(onward, 0, 3)
    both(hop, 1, 3)
    both(plane, 1, 1)
    corner(0)
    out1 = pltpu.make_async_copy(w1, wa1, ls.at[3])
    out1.start()
    kq = mix(xh[...], w1[:, 0 : 2 * heads * F], ((1,), (0,)))
    qk = jnp.transpose(kq).astype(bf16)
    for mb in range(16 // heads):
        for k in range(heads):
            t = k + heads * mb
            cols = slice(mb * count, (mb + 1) * count)
            pack[t, 0:F, :] = qk[k * F : (k + 1) * F, cols]
            pack[t, F : 2 * F, :] = qk[(heads + k) * F : (heads + k + 1) * F, cols]
    for c in range(heads * DV // COLS):
        at = 2 * heads * F + c * COLS
        val = mix(xh[...], w1[:, at : at + COLS], ((1,), (0,))).astype(bf16)
        for mb in range(16 // heads):
            for i in range(COLS // DV):
                t = c * (COLS // DV) + i + heads * mb
                pack[t, 2 * F :, :] = val[mb * count : (mb + 1) * count, i * DV : (i + 1) * DV]
    keep = pltpu.make_async_copy(pack.at[me], got.at[me], ls.at[4])
    keep.start()
    for d in range(1, 16):
        there = (me + d) % 16
        go(remote(pack.at[there], got.at[me], e1s.at[d], e1r.at[d], there, h))
    line()
    onward(1, UP, 0)
    both(plane, 1, 2)
    both(onward, 1, 1)
    both(plane, 1, 3)
    both(onward, 1, 2)
    keep.wait()
    for d in range(1, 16):
        arrived(got.at[(me + 16 - d) % 16], e1s.at[d], e1r.at[d], me, h)
    m_plane(0)
    both(onward, 1, 3)
    spread(got, q_t, k_t, va)
    causal = lower(CHUNK)
    for qi in range(va.shape[0] // CHUNK):
        attend_rows(qi, q_t, k_t, va, ratio, den, causal)
    for b in range(16):
        ob[b, :, :] = ratio[b * count : (b + 1) * count, :].astype(bf16)

    def window(source):
        return heads_out.at[
            pl.ds(pl.multiple_of((source // heads) * count, count), count),
            pl.ds(pl.multiple_of((source % heads) * DV, DV), DV),
        ]

    keep = pltpu.make_async_copy(ob.at[me], window(me), ls.at[4])
    keep.start()
    for d in range(1, 16):
        there = (me + d) % 16
        go(remote(ob.at[there], window(me), e2s.at[d], e2r.at[d], there, h))
    m_onward(0)
    corner(1)
    out2 = pltpu.make_async_copy(w2, wa2, ls.at[5])
    out2.start()
    keep.wait()
    for d in range(1, 16):
        arrived(window((me + 16 - d) % 16), e2s.at[d], e2r.at[d], me, h)
    wide = part.shape[1]
    for c in range(wide // COLS):
        cols = pl.ds(c * COLS, COLS)
        part[:, c * COLS : (c + 1) * COLS] = mix(
            heads_out[...], w2[c * COLS : (c + 1) * COLS, :], ((1,), (1,))
        )
        go(remote(part.at[:, cols], other.at[:, cols], ws.at[c], wr.at[c], me, 1 - h))
    m_plane(1)
    m_plane(3)
    for c in range(wide // COLS):
        cols = pl.ds(c * COLS, COLS)
        arrived(other.at[:, cols], ws.at[c], wr.at[c], me, 1 - h)

    def one(mb):
        def body(turn, carry):
            row = pl.ds(pl.multiple_of(turn * 16, 16), 16)
            flat = pl.ds(pl.multiple_of(mb * count + turn * 16, 16), 16)
            mid = xin[mb, row, :].astype(f32) + (part[flat, :] + other[flat, :])
            middle[mb, row, :] = mid
            scale = lax.rsqrt(jnp.mean(mid * mid, axis=-1, keepdims=True) + epsilon)
            near[z, mb, row, :] = (mid * scale).astype(bf16)
            return carry

        lax.fori_loop(0, count // 16, body, 0)

    one(h)
    offer(NEAR)
    offer(COT, cot.at[h])
    one(1 - h)
    kept[3].wait()
    m_onward(1)
    m_onward(3)
    both(hop, NEAR, 1)
    both(across, NEAR, 1)
    both(hop, COT, 1)
    both(across, COT, 1)
    m_plane(2)
    both(hop, NEAR, 2)
    both(across, NEAR, 2)
    both(hop, COT, 2)
    both(across, COT, 2)
    m_onward(2)
    both(hop, NEAR, 3)
    both(across, NEAR, 3)
    both(hop, COT, 3)
    both(across, COT, 3)
    for d in ORDER:
        corner_set(2, d, (z + ZED - d) % ZED, None)
    for kind in (NEAR, COT):
        for step in (1, 2, 3):
            both(across_done, kind, step)
    out1.wait()
    out2.wait()
    for true, copy in late:
        when(true, copy.wait_send)


def front(a1, a2, m, cot, xh, xin):
    mbs, count, wide = xin.shape
    depth = 16 * count
    wide1, wide2 = a1.shape[1], a2.shape[1]
    shape = jax.ShapeDtypeStruct
    return pl.pallas_call(
        front_kernel,
        out_shape=(
            shape((wide, wide1), bf16),
            shape((wide, wide2), bf16),
            shape((wide, m.shape[2]), bf16),
            shape((ZED,) + cot.shape, bf16),
            shape((16, 2 * F + DV, count), bf16),
            shape((depth, DV), f32),
            shape((depth, DV), f32),
            shape((mbs * count, wide2), bf16),
            shape(xin.shape, f32),
            shape((ZED,) + xin.shape, bf16),
        ),
        in_specs=[ANY] * 4 + [VMEM] * 2,
        out_specs=(ANY,) * 4 + (VMEM,) * 6,
        scratch_shapes=[
            pltpu.VMEM((wide, wide1), bf16),
            pltpu.VMEM((wide, wide2), bf16),
            pltpu.VMEM((16, 2 * F + DV, count), bf16),
            pltpu.VMEM((F, depth), bf16),
            pltpu.VMEM((F, depth), bf16),
            pltpu.VMEM((depth, 2 * DV), bf16),
            pltpu.VMEM((16, count, DV), bf16),
            pltpu.VMEM((mbs * count, wide), f32),
            pltpu.VMEM((mbs * count, wide), f32),
            DMA((7,)), DMA((4,)), DMA((4,)), DMA((4, 2, 4)), DMA((4, 2, 4)), DMA((3, 7, 4)), DMA((3, 7, 4)),
            DMA((16,)), DMA((16,)), DMA((16,)), DMA((16,)),
            DMA((wide // COLS,)), DMA((wide // COLS,)), DMA((4, 2, 4)), DMA((4, 2, 4)),
        ],
        compiler_params=params(),
        name="front",
    )(a1, a2, m, cot, xh, xin)


def attend_back_body(got, ratio, den, d_o, d_qk, d_v, q_t, k_t, va, da, dn_t):
    spread(got, q_t, k_t, va)
    depth = va.shape[0]
    lane = lax.broadcasted_iota(jnp.int32, (CHUNK, DV), 1)
    for qi in range(depth // CHUNK):
        qs = slice(qi * CHUNK, (qi + 1) * CHUNK)
        dn = d_o[qs, :].astype(f32) / den[qs, :]
        dd = -jnp.sum(dn * ratio[qs, :], axis=-1, keepdims=True)
        big = dd.astype(bf16).astype(f32)
        da[qs, 0:DV] = dn.astype(bf16)
        da[qs, DV:] = jnp.where(lane == 0, big, jnp.where(lane == 1, dd - big, 0.0)).astype(bf16)
        dn_t[:, qs] = jnp.transpose(dn).astype(bf16)
    causal = lower(CHUNK)
    for kj in range(depth // CHUNK):
        ks = slice(kj * CHUNK, (kj + 1) * CHUNK)
        acc_k = jnp.zeros((F, CHUNK), f32)
        acc_v = jnp.zeros((DV, CHUNK), f32)
        for qi in range(kj, depth // CHUNK):
            qs = slice(qi * CHUNK, (qi + 1) * CHUNK)
            s = mix(q_t[:, qs], k_t[:, ks], ((0,), (0,)))
            p = 1.0 + s * (0.25 + s * (1.0 / 32.0))
            d_s = mix(da[qs, :], va[ks, :], ((1,), (1,))) * (0.25 + s * (1.0 / 16.0))
            if kj == qi:
                p = jnp.where(causal, p, 0.0)
                d_s = jnp.where(causal, d_s, 0.0)
            d_s = d_s.astype(bf16)
            acc_v = acc_v + mix(dn_t[:, qs], p.astype(bf16), ((1,), (0,)))
            acc_k = acc_k + mix(q_t[:, qs], d_s, ((1,), (0,)))
            d_q = mix(k_t[:, ks], d_s, ((1,), (1,)))
            d_qk[0:F, qs] = d_q if kj == 0 else d_qk[0:F, qs] + d_q
        d_qk[F : 2 * F, ks] = acc_k
        d_v[ks, :] = jnp.transpose(acc_v)


FAR = (2, 1, 3, 0)


def chunk(turn):
    return pl.ds(pl.multiple_of(turn * 16, 16), 16)


class Scatter:
    def __init__(self, g, low_acc, high_acc, fin, out, r1x, r1y, r2x, r2y, s, q, go):
        self.g, self.low_acc, self.high_acc, self.fin, self.out = g, low_acc, high_acc, fin, out
        self.r1x, self.r1y, self.r2x, self.r2y, self.s, self.q = r1x, r1y, r2x, r2y, s, q
        self.go = go
        self.x, self.y, self.z, self.h = where_am_i()
        self.me = index_of(self.z, self.y, self.x)
        self.at_x = index_of(self.z, self.y, 1 - self.x)
        self.at_y = index_of(self.z, 1 - self.y, self.x)
        self.half = r1x.shape[-1]
        self.low, self.high = pl.ds(0, self.half), pl.ds(self.half, self.half)

    def first(self, d):
        zz, x, y, g = (self.z + d) % ZED, self.x, self.y, self.g
        self.go(remote(g.at[zz, :, 1 - x, :, self.low], self.r1x.at[d], self.s.at[d, 0], self.q.at[d, 0], self.at_x, self.h))
        self.go(remote(g.at[zz, 1 - y, :, :, self.high], self.r1y.at[d], self.s.at[d, 1], self.q.at[d, 1], self.at_y, self.h))

    def second(self, d):
        x, y, me, h, r1x, r1y = self.x, self.y, self.me, self.h, self.r1x, self.r1y
        arrived(r1x.at[d], self.s.at[d, 0], self.q.at[d, 0], me, h)
        arrived(r1y.at[d], self.s.at[d, 1], self.q.at[d, 1], me, h)
        low_acc, high_acc = self.low_acc(d), self.high_acc(d)

        def body(i, carry):
            row = chunk(i)
            low_acc[row, :] = (
                low_acc[row, :].astype(f32) + r1x[d, 1 - y, row, :].astype(f32)
            ).astype(bf16)
            high_acc[row, :] = (
                high_acc[row, :].astype(f32) + r1y[d, 1 - x, row, :].astype(f32)
            ).astype(bf16)
            return carry

        lax.fori_loop(0, 8, body, 0)
        self.go(remote(low_acc, self.r2y.at[d], self.s.at[d, 2], self.q.at[d, 2], self.at_y, h))
        self.go(remote(high_acc, self.r2x.at[d], self.s.at[d, 3], self.q.at[d, 3], self.at_x, h))

    def third(self, d):
        x, y, me, h, z = self.x, self.y, self.me, self.h, self.z
        arrived(self.r2y.at[d], self.s.at[d, 2], self.q.at[d, 2], me, h)
        arrived(self.r2x.at[d], self.s.at[d, 3], self.q.at[d, 3], me, h)
        fin, low, high = self.fin(d), self.low, self.high
        target = fin if d else self.out.at[z]

        def body(i, carry):
            row = chunk(i)
            target[row, low] = (
                fin[row, low].astype(f32)
                + self.r1x[d, y, row, :].astype(f32)
                + self.r2y[d, row, :].astype(f32)
            ).astype(bf16)
            target[row, high] = (
                fin[row, high].astype(f32)
                + self.r1y[d, x, row, :].astype(f32)
                + self.r2x[d, row, :].astype(f32)
            ).astype(bf16)
            return carry

        lax.fori_loop(0, 8, body, 0)
        if d:
            there = index_of((z + d) % ZED, y, x)
            self.go(remote(fin, self.out.at[z], self.s.at[d, 4], self.q.at[d, 4], there, h))

    def last(self):
        for d in (1, 3, 2):
            arrived(
                self.out.at[(self.z + ZED - d) % ZED], self.s.at[d, 4], self.q.at[d, 4], self.me, self.h
            )


class Combine:
    def __init__(self, t, out, other, summed, landed, ls, s, q, go):
        self.t, self.out, self.other, self.summed, self.landed = t, out, other, summed, landed
        self.ls, self.s, self.q, self.go = ls, s, q, go
        self.x, self.y, self.z, self.h = where_am_i()
        self.me = index_of(self.z, self.y, self.x)

    def begin(self):
        t, h, other = self.t, self.h, self.other
        self.own = {}
        for d in FAR:
            zz = (self.z + d) % ZED
            self.own[d] = pltpu.make_async_copy(t.at[zz, h], self.summed.at[d], self.ls.at[d])
            self.own[d].start()
            self.go(remote(t.at[zz, 1 - h], other.at[d], self.s.at[d, 0], self.q.at[d, 0], self.me, 1 - h))

    def spread(self):
        summed, other = self.summed, self.other
        for d in FAR:
            zz = (self.z + d) % ZED
            self.own[d].wait()
            arrived(other.at[d], self.s.at[d, 0], self.q.at[d, 0], self.me, 1 - self.h)

            def add(turn, carry):
                row = chunk(turn)
                summed[d, row, :] = (
                    summed[d, row, :].astype(f32) + other[d, row, :].astype(f32)
                ).astype(bf16)
                return carry

            lax.fori_loop(0, 8, add, 0)
            if d:
                there = index_of(zz, self.y, self.x)
                self.go(remote(summed.at[d], self.landed.at[d], self.s.at[d, 1], self.q.at[d, 1], there, self.h))

    def total(self):
        summed, landed, out, h = self.summed, self.landed, self.out, self.h
        for d in (1, 3, 2):
            arrived(landed.at[d], self.s.at[d, 1], self.q.at[d, 1], self.me, h)

        def body(turn, carry):
            row = chunk(turn)
            acc = summed[0, row, :].astype(f32)
            for d in (1, 2, 3):
                acc = acc + landed[d, row, :].astype(f32)
            out[h, row, :] = acc.astype(bf16)
            return carry

        lax.fori_loop(0, 8, body, 0)
        self.go(remote(out.at[h], out.at[h], self.s.at[0, 1], self.q.at[0, 1], self.me, 1 - h))

    def done(self):
        arrived(self.out.at[1 - self.h], self.s.at[0, 1], self.q.at[0, 1], self.me, 1 - self.h)


def back_kernel(
    gm, t, wo, mid, cot, got, ratio, den,
    zm, d_mid, d_att, home,
    r1x, r1y, r2x, r2y, f1, f2, fin, e2, other, summed, landed, w2, pack, d_o, d_qk, d_v,
    q_t, k_t, va, da, dn_t, pack2,
    ls, fs, gs, gq, cs, cq, e1s, e1r, e2s, e2r,
):
    x, y, z, h = where_am_i()
    me = index_of(z, y, x)
    count = mid.shape[1]
    heads = 16 // mid.shape[0]
    late = []

    def go(copy):
        copy.start()
        late.append(copy)

    combine = Combine(t, e2, other, summed, landed, ls, cs, cq, go)
    scatter = Scatter(
        gm, lambda d: f1.at[d], lambda d: f2.at[d], lambda d: fin.at[d], zm,
        r1x, r1y, r2x, r2y, gs, gq, go,
    )
    combine.begin()
    for d in FAR:
        scatter.first(d)
    keep = {}
    for d in FAR:
        zz = (z + d) % ZED
        keep[d] = [
            pltpu.make_async_copy(gm.at[zz, 1 - y, x, :, scatter.low], f1.at[d], fs.at[d, 0]),
            pltpu.make_async_copy(gm.at[zz, y, 1 - x, :, scatter.high], f2.at[d], fs.at[d, 1]),
            pltpu.make_async_copy(gm.at[zz, y, x], fin.at[d], fs.at[d, 2]),
        ]
        for copy in keep[d]:
            copy.start()
    weight = pltpu.make_async_copy(wo, w2, ls.at[4])
    weight.start()
    combine.spread()
    for d in FAR:
        for copy in keep[d]:
            copy.wait()
    weight.wait()
    scatter.second(2)
    scatter.second(1)
    combine.total()
    combine.done()

    for mb in range(mid.shape[0]):

        def body(turn, carry):
            row = chunk(turn)
            m = mid[mb, row, :]
            scale = lax.rsqrt(jnp.mean(m * m, axis=-1, keepdims=True) + epsilon)
            hat = m * scale
            e = e2[mb, row, :].astype(f32)
            d_m = cot[mb, row, :].astype(f32) + scale * (
                e - hat * jnp.mean(e * hat, axis=-1, keepdims=True)
            )
            d_mid[mb, row, :] = d_m
            d_att[pl.ds(pl.multiple_of(mb * count + turn * 16, 16), 16), :] = d_m.astype(bf16)
            return carry

        lax.fori_loop(0, count // 16, body, 0)
    for c in range(heads * DV // COLS):
        val = mix(d_att[...], w2[:, c * COLS : (c + 1) * COLS], ((1,), (0,))).astype(bf16)
        for mb in range(16 // heads):
            for i in range(COLS // DV):
                pack[c * (COLS // DV) + i + heads * mb, :, :] = val[
                    mb * count : (mb + 1) * count, i * DV : (i + 1) * DV
                ]

    def window(source):
        return d_o.at[pl.ds(pl.multiple_of(source * count, count), count)]

    own = pltpu.make_async_copy(pack.at[me], window(me), ls.at[5])
    own.start()
    for d in range(1, 16):
        there = (me + d) % 16
        go(remote(pack.at[there], window(me), e1s.at[d], e1r.at[d], there, h))
    scatter.second(3)
    own.wait()
    for d in range(1, 16):
        arrived(window((me + 16 - d) % 16), e1s.at[d], e1r.at[d], me, h)
    scatter.second(0)
    scatter.third(2)
    attend_back_body(got, ratio, den, d_o, d_qk, d_v, q_t, k_t, va, da, dn_t)
    for b in range(16):
        pack2[b, 0 : 2 * F, :] = d_qk[:, b * count : (b + 1) * count].astype(bf16)
        pack2[b, 2 * F :, :] = d_v[b * count : (b + 1) * count, :].astype(bf16)
    own = pltpu.make_async_copy(pack2.at[me], home.at[me], ls.at[5])
    own.start()
    for d in range(1, 16):
        there = (me + d) % 16
        go(remote(pack2.at[there], home.at[me], e2s.at[d], e2r.at[d], there, h))
    scatter.third(1)
    scatter.third(3)
    scatter.third(0)
    own.wait()
    for d in range(1, 16):
        arrived(home.at[(me + 16 - d) % 16], e2s.at[d], e2r.at[d], me, h)
    scatter.last()
    for copy in late:
        copy.wait_send()


def scatter_room(wide):
    return [
        pltpu.VMEM((4, 2, 128, wide // 2), bf16),
        pltpu.VMEM((4, 2, 128, wide // 2), bf16),
        pltpu.VMEM((4, 128, wide // 2), bf16),
        pltpu.VMEM((4, 128, wide // 2), bf16),
    ]


def back(gm, t, wo, mid, cot, got, ratio, den):
    mbs, count, wide = cot.shape
    depth = 16 * count
    shape = jax.ShapeDtypeStruct
    cols = gm.shape[-1]
    line = pltpu.VMEM((ZED, count, wide), bf16)
    return pl.pallas_call(
        back_kernel,
        out_shape=(
            shape((ZED, 128, cols), bf16),
            shape(cot.shape, f32),
            shape((mbs * count, wide), bf16),
            shape((16, 2 * F + DV, count), bf16),
        ),
        in_specs=[ANY] * 3 + [VMEM] * 5,
        out_specs=(VMEM,) * 4,
        scratch_shapes=scatter_room(cols) + [
            pltpu.VMEM((4, 128, cols // 2), bf16),
            pltpu.VMEM((4, 128, cols // 2), bf16),
            pltpu.VMEM((4, 128, cols), bf16),
            pltpu.VMEM(cot.shape, bf16), line, line, line,
            pltpu.VMEM(wo.shape, bf16),
            pltpu.VMEM((16, count, DV), bf16),
            pltpu.VMEM((depth, DV), bf16),
            pltpu.VMEM((2 * F, depth), f32),
            pltpu.VMEM((depth, DV), f32),
            pltpu.VMEM((F, depth), bf16),
            pltpu.VMEM((F, depth), bf16),
            pltpu.VMEM((depth, 2 * DV), bf16),
            pltpu.VMEM((depth, 2 * DV), bf16),
            pltpu.VMEM((DV, depth), bf16),
            pltpu.VMEM((16, 2 * F + DV, count), bf16),
            DMA((6,)), DMA((4, 3)), DMA((4, 5)), DMA((4, 5)), DMA((4, 2)), DMA((4, 2)),
            DMA((16,)), DMA((16,)), DMA((16,)), DMA((16,)),
        ],
        compiler_params=params(),
        name="back",
    )(gm.reshape(ZED, 2, 2, 128, cols), t, wo, mid, cot, got, ratio, den)


def end_kernel(
    t, home, xh, d_att, heads_out, wa1, d_mid, xin, mid,
    za, d_in, outputs,
    g, r1x, r1y, r2x, r2y, branch, other, summed, landed, w1, dqk_t, dqkv, part, swap,
    ls, gs, gq, cs, cq, ws, wr,
):
    x, y, z, h = where_am_i()
    me = index_of(z, y, x)
    mbs, count, wide = xin.shape
    heads = 16 // mbs
    qk, vv = 2 * heads * F, heads * DV
    late = []

    def go(copy):
        copy.start()
        late.append(copy)

    combine = Combine(t, branch, other, summed, landed, ls, cs, cq, go)
    scatter = Scatter(
        g,
        lambda d: g.at[(z + d) % ZED, 1 - y, x, :, pl.ds(0, g.shape[-1] // 2)],
        lambda d: g.at[(z + d) % ZED, y, 1 - x, :, pl.ds(g.shape[-1] // 2, g.shape[-1] // 2)],
        lambda d: g.at[(z + d) % ZED, y, x],
        za, r1x, r1y, r2x, r2y, gs, gq, go,
    )
    combine.begin()
    weight = pltpu.make_async_copy(wa1, w1, ls.at[4])
    weight.start()
    for mb in range(mbs):
        cols = slice(mb * count, (mb + 1) * count)
        for k in range(heads):
            block = home.at[k + heads * mb]
            dqk_t[k * F : (k + 1) * F, cols] = block[0:F, :].astype(f32)
            dqk_t[(heads + k) * F : (heads + k + 1) * F, cols] = block[F : 2 * F, :].astype(f32)
            dqkv[cols, qk + k * DV : qk + (k + 1) * DV] = block[2 * F :, :]
    dqkv[:, 0:qk] = jnp.transpose(dqk_t[...]).astype(bf16)
    for n, d in enumerate(FAR):
        zz = (z + d) % ZED
        for yy in range(2):
            for xx in range(2):
                at = pl.ds(pl.multiple_of(index_of(zz, yy, xx) * 128, 128), 128)
                g[zz, yy, xx, :, 0 : qk + vv] = mix(xh[:, at], dqkv[...], ((0,), (0,))).astype(bf16)
                g[zz, yy, xx, :, qk + vv :] = mix(d_att[:, at], heads_out[...], ((0,), (0,))).astype(bf16)
        scatter.first(d)
        if n == 0:
            combine.spread()
    weight.wait()
    for c in range(wide // COLS):
        cols = pl.ds(c * COLS, COLS)
        part[:, c * COLS : (c + 1) * COLS] = mix(dqkv[...], w1[c * COLS : (c + 1) * COLS, :], ((1,), (1,)))
        go(remote(part.at[:, cols], swap.at[:, cols], ws.at[c], wr.at[c], me, 1 - h))
    scatter.second(2)
    for c in range(wide // COLS):
        cols = pl.ds(c * COLS, COLS)
        arrived(swap.at[:, cols], ws.at[c], wr.at[c], me, 1 - h)
    for mb in range(mbs):

        def body(turn, carry):
            row = chunk(turn)
            flat = pl.ds(pl.multiple_of(mb * count + turn * 16, 16), 16)
            v = xin[mb, row, :].astype(f32)
            scale = lax.rsqrt(jnp.mean(v * v, axis=-1, keepdims=True) + epsilon)
            hat = v * scale
            e = part[flat, :] + swap[flat, :]
            d_in[mb, row, :] = (
                d_mid[mb, row, :] + scale * (e - hat * jnp.mean(e * hat, axis=-1, keepdims=True))
            ).astype(bf16)
            return carry

        lax.fori_loop(0, count // 16, body, 0)
    scatter.second(1)
    scatter.third(2)
    scatter.second(3)
    scatter.third(1)
    scatter.second(0)
    scatter.third(3)
    combine.total()
    scatter.third(0)
    combine.done()
    for mb in range(mbs):

        def body(turn, carry):
            row = chunk(turn)
            outputs[mb, row, :] = (mid[mb, row, :] + branch[mb, row, :].astype(f32)).astype(bf16)
            return carry

        lax.fori_loop(0, count // 16, body, 0)
    scatter.last()
    for copy in late:
        copy.wait_send()


def end(t, home, xh, d_att, heads_out, wa1, d_mid, xin, mid):
    mbs, count, wide = xin.shape
    shape = jax.ShapeDtypeStruct
    cols = wa1.shape[1] + heads_out.shape[1]
    line = pltpu.VMEM((ZED, count, wide), bf16)
    return pl.pallas_call(
        end_kernel,
        out_shape=(shape((ZED, 128, cols), bf16), shape(xin.shape, bf16), shape(xin.shape, bf16)),
        in_specs=[ANY] + [VMEM] * 4 + [ANY] + [VMEM] * 3,
        out_specs=(VMEM,) * 3,
        scratch_shapes=[pltpu.VMEM((ZED, 2, 2, 128, cols), bf16)] + scatter_room(cols) + [
            pltpu.VMEM(xin.shape, bf16), line, line, line,
            pltpu.VMEM(wa1.shape, bf16),
            pltpu.VMEM((mbs * count, mbs * count), f32),
            pltpu.VMEM((mbs * count, wa1.shape[1]), bf16),
            pltpu.VMEM((mbs * count, wide), f32),
            pltpu.VMEM((mbs * count, wide), f32),
            DMA((6,)), DMA((4, 5)), DMA((4, 5)), DMA((4, 2)), DMA((4, 2)),
            DMA((wide // COLS,)), DMA((wide // COLS,)),
        ],
        compiler_params=params(),
        name="end",
    )(t, home, xh, d_att, heads_out, wa1, d_mid, xin, mid)


def fast(
    inputs, norm_gain1, w_query, w_key, w_value, w_out, norm_gain2, w_gate, w_up, w_down, cotangent
):
    mbs, count, wide = inputs.shape
    heads = w_query.shape[1] // F
    units = w_gate.shape[1] // ZED
    room = -(-units // 128) * 128
    qk, vv = 2 * heads * F, heads * DV
    rows = w_query.shape[0]
    gain1, gain2 = norm_gain1.astype(f32)[:, None], norm_gain2.astype(f32)[:, None]

    def folded(weight, gain):
        return (weight.astype(f32) * gain).astype(bf16)

    a1 = jnp.concatenate([folded(w_query, gain1), folded(w_key, gain1), folded(w_value, gain1)], axis=1)

    def cut(weight):
        pieces = jnp.transpose(weight.reshape(rows, ZED, units), (1, 0, 2))
        return jnp.pad(pieces, ((0, 0), (0, 0), (0, room - units)))

    m = jnp.concatenate([cut(folded(w_gate, gain2)), cut(folded(w_up, gain2)), cut(w_down.T)], axis=2)
    stream = inputs.astype(f32).reshape(mbs * count, wide)
    r1 = lax.rsqrt(jnp.mean(stream * stream, axis=-1, keepdims=True) + epsilon)
    xh1 = (stream * r1).astype(bf16)
    wa1, w_o, wm, gg, got, ratio, den, heads_out, middle, near = front(
        a1, w_out.T, m, cotangent, xh1, inputs
    )
    w_g, w_u, w_d = wm[:, :room], wm[:, room : 2 * room], wm[:, 2 * room :]
    many = ZED * mbs * count
    n2 = near.reshape(many, wide)
    up_g = gg.reshape(many, wide)
    gate = mix(n2, w_g, ((1,), (0,)))
    up = mix(n2, w_u, ((1,), (0,)))
    d_hidden = mix(up_g, w_d, ((1,), (0,)))
    sig = jax.nn.sigmoid(gate)
    silu = gate * sig
    hidden = (silu * up).astype(bf16)
    d_gate = (d_hidden * up * sig * (1.0 + gate * (1.0 - sig))).astype(bf16)
    d_up = (d_hidden * silu).astype(bf16)
    branch = mix(hidden, w_d, ((1,), (1,))).astype(bf16)
    d_n2 = (mix(d_gate, w_g, ((1,), (1,))) + mix(d_up, w_u, ((1,), (1,)))).astype(bf16)
    first = ((0,), (0,))
    gm = jnp.concatenate(
        [mix(n2, d_gate, first), mix(n2, d_up, first), mix(up_g, hidden, first)], axis=1
    ).astype(bf16)
    lines = (ZED, mbs, count, wide)
    zm, d_mid, d_att, home = back(
        gm, d_n2.reshape(lines), w_o, middle, cotangent, got, ratio, den
    )
    za, input_grad, outputs = end(
        branch.reshape(lines), home, xh1, d_att, heads_out, wa1, d_mid, inputs, middle
    )
    za = jnp.sum(za.astype(f32), axis=0)
    zm = zm.astype(f32)

    def joined(piece):
        return jnp.transpose(piece[:, :, :units], (1, 0, 2)).reshape(rows, ZED * units)

    g_gate, g_up, g_down = joined(zm[:, :, :room]), joined(zm[:, :, room : 2 * room]), joined(zm[:, :, 2 * room :])
    s_q, s_k, s_v = za[:, : qk // 2], za[:, qk // 2 : qk], za[:, qk : qk + vv]
    g_gain1 = (
        jnp.sum(w_query.astype(f32) * s_q, axis=1)
        + jnp.sum(w_key.astype(f32) * s_k, axis=1)
        + jnp.sum(w_value.astype(f32) * s_v, axis=1)
    )
    g_gain2 = jnp.sum(w_gate.astype(f32) * g_gate, axis=1) + jnp.sum(w_up.astype(f32) * g_up, axis=1)
    gains = lax.psum(jnp.stack([g_gain1, g_gain2]), "head")
    return (
        outputs,
        input_grad,
        gains[0],
        s_q * gain1,
        s_k * gain1,
        s_v * gain1,
        za[:, qk + vv :].T,
        gains[1],
        g_gate * gain2,
        g_up * gain2,
        g_down.T,
    )


def solution(mesh):
    return jax.shard_map(
        fast if mesh.shape["seq"] == 16 else local,
        mesh=mesh,
        in_specs=(
            P(None, "seq", None),
            P("seq"),
            P("seq", "head"),
            P("seq", "head"),
            P("seq", "head"),
            P("head", "seq"),
            P("seq"),
            P("seq", "head"),
            P("seq", "head"),
            P("head", "seq"),
            P(None, "seq", None),
        ),
        out_specs=(
            P(None, "seq", None),
            P(None, "seq", None),
            P("seq"),
            P("seq", "head"),
            P("seq", "head"),
            P("seq", "head"),
            P("head", "seq"),
            P("seq"),
            P("seq", "head"),
            P("seq", "head"),
            P("head", "seq"),
        ),
        check_vma=False,
    )
```

```python
import jax
import jax.numpy as jnp
from jax import lax
from jax.experimental import pallas as pl
from jax.experimental.pallas import tpu as pltpu
from jax.sharding import PartitionSpec as P

F = 16
DV = 128


epsilon = 1e-05
highest = lax.Precision.HIGHEST


def entering(part, axis, combine, identity, reverse):
    count = lax.axis_size(axis)
    place = lax.axis_index(axis)
    ahead = count - 1 - place if reverse else place
    gathered = jax.tree.map(lambda a: lax.all_gather(a, axis), part)
    state = jax.tree.map(lambda a, e: jnp.zeros_like(a) + jnp.asarray(e, a.dtype), part, identity)

    def one(turn, state):
        source = count - 1 - turn if reverse else turn
        return combine(
            state, jax.tree.map(lambda a: lax.dynamic_index_in_dim(a, source, 0, False), gathered)
        )

    return lax.fori_loop(0, ahead, one, state)


def rms_apply(values, gain):
    scale = lax.rsqrt(jnp.mean(values * values, axis=-1, keepdims=True) + epsilon)
    return values * scale * gain


def feature_map(projected):
    count = projected.shape[0]
    pieces = projected.reshape(count, -1, F)
    square = (pieces[:, :, :, None] * pieces[:, :, None, :]).reshape(count, pieces.shape[1], F * F)
    return jnp.concatenate(
        [jnp.ones_like(pieces[:, :, :1]), pieces * F ** (-0.25), square * (2.0 * F) ** (-0.5)],
        axis=-1,
    )


def swiglu(gate, up_part):
    return jax.nn.silu(gate) * up_part


def round_trip(values):
    return lax.optimization_barrier(values.astype(jnp.bfloat16)).astype(jnp.float32)


def add_pair(earlier, later):
    return (earlier[0] + later[0], earlier[1] + later[1])


def block_pass(tokens, upstream, gathered):
    gain_one, query_w, key_w, value_w, out_w, gain_two, gate_w, up_w, down_w = gathered
    f32 = jnp.float32
    bf16 = jnp.bfloat16
    stream = tokens.astype(f32)
    count = stream.shape[0]
    normed_f, norm_one_pull = jax.vjp(rms_apply, stream, gain_one.astype(f32))
    normed = normed_f.astype(bf16)
    queries = jnp.dot(normed, query_w, preferred_element_type=f32)
    keys_all = jnp.dot(normed, key_w, preferred_element_type=f32)
    values = jnp.dot(normed, value_w, preferred_element_type=f32).astype(bf16)
    query_feat_f, query_pull = jax.vjp(feature_map, queries)
    key_feat_f, key_pull = jax.vjp(feature_map, keys_all)
    query_feat = jnp.transpose(query_feat_f.astype(bf16), (1, 0, 2))
    key_feat = jnp.transpose(key_feat_f.astype(bf16), (1, 0, 2))
    value_heads = jnp.transpose(values.reshape(count, -1, DV), (1, 0, 2))
    causal = (jnp.arange(count)[:, None] >= jnp.arange(count)[None, :]).astype(f32)
    scores = jnp.einsum("htf,hsf->hts", query_feat, key_feat, preferred_element_type=f32) * causal
    weighted = scores.astype(bf16)
    num_local = jnp.einsum("hts,hsd->htd", weighted, value_heads, preferred_element_type=f32)
    den_local = jnp.sum(weighted.astype(f32), axis=-1)
    states = jnp.einsum("hsf,hsd->hfd", key_feat, value_heads, preferred_element_type=f32)
    totals = jnp.sum(key_feat.astype(f32), axis=1)
    state_before, total_before = entering(
        (states, totals), "seq", add_pair, (jnp.zeros_like(states), jnp.zeros_like(totals)), False
    )
    query_wide = query_feat.astype(f32)
    numer = num_local + jnp.einsum("htf,hfd->htd", query_wide, state_before, precision=highest)
    denom = den_local + jnp.einsum("htf,hf->ht", query_wide, total_before, precision=highest)
    ratio = numer / denom[..., None]
    heads_out = jnp.transpose(ratio, (1, 0, 2)).reshape(count, -1).astype(bf16)
    attended = lax.psum(jnp.dot(heads_out, out_w, preferred_element_type=f32), "head")
    middle = stream + attended
    normed_two_f, norm_two_pull = jax.vjp(rms_apply, middle, gain_two.astype(f32))
    normed_two = normed_two_f.astype(bf16)
    gate = jnp.dot(normed_two, gate_w, preferred_element_type=f32)
    up_part = jnp.dot(normed_two, up_w, preferred_element_type=f32)
    active, active_pull = jax.vjp(swiglu, gate, up_part)
    hidden = active.astype(bf16)
    branch = lax.psum(
        jnp.dot(hidden, down_w, preferred_element_type=f32).astype(jnp.bfloat16), "head"
    ).astype(jnp.float32)
    result = (middle + branch).astype(bf16)
    grad_down = jnp.dot(hidden.T, upstream, preferred_element_type=f32)
    d_hidden = jnp.dot(upstream, down_w.T, preferred_element_type=f32)
    d_gate_f, d_up_f = active_pull(d_hidden)
    d_gate = d_gate_f.astype(bf16)
    d_up = d_up_f.astype(bf16)
    grad_gate = jnp.dot(normed_two.T, d_gate, preferred_element_type=f32)
    grad_up = jnp.dot(normed_two.T, d_up, preferred_element_type=f32)
    d_normed_two = lax.psum(
        jnp.dot(d_gate, gate_w.T, preferred_element_type=f32)
        + jnp.dot(d_up, up_w.T, preferred_element_type=f32),
        "head",
    )
    d_middle_norm, grad_gain2 = norm_two_pull(d_normed_two)
    d_middle = upstream.astype(f32) + d_middle_norm
    d_attended = d_middle.astype(bf16)
    grad_out = jnp.dot(heads_out.T, d_attended, preferred_element_type=f32)
    d_heads = jnp.transpose(
        jnp.dot(d_attended, out_w.T, preferred_element_type=f32).reshape(count, -1, DV), (1, 0, 2)
    )
    d_numer = (d_heads / denom[..., None]).astype(bf16)
    d_denom = -jnp.sum(d_heads * ratio, axis=-1) / denom
    d_numer_wide = d_numer.astype(f32)
    d_before = jnp.einsum("htf,htd->hfd", query_wide, d_numer_wide, precision=highest)
    d_total_before = jnp.einsum("htf,ht->hf", query_wide, d_denom, precision=highest)
    d_state, d_total = entering(
        (d_before, d_total_before),
        "seq",
        add_pair,
        (jnp.zeros_like(d_before), jnp.zeros_like(d_total_before)),
        True,
    )
    d_scores = (
        (
            jnp.einsum("htd,hsd->hts", d_numer, value_heads, preferred_element_type=f32)
            + d_denom[..., None]
        )
        * causal
    ).astype(bf16)
    d_values = jnp.einsum(
        "hts,htd->hsd", weighted, d_numer, preferred_element_type=f32
    ) + jnp.einsum("hsf,hfd->hsd", key_feat.astype(f32), d_state, precision=highest)
    d_query_feat = (
        jnp.einsum("hts,hsf->htf", d_scores, key_feat, preferred_element_type=f32)
        + jnp.einsum("htd,hfd->htf", d_numer_wide, state_before, precision=highest)
        + d_denom[..., None] * total_before[:, None, :]
    )
    d_key_feat = (
        jnp.einsum("hts,htf->hsf", d_scores, query_feat, preferred_element_type=f32)
        + jnp.einsum("hsd,hfd->hsf", value_heads.astype(f32), d_state, precision=highest)
        + d_total[:, None, :]
    )
    d_queries = query_pull(jnp.transpose(round_trip(d_query_feat), (1, 0, 2)))[0].astype(bf16)
    d_keys = key_pull(jnp.transpose(round_trip(d_key_feat), (1, 0, 2)))[0].astype(bf16)
    d_values_flat = jnp.transpose(d_values, (1, 0, 2)).reshape(count, -1).astype(bf16)
    grad_query = jnp.dot(normed.T, d_queries, preferred_element_type=f32)
    grad_key = jnp.dot(normed.T, d_keys, preferred_element_type=f32)
    grad_value = jnp.dot(normed.T, d_values_flat, preferred_element_type=f32)
    d_normed_part = (
        jnp.dot(d_queries, query_w.T, preferred_element_type=f32)
        + jnp.dot(d_keys, key_w.T, preferred_element_type=f32)
        + jnp.dot(d_values_flat, value_w.T, preferred_element_type=f32)
    )
    d_normed = lax.psum(d_normed_part.astype(jnp.bfloat16), "head").astype(jnp.float32)
    d_stream_norm, grad_gain1 = norm_one_pull(d_normed)
    input_grad = (d_middle + d_stream_norm).astype(bf16)
    return (
        result,
        input_grad,
        grad_gain1,
        grad_query,
        grad_key,
        grad_value,
        grad_out,
        grad_gain2,
        grad_gate,
        grad_up,
        grad_down,
    )


def local(
    inputs, norm_gain1, w_query, w_key, w_value, w_out, norm_gain2, w_gate, w_up, w_down, cotangent
):
    micro = inputs.shape[0]
    summed = None
    results = []
    input_grads = []
    for step_index in range(micro):
        gathered = (
            lax.all_gather(norm_gain1, "seq", axis=0, tiled=True),
            lax.all_gather(w_query, "seq", axis=0, tiled=True),
            lax.all_gather(w_key, "seq", axis=0, tiled=True),
            lax.all_gather(w_value, "seq", axis=0, tiled=True),
            lax.all_gather(w_out, "seq", axis=1, tiled=True),
            lax.all_gather(norm_gain2, "seq", axis=0, tiled=True),
            lax.all_gather(w_gate, "seq", axis=0, tiled=True),
            lax.all_gather(w_up, "seq", axis=0, tiled=True),
            lax.all_gather(w_down, "seq", axis=1, tiled=True),
        )
        (
            result,
            input_grad,
            grad_gain1,
            grad_query,
            grad_key,
            grad_value,
            grad_out,
            grad_gain2,
            grad_gate,
            grad_up,
            grad_down,
        ) = block_pass(inputs[step_index], cotangent[step_index], gathered)
        results.append(result)
        input_grads.append(input_grad)
        fresh = (
            lax.psum_scatter(grad_gain1, "seq", scatter_dimension=0, tiled=True),
            lax.psum_scatter(grad_query, "seq", scatter_dimension=0, tiled=True),
            lax.psum_scatter(grad_key, "seq", scatter_dimension=0, tiled=True),
            lax.psum_scatter(grad_value, "seq", scatter_dimension=0, tiled=True),
            lax.psum_scatter(grad_out, "seq", scatter_dimension=1, tiled=True),
            lax.psum_scatter(grad_gain2, "seq", scatter_dimension=0, tiled=True),
            lax.psum_scatter(grad_gate, "seq", scatter_dimension=0, tiled=True),
            lax.psum_scatter(grad_up, "seq", scatter_dimension=0, tiled=True),
            lax.psum_scatter(grad_down, "seq", scatter_dimension=1, tiled=True),
        )
        summed = (
            fresh
            if summed is None
            else tuple((older + newer for older, newer in zip(summed, fresh)))
        )
    return (
        jnp.stack(results),
        jnp.stack(input_grads),
        summed[0],
        summed[1],
        summed[2],
        summed[3],
        summed[4],
        summed[5],
        summed[6],
        summed[7],
        summed[8],
    )


MESH = pl.DeviceIdType.MESH
bf16 = jnp.bfloat16
f32 = jnp.float32
ZED = 4
VMEM_LIMIT = 60 * 1024 * 1024


def where_am_i():
    place = lax.axis_index("seq")
    return place % 2, (place // 2) % 2, place // 4, lax.axis_index("head")


def index_of(z, y, x):
    return (z * 2 + y) * 2 + x


def remote(src, dst, send, recv, place, head):
    return pltpu.make_async_remote_copy(
        src_ref=src, dst_ref=dst, send_sem=send, recv_sem=recv, device_id=(place, head),
        device_id_type=MESH,
    )


def arrived(dst, send, recv, place, head):
    remote(dst, dst, send, recv, place, head).wait_recv()


def params():
    return pltpu.CompilerParams(has_side_effects=True, vmem_limit_bytes=VMEM_LIMIT)


ANY = pl.BlockSpec(memory_space=pl.ANY)
VMEM = pl.BlockSpec(memory_space=pltpu.VMEM)
DMA = pltpu.SemaphoreType.DMA
ORDER = (0, 1, 3, 2)


def mix(a, b, over):
    return lax.dot_general(a, b, (over, ((), ())), preferred_element_type=f32)


CHUNK = 512
COLS = 256


def spread(got, q_t, k_t, va):
    count = got.shape[2]
    for b in range(got.shape[0]):
        q_t[:, b * count : (b + 1) * count] = got[b, 0:F, :]
        k_t[:, b * count : (b + 1) * count] = got[b, F : 2 * F, :]
        va[b * count : (b + 1) * count, 0:DV] = got[b, 2 * F :, :]
    va[:, DV:] = jnp.ones((va.shape[0], va.shape[1] - DV), bf16)


def lower(count):
    return lax.broadcasted_iota(jnp.int32, (count, count), 0) >= lax.broadcasted_iota(
        jnp.int32, (count, count), 1
    )


def attend_rows(qi, q_t, k_t, va, ratio, den, causal):
    qs = slice(qi * CHUNK, (qi + 1) * CHUNK)
    acc = jnp.zeros((CHUNK, va.shape[1]), f32)
    for kj in range(qi + 1):
        ks = slice(kj * CHUNK, (kj + 1) * CHUNK)
        s = mix(q_t[:, qs], k_t[:, ks], ((0,), (0,)))
        p = 1.0 + s * (0.25 + s * (1.0 / 32.0))
        if kj == qi:
            p = jnp.where(causal, p, 0.0)
        acc = acc + mix(p.astype(bf16), va[ks, :], ((1,), (0,)))
    ratio[qs, :] = acc[:, :DV] / acc[:, DV:]
    den[qs, :] = acc[:, DV:]


def front_kernel(
    a1, a2, m, cot, xh, xin,
    wa1, wa2, wm, gg, got, ratio, den, heads_out, middle, near,
    w1, w2, pack, q_t, k_t, va, ob, part, other,
    ls, zs, zr, us, ur, ps, pr, e1s, e1r, e2s, e2r, ws, wr, ds, dr,
):
    x, y, z, h = where_am_i()
    me = index_of(z, y, x)
    at_x, at_y = index_of(z, y, 1 - x), index_of(z, 1 - y, x)
    count = xin.shape[1]
    heads = 16 // xin.shape[0]
    late = []

    def when(true, do):
        if true is None:
            do()
        else:
            pl.when(true)(do)

    def go(copy, true=None):
        when(true, copy.start)
        late.append((true, copy))

    def rows(zz, yy, xx):
        return pl.ds(pl.multiple_of(index_of(zz, yy, xx) * 128, 128), 128)

    mine = rows(z, y, x)
    kept = [
        pltpu.make_async_copy(a1, w1.at[mine], ls.at[0]),
        pltpu.make_async_copy(a2, w2.at[mine], ls.at[1]),
        pltpu.make_async_copy(m.at[z], wm.at[mine], ls.at[2]),
        pltpu.make_async_copy(cot, gg.at[z], ls.at[6]),
    ]
    for copy in kept:
        copy.start()
    dest = (w1, w2, wm)
    UP, DOWN = 0, 1
    COT, NEAR = 2, 3

    def held(kind, zz):
        return (lambda: w1.at[rows(zz, y, x)], lambda: w2.at[rows(zz, y, x)],
                lambda: gg.at[zz, h], lambda: near.at[zz, h])[kind]()

    def origin(way, step):
        return (z + ZED - step) % ZED if way == UP else (z + step) % ZED

    def valid(way, step):
        return z >= step if way == UP else z <= ZED - 1 - step

    def pass_on(kind, way, step, src, true):
        there = index_of((z + 1) % ZED if way == UP else (z + ZED - 1) % ZED, y, x)
        block = held(kind, origin(way, step))
        go(remote(block if src is None else src, block, us.at[kind, way, step], ur.at[kind, way, step + 1], there, h), true)

    def offer(kind, src=None):
        pass_on(kind, UP, 0, src, z < ZED - 1)
        pass_on(kind, DOWN, 0, src, z > 0)

    def hop(kind, way, step):
        block = held(kind, origin(way, step))
        when(
            valid(way, step),
            lambda: arrived(block, us.at[kind, way, step], ur.at[kind, way, step], me, h),
        )
        if step < ZED - 1:
            more = z < ZED - 1 if way == UP else z > 0
            pass_on(kind, way, step, None, valid(way, step) & more)

    def across(kind, way, step):
        zz = origin(way, step)
        block = held(kind, zz)
        go(remote(block, block, ds.at[kind, way, step], dr.at[kind, way, step], me, 1 - h), valid(way, step))

    def across_done(kind, way, step):
        zz = origin(way, step)
        block = (gg if kind == COT else near).at[zz, 1 - h]
        when(
            valid(way, step),
            lambda: arrived(block, ds.at[kind, way, step], dr.at[kind, way, step], me, 1 - h),
        )

    def both(do, kind, step):
        do(kind, UP, step)
        do(kind, DOWN, step)

    partner = (z, z + 1 - 2 * (z % 2), ZED - 1 - z, (z + 2) % ZED)

    def line(d):
        zz = partner[d]
        go(remote(m.at[zz], wm.at[mine], zs.at[d], zr.at[d], index_of(zz, y, x), h))

    def slot_of(way, step):
        return step if way == UP else 3 + step if step else 0

    def plane_set(kind, slot, zz, true):
        block = dest[kind].at[rows(zz, y, x)]
        go(remote(block, block, ps.at[kind, slot, 0], pr.at[kind, slot, 0], at_x, h), true)
        go(remote(block, block, ps.at[kind, slot, 1], pr.at[kind, slot, 1], at_y, h), true)

    def onward_set(kind, slot, zz, true):
        w = dest[kind]
        half = w.shape[1] // 2
        from_x, from_y = rows(zz, y, 1 - x), rows(zz, 1 - y, x)

        def wait():
            arrived(w.at[from_x], ps.at[kind, slot, 0], pr.at[kind, slot, 0], me, h)
            arrived(w.at[from_y], ps.at[kind, slot, 1], pr.at[kind, slot, 1], me, h)

        when(true, wait)
        left = w.at[from_y, pl.ds(0, half)]
        right = w.at[from_x, pl.ds(half, half)]
        go(remote(left, left, ps.at[kind, slot, 2], pr.at[kind, slot, 2], at_x, h), true)
        go(remote(right, right, ps.at[kind, slot, 3], pr.at[kind, slot, 3], at_y, h), true)

    def corner_set(kind, slot, zz, true):
        w = dest[kind]
        half = w.shape[1] // 2
        far = rows(zz, 1 - y, 1 - x)

        def wait():
            arrived(w.at[far, pl.ds(0, half)], ps.at[kind, slot, 2], pr.at[kind, slot, 2], me, h)
            arrived(w.at[far, pl.ds(half, half)], ps.at[kind, slot, 3], pr.at[kind, slot, 3], me, h)

        when(true, wait)

    def plane(kind, way, step):
        if step == 0:
            kept[kind].wait()
        plane_set(kind, slot_of(way, step), origin(way, step), valid(way, step) if step else None)

    def onward(kind, way, step):
        onward_set(kind, slot_of(way, step), origin(way, step), valid(way, step) if step else None)

    def corner(kind):
        corner_set(kind, 0, z, None)
        for step in (1, 2, 3):
            for way in (UP, DOWN):
                corner_set(kind, slot_of(way, step), origin(way, step), valid(way, step))

    def m_plane(d):
        zz = partner[d]
        if d:
            arrived(wm.at[rows(zz, y, x)], zs.at[d], zr.at[d], me, h)
        else:
            kept[2].wait()
        plane_set(2, d, zz, None)

    def m_onward(d):
        onward_set(2, d, partner[d], None)

    offer(0, a1)
    plane(0, UP, 0)
    for way in (UP, DOWN):
        hop(0, way, 1)
        plane(0, way, 1)
    onward(0, UP, 0)
    for way in (UP, DOWN):
        hop(0, way, 2)
        plane(0, way, 2)
    offer(1, a2)
    both(onward, 0, 1)
    for way in (UP, DOWN):
        hop(0, way, 3)
        plane(0, way, 3)
    both(onward, 0, 2)
    both(hop, 1, 1)
    plane(1, UP, 0)
    both(onward, 0, 3)
    both(hop, 1, 2)
    both(plane, 1, 1)
    both(hop, 1, 3)
    line(1)
    line(2)
    corner(0)
    out1 = pltpu.make_async_copy(w1, wa1, ls.at[3])
    out1.start()
    kq = mix(xh[...], w1[:, 0 : 2 * heads * F], ((1,), (0,)))
    qk = jnp.transpose(kq).astype(bf16)
    for mb in range(16 // heads):
        for k in range(heads):
            t = k + heads * mb
            cols = slice(mb * count, (mb + 1) * count)
            pack[t, 0:F, :] = qk[k * F : (k + 1) * F, cols]
            pack[t, F : 2 * F, :] = qk[(heads + k) * F : (heads + k + 1) * F, cols]
    for c in range(heads * DV // COLS):
        at = 2 * heads * F + c * COLS
        val = mix(xh[...], w1[:, at : at + COLS], ((1,), (0,))).astype(bf16)
        for mb in range(16 // heads):
            for i in range(COLS // DV):
                t = c * (COLS // DV) + i + heads * mb
                pack[t, 2 * F :, :] = val[mb * count : (mb + 1) * count, i * DV : (i + 1) * DV]
    keep = pltpu.make_async_copy(pack.at[me], got.at[me], ls.at[4])
    keep.start()
    for d in range(1, 16):
        there = (me + d) % 16
        go(remote(pack.at[there], got.at[me], e1s.at[d], e1r.at[d], there, h))
    onward(1, UP, 0)
    both(plane, 1, 2)
    both(onward, 1, 1)
    both(plane, 1, 3)
    both(onward, 1, 2)
    keep.wait()
    for d in range(1, 16):
        arrived(got.at[(me + 16 - d) % 16], e1s.at[d], e1r.at[d], me, h)
    line(3)
    both(onward, 1, 3)
    spread(got, q_t, k_t, va)
    causal = lower(CHUNK)
    for qi in range(va.shape[0] // CHUNK):
        attend_rows(qi, q_t, k_t, va, ratio, den, causal)
    for b in range(16):
        ob[b, :, :] = ratio[b * count : (b + 1) * count, :].astype(bf16)

    def window(source):
        return heads_out.at[
            pl.ds(pl.multiple_of((source // heads) * count, count), count),
            pl.ds(pl.multiple_of((source % heads) * DV, DV), DV),
        ]

    keep = pltpu.make_async_copy(ob.at[me], window(me), ls.at[4])
    keep.start()
    for d in range(1, 16):
        there = (me + d) % 16
        go(remote(ob.at[there], window(me), e2s.at[d], e2r.at[d], there, h))
    m_plane(0)
    corner(1)
    out2 = pltpu.make_async_copy(w2, wa2, ls.at[5])
    out2.start()
    keep.wait()
    for d in range(1, 16):
        arrived(window((me + 16 - d) % 16), e2s.at[d], e2r.at[d], me, h)
    wide = part.shape[1]
    for c in range(wide // COLS):
        cols = pl.ds(c * COLS, COLS)
        part[:, c * COLS : (c + 1) * COLS] = mix(
            heads_out[...], w2[c * COLS : (c + 1) * COLS, :], ((1,), (1,))
        )
        go(remote(part.at[:, cols], other.at[:, cols], ws.at[c], wr.at[c], me, 1 - h))
    m_onward(0)
    m_plane(1)
    for c in range(wide // COLS):
        cols = pl.ds(c * COLS, COLS)
        arrived(other.at[:, cols], ws.at[c], wr.at[c], me, 1 - h)

    def one(mb):
        def body(turn, carry):
            row = pl.ds(pl.multiple_of(turn * 16, 16), 16)
            flat = pl.ds(pl.multiple_of(mb * count + turn * 16, 16), 16)
            mid = xin[mb, row, :].astype(f32) + (part[flat, :] + other[flat, :])
            middle[mb, row, :] = mid
            scale = lax.rsqrt(jnp.mean(mid * mid, axis=-1, keepdims=True) + epsilon)
            near[z, mb, row, :] = (mid * scale).astype(bf16)
            return carry

        lax.fori_loop(0, count // 16, body, 0)

    one(h)
    offer(NEAR)
    one(1 - h)
    m_onward(1)
    m_plane(2)
    both(hop, NEAR, 1)
    both(across, NEAR, 1)
    both(hop, NEAR, 2)
    both(across, NEAR, 2)
    offer(COT, cot.at[h])
    kept[3].wait()
    m_onward(2)
    m_plane(3)
    both(hop, NEAR, 3)
    both(across, NEAR, 3)
    both(hop, COT, 1)
    both(across, COT, 1)
    m_onward(3)
    both(hop, COT, 2)
    both(across, COT, 2)
    both(hop, COT, 3)
    both(across, COT, 3)
    for d in range(4):
        corner_set(2, d, partner[d], None)
    for kind in (NEAR, COT):
        for step in (1, 2, 3):
            both(across_done, kind, step)
    out1.wait()
    out2.wait()
    for true, copy in late:
        when(true, copy.wait_send)


def front(a1, a2, m, cot, xh, xin):
    mbs, count, wide = xin.shape
    depth = 16 * count
    wide1, wide2 = a1.shape[1], a2.shape[1]
    shape = jax.ShapeDtypeStruct
    return pl.pallas_call(
        front_kernel,
        out_shape=(
            shape((wide, wide1), bf16),
            shape((wide, wide2), bf16),
            shape((wide, m.shape[2]), bf16),
            shape((ZED,) + cot.shape, bf16),
            shape((16, 2 * F + DV, count), bf16),
            shape((depth, DV), f32),
            shape((depth, DV), f32),
            shape((mbs * count, wide2), bf16),
            shape(xin.shape, f32),
            shape((ZED,) + xin.shape, bf16),
        ),
        in_specs=[ANY] * 4 + [VMEM] * 2,
        out_specs=(ANY,) * 4 + (VMEM,) * 6,
        scratch_shapes=[
            pltpu.VMEM((wide, wide1), bf16),
            pltpu.VMEM((wide, wide2), bf16),
            pltpu.VMEM((16, 2 * F + DV, count), bf16),
            pltpu.VMEM((F, depth), bf16),
            pltpu.VMEM((F, depth), bf16),
            pltpu.VMEM((depth, 2 * DV), bf16),
            pltpu.VMEM((16, count, DV), bf16),
            pltpu.VMEM((mbs * count, wide), f32),
            pltpu.VMEM((mbs * count, wide), f32),
            DMA((7,)), DMA((4,)), DMA((4,)), DMA((4, 2, 4)), DMA((4, 2, 4)), DMA((3, 7, 4)), DMA((3, 7, 4)),
            DMA((16,)), DMA((16,)), DMA((16,)), DMA((16,)),
            DMA((wide // COLS,)), DMA((wide // COLS,)), DMA((4, 2, 4)), DMA((4, 2, 4)),
        ],
        compiler_params=params(),
        name="front",
    )(a1, a2, m, cot, xh, xin)


def attend_back_body(got, ratio, den, d_o, d_qk, d_v, q_t, k_t, va, da, dn_t):
    spread(got, q_t, k_t, va)
    depth = va.shape[0]
    lane = lax.broadcasted_iota(jnp.int32, (CHUNK, DV), 1)
    for qi in range(depth // CHUNK):
        qs = slice(qi * CHUNK, (qi + 1) * CHUNK)
        dn = d_o[qs, :].astype(f32) / den[qs, :]
        dd = -jnp.sum(dn * ratio[qs, :], axis=-1, keepdims=True)
        big = dd.astype(bf16).astype(f32)
        da[qs, 0:DV] = dn.astype(bf16)
        da[qs, DV:] = jnp.where(lane == 0, big, jnp.where(lane == 1, dd - big, 0.0)).astype(bf16)
        dn_t[:, qs] = jnp.transpose(dn).astype(bf16)
    causal = lower(CHUNK)
    for kj in range(depth // CHUNK):
        ks = slice(kj * CHUNK, (kj + 1) * CHUNK)
        acc_k = jnp.zeros((F, CHUNK), f32)
        acc_v = jnp.zeros((DV, CHUNK), f32)
        for qi in range(kj, depth // CHUNK):
            qs = slice(qi * CHUNK, (qi + 1) * CHUNK)
            s = mix(q_t[:, qs], k_t[:, ks], ((0,), (0,)))
            p = 1.0 + s * (0.25 + s * (1.0 / 32.0))
            d_s = mix(da[qs, :], va[ks, :], ((1,), (1,))) * (0.25 + s * (1.0 / 16.0))
            if kj == qi:
                p = jnp.where(causal, p, 0.0)
                d_s = jnp.where(causal, d_s, 0.0)
            d_s = d_s.astype(bf16)
            acc_v = acc_v + mix(dn_t[:, qs], p.astype(bf16), ((1,), (0,)))
            acc_k = acc_k + mix(q_t[:, qs], d_s, ((1,), (0,)))
            d_q = mix(k_t[:, ks], d_s, ((1,), (1,)))
            d_qk[0:F, qs] = d_q if kj == 0 else d_qk[0:F, qs] + d_q
        d_qk[F : 2 * F, ks] = acc_k
        d_v[ks, :] = jnp.transpose(acc_v)


FAR = (2, 1, 3, 0)


def chunk(turn):
    return pl.ds(pl.multiple_of(turn * 16, 16), 16)


class Scatter:
    def __init__(self, g, low_acc, high_acc, fin, out, r1x, r1y, r2x, r2y, s, q, go):
        self.g, self.low_acc, self.high_acc, self.fin, self.out = g, low_acc, high_acc, fin, out
        self.r1x, self.r1y, self.r2x, self.r2y, self.s, self.q = r1x, r1y, r2x, r2y, s, q
        self.go = go
        self.x, self.y, self.z, self.h = where_am_i()
        self.me = index_of(self.z, self.y, self.x)
        self.at_x = index_of(self.z, self.y, 1 - self.x)
        self.at_y = index_of(self.z, 1 - self.y, self.x)
        self.half = r1x.shape[-1]
        self.low, self.high = pl.ds(0, self.half), pl.ds(self.half, self.half)

    def first_copies(self, d):
        zz, x, y, g = (self.z + d) % ZED, self.x, self.y, self.g
        return (
            remote(g.at[zz, :, 1 - x, :, self.low], self.r1x.at[d], self.s.at[d, 0], self.q.at[d, 0], self.at_x, self.h),
            remote(g.at[zz, 1 - y, :, :, self.high], self.r1y.at[d], self.s.at[d, 1], self.q.at[d, 1], self.at_y, self.h),
        )

    def first(self, d):
        for copy in self.first_copies(d):
            self.go(copy)

    def second(self, d):
        x, y, me, h, r1x, r1y = self.x, self.y, self.me, self.h, self.r1x, self.r1y
        arrived(r1x.at[d], self.s.at[d, 0], self.q.at[d, 0], me, h)
        arrived(r1y.at[d], self.s.at[d, 1], self.q.at[d, 1], me, h)
        low_acc, high_acc = self.low_acc(d), self.high_acc(d)

        def body(i, carry):
            row = chunk(i)
            low_acc[row, :] = (
                low_acc[row, :].astype(f32) + r1x[d, 1 - y, row, :].astype(f32)
            ).astype(bf16)
            high_acc[row, :] = (
                high_acc[row, :].astype(f32) + r1y[d, 1 - x, row, :].astype(f32)
            ).astype(bf16)
            return carry

        lax.fori_loop(0, 8, body, 0)
        self.go(remote(low_acc, self.r2y.at[d], self.s.at[d, 2], self.q.at[d, 2], self.at_y, h))
        self.go(remote(high_acc, self.r2x.at[d], self.s.at[d, 3], self.q.at[d, 3], self.at_x, h))

    def third(self, d):
        x, y, me, h, z = self.x, self.y, self.me, self.h, self.z
        arrived(self.r2y.at[d], self.s.at[d, 2], self.q.at[d, 2], me, h)
        arrived(self.r2x.at[d], self.s.at[d, 3], self.q.at[d, 3], me, h)
        fin, low, high = self.fin(d), self.low, self.high
        target = fin if d else self.out.at[z]

        def body(i, carry):
            row = chunk(i)
            target[row, low] = (
                fin[row, low].astype(f32)
                + self.r1x[d, y, row, :].astype(f32)
                + self.r2y[d, row, :].astype(f32)
            ).astype(bf16)
            target[row, high] = (
                fin[row, high].astype(f32)
                + self.r1y[d, x, row, :].astype(f32)
                + self.r2x[d, row, :].astype(f32)
            ).astype(bf16)
            return carry

        lax.fori_loop(0, 8, body, 0)
        if d:
            there = index_of((z + d) % ZED, y, x)
            self.go(remote(fin, self.out.at[z], self.s.at[d, 4], self.q.at[d, 4], there, h))

    def last(self):
        for d in (1, 3, 2):
            arrived(
                self.out.at[(self.z + ZED - d) % ZED], self.s.at[d, 4], self.q.at[d, 4], self.me, self.h
            )


class Combine:
    def __init__(self, t, out, other, summed, landed, ls, s, q, go):
        self.t, self.out, self.other, self.summed, self.landed = t, out, other, summed, landed
        self.ls, self.s, self.q, self.go = ls, s, q, go
        self.x, self.y, self.z, self.h = where_am_i()
        self.me = index_of(self.z, self.y, self.x)

    def begin(self):
        t, h, other = self.t, self.h, self.other
        self.own = {}
        for d in FAR:
            zz = (self.z + d) % ZED
            self.own[d] = pltpu.make_async_copy(t.at[zz, h], self.summed.at[d], self.ls.at[d])
            self.own[d].start()
            self.go(remote(t.at[zz, 1 - h], other.at[d], self.s.at[d, 0], self.q.at[d, 0], self.me, 1 - h))

    def spread(self):
        summed, other = self.summed, self.other
        for d in FAR:
            zz = (self.z + d) % ZED
            self.own[d].wait()
            arrived(other.at[d], self.s.at[d, 0], self.q.at[d, 0], self.me, 1 - self.h)

            def add(turn, carry):
                row = chunk(turn)
                summed[d, row, :] = (
                    summed[d, row, :].astype(f32) + other[d, row, :].astype(f32)
                ).astype(bf16)
                return carry

            lax.fori_loop(0, 8, add, 0)
            if d:
                there = index_of(zz, self.y, self.x)
                self.go(remote(summed.at[d], self.landed.at[d], self.s.at[d, 1], self.q.at[d, 1], there, self.h))

    def total(self):
        summed, landed, out, h = self.summed, self.landed, self.out, self.h
        for d in (1, 3, 2):
            arrived(landed.at[d], self.s.at[d, 1], self.q.at[d, 1], self.me, h)

        def body(turn, carry):
            row = chunk(turn)
            acc = summed[0, row, :].astype(f32)
            for d in (1, 2, 3):
                acc = acc + landed[d, row, :].astype(f32)
            out[h, row, :] = acc.astype(bf16)
            return carry

        lax.fori_loop(0, 8, body, 0)
        self.go(remote(out.at[h], out.at[h], self.s.at[0, 1], self.q.at[0, 1], self.me, 1 - h))

    def done(self):
        arrived(self.out.at[1 - self.h], self.s.at[0, 1], self.q.at[0, 1], self.me, 1 - self.h)


def back_kernel(
    near, gg, dg, du, hid, t, wo, mid, cot, got, ratio, den,
    zm, d_mid, d_att, home,
    g, r1x, r1y, r2x, r2y, e2, other, summed, landed, w2, pack, d_o, d_qk, d_v,
    q_t, k_t, va, da, dn_t, pack2, nbuf, gbuf, turned,
    ls, fs, gs, gq, cs, cq, e1s, e1r, e2s, e2r,
):
    x, y, z, h = where_am_i()
    me = index_of(z, y, x)
    count = mid.shape[1]
    heads = 16 // mid.shape[0]
    room = dg.shape[1]
    late = []

    def go(copy):
        copy.start()
        late.append(copy)

    def fetch(i):
        cols = pl.ds(pl.multiple_of(((z + ZED - 1 - i) % ZED) * 512, 512), 512)
        return (
            pltpu.make_async_copy(near.at[:, cols], nbuf.at[i % 2], fs.at[i % 2, 0]),
            pltpu.make_async_copy(gg.at[:, cols], gbuf.at[i % 2], fs.at[i % 2, 1]),
        )

    for copy in fetch(0):
        copy.start()
    combine = Combine(t, e2, other, summed, landed, ls, cs, cq, go)
    scatter = Scatter(
        g,
        lambda d: g.at[(z + d) % ZED, 1 - y, x, :, pl.ds(0, g.shape[-1] // 2)],
        lambda d: g.at[(z + d) % ZED, y, 1 - x, :, pl.ds(g.shape[-1] // 2, g.shape[-1] // 2)],
        lambda d: g.at[(z + d) % ZED, y, x],
        zm, r1x, r1y, r2x, r2y, gs, gq, go,
    )
    combine.begin()
    weight = pltpu.make_async_copy(wo, w2, ls.at[4])
    weight.start()
    combine.spread()

    def block(i, carry):
        d = ZED - 1 - i
        zz = (z + d) % ZED

        @pl.when(i < ZED - 1)
        def _():
            for copy in fetch(i + 1):
                copy.start()

        for copy in fetch(i):
            copy.wait()
        for buf, terms in ((nbuf, (dg, du)), (gbuf, (hid,))):
            turned[...] = jnp.transpose(buf[i % 2])
            for term in terms:
                base = {id(dg): 0, id(du): room, id(hid): 2 * room}[id(term)]

                def piece(c, carry):
                    src = pl.ds(pl.multiple_of(c * COLS, COLS), COLS)
                    dst = pl.ds(pl.multiple_of(base + c * COLS, COLS), COLS)
                    res = mix(turned[...], term[:, src], ((1,), (0,))).astype(bf16)
                    for n in range(4):
                        g[zz, n // 2, n % 2, :, dst] = res[n * 128 : (n + 1) * 128, :]
                    return carry

                lax.fori_loop(0, room // COLS, piece, 0)
        for copy in scatter.first_copies(d):
            copy.start()
        return carry

    lax.fori_loop(0, ZED, block, 0)
    for d in range(ZED):
        late.extend(scatter.first_copies(d))
    weight.wait()
    scatter.second(3)
    combine.total()
    combine.done()

    for mb in range(mid.shape[0]):

        def body(turn, carry):
            row = chunk(turn)
            m = mid[mb, row, :]
            scale = lax.rsqrt(jnp.mean(m * m, axis=-1, keepdims=True) + epsilon)
            hat = m * scale
            e = e2[mb, row, :].astype(f32)
            d_m = cot[mb, row, :].astype(f32) + scale * (
                e - hat * jnp.mean(e * hat, axis=-1, keepdims=True)
            )
            d_mid[mb, row, :] = d_m
            d_att[pl.ds(pl.multiple_of(mb * count + turn * 16, 16), 16), :] = d_m.astype(bf16)
            return carry

        lax.fori_loop(0, count // 16, body, 0)
    for c in range(heads * DV // COLS):
        val = mix(d_att[...], w2[:, c * COLS : (c + 1) * COLS], ((1,), (0,))).astype(bf16)
        for mb in range(16 // heads):
            for i in range(COLS // DV):
                pack[c * (COLS // DV) + i + heads * mb, :, :] = val[
                    mb * count : (mb + 1) * count, i * DV : (i + 1) * DV
                ]

    def window(source):
        return d_o.at[pl.ds(pl.multiple_of(source * count, count), count)]

    own = pltpu.make_async_copy(pack.at[me], window(me), ls.at[5])
    own.start()
    for d in range(1, 16):
        there = (me + d) % 16
        go(remote(pack.at[there], window(me), e1s.at[d], e1r.at[d], there, h))
    scatter.second(2)
    own.wait()
    for d in range(1, 16):
        arrived(window((me + 16 - d) % 16), e1s.at[d], e1r.at[d], me, h)
    scatter.third(3)
    scatter.second(1)
    attend_back_body(got, ratio, den, d_o, d_qk, d_v, q_t, k_t, va, da, dn_t)
    for b in range(16):
        pack2[b, 0 : 2 * F, :] = d_qk[:, b * count : (b + 1) * count].astype(bf16)
        pack2[b, 2 * F :, :] = d_v[b * count : (b + 1) * count, :].astype(bf16)
    own = pltpu.make_async_copy(pack2.at[me], home.at[me], ls.at[5])
    own.start()
    for d in range(1, 16):
        there = (me + d) % 16
        go(remote(pack2.at[there], home.at[me], e2s.at[d], e2r.at[d], there, h))
    scatter.third(2)
    scatter.second(0)
    scatter.third(1)
    scatter.third(0)
    own.wait()
    for d in range(1, 16):
        arrived(home.at[(me + 16 - d) % 16], e2s.at[d], e2r.at[d], me, h)
    scatter.last()
    for copy in late:
        copy.wait_send()


def scatter_room(wide):
    return [
        pltpu.VMEM((4, 2, 128, wide // 2), bf16),
        pltpu.VMEM((4, 2, 128, wide // 2), bf16),
        pltpu.VMEM((4, 128, wide // 2), bf16),
        pltpu.VMEM((4, 128, wide // 2), bf16),
    ]


def back(near, gg, dg, du, hid, t, wo, mid, cot, got, ratio, den):
    mbs, count, wide = cot.shape
    depth = 16 * count
    shape = jax.ShapeDtypeStruct
    cols = 3 * dg.shape[1]
    line = pltpu.VMEM((ZED, count, wide), bf16)
    return pl.pallas_call(
        back_kernel,
        out_shape=(
            shape((ZED, 128, cols), bf16),
            shape(cot.shape, f32),
            shape((mbs * count, wide), bf16),
            shape((16, 2 * F + DV, count), bf16),
        ),
        in_specs=[ANY] * 2 + [VMEM] * 3 + [ANY] * 2 + [VMEM] * 5,
        out_specs=(VMEM,) * 4,
        scratch_shapes=[pltpu.VMEM((ZED, 2, 2, 128, cols), bf16)] + scatter_room(cols) + [
            pltpu.VMEM(cot.shape, bf16), line, line, line,
            pltpu.VMEM(wo.shape, bf16),
            pltpu.VMEM((16, count, DV), bf16),
            pltpu.VMEM((depth, DV), bf16),
            pltpu.VMEM((2 * F, depth), f32),
            pltpu.VMEM((depth, DV), f32),
            pltpu.VMEM((F, depth), bf16),
            pltpu.VMEM((F, depth), bf16),
            pltpu.VMEM((depth, 2 * DV), bf16),
            pltpu.VMEM((depth, 2 * DV), bf16),
            pltpu.VMEM((DV, depth), bf16),
            pltpu.VMEM((16, 2 * F + DV, count), bf16),
            pltpu.VMEM((2, near.shape[0], 512), bf16),
            pltpu.VMEM((2, near.shape[0], 512), bf16),
            pltpu.VMEM((512, near.shape[0]), bf16),
            DMA((6,)), DMA((2, 2)), DMA((4, 5)), DMA((4, 5)), DMA((4, 2)), DMA((4, 2)),
            DMA((16,)), DMA((16,)), DMA((16,)), DMA((16,)),
        ],
        compiler_params=params(),
        name="back",
    )(near, gg, dg, du, hid, t, wo, mid, cot, got, ratio, den)


def end_kernel(
    t, home, xh, d_att, heads_out, wa1, d_mid, xin, mid,
    za, d_in, outputs,
    g, r1x, r1y, r2x, r2y, branch, other, summed, landed, w1, dqk_t, dqkv, part, swap,
    ls, gs, gq, cs, cq, ws, wr,
):
    x, y, z, h = where_am_i()
    me = index_of(z, y, x)
    mbs, count, wide = xin.shape
    heads = 16 // mbs
    qk, vv = 2 * heads * F, heads * DV
    late = []

    def go(copy):
        copy.start()
        late.append(copy)

    combine = Combine(t, branch, other, summed, landed, ls, cs, cq, go)
    scatter = Scatter(
        g,
        lambda d: g.at[(z + d) % ZED, 1 - y, x, :, pl.ds(0, g.shape[-1] // 2)],
        lambda d: g.at[(z + d) % ZED, y, 1 - x, :, pl.ds(g.shape[-1] // 2, g.shape[-1] // 2)],
        lambda d: g.at[(z + d) % ZED, y, x],
        za, r1x, r1y, r2x, r2y, gs, gq, go,
    )
    combine.begin()
    weight = pltpu.make_async_copy(wa1, w1, ls.at[4])
    weight.start()
    for mb in range(mbs):
        cols = slice(mb * count, (mb + 1) * count)
        for k in range(heads):
            block = home.at[k + heads * mb]
            dqk_t[k * F : (k + 1) * F, cols] = block[0:F, :].astype(f32)
            dqk_t[(heads + k) * F : (heads + k + 1) * F, cols] = block[F : 2 * F, :].astype(f32)
            dqkv[cols, qk + k * DV : qk + (k + 1) * DV] = block[2 * F :, :]
    dqkv[:, 0:qk] = jnp.transpose(dqk_t[...]).astype(bf16)
    for n, d in enumerate(FAR):
        zz = (z + d) % ZED
        for yy in range(2):
            for xx in range(2):
                at = pl.ds(pl.multiple_of(index_of(zz, yy, xx) * 128, 128), 128)
                g[zz, yy, xx, :, 0 : qk + vv] = mix(xh[:, at], dqkv[...], ((0,), (0,))).astype(bf16)
                g[zz, yy, xx, :, qk + vv :] = mix(d_att[:, at], heads_out[...], ((0,), (0,))).astype(bf16)
        scatter.first(d)
        if n == 0:
            combine.spread()
    weight.wait()
    for c in range(wide // COLS):
        cols = pl.ds(c * COLS, COLS)
        part[:, c * COLS : (c + 1) * COLS] = mix(dqkv[...], w1[c * COLS : (c + 1) * COLS, :], ((1,), (1,)))
        go(remote(part.at[:, cols], swap.at[:, cols], ws.at[c], wr.at[c], me, 1 - h))
    scatter.second(2)
    for c in range(wide // COLS):
        cols = pl.ds(c * COLS, COLS)
        arrived(swap.at[:, cols], ws.at[c], wr.at[c], me, 1 - h)
    for mb in range(mbs):

        def body(turn, carry):
            row = chunk(turn)
            flat = pl.ds(pl.multiple_of(mb * count + turn * 16, 16), 16)
            v = xin[mb, row, :].astype(f32)
            scale = lax.rsqrt(jnp.mean(v * v, axis=-1, keepdims=True) + epsilon)
            hat = v * scale
            e = part[flat, :] + swap[flat, :]
            d_in[mb, row, :] = (
                d_mid[mb, row, :] + scale * (e - hat * jnp.mean(e * hat, axis=-1, keepdims=True))
            ).astype(bf16)
            return carry

        lax.fori_loop(0, count // 16, body, 0)
    scatter.second(1)
    scatter.third(2)
    scatter.second(3)
    scatter.third(1)
    scatter.second(0)
    scatter.third(3)
    combine.total()
    scatter.third(0)
    combine.done()
    for mb in range(mbs):

        def body(turn, carry):
            row = chunk(turn)
            outputs[mb, row, :] = (mid[mb, row, :] + branch[mb, row, :].astype(f32)).astype(bf16)
            return carry

        lax.fori_loop(0, count // 16, body, 0)
    scatter.last()
    for copy in late:
        copy.wait_send()


def end(t, home, xh, d_att, heads_out, wa1, d_mid, xin, mid):
    mbs, count, wide = xin.shape
    shape = jax.ShapeDtypeStruct
    cols = wa1.shape[1] + heads_out.shape[1]
    line = pltpu.VMEM((ZED, count, wide), bf16)
    return pl.pallas_call(
        end_kernel,
        out_shape=(shape((ZED, 128, cols), bf16), shape(xin.shape, bf16), shape(xin.shape, bf16)),
        in_specs=[ANY] + [VMEM] * 4 + [ANY] + [VMEM] * 3,
        out_specs=(VMEM,) * 3,
        scratch_shapes=[pltpu.VMEM((ZED, 2, 2, 128, cols), bf16)] + scatter_room(cols) + [
            pltpu.VMEM(xin.shape, bf16), line, line, line,
            pltpu.VMEM(wa1.shape, bf16),
            pltpu.VMEM((mbs * count, mbs * count), f32),
            pltpu.VMEM((mbs * count, wa1.shape[1]), bf16),
            pltpu.VMEM((mbs * count, wide), f32),
            pltpu.VMEM((mbs * count, wide), f32),
            DMA((6,)), DMA((4, 5)), DMA((4, 5)), DMA((4, 2)), DMA((4, 2)),
            DMA((wide // COLS,)), DMA((wide // COLS,)),
        ],
        compiler_params=params(),
        name="end",
    )(t, home, xh, d_att, heads_out, wa1, d_mid, xin, mid)


def finish_kernel(
    zm, za, wq, wk, wv, wg, wu, g1, g2, o_q, o_k, o_v, o_out, o_g, o_u, o_d, gains
):
    units = wg.shape[1] // ZED
    room = zm.shape[2] // 3
    nq, nv = wq.shape[1], wv.shape[1]
    lanes = g1.shape[1]

    def fold(prod):
        acc = prod[:, 0:lanes]
        for c in range(1, prod.shape[1] // lanes):
            acc = acc + prod[:, c * lanes : (c + 1) * lanes]
        return acc

    def total(cols):
        acc = za[0, :, cols].astype(f32)
        for n in range(1, ZED):
            acc = acc + za[n, :, cols].astype(f32)
        return acc

    first = jnp.zeros((zm.shape[1], lanes), f32)
    at = 0
    for w, out in ((wq, o_q), (wk, o_k), (wv, o_v)):
        for c in range(w.shape[1] // lanes):
            cols = slice(c * lanes, (c + 1) * lanes)
            value = total(slice(at + c * lanes, at + (c + 1) * lanes))
            out[:, cols] = value * g1[...]
            first = first + value * w[:, cols].astype(f32)
        at += w.shape[1]
    for c in range(nv // lanes):
        o_out[c * lanes : (c + 1) * lanes, :] = jnp.transpose(
            total(slice(at + c * lanes, at + (c + 1) * lanes))
        )
    second = jnp.zeros((zm.shape[1], lanes), f32)
    whole = units // lanes * lanes
    for n in range(ZED):
        for base, w, out in ((0, wg, o_g), (room, wu, o_u)):
            for c in range(0, units, lanes):
                size = min(lanes, units - c)
                cols = slice(n * units + c, n * units + c + size)
                value = zm[n, :, base + c : base + c + size].astype(f32)
                out[:, cols] = value * g2[:, 0:size]
                prod = value * w[:, cols].astype(f32)
                if size == lanes:
                    second = second + prod
                else:
                    second = second + jnp.concatenate(
                        [prod, jnp.zeros((prod.shape[0], lanes - size), f32)], axis=1
                    )
        for c in range(0, units, lanes):
            size = min(lanes, units - c)
            value = jnp.transpose(zm[n, :, 2 * room + c : 2 * room + c + lanes].astype(f32))
            o_d[n * units + c : n * units + c + size, :] = value[0:size, :]
    gains[0:1, :] = jnp.sum(jnp.transpose(first), axis=0, keepdims=True)
    gains[1:2, :] = jnp.sum(jnp.transpose(second), axis=0, keepdims=True)


def finish(zm, za, wq, wk, wv, wg, wu, g1, g2, w_out, w_down):
    shape = lambda w: jax.ShapeDtypeStruct(w.shape, f32)
    return pl.pallas_call(
        finish_kernel,
        out_shape=(
            shape(wq), shape(wk), shape(wv), shape(w_out), shape(wg), shape(wu), shape(w_down),
            jax.ShapeDtypeStruct((2, 128), f32),
        ),
        in_specs=[VMEM] * 9,
        out_specs=(VMEM,) * 8,
        compiler_params=pltpu.CompilerParams(vmem_limit_bytes=VMEM_LIMIT),
        name="finish",
    )(zm, za, wq, wk, wv, wg, wu, g1, g2)


def fast(
    inputs, norm_gain1, w_query, w_key, w_value, w_out, norm_gain2, w_gate, w_up, w_down, cotangent
):
    mbs, count, wide = inputs.shape
    heads = w_query.shape[1] // F
    units = w_gate.shape[1] // ZED
    room = -(-units // 128) * 128
    qk, vv = 2 * heads * F, heads * DV
    rows = w_query.shape[0]
    gain1, gain2 = norm_gain1.astype(f32)[:, None], norm_gain2.astype(f32)[:, None]

    def folded(weight, gain):
        return (weight.astype(f32) * gain).astype(bf16)

    a1 = jnp.concatenate([folded(w_query, gain1), folded(w_key, gain1), folded(w_value, gain1)], axis=1)

    def cut(weight):
        pieces = jnp.transpose(weight.reshape(rows, ZED, units), (1, 0, 2))
        return jnp.pad(pieces, ((0, 0), (0, 0), (0, room - units)))

    m = jnp.concatenate([cut(folded(w_gate, gain2)), cut(folded(w_up, gain2)), cut(w_down.T)], axis=2)
    stream = inputs.astype(f32).reshape(mbs * count, wide)
    r1 = lax.rsqrt(jnp.mean(stream * stream, axis=-1, keepdims=True) + epsilon)
    xh1 = (stream * r1).astype(bf16)
    wa1, w_o, wm, gg, got, ratio, den, heads_out, middle, near = front(
        a1, w_out.T, m, cotangent, xh1, inputs
    )
    w_g, w_u, w_d = wm[:, :room], wm[:, room : 2 * room], wm[:, 2 * room :]
    many = ZED * mbs * count
    n2 = near.reshape(many, wide)
    up_g = gg.reshape(many, wide)
    gate = mix(n2, w_g, ((1,), (0,)))
    up = mix(n2, w_u, ((1,), (0,)))
    d_hidden = mix(up_g, w_d, ((1,), (0,)))
    sig = jax.nn.sigmoid(gate)
    silu = gate * sig
    hidden = (silu * up).astype(bf16)
    d_gate = (d_hidden * up * sig * (1.0 + gate * (1.0 - sig))).astype(bf16)
    d_up = (d_hidden * silu).astype(bf16)
    branch = mix(hidden, w_d, ((1,), (1,))).astype(bf16)
    d_n2 = (mix(d_gate, w_g, ((1,), (1,))) + mix(d_up, w_u, ((1,), (1,)))).astype(bf16)
    lines = (ZED, mbs, count, wide)
    zm, d_mid, d_att, home = back(
        n2, up_g, d_gate, d_up, hidden, d_n2.reshape(lines), w_o, middle, cotangent, got, ratio, den
    )
    za, input_grad, outputs = end(
        branch.reshape(lines), home, xh1, d_att, heads_out, wa1, d_mid, inputs, middle
    )
    full = (rows, 128)
    o_q, o_k, o_v, o_out, o_g, o_u, o_d, gains = finish(
        zm, za, w_query, w_key, w_value, w_gate, w_up,
        jnp.broadcast_to(gain1, full), jnp.broadcast_to(gain2, full), w_out, w_down,
    )
    gains = lax.psum(gains, "head")
    return (outputs, input_grad, gains[0], o_q, o_k, o_v, o_out, gains[1], o_g, o_u, o_d)


def solution(mesh):
    return jax.shard_map(
        fast if mesh.shape["seq"] == 16 else local,
        mesh=mesh,
        in_specs=(
            P(None, "seq", None),
            P("seq"),
            P("seq", "head"),
            P("seq", "head"),
            P("seq", "head"),
            P("head", "seq"),
            P("seq"),
            P("seq", "head"),
            P("seq", "head"),
            P("head", "seq"),
            P(None, "seq", None),
        ),
        out_specs=(
            P(None, "seq", None),
            P(None, "seq", None),
            P("seq"),
            P("seq", "head"),
            P("seq", "head"),
            P("seq", "head"),
            P("head", "seq"),
            P("seq"),
            P("seq", "head"),
            P("seq", "head"),
            P("head", "seq"),
        ),
        check_vma=False,
    )
```

```python
import jax
import jax.numpy as jnp
from jax import lax
from jax.experimental import pallas as pl
from jax.experimental.pallas import tpu as pltpu
from jax.sharding import PartitionSpec as P

F = 16
DV = 128


epsilon = 1e-05
highest = lax.Precision.HIGHEST


def entering(part, axis, combine, identity, reverse):
    count = lax.axis_size(axis)
    place = lax.axis_index(axis)
    ahead = count - 1 - place if reverse else place
    gathered = jax.tree.map(lambda a: lax.all_gather(a, axis), part)
    state = jax.tree.map(lambda a, e: jnp.zeros_like(a) + jnp.asarray(e, a.dtype), part, identity)

    def one(turn, state):
        source = count - 1 - turn if reverse else turn
        return combine(
            state, jax.tree.map(lambda a: lax.dynamic_index_in_dim(a, source, 0, False), gathered)
        )

    return lax.fori_loop(0, ahead, one, state)


def rms_apply(values, gain):
    scale = lax.rsqrt(jnp.mean(values * values, axis=-1, keepdims=True) + epsilon)
    return values * scale * gain


def feature_map(projected):
    count = projected.shape[0]
    pieces = projected.reshape(count, -1, F)
    square = (pieces[:, :, :, None] * pieces[:, :, None, :]).reshape(count, pieces.shape[1], F * F)
    return jnp.concatenate(
        [jnp.ones_like(pieces[:, :, :1]), pieces * F ** (-0.25), square * (2.0 * F) ** (-0.5)],
        axis=-1,
    )


def swiglu(gate, up_part):
    return jax.nn.silu(gate) * up_part


def round_trip(values):
    return lax.optimization_barrier(values.astype(jnp.bfloat16)).astype(jnp.float32)


def add_pair(earlier, later):
    return (earlier[0] + later[0], earlier[1] + later[1])


def block_pass(tokens, upstream, gathered):
    gain_one, query_w, key_w, value_w, out_w, gain_two, gate_w, up_w, down_w = gathered
    f32 = jnp.float32
    bf16 = jnp.bfloat16
    stream = tokens.astype(f32)
    count = stream.shape[0]
    normed_f, norm_one_pull = jax.vjp(rms_apply, stream, gain_one.astype(f32))
    normed = normed_f.astype(bf16)
    queries = jnp.dot(normed, query_w, preferred_element_type=f32)
    keys_all = jnp.dot(normed, key_w, preferred_element_type=f32)
    values = jnp.dot(normed, value_w, preferred_element_type=f32).astype(bf16)
    query_feat_f, query_pull = jax.vjp(feature_map, queries)
    key_feat_f, key_pull = jax.vjp(feature_map, keys_all)
    query_feat = jnp.transpose(query_feat_f.astype(bf16), (1, 0, 2))
    key_feat = jnp.transpose(key_feat_f.astype(bf16), (1, 0, 2))
    value_heads = jnp.transpose(values.reshape(count, -1, DV), (1, 0, 2))
    causal = (jnp.arange(count)[:, None] >= jnp.arange(count)[None, :]).astype(f32)
    scores = jnp.einsum("htf,hsf->hts", query_feat, key_feat, preferred_element_type=f32) * causal
    weighted = scores.astype(bf16)
    num_local = jnp.einsum("hts,hsd->htd", weighted, value_heads, preferred_element_type=f32)
    den_local = jnp.sum(weighted.astype(f32), axis=-1)
    states = jnp.einsum("hsf,hsd->hfd", key_feat, value_heads, preferred_element_type=f32)
    totals = jnp.sum(key_feat.astype(f32), axis=1)
    state_before, total_before = entering(
        (states, totals), "seq", add_pair, (jnp.zeros_like(states), jnp.zeros_like(totals)), False
    )
    query_wide = query_feat.astype(f32)
    numer = num_local + jnp.einsum("htf,hfd->htd", query_wide, state_before, precision=highest)
    denom = den_local + jnp.einsum("htf,hf->ht", query_wide, total_before, precision=highest)
    ratio = numer / denom[..., None]
    heads_out = jnp.transpose(ratio, (1, 0, 2)).reshape(count, -1).astype(bf16)
    attended = lax.psum(jnp.dot(heads_out, out_w, preferred_element_type=f32), "head")
    middle = stream + attended
    normed_two_f, norm_two_pull = jax.vjp(rms_apply, middle, gain_two.astype(f32))
    normed_two = normed_two_f.astype(bf16)
    gate = jnp.dot(normed_two, gate_w, preferred_element_type=f32)
    up_part = jnp.dot(normed_two, up_w, preferred_element_type=f32)
    active, active_pull = jax.vjp(swiglu, gate, up_part)
    hidden = active.astype(bf16)
    branch = lax.psum(
        jnp.dot(hidden, down_w, preferred_element_type=f32).astype(jnp.bfloat16), "head"
    ).astype(jnp.float32)
    result = (middle + branch).astype(bf16)
    grad_down = jnp.dot(hidden.T, upstream, preferred_element_type=f32)
    d_hidden = jnp.dot(upstream, down_w.T, preferred_element_type=f32)
    d_gate_f, d_up_f = active_pull(d_hidden)
    d_gate = d_gate_f.astype(bf16)
    d_up = d_up_f.astype(bf16)
    grad_gate = jnp.dot(normed_two.T, d_gate, preferred_element_type=f32)
    grad_up = jnp.dot(normed_two.T, d_up, preferred_element_type=f32)
    d_normed_two = lax.psum(
        jnp.dot(d_gate, gate_w.T, preferred_element_type=f32)
        + jnp.dot(d_up, up_w.T, preferred_element_type=f32),
        "head",
    )
    d_middle_norm, grad_gain2 = norm_two_pull(d_normed_two)
    d_middle = upstream.astype(f32) + d_middle_norm
    d_attended = d_middle.astype(bf16)
    grad_out = jnp.dot(heads_out.T, d_attended, preferred_element_type=f32)
    d_heads = jnp.transpose(
        jnp.dot(d_attended, out_w.T, preferred_element_type=f32).reshape(count, -1, DV), (1, 0, 2)
    )
    d_numer = (d_heads / denom[..., None]).astype(bf16)
    d_denom = -jnp.sum(d_heads * ratio, axis=-1) / denom
    d_numer_wide = d_numer.astype(f32)
    d_before = jnp.einsum("htf,htd->hfd", query_wide, d_numer_wide, precision=highest)
    d_total_before = jnp.einsum("htf,ht->hf", query_wide, d_denom, precision=highest)
    d_state, d_total = entering(
        (d_before, d_total_before),
        "seq",
        add_pair,
        (jnp.zeros_like(d_before), jnp.zeros_like(d_total_before)),
        True,
    )
    d_scores = (
        (
            jnp.einsum("htd,hsd->hts", d_numer, value_heads, preferred_element_type=f32)
            + d_denom[..., None]
        )
        * causal
    ).astype(bf16)
    d_values = jnp.einsum(
        "hts,htd->hsd", weighted, d_numer, preferred_element_type=f32
    ) + jnp.einsum("hsf,hfd->hsd", key_feat.astype(f32), d_state, precision=highest)
    d_query_feat = (
        jnp.einsum("hts,hsf->htf", d_scores, key_feat, preferred_element_type=f32)
        + jnp.einsum("htd,hfd->htf", d_numer_wide, state_before, precision=highest)
        + d_denom[..., None] * total_before[:, None, :]
    )
    d_key_feat = (
        jnp.einsum("hts,htf->hsf", d_scores, query_feat, preferred_element_type=f32)
        + jnp.einsum("hsd,hfd->hsf", value_heads.astype(f32), d_state, precision=highest)
        + d_total[:, None, :]
    )
    d_queries = query_pull(jnp.transpose(round_trip(d_query_feat), (1, 0, 2)))[0].astype(bf16)
    d_keys = key_pull(jnp.transpose(round_trip(d_key_feat), (1, 0, 2)))[0].astype(bf16)
    d_values_flat = jnp.transpose(d_values, (1, 0, 2)).reshape(count, -1).astype(bf16)
    grad_query = jnp.dot(normed.T, d_queries, preferred_element_type=f32)
    grad_key = jnp.dot(normed.T, d_keys, preferred_element_type=f32)
    grad_value = jnp.dot(normed.T, d_values_flat, preferred_element_type=f32)
    d_normed_part = (
        jnp.dot(d_queries, query_w.T, preferred_element_type=f32)
        + jnp.dot(d_keys, key_w.T, preferred_element_type=f32)
        + jnp.dot(d_values_flat, value_w.T, preferred_element_type=f32)
    )
    d_normed = lax.psum(d_normed_part.astype(jnp.bfloat16), "head").astype(jnp.float32)
    d_stream_norm, grad_gain1 = norm_one_pull(d_normed)
    input_grad = (d_middle + d_stream_norm).astype(bf16)
    return (
        result,
        input_grad,
        grad_gain1,
        grad_query,
        grad_key,
        grad_value,
        grad_out,
        grad_gain2,
        grad_gate,
        grad_up,
        grad_down,
    )


def local(
    inputs, norm_gain1, w_query, w_key, w_value, w_out, norm_gain2, w_gate, w_up, w_down, cotangent
):
    micro = inputs.shape[0]
    summed = None
    results = []
    input_grads = []
    for step_index in range(micro):
        gathered = (
            lax.all_gather(norm_gain1, "seq", axis=0, tiled=True),
            lax.all_gather(w_query, "seq", axis=0, tiled=True),
            lax.all_gather(w_key, "seq", axis=0, tiled=True),
            lax.all_gather(w_value, "seq", axis=0, tiled=True),
            lax.all_gather(w_out, "seq", axis=1, tiled=True),
            lax.all_gather(norm_gain2, "seq", axis=0, tiled=True),
            lax.all_gather(w_gate, "seq", axis=0, tiled=True),
            lax.all_gather(w_up, "seq", axis=0, tiled=True),
            lax.all_gather(w_down, "seq", axis=1, tiled=True),
        )
        (
            result,
            input_grad,
            grad_gain1,
            grad_query,
            grad_key,
            grad_value,
            grad_out,
            grad_gain2,
            grad_gate,
            grad_up,
            grad_down,
        ) = block_pass(inputs[step_index], cotangent[step_index], gathered)
        results.append(result)
        input_grads.append(input_grad)
        fresh = (
            lax.psum_scatter(grad_gain1, "seq", scatter_dimension=0, tiled=True),
            lax.psum_scatter(grad_query, "seq", scatter_dimension=0, tiled=True),
            lax.psum_scatter(grad_key, "seq", scatter_dimension=0, tiled=True),
            lax.psum_scatter(grad_value, "seq", scatter_dimension=0, tiled=True),
            lax.psum_scatter(grad_out, "seq", scatter_dimension=1, tiled=True),
            lax.psum_scatter(grad_gain2, "seq", scatter_dimension=0, tiled=True),
            lax.psum_scatter(grad_gate, "seq", scatter_dimension=0, tiled=True),
            lax.psum_scatter(grad_up, "seq", scatter_dimension=0, tiled=True),
            lax.psum_scatter(grad_down, "seq", scatter_dimension=1, tiled=True),
        )
        summed = (
            fresh
            if summed is None
            else tuple((older + newer for older, newer in zip(summed, fresh)))
        )
    return (
        jnp.stack(results),
        jnp.stack(input_grads),
        summed[0],
        summed[1],
        summed[2],
        summed[3],
        summed[4],
        summed[5],
        summed[6],
        summed[7],
        summed[8],
    )


MESH = pl.DeviceIdType.MESH
bf16 = jnp.bfloat16
f32 = jnp.float32
ZED = 4
VMEM_LIMIT = 60 * 1024 * 1024


def where_am_i():
    place = lax.axis_index("seq")
    return place % 2, (place // 2) % 2, place // 4, lax.axis_index("head")


def index_of(z, y, x):
    return (z * 2 + y) * 2 + x


def remote(src, dst, send, recv, place, head):
    return pltpu.make_async_remote_copy(
        src_ref=src, dst_ref=dst, send_sem=send, recv_sem=recv, device_id=(place, head),
        device_id_type=MESH,
    )


def arrived(dst, send, recv, place, head):
    remote(dst, dst, send, recv, place, head).wait_recv()


def params():
    return pltpu.CompilerParams(has_side_effects=True, vmem_limit_bytes=VMEM_LIMIT)


ANY = pl.BlockSpec(memory_space=pl.ANY)
VMEM = pl.BlockSpec(memory_space=pltpu.VMEM)
DMA = pltpu.SemaphoreType.DMA
ORDER = (0, 1, 3, 2)


def mix(a, b, over):
    return lax.dot_general(a, b, (over, ((), ())), preferred_element_type=f32)


CHUNK = 512
COLS = 256


def spread(got, q_t, k_t, va):
    count = got.shape[2]
    for b in range(got.shape[0]):
        q_t[:, b * count : (b + 1) * count] = got[b, 0:F, :]
        k_t[:, b * count : (b + 1) * count] = got[b, F : 2 * F, :]
        va[b * count : (b + 1) * count, 0:DV] = got[b, 2 * F :, :]
    va[:, DV:] = jnp.ones((va.shape[0], va.shape[1] - DV), bf16)


def lower(count):
    return lax.broadcasted_iota(jnp.int32, (count, count), 0) >= lax.broadcasted_iota(
        jnp.int32, (count, count), 1
    )


def attend_rows(qi, q_t, k_t, va, ratio, den, causal):
    qs = slice(qi * CHUNK, (qi + 1) * CHUNK)
    acc = jnp.zeros((CHUNK, va.shape[1]), f32)
    for kj in range(qi + 1):
        ks = slice(kj * CHUNK, (kj + 1) * CHUNK)
        s = mix(q_t[:, qs], k_t[:, ks], ((0,), (0,)))
        p = 1.0 + s * (0.25 + s * (1.0 / 32.0))
        if kj == qi:
            p = jnp.where(causal, p, 0.0)
        acc = acc + mix(p.astype(bf16), va[ks, :], ((1,), (0,)))
    ratio[qs, :] = acc[:, :DV] / acc[:, DV:]
    den[qs, :] = acc[:, DV:]


def column(gain):
    count = gain.shape[1]
    return jnp.transpose(jnp.broadcast_to(gain[...].astype(f32), (count, count)))


def front_kernel(
    wq, wk, wv, w_out, wg, wu, wd, g1, g2, cot, xin,
    wa1, wa2, wm, gg, got, ratio, den, heads_out, middle, near, xh,
    a1, a2, m, w1, w2, pack, q_t, k_t, va, ob, part, other,
    ls, zs, zr, us, ur, ps, pr, e1s, e1r, e2s, e2r, ws, wr, ds, dr,
):
    x, y, z, h = where_am_i()
    me = index_of(z, y, x)
    at_x, at_y = index_of(z, y, 1 - x), index_of(z, 1 - y, x)
    count = xin.shape[1]
    heads = 16 // xin.shape[0]
    late = []

    def when(true, do):
        if true is None:
            do()
        else:
            pl.when(true)(do)

    def go(copy, true=None):
        when(true, copy.start)
        late.append((true, copy))

    def rows(zz, yy, xx):
        return pl.ds(pl.multiple_of(index_of(zz, yy, xx) * 128, 128), 128)

    mine = rows(z, y, x)
    kept = [
        pltpu.make_async_copy(a1, w1.at[mine], ls.at[0]),
        pltpu.make_async_copy(a2, w2.at[mine], ls.at[1]),
        pltpu.make_async_copy(m.at[z], wm.at[mine], ls.at[2]),
        pltpu.make_async_copy(cot, gg.at[z], ls.at[6]),
    ]
    lanes = g1.shape[1]
    scale = column(g1)
    at = 0
    for w in (wq, wk, wv):
        for c in range(0, w.shape[1], lanes):
            a1[:, at + c : at + c + lanes] = (w[:, c : c + lanes].astype(f32) * scale).astype(bf16)
        at += w.shape[1]
    kept[0].start()
    kept[3].start()
    dest = (w1, w2, wm)
    UP, DOWN = 0, 1
    COT, NEAR = 2, 3

    def held(kind, zz):
        return (lambda: w1.at[rows(zz, y, x)], lambda: w2.at[rows(zz, y, x)],
                lambda: gg.at[zz, h], lambda: near.at[zz, h])[kind]()

    def origin(way, step):
        return (z + ZED - step) % ZED if way == UP else (z + step) % ZED

    def valid(way, step):
        return z >= step if way == UP else z <= ZED - 1 - step

    def pass_on(kind, way, step, src, true):
        there = index_of((z + 1) % ZED if way == UP else (z + ZED - 1) % ZED, y, x)
        block = held(kind, origin(way, step))
        go(remote(block if src is None else src, block, us.at[kind, way, step], ur.at[kind, way, step + 1], there, h), true)

    def offer(kind, src=None):
        pass_on(kind, UP, 0, src, z < ZED - 1)
        pass_on(kind, DOWN, 0, src, z > 0)

    def hop(kind, way, step):
        block = held(kind, origin(way, step))
        when(
            valid(way, step),
            lambda: arrived(block, us.at[kind, way, step], ur.at[kind, way, step], me, h),
        )
        if step < ZED - 1:
            more = z < ZED - 1 if way == UP else z > 0
            pass_on(kind, way, step, None, valid(way, step) & more)

    def across(kind, way, step):
        zz = origin(way, step)
        block = held(kind, zz)
        go(remote(block, block, ds.at[kind, way, step], dr.at[kind, way, step], me, 1 - h), valid(way, step))

    def across_done(kind, way, step):
        zz = origin(way, step)
        block = (gg if kind == COT else near).at[zz, 1 - h]
        when(
            valid(way, step),
            lambda: arrived(block, ds.at[kind, way, step], dr.at[kind, way, step], me, 1 - h),
        )

    def both(do, kind, step):
        do(kind, UP, step)
        do(kind, DOWN, step)

    partner = (z, z + 1 - 2 * (z % 2), ZED - 1 - z, (z + 2) % ZED)

    inner = (z > 0) & (z < ZED - 1)
    outer = (z == 0) | (z == ZED - 1)

    def line(d, true=None):
        zz = partner[d]
        copy = remote(m.at[zz], wm.at[mine], zs.at[d], zr.at[d], index_of(zz, y, x), h)
        go(copy, true)

    def slot_of(way, step):
        return step if way == UP else 3 + step if step else 0

    def plane_set(kind, slot, zz, true):
        block = dest[kind].at[rows(zz, y, x)]
        go(remote(block, block, ps.at[kind, slot, 0], pr.at[kind, slot, 0], at_x, h), true)
        go(remote(block, block, ps.at[kind, slot, 1], pr.at[kind, slot, 1], at_y, h), true)

    def onward_set(kind, slot, zz, true):
        w = dest[kind]
        half = w.shape[1] // 2
        from_x, from_y = rows(zz, y, 1 - x), rows(zz, 1 - y, x)

        def wait():
            arrived(w.at[from_x], ps.at[kind, slot, 0], pr.at[kind, slot, 0], me, h)
            arrived(w.at[from_y], ps.at[kind, slot, 1], pr.at[kind, slot, 1], me, h)

        when(true, wait)
        left = w.at[from_y, pl.ds(0, half)]
        right = w.at[from_x, pl.ds(half, half)]
        go(remote(left, left, ps.at[kind, slot, 2], pr.at[kind, slot, 2], at_x, h), true)
        go(remote(right, right, ps.at[kind, slot, 3], pr.at[kind, slot, 3], at_y, h), true)

    def corner_set(kind, slot, zz, true):
        w = dest[kind]
        half = w.shape[1] // 2
        far = rows(zz, 1 - y, 1 - x)

        def wait():
            arrived(w.at[far, pl.ds(0, half)], ps.at[kind, slot, 2], pr.at[kind, slot, 2], me, h)
            arrived(w.at[far, pl.ds(half, half)], ps.at[kind, slot, 3], pr.at[kind, slot, 3], me, h)

        when(true, wait)

    def plane(kind, way, step):
        if step == 0:
            kept[kind].wait()
        plane_set(kind, slot_of(way, step), origin(way, step), valid(way, step) if step else None)

    def onward(kind, way, step):
        onward_set(kind, slot_of(way, step), origin(way, step), valid(way, step) if step else None)

    def corner(kind):
        corner_set(kind, 0, z, None)
        for step in (1, 2, 3):
            for way in (UP, DOWN):
                corner_set(kind, slot_of(way, step), origin(way, step), valid(way, step))

    def m_plane(d):
        zz = partner[d]
        if d:
            arrived(wm.at[rows(zz, y, x)], zs.at[d], zr.at[d], me, h)
        else:
            kept[2].wait()
        plane_set(2, d, zz, None)

    def m_onward(d):
        onward_set(2, d, partner[d], None)

    offer(0, a1)
    plane(0, UP, 0)
    for c in range(0, w_out.shape[0], lanes):
        a2[:, c : c + lanes] = jnp.transpose(w_out[c : c + lanes, :].astype(f32)).astype(bf16)
    kept[1].start()
    for way in (UP, DOWN):
        hop(0, way, 1)
        plane(0, way, 1)
    units = wg.shape[1] // ZED
    room = m.shape[2] // 3
    scale = column(g2)
    for n in range(ZED):
        for part_at, w in ((0, wg), (room, wu)):
            for c in range(0, units, lanes):
                size = min(lanes, units - c)
                m[n, :, part_at + c : part_at + c + size] = (
                    w[:, n * units + c : n * units + c + size].astype(f32) * scale[:, 0:size]
                ).astype(bf16)
        for c in range(0, units, lanes):
            size = min(lanes, units - c)
            m[n, :, 2 * room + c : 2 * room + c + size] = jnp.transpose(
                wd[n * units + c : n * units + c + size, :].astype(f32)
            ).astype(bf16)
        for part_at in (0, room, 2 * room):
            m[n, :, part_at + units : part_at + room] = jnp.zeros((lanes, room - units), bf16)
    kept[2].start()
    onward(0, UP, 0)
    for way in (UP, DOWN):
        hop(0, way, 2)
        plane(0, way, 2)
    offer(1, a2)
    both(onward, 0, 1)
    for way in (UP, DOWN):
        hop(0, way, 3)
        plane(0, way, 3)
    both(onward, 0, 2)
    both(hop, 1, 1)
    plane(1, UP, 0)
    for mb in range(xin.shape[0]):

        def normed(turn, carry):
            row = pl.ds(pl.multiple_of(turn * 16, 16), 16)
            v = xin[mb, row, :].astype(f32)
            r = lax.rsqrt(jnp.mean(v * v, axis=-1, keepdims=True) + epsilon)
            xh[pl.ds(pl.multiple_of(mb * count + turn * 16, 16), 16), :] = (v * r).astype(bf16)
            return carry

        lax.fori_loop(0, count // 16, normed, 0)
    both(onward, 0, 3)
    both(hop, 1, 2)
    both(hop, 1, 3)
    line(1)
    line(2, inner)
    corner(0)
    out1 = pltpu.make_async_copy(w1, wa1, ls.at[3])
    out1.start()
    kq = mix(xh[...], w1[:, 0 : 2 * heads * F], ((1,), (0,)))
    qk = jnp.transpose(kq).astype(bf16)
    for mb in range(16 // heads):
        for k in range(heads):
            t = k + heads * mb
            cols = slice(mb * count, (mb + 1) * count)
            pack[t, 0:F, :] = qk[k * F : (k + 1) * F, cols]
            pack[t, F : 2 * F, :] = qk[(heads + k) * F : (heads + k + 1) * F, cols]
    for c in range(heads * DV // COLS):
        at = 2 * heads * F + c * COLS
        val = mix(xh[...], w1[:, at : at + COLS], ((1,), (0,))).astype(bf16)
        for mb in range(16 // heads):
            for i in range(COLS // DV):
                t = c * (COLS // DV) + i + heads * mb
                pack[t, 2 * F :, :] = val[mb * count : (mb + 1) * count, i * DV : (i + 1) * DV]
    keep = pltpu.make_async_copy(pack.at[me], got.at[me], ls.at[4])
    keep.start()
    for d in range(1, 16):
        there = (me + d) % 16
        go(remote(pack.at[there], got.at[me], e1s.at[d], e1r.at[d], there, h))
    line(2, outer)
    line(3, inner)
    both(plane, 1, 1)
    onward(1, UP, 0)
    both(plane, 1, 2)
    both(onward, 1, 1)
    both(plane, 1, 3)
    both(onward, 1, 2)
    keep.wait()
    for d in range(1, 16):
        arrived(got.at[(me + 16 - d) % 16], e1s.at[d], e1r.at[d], me, h)
    both(onward, 1, 3)
    spread(got, q_t, k_t, va)
    causal = lower(CHUNK)
    for qi in range(va.shape[0] // CHUNK):
        attend_rows(qi, q_t, k_t, va, ratio, den, causal)
    for b in range(16):
        ob[b, :, :] = ratio[b * count : (b + 1) * count, :].astype(bf16)

    def window(source):
        return heads_out.at[
            pl.ds(pl.multiple_of((source // heads) * count, count), count),
            pl.ds(pl.multiple_of((source % heads) * DV, DV), DV),
        ]

    keep = pltpu.make_async_copy(ob.at[me], window(me), ls.at[4])
    keep.start()
    for d in range(1, 16):
        there = (me + d) % 16
        go(remote(ob.at[there], window(me), e2s.at[d], e2r.at[d], there, h))
    line(3, outer)
    offer(COT, cot.at[h])
    m_plane(0)
    m_plane(1)
    corner(1)
    out2 = pltpu.make_async_copy(w2, wa2, ls.at[5])
    out2.start()
    keep.wait()
    for d in range(1, 16):
        arrived(window((me + 16 - d) % 16), e2s.at[d], e2r.at[d], me, h)
    wide = part.shape[1]
    for c in range(wide // COLS):
        cols = pl.ds(c * COLS, COLS)
        part[:, c * COLS : (c + 1) * COLS] = mix(
            heads_out[...], w2[c * COLS : (c + 1) * COLS, :], ((1,), (1,))
        )
        go(remote(part.at[:, cols], other.at[:, cols], ws.at[c], wr.at[c], me, 1 - h))
    m_onward(0)
    both(hop, COT, 1)
    m_plane(2)
    for c in range(wide // COLS):
        cols = pl.ds(c * COLS, COLS)
        arrived(other.at[:, cols], ws.at[c], wr.at[c], me, 1 - h)

    def one(mb):
        def body(turn, carry):
            row = pl.ds(pl.multiple_of(turn * 16, 16), 16)
            flat = pl.ds(pl.multiple_of(mb * count + turn * 16, 16), 16)
            mid = xin[mb, row, :].astype(f32) + (part[flat, :] + other[flat, :])
            middle[mb, row, :] = mid
            scale = lax.rsqrt(jnp.mean(mid * mid, axis=-1, keepdims=True) + epsilon)
            near[z, mb, row, :] = (mid * scale).astype(bf16)
            return carry

        lax.fori_loop(0, count // 16, body, 0)

    one(h)
    offer(NEAR)
    one(1 - h)
    m_onward(1)
    both(hop, COT, 2)
    m_plane(3)
    kept[3].wait()
    both(across, COT, 1)
    both(across, COT, 2)
    both(hop, NEAR, 1)
    both(across, NEAR, 1)
    m_onward(2)
    both(hop, COT, 3)
    both(across, COT, 3)
    both(hop, NEAR, 2)
    both(across, NEAR, 2)
    m_onward(3)
    both(hop, NEAR, 3)
    both(across, NEAR, 3)
    for d in range(4):
        corner_set(2, d, partner[d], None)
    for kind in (NEAR, COT):
        for step in (1, 2, 3):
            both(across_done, kind, step)
    out1.wait()
    out2.wait()
    for true, copy in late:
        when(true, copy.wait_send)


def front(wq, wk, wv, w_out, wg, wu, wd, g1, g2, cot, xin):
    mbs, count, wide = xin.shape
    depth = 16 * count
    wide1, wide2 = wq.shape[1] + wk.shape[1] + wv.shape[1], w_out.shape[0]
    wide3 = 3 * (-(-wg.shape[1] // ZED // 256) * 256)
    shape = jax.ShapeDtypeStruct
    return pl.pallas_call(
        front_kernel,
        out_shape=(
            shape((wide, wide1), bf16),
            shape((wide, wide2), bf16),
            shape((wide, wide3), bf16),
            shape((ZED,) + cot.shape, bf16),
            shape((16, 2 * F + DV, count), bf16),
            shape((depth, DV), f32),
            shape((depth, DV), f32),
            shape((mbs * count, wide2), bf16),
            shape(xin.shape, f32),
            shape((ZED,) + xin.shape, bf16),
            shape((mbs * count, wide), bf16),
        ),
        in_specs=[VMEM] * 9 + [ANY] + [VMEM],
        out_specs=(ANY,) * 4 + (VMEM,) * 7,
        scratch_shapes=[
            pltpu.VMEM((wq.shape[0], wide1), bf16),
            pltpu.VMEM((wq.shape[0], wide2), bf16),
            pltpu.VMEM((ZED, wq.shape[0], wide3), bf16),
            pltpu.VMEM((wide, wide1), bf16),
            pltpu.VMEM((wide, wide2), bf16),
            pltpu.VMEM((16, 2 * F + DV, count), bf16),
            pltpu.VMEM((F, depth), bf16),
            pltpu.VMEM((F, depth), bf16),
            pltpu.VMEM((depth, 2 * DV), bf16),
            pltpu.VMEM((16, count, DV), bf16),
            pltpu.VMEM((mbs * count, wide), f32),
            pltpu.VMEM((mbs * count, wide), f32),
            DMA((7,)), DMA((4,)), DMA((4,)), DMA((4, 2, 4)), DMA((4, 2, 4)), DMA((3, 7, 4)), DMA((3, 7, 4)),
            DMA((16,)), DMA((16,)), DMA((16,)), DMA((16,)),
            DMA((wide // COLS,)), DMA((wide // COLS,)), DMA((4, 2, 4)), DMA((4, 2, 4)),
        ],
        compiler_params=params(),
        name="front",
    )(wq, wk, wv, w_out, wg, wu, wd, g1, g2, cot, xin)


def attend_back_body(got, ratio, den, d_o, d_qk, d_v, q_t, k_t, va, da, dn_t):
    spread(got, q_t, k_t, va)
    depth = va.shape[0]
    lane = lax.broadcasted_iota(jnp.int32, (CHUNK, DV), 1)
    for qi in range(depth // CHUNK):
        qs = slice(qi * CHUNK, (qi + 1) * CHUNK)
        dn = d_o[qs, :].astype(f32) / den[qs, :]
        dd = -jnp.sum(dn * ratio[qs, :], axis=-1, keepdims=True)
        big = dd.astype(bf16).astype(f32)
        da[qs, 0:DV] = dn.astype(bf16)
        da[qs, DV:] = jnp.where(lane == 0, big, jnp.where(lane == 1, dd - big, 0.0)).astype(bf16)
        dn_t[:, qs] = jnp.transpose(dn).astype(bf16)
    causal = lower(CHUNK)
    for kj in range(depth // CHUNK):
        ks = slice(kj * CHUNK, (kj + 1) * CHUNK)
        acc_k = jnp.zeros((F, CHUNK), f32)
        acc_v = jnp.zeros((DV, CHUNK), f32)
        for qi in range(kj, depth // CHUNK):
            qs = slice(qi * CHUNK, (qi + 1) * CHUNK)
            s = mix(q_t[:, qs], k_t[:, ks], ((0,), (0,)))
            p = 1.0 + s * (0.25 + s * (1.0 / 32.0))
            d_s = mix(da[qs, :], va[ks, :], ((1,), (1,))) * (0.25 + s * (1.0 / 16.0))
            if kj == qi:
                p = jnp.where(causal, p, 0.0)
                d_s = jnp.where(causal, d_s, 0.0)
            d_s = d_s.astype(bf16)
            acc_v = acc_v + mix(dn_t[:, qs], p.astype(bf16), ((1,), (0,)))
            acc_k = acc_k + mix(q_t[:, qs], d_s, ((1,), (0,)))
            d_q = mix(k_t[:, ks], d_s, ((1,), (1,)))
            d_qk[0:F, qs] = d_q if kj == 0 else d_qk[0:F, qs] + d_q
        d_qk[F : 2 * F, ks] = acc_k
        d_v[ks, :] = jnp.transpose(acc_v)


FAR = (2, 1, 3, 0)


def chunk(turn):
    return pl.ds(pl.multiple_of(turn * 16, 16), 16)


class Scatter:
    def __init__(self, g, low_acc, high_acc, fin, out, r1x, r1y, r2x, r2y, s, q, go):
        self.g, self.low_acc, self.high_acc, self.fin, self.out = g, low_acc, high_acc, fin, out
        self.r1x, self.r1y, self.r2x, self.r2y, self.s, self.q = r1x, r1y, r2x, r2y, s, q
        self.go = go
        self.x, self.y, self.z, self.h = where_am_i()
        self.me = index_of(self.z, self.y, self.x)
        self.at_x = index_of(self.z, self.y, 1 - self.x)
        self.at_y = index_of(self.z, 1 - self.y, self.x)
        self.half = r1x.shape[-1]
        self.low, self.high = pl.ds(0, self.half), pl.ds(self.half, self.half)

    def first_copies(self, d):
        zz, x, y, g = (self.z + d) % ZED, self.x, self.y, self.g
        return (
            remote(g.at[zz, :, 1 - x, :, self.low], self.r1x.at[d], self.s.at[d, 0], self.q.at[d, 0], self.at_x, self.h),
            remote(g.at[zz, 1 - y, :, :, self.high], self.r1y.at[d], self.s.at[d, 1], self.q.at[d, 1], self.at_y, self.h),
        )

    def first(self, d):
        for copy in self.first_copies(d):
            self.go(copy)

    def second_copies(self, d):
        return (
            remote(self.low_acc(d), self.r2y.at[d], self.s.at[d, 2], self.q.at[d, 2], self.at_y, self.h),
            remote(self.high_acc(d), self.r2x.at[d], self.s.at[d, 3], self.q.at[d, 3], self.at_x, self.h),
        )

    def second_sum(self, d):
        x, y, me, h, r1x, r1y = self.x, self.y, self.me, self.h, self.r1x, self.r1y
        arrived(r1x.at[d], self.s.at[d, 0], self.q.at[d, 0], me, h)
        arrived(r1y.at[d], self.s.at[d, 1], self.q.at[d, 1], me, h)
        low_acc, high_acc = self.low_acc(d), self.high_acc(d)

        def body(i, carry):
            row = chunk(i)
            low_acc[row, :] = (
                low_acc[row, :].astype(f32) + r1x[d, 1 - y, row, :].astype(f32)
            ).astype(bf16)
            high_acc[row, :] = (
                high_acc[row, :].astype(f32) + r1y[d, 1 - x, row, :].astype(f32)
            ).astype(bf16)
            return carry

        lax.fori_loop(0, 8, body, 0)

    def second(self, d):
        self.second_sum(d)
        for copy in self.second_copies(d):
            self.go(copy)

    def third(self, d):
        x, y, me, h, z = self.x, self.y, self.me, self.h, self.z
        arrived(self.r2y.at[d], self.s.at[d, 2], self.q.at[d, 2], me, h)
        arrived(self.r2x.at[d], self.s.at[d, 3], self.q.at[d, 3], me, h)
        fin, low, high = self.fin(d), self.low, self.high
        target = fin if d else self.out.at[z]

        def body(i, carry):
            row = chunk(i)
            target[row, low] = (
                fin[row, low].astype(f32)
                + self.r1x[d, y, row, :].astype(f32)
                + self.r2y[d, row, :].astype(f32)
            ).astype(bf16)
            target[row, high] = (
                fin[row, high].astype(f32)
                + self.r1y[d, x, row, :].astype(f32)
                + self.r2x[d, row, :].astype(f32)
            ).astype(bf16)
            return carry

        lax.fori_loop(0, 8, body, 0)
        if d:
            there = index_of((z + d) % ZED, y, x)
            self.go(remote(fin, self.out.at[z], self.s.at[d, 4], self.q.at[d, 4], there, h))

    def last(self):
        for d in (1, 3, 2):
            arrived(
                self.out.at[(self.z + ZED - d) % ZED], self.s.at[d, 4], self.q.at[d, 4], self.me, self.h
            )


class Combine:
    def __init__(self, t, out, other, summed, landed, ls, s, q, go):
        self.t, self.out, self.other, self.summed, self.landed = t, out, other, summed, landed
        self.ls, self.s, self.q, self.go = ls, s, q, go
        self.x, self.y, self.z, self.h = where_am_i()
        self.me = index_of(self.z, self.y, self.x)

    def begin(self):
        t, h, other = self.t, self.h, self.other
        self.own = {}
        for d in FAR:
            zz = (self.z + d) % ZED
            self.own[d] = pltpu.make_async_copy(t.at[zz, h], self.summed.at[d], self.ls.at[d])
            self.own[d].start()
            self.go(remote(t.at[zz, 1 - h], other.at[d], self.s.at[d, 0], self.q.at[d, 0], self.me, 1 - h))

    def spread(self):
        summed, other = self.summed, self.other
        for d in FAR:
            zz = (self.z + d) % ZED
            self.own[d].wait()
            arrived(other.at[d], self.s.at[d, 0], self.q.at[d, 0], self.me, 1 - self.h)

            def add(turn, carry):
                row = chunk(turn)
                summed[d, row, :] = (
                    summed[d, row, :].astype(f32) + other[d, row, :].astype(f32)
                ).astype(bf16)
                return carry

            lax.fori_loop(0, 8, add, 0)
            if d:
                there = index_of(zz, self.y, self.x)
                self.go(remote(summed.at[d], self.landed.at[d], self.s.at[d, 1], self.q.at[d, 1], there, self.h))

    def total(self):
        summed, landed, out, h = self.summed, self.landed, self.out, self.h
        for d in (1, 3, 2):
            arrived(landed.at[d], self.s.at[d, 1], self.q.at[d, 1], self.me, h)

        def body(turn, carry):
            row = chunk(turn)
            acc = summed[0, row, :].astype(f32)
            for d in (1, 2, 3):
                acc = acc + landed[d, row, :].astype(f32)
            out[h, row, :] = acc.astype(bf16)
            return carry

        lax.fori_loop(0, 8, body, 0)
        self.go(remote(out.at[h], out.at[h], self.s.at[0, 1], self.q.at[0, 1], self.me, 1 - h))

    def done(self):
        arrived(self.out.at[1 - self.h], self.s.at[0, 1], self.q.at[0, 1], self.me, 1 - self.h)


def back_kernel(
    near, gg, dg, du, hid, t, wo, wm, mid, cot, got, ratio, den,
    zm, d_mid, d_att, home, tb,
    g, r1x, r1y, r2x, r2y, e2, other, summed, landed, w2, pack, d_o, d_qk, d_v,
    q_t, k_t, va, da, dn_t, pack2, nbuf, gbuf, turned, stage,
    ls, fs, bs, gs, gq, cs, cq, e1s, e1r, e2s, e2r,
):
    x, y, z, h = where_am_i()
    me = index_of(z, y, x)
    count = mid.shape[1]
    heads = 16 // mid.shape[0]
    room = dg.shape[1]
    late = []

    def go(copy):
        copy.start()
        late.append(copy)

    def fetch(i):
        cols = pl.ds(pl.multiple_of(((z + ZED - 1 - i) % ZED) * 512, 512), 512)
        return (
            pltpu.make_async_copy(near.at[:, cols], nbuf.at[i % 2], fs.at[i % 2, 0]),
            pltpu.make_async_copy(gg.at[:, cols], gbuf.at[i % 2], fs.at[i % 2, 1]),
        )

    for copy in fetch(0):
        copy.start()
    combine = Combine(t, e2, other, summed, landed, ls, cs, cq, go)
    scatter = Scatter(
        g,
        lambda d: g.at[(z + d) % ZED, 1 - y, x, :, pl.ds(0, g.shape[-1] // 2)],
        lambda d: g.at[(z + d) % ZED, y, 1 - x, :, pl.ds(g.shape[-1] // 2, g.shape[-1] // 2)],
        lambda d: g.at[(z + d) % ZED, y, x],
        zm, r1x, r1y, r2x, r2y, gs, gq, go,
    )
    combine.begin()
    weight = pltpu.make_async_copy(wo, w2, ls.at[4])
    weight.start()
    combine.spread()

    def block(i, carry):
        d = ZED - 1 - i
        zz = (z + d) % ZED

        @pl.when(i < ZED - 1)
        def _():
            for copy in fetch(i + 1):
                copy.start()

        for copy in fetch(i):
            copy.wait()
        for buf, terms in ((nbuf, (dg, du)), (gbuf, (hid,))):
            turned[...] = jnp.transpose(buf[i % 2])
            for term in terms:
                base = {id(dg): 0, id(du): room, id(hid): 2 * room}[id(term)]

                def piece(c, carry):
                    src = pl.ds(pl.multiple_of(c * COLS, COLS), COLS)
                    dst = pl.ds(pl.multiple_of(base + c * COLS, COLS), COLS)
                    res = mix(turned[...], term[:, src], ((1,), (0,))).astype(bf16)
                    for n in range(4):
                        g[zz, n // 2, n % 2, :, dst] = res[n * 128 : (n + 1) * 128, :]
                    return carry

                lax.fori_loop(0, room // COLS, piece, 0)
        @pl.when(i < ZED - 1)
        def _():
            for copy in scatter.first_copies(d):
                copy.start()

        @pl.when((i > 0) & (i < ZED - 1))
        def _():
            scatter.second_sum(d + 1)
            for copy in scatter.second_copies(d + 1):
                copy.start()

        return carry

    lax.fori_loop(0, ZED, block, 0)
    for d in (1, 2, 3):
        late.extend(scatter.first_copies(d))
    for d in (2, 3):
        late.extend(scatter.second_copies(d))
    half = near.shape[1] // 2
    shards = []
    for r in range(2):
        at = pl.ds(r * half, half)
        shards.append(
            (
                pltpu.make_async_copy(wm.at[at, pl.ds(2 * room, 512)], nbuf.at[r], fs.at[r, 0]),
                pltpu.make_async_copy(
                    wm.at[at, pl.ds(2 * room + 512, room - 512)],
                    gbuf.at[r, :, pl.ds(0, room - 512)],
                    fs.at[r, 1],
                ),
            )
        )
        for copy in shards[r]:
            copy.start()
    weight.wait()
    scatter.third(3)
    combine.total()
    combine.done()

    for mb in range(mid.shape[0]):

        def body(turn, carry):
            row = chunk(turn)
            m = mid[mb, row, :]
            scale = lax.rsqrt(jnp.mean(m * m, axis=-1, keepdims=True) + epsilon)
            hat = m * scale
            e = e2[mb, row, :].astype(f32)
            d_m = cot[mb, row, :].astype(f32) + scale * (
                e - hat * jnp.mean(e * hat, axis=-1, keepdims=True)
            )
            d_mid[mb, row, :] = d_m
            d_att[pl.ds(pl.multiple_of(mb * count + turn * 16, 16), 16), :] = d_m.astype(bf16)
            return carry

        lax.fori_loop(0, count // 16, body, 0)
    for c in range(heads * DV // COLS):
        val = mix(d_att[...], w2[:, c * COLS : (c + 1) * COLS], ((1,), (0,))).astype(bf16)
        for mb in range(16 // heads):
            for i in range(COLS // DV):
                pack[c * (COLS // DV) + i + heads * mb, :, :] = val[
                    mb * count : (mb + 1) * count, i * DV : (i + 1) * DV
                ]

    def window(source):
        return d_o.at[pl.ds(pl.multiple_of(source * count, count), count)]

    own = pltpu.make_async_copy(pack.at[me], window(me), ls.at[5])
    own.start()
    for d in range(1, 16):
        there = (me + d) % 16
        go(remote(pack.at[there], window(me), e1s.at[d], e1r.at[d], there, h))
    scatter.second(1)
    scatter.first(0)
    scatter.third(2)
    stored = {}
    for n in range(2 * half // COLS):
        r, c = n // (half // COLS), n % (half // COLS)
        if c == 0:
            for copy in shards[r]:
                copy.wait()
        if n > 1:
            stored[n - 2].wait()
        at = slice(c * COLS, (c + 1) * COLS)
        stage[n % 2, :, :] = (
            mix(hid[:, 0:512], nbuf[r, at, :], ((1,), (1,)))
            + mix(hid[:, 512:room], gbuf[r, at, 0 : room - 512], ((1,), (1,)))
        ).astype(bf16)
        stored[n] = pltpu.make_async_copy(
            stage.at[n % 2], tb.at[:, pl.ds(n * COLS, COLS)], bs.at[n % 2]
        )
        stored[n].start()
    own.wait()
    for d in range(1, 16):
        arrived(window((me + 16 - d) % 16), e1s.at[d], e1r.at[d], me, h)
    attend_back_body(got, ratio, den, d_o, d_qk, d_v, q_t, k_t, va, da, dn_t)
    for b in range(16):
        pack2[b, 0 : 2 * F, :] = d_qk[:, b * count : (b + 1) * count].astype(bf16)
        pack2[b, 2 * F :, :] = d_v[b * count : (b + 1) * count, :].astype(bf16)
    own = pltpu.make_async_copy(pack2.at[me], home.at[me], ls.at[5])
    own.start()
    for d in range(1, 16):
        there = (me + d) % 16
        go(remote(pack2.at[there], home.at[me], e2s.at[d], e2r.at[d], there, h))
    stored[2 * half // COLS - 2].wait()
    stored[2 * half // COLS - 1].wait()
    scatter.third(1)
    scatter.second(0)
    scatter.third(0)
    own.wait()
    for d in range(1, 16):
        arrived(home.at[(me + 16 - d) % 16], e2s.at[d], e2r.at[d], me, h)
    scatter.last()
    for copy in late:
        copy.wait_send()


def scatter_room(wide):
    return [
        pltpu.VMEM((4, 2, 128, wide // 2), bf16),
        pltpu.VMEM((4, 2, 128, wide // 2), bf16),
        pltpu.VMEM((4, 128, wide // 2), bf16),
        pltpu.VMEM((4, 128, wide // 2), bf16),
    ]


def back(near, gg, dg, du, hid, t, wo, wm, mid, cot, got, ratio, den):
    mbs, count, wide = cot.shape
    depth = 16 * count
    shape = jax.ShapeDtypeStruct
    cols = 3 * dg.shape[1]
    line = pltpu.VMEM((ZED, count, wide), bf16)
    return pl.pallas_call(
        back_kernel,
        out_shape=(
            shape((ZED, 128, cols), bf16),
            shape(cot.shape, f32),
            shape((mbs * count, wide), bf16),
            shape((16, 2 * F + DV, count), bf16),
            shape(near.shape, bf16),
        ),
        in_specs=[ANY] * 2 + [VMEM] * 3 + [ANY] * 3 + [VMEM] * 5,
        out_specs=(VMEM,) * 4 + (ANY,),
        scratch_shapes=[pltpu.VMEM((ZED, 2, 2, 128, cols), bf16)] + scatter_room(cols) + [
            pltpu.VMEM(cot.shape, bf16), line, line, line,
            pltpu.VMEM(wo.shape, bf16),
            pltpu.VMEM((16, count, DV), bf16),
            pltpu.VMEM((depth, DV), bf16),
            pltpu.VMEM((2 * F, depth), f32),
            pltpu.VMEM((depth, DV), f32),
            pltpu.VMEM((F, depth), bf16),
            pltpu.VMEM((F, depth), bf16),
            pltpu.VMEM((depth, 2 * DV), bf16),
            pltpu.VMEM((depth, 2 * DV), bf16),
            pltpu.VMEM((DV, depth), bf16),
            pltpu.VMEM((16, 2 * F + DV, count), bf16),
            pltpu.VMEM((2, near.shape[0], 512), bf16),
            pltpu.VMEM((2, near.shape[0], 512), bf16),
            pltpu.VMEM((512, near.shape[0]), bf16),
            pltpu.VMEM((2, near.shape[0], COLS), bf16),
            DMA((6,)), DMA((2, 2)), DMA((2,)), DMA((4, 5)), DMA((4, 5)), DMA((4, 2)), DMA((4, 2)),
            DMA((16,)), DMA((16,)), DMA((16,)), DMA((16,)),
        ],
        compiler_params=params(),
        name="back",
    )(near, gg, dg, du, hid, t, wo, wm, mid, cot, got, ratio, den)


def end_kernel(
    t, home, xh, d_att, heads_out, wa1, d_mid, xin, mid,
    za, d_in, outputs,
    g, r1x, r1y, r2x, r2y, branch, other, summed, landed, w1, dqk_t, dqkv, part, swap,
    ls, gs, gq, cs, cq, ws, wr,
):
    x, y, z, h = where_am_i()
    me = index_of(z, y, x)
    mbs, count, wide = xin.shape
    heads = 16 // mbs
    qk, vv = 2 * heads * F, heads * DV
    late = []

    def go(copy):
        copy.start()
        late.append(copy)

    combine = Combine(t, branch, other, summed, landed, ls, cs, cq, go)
    scatter = Scatter(
        g,
        lambda d: g.at[(z + d) % ZED, 1 - y, x, :, pl.ds(0, g.shape[-1] // 2)],
        lambda d: g.at[(z + d) % ZED, y, 1 - x, :, pl.ds(g.shape[-1] // 2, g.shape[-1] // 2)],
        lambda d: g.at[(z + d) % ZED, y, x],
        za, r1x, r1y, r2x, r2y, gs, gq, go,
    )
    combine.begin()
    weight = pltpu.make_async_copy(wa1, w1, ls.at[4])
    weight.start()
    for mb in range(mbs):
        cols = slice(mb * count, (mb + 1) * count)
        for k in range(heads):
            block = home.at[k + heads * mb]
            dqk_t[k * F : (k + 1) * F, cols] = block[0:F, :].astype(f32)
            dqk_t[(heads + k) * F : (heads + k + 1) * F, cols] = block[F : 2 * F, :].astype(f32)
            dqkv[cols, qk + k * DV : qk + (k + 1) * DV] = block[2 * F :, :]
    dqkv[:, 0:qk] = jnp.transpose(dqk_t[...]).astype(bf16)
    for n, d in enumerate(FAR):
        zz = (z + d) % ZED
        for yy in range(2):
            for xx in range(2):
                at = pl.ds(pl.multiple_of(index_of(zz, yy, xx) * 128, 128), 128)
                g[zz, yy, xx, :, 0 : qk + vv] = mix(xh[:, at], dqkv[...], ((0,), (0,))).astype(bf16)
                g[zz, yy, xx, :, qk + vv :] = mix(d_att[:, at], heads_out[...], ((0,), (0,))).astype(bf16)
        scatter.first(d)
        if n == 0:
            combine.spread()
    weight.wait()
    for c in range(wide // COLS):
        cols = pl.ds(c * COLS, COLS)
        part[:, c * COLS : (c + 1) * COLS] = mix(dqkv[...], w1[c * COLS : (c + 1) * COLS, :], ((1,), (1,)))
        go(remote(part.at[:, cols], swap.at[:, cols], ws.at[c], wr.at[c], me, 1 - h))
    scatter.second(2)
    for c in range(wide // COLS):
        cols = pl.ds(c * COLS, COLS)
        arrived(swap.at[:, cols], ws.at[c], wr.at[c], me, 1 - h)
    for mb in range(mbs):

        def body(turn, carry):
            row = chunk(turn)
            flat = pl.ds(pl.multiple_of(mb * count + turn * 16, 16), 16)
            v = xin[mb, row, :].astype(f32)
            scale = lax.rsqrt(jnp.mean(v * v, axis=-1, keepdims=True) + epsilon)
            hat = v * scale
            e = part[flat, :] + swap[flat, :]
            d_in[mb, row, :] = (
                d_mid[mb, row, :] + scale * (e - hat * jnp.mean(e * hat, axis=-1, keepdims=True))
            ).astype(bf16)
            return carry

        lax.fori_loop(0, count // 16, body, 0)
    scatter.second(1)
    scatter.third(2)
    scatter.second(3)
    scatter.third(1)
    scatter.second(0)
    scatter.third(3)
    combine.total()
    scatter.third(0)
    combine.done()
    for mb in range(mbs):

        def body(turn, carry):
            row = chunk(turn)
            outputs[mb, row, :] = (mid[mb, row, :] + branch[mb, row, :].astype(f32)).astype(bf16)
            return carry

        lax.fori_loop(0, count // 16, body, 0)
    scatter.last()
    for copy in late:
        copy.wait_send()


def end(t, home, xh, d_att, heads_out, wa1, d_mid, xin, mid):
    mbs, count, wide = xin.shape
    shape = jax.ShapeDtypeStruct
    cols = wa1.shape[1] + heads_out.shape[1]
    line = pltpu.VMEM((ZED, count, wide), bf16)
    return pl.pallas_call(
        end_kernel,
        out_shape=(shape((ZED, 128, cols), bf16), shape(xin.shape, bf16), shape(xin.shape, bf16)),
        in_specs=[ANY] + [VMEM] * 4 + [ANY] + [VMEM] * 3,
        out_specs=(VMEM,) * 3,
        scratch_shapes=[pltpu.VMEM((ZED, 2, 2, 128, cols), bf16)] + scatter_room(cols) + [
            pltpu.VMEM(xin.shape, bf16), line, line, line,
            pltpu.VMEM(wa1.shape, bf16),
            pltpu.VMEM((mbs * count, mbs * count), f32),
            pltpu.VMEM((mbs * count, wa1.shape[1]), bf16),
            pltpu.VMEM((mbs * count, wide), f32),
            pltpu.VMEM((mbs * count, wide), f32),
            DMA((6,)), DMA((4, 5)), DMA((4, 5)), DMA((4, 2)), DMA((4, 2)),
            DMA((wide // COLS,)), DMA((wide // COLS,)),
        ],
        compiler_params=params(),
        name="end",
    )(t, home, xh, d_att, heads_out, wa1, d_mid, xin, mid)


def finish_kernel(
    zm, za, wq, wk, wv, wg, wu, g1, g2, o_q, o_k, o_v, o_out, o_g, o_u, o_d, gains
):
    units = wg.shape[1] // ZED
    room = zm.shape[2] // 3
    nq, nv = wq.shape[1], wv.shape[1]
    lanes = g1.shape[1]
    scale1, scale2 = column(g1), column(g2)

    def total(cols):
        acc = za[0, :, cols].astype(f32)
        for n in range(1, ZED):
            acc = acc + za[n, :, cols].astype(f32)
        return acc

    first = jnp.zeros((zm.shape[1], lanes), f32)
    at = 0
    for w, out in ((wq, o_q), (wk, o_k), (wv, o_v)):
        for c in range(w.shape[1] // lanes):
            cols = slice(c * lanes, (c + 1) * lanes)
            value = total(slice(at + c * lanes, at + (c + 1) * lanes))
            out[:, cols] = value * scale1
            first = first + value * w[:, cols].astype(f32)
        at += w.shape[1]
    for c in range(nv // lanes):
        o_out[c * lanes : (c + 1) * lanes, :] = jnp.transpose(
            total(slice(at + c * lanes, at + (c + 1) * lanes))
        )
    second = jnp.zeros((zm.shape[1], lanes), f32)
    for n in range(ZED):
        for base, w, out in ((0, wg, o_g), (room, wu, o_u)):
            for c in range(0, units, lanes):
                size = min(lanes, units - c)
                cols = slice(n * units + c, n * units + c + size)
                value = zm[n, :, base + c : base + c + size].astype(f32)
                out[:, cols] = value * scale2[:, 0:size]
                prod = value * w[:, cols].astype(f32)
                if size == lanes:
                    second = second + prod
                else:
                    second = second + jnp.concatenate(
                        [prod, jnp.zeros((prod.shape[0], lanes - size), f32)], axis=1
                    )
        for c in range(0, units, lanes):
            size = min(lanes, units - c)
            value = jnp.transpose(zm[n, :, 2 * room + c : 2 * room + c + lanes].astype(f32))
            o_d[n * units + c : n * units + c + size, :] = value[0:size, :]
    gains[0:1, :] = jnp.sum(jnp.transpose(first), axis=0, keepdims=True)
    gains[1:2, :] = jnp.sum(jnp.transpose(second), axis=0, keepdims=True)


def finish(zm, za, wq, wk, wv, wg, wu, g1, g2, w_out, w_down):
    shape = lambda w: jax.ShapeDtypeStruct(w.shape, f32)
    return pl.pallas_call(
        finish_kernel,
        out_shape=(
            shape(wq), shape(wk), shape(wv), shape(w_out), shape(wg), shape(wu), shape(w_down),
            jax.ShapeDtypeStruct((2, 128), f32),
        ),
        in_specs=[VMEM] * 9,
        out_specs=(VMEM,) * 8,
        compiler_params=pltpu.CompilerParams(vmem_limit_bytes=VMEM_LIMIT),
        name="finish",
    )(zm, za, wq, wk, wv, wg, wu, g1, g2)


def fast(
    inputs, norm_gain1, w_query, w_key, w_value, w_out, norm_gain2, w_gate, w_up, w_down, cotangent
):
    mbs, count, wide = inputs.shape
    rows = w_query.shape[0]
    gain1, gain2 = norm_gain1.reshape(1, rows), norm_gain2.reshape(1, rows)
    wa1, w_o, wm, gg, got, ratio, den, heads_out, middle, near, xh1 = front(
        w_query, w_key, w_value, w_out, w_gate, w_up, w_down, gain1, gain2, cotangent, inputs
    )
    room = wm.shape[1] // 3
    w_g, w_u, w_d = wm[:, :room], wm[:, room : 2 * room], wm[:, 2 * room :]
    many = ZED * mbs * count
    n2 = near.reshape(many, wide)
    up_g = gg.reshape(many, wide)
    gate = mix(n2, w_g, ((1,), (0,)))
    up = mix(n2, w_u, ((1,), (0,)))
    d_hidden = mix(up_g, w_d, ((1,), (0,)))
    sig = jax.nn.sigmoid(gate)
    silu = gate * sig
    hidden = (silu * up).astype(bf16)
    d_gate = (d_hidden * up * sig * (1.0 + gate * (1.0 - sig))).astype(bf16)
    d_up = (d_hidden * silu).astype(bf16)
    d_n2 = (mix(d_gate, w_g, ((1,), (1,))) + mix(d_up, w_u, ((1,), (1,)))).astype(bf16)
    lines = (ZED, mbs, count, wide)
    zm, d_mid, d_att, home, branch = back(
        n2, up_g, d_gate, d_up, hidden, d_n2.reshape(lines), w_o, wm, middle, cotangent, got, ratio, den
    )
    za, input_grad, outputs = end(
        branch.reshape(lines), home, xh1, d_att, heads_out, wa1, d_mid, inputs, middle
    )
    o_q, o_k, o_v, o_out, o_g, o_u, o_d, gains = finish(
        zm, za, w_query, w_key, w_value, w_gate, w_up,
        gain1, gain2, w_out, w_down,
    )
    gains = lax.psum(gains, "head")
    return (outputs, input_grad, gains[0], o_q, o_k, o_v, o_out, gains[1], o_g, o_u, o_d)


def solution(mesh):
    return jax.shard_map(
        fast if mesh.shape["seq"] == 16 else local,
        mesh=mesh,
        in_specs=(
            P(None, "seq", None),
            P("seq"),
            P("seq", "head"),
            P("seq", "head"),
            P("seq", "head"),
            P("head", "seq"),
            P("seq"),
            P("seq", "head"),
            P("seq", "head"),
            P("head", "seq"),
            P(None, "seq", None),
        ),
        out_specs=(
            P(None, "seq", None),
            P(None, "seq", None),
            P("seq"),
            P("seq", "head"),
            P("seq", "head"),
            P("seq", "head"),
            P("head", "seq"),
            P("seq"),
            P("seq", "head"),
            P("seq", "head"),
            P("head", "seq"),
        ),
        check_vma=False,
    )
```

```python
import jax
import jax.numpy as jnp
from jax import lax
from jax.experimental import pallas as pl
from jax.experimental.pallas import tpu as pltpu
from jax.sharding import PartitionSpec as P

F = 16
DV = 128


epsilon = 1e-05
highest = lax.Precision.HIGHEST


def entering(part, axis, combine, identity, reverse):
    count = lax.axis_size(axis)
    place = lax.axis_index(axis)
    ahead = count - 1 - place if reverse else place
    gathered = jax.tree.map(lambda a: lax.all_gather(a, axis), part)
    state = jax.tree.map(lambda a, e: jnp.zeros_like(a) + jnp.asarray(e, a.dtype), part, identity)

    def one(turn, state):
        source = count - 1 - turn if reverse else turn
        return combine(
            state, jax.tree.map(lambda a: lax.dynamic_index_in_dim(a, source, 0, False), gathered)
        )

    return lax.fori_loop(0, ahead, one, state)


def rms_apply(values, gain):
    scale = lax.rsqrt(jnp.mean(values * values, axis=-1, keepdims=True) + epsilon)
    return values * scale * gain


def feature_map(projected):
    count = projected.shape[0]
    pieces = projected.reshape(count, -1, F)
    square = (pieces[:, :, :, None] * pieces[:, :, None, :]).reshape(count, pieces.shape[1], F * F)
    return jnp.concatenate(
        [jnp.ones_like(pieces[:, :, :1]), pieces * F ** (-0.25), square * (2.0 * F) ** (-0.5)],
        axis=-1,
    )


def swiglu(gate, up_part):
    return jax.nn.silu(gate) * up_part


def round_trip(values):
    return lax.optimization_barrier(values.astype(jnp.bfloat16)).astype(jnp.float32)


def add_pair(earlier, later):
    return (earlier[0] + later[0], earlier[1] + later[1])


def block_pass(tokens, upstream, gathered):
    gain_one, query_w, key_w, value_w, out_w, gain_two, gate_w, up_w, down_w = gathered
    f32 = jnp.float32
    bf16 = jnp.bfloat16
    stream = tokens.astype(f32)
    count = stream.shape[0]
    normed_f, norm_one_pull = jax.vjp(rms_apply, stream, gain_one.astype(f32))
    normed = normed_f.astype(bf16)
    queries = jnp.dot(normed, query_w, preferred_element_type=f32)
    keys_all = jnp.dot(normed, key_w, preferred_element_type=f32)
    values = jnp.dot(normed, value_w, preferred_element_type=f32).astype(bf16)
    query_feat_f, query_pull = jax.vjp(feature_map, queries)
    key_feat_f, key_pull = jax.vjp(feature_map, keys_all)
    query_feat = jnp.transpose(query_feat_f.astype(bf16), (1, 0, 2))
    key_feat = jnp.transpose(key_feat_f.astype(bf16), (1, 0, 2))
    value_heads = jnp.transpose(values.reshape(count, -1, DV), (1, 0, 2))
    causal = (jnp.arange(count)[:, None] >= jnp.arange(count)[None, :]).astype(f32)
    scores = jnp.einsum("htf,hsf->hts", query_feat, key_feat, preferred_element_type=f32) * causal
    weighted = scores.astype(bf16)
    num_local = jnp.einsum("hts,hsd->htd", weighted, value_heads, preferred_element_type=f32)
    den_local = jnp.sum(weighted.astype(f32), axis=-1)
    states = jnp.einsum("hsf,hsd->hfd", key_feat, value_heads, preferred_element_type=f32)
    totals = jnp.sum(key_feat.astype(f32), axis=1)
    state_before, total_before = entering(
        (states, totals), "seq", add_pair, (jnp.zeros_like(states), jnp.zeros_like(totals)), False
    )
    query_wide = query_feat.astype(f32)
    numer = num_local + jnp.einsum("htf,hfd->htd", query_wide, state_before, precision=highest)
    denom = den_local + jnp.einsum("htf,hf->ht", query_wide, total_before, precision=highest)
    ratio = numer / denom[..., None]
    heads_out = jnp.transpose(ratio, (1, 0, 2)).reshape(count, -1).astype(bf16)
    attended = lax.psum(jnp.dot(heads_out, out_w, preferred_element_type=f32), "head")
    middle = stream + attended
    normed_two_f, norm_two_pull = jax.vjp(rms_apply, middle, gain_two.astype(f32))
    normed_two = normed_two_f.astype(bf16)
    gate = jnp.dot(normed_two, gate_w, preferred_element_type=f32)
    up_part = jnp.dot(normed_two, up_w, preferred_element_type=f32)
    active, active_pull = jax.vjp(swiglu, gate, up_part)
    hidden = active.astype(bf16)
    branch = lax.psum(
        jnp.dot(hidden, down_w, preferred_element_type=f32).astype(jnp.bfloat16), "head"
    ).astype(jnp.float32)
    result = (middle + branch).astype(bf16)
    grad_down = jnp.dot(hidden.T, upstream, preferred_element_type=f32)
    d_hidden = jnp.dot(upstream, down_w.T, preferred_element_type=f32)
    d_gate_f, d_up_f = active_pull(d_hidden)
    d_gate = d_gate_f.astype(bf16)
    d_up = d_up_f.astype(bf16)
    grad_gate = jnp.dot(normed_two.T, d_gate, preferred_element_type=f32)
    grad_up = jnp.dot(normed_two.T, d_up, preferred_element_type=f32)
    d_normed_two = lax.psum(
        jnp.dot(d_gate, gate_w.T, preferred_element_type=f32)
        + jnp.dot(d_up, up_w.T, preferred_element_type=f32),
        "head",
    )
    d_middle_norm, grad_gain2 = norm_two_pull(d_normed_two)
    d_middle = upstream.astype(f32) + d_middle_norm
    d_attended = d_middle.astype(bf16)
    grad_out = jnp.dot(heads_out.T, d_attended, preferred_element_type=f32)
    d_heads = jnp.transpose(
        jnp.dot(d_attended, out_w.T, preferred_element_type=f32).reshape(count, -1, DV), (1, 0, 2)
    )
    d_numer = (d_heads / denom[..., None]).astype(bf16)
    d_denom = -jnp.sum(d_heads * ratio, axis=-1) / denom
    d_numer_wide = d_numer.astype(f32)
    d_before = jnp.einsum("htf,htd->hfd", query_wide, d_numer_wide, precision=highest)
    d_total_before = jnp.einsum("htf,ht->hf", query_wide, d_denom, precision=highest)
    d_state, d_total = entering(
        (d_before, d_total_before),
        "seq",
        add_pair,
        (jnp.zeros_like(d_before), jnp.zeros_like(d_total_before)),
        True,
    )
    d_scores = (
        (
            jnp.einsum("htd,hsd->hts", d_numer, value_heads, preferred_element_type=f32)
            + d_denom[..., None]
        )
        * causal
    ).astype(bf16)
    d_values = jnp.einsum(
        "hts,htd->hsd", weighted, d_numer, preferred_element_type=f32
    ) + jnp.einsum("hsf,hfd->hsd", key_feat.astype(f32), d_state, precision=highest)
    d_query_feat = (
        jnp.einsum("hts,hsf->htf", d_scores, key_feat, preferred_element_type=f32)
        + jnp.einsum("htd,hfd->htf", d_numer_wide, state_before, precision=highest)
        + d_denom[..., None] * total_before[:, None, :]
    )
    d_key_feat = (
        jnp.einsum("hts,htf->hsf", d_scores, query_feat, preferred_element_type=f32)
        + jnp.einsum("hsd,hfd->hsf", value_heads.astype(f32), d_state, precision=highest)
        + d_total[:, None, :]
    )
    d_queries = query_pull(jnp.transpose(round_trip(d_query_feat), (1, 0, 2)))[0].astype(bf16)
    d_keys = key_pull(jnp.transpose(round_trip(d_key_feat), (1, 0, 2)))[0].astype(bf16)
    d_values_flat = jnp.transpose(d_values, (1, 0, 2)).reshape(count, -1).astype(bf16)
    grad_query = jnp.dot(normed.T, d_queries, preferred_element_type=f32)
    grad_key = jnp.dot(normed.T, d_keys, preferred_element_type=f32)
    grad_value = jnp.dot(normed.T, d_values_flat, preferred_element_type=f32)
    d_normed_part = (
        jnp.dot(d_queries, query_w.T, preferred_element_type=f32)
        + jnp.dot(d_keys, key_w.T, preferred_element_type=f32)
        + jnp.dot(d_values_flat, value_w.T, preferred_element_type=f32)
    )
    d_normed = lax.psum(d_normed_part.astype(jnp.bfloat16), "head").astype(jnp.float32)
    d_stream_norm, grad_gain1 = norm_one_pull(d_normed)
    input_grad = (d_middle + d_stream_norm).astype(bf16)
    return (
        result,
        input_grad,
        grad_gain1,
        grad_query,
        grad_key,
        grad_value,
        grad_out,
        grad_gain2,
        grad_gate,
        grad_up,
        grad_down,
    )


def local(
    inputs, norm_gain1, w_query, w_key, w_value, w_out, norm_gain2, w_gate, w_up, w_down, cotangent
):
    micro = inputs.shape[0]
    summed = None
    results = []
    input_grads = []
    for step_index in range(micro):
        gathered = (
            lax.all_gather(norm_gain1, "seq", axis=0, tiled=True),
            lax.all_gather(w_query, "seq", axis=0, tiled=True),
            lax.all_gather(w_key, "seq", axis=0, tiled=True),
            lax.all_gather(w_value, "seq", axis=0, tiled=True),
            lax.all_gather(w_out, "seq", axis=1, tiled=True),
            lax.all_gather(norm_gain2, "seq", axis=0, tiled=True),
            lax.all_gather(w_gate, "seq", axis=0, tiled=True),
            lax.all_gather(w_up, "seq", axis=0, tiled=True),
            lax.all_gather(w_down, "seq", axis=1, tiled=True),
        )
        (
            result,
            input_grad,
            grad_gain1,
            grad_query,
            grad_key,
            grad_value,
            grad_out,
            grad_gain2,
            grad_gate,
            grad_up,
            grad_down,
        ) = block_pass(inputs[step_index], cotangent[step_index], gathered)
        results.append(result)
        input_grads.append(input_grad)
        fresh = (
            lax.psum_scatter(grad_gain1, "seq", scatter_dimension=0, tiled=True),
            lax.psum_scatter(grad_query, "seq", scatter_dimension=0, tiled=True),
            lax.psum_scatter(grad_key, "seq", scatter_dimension=0, tiled=True),
            lax.psum_scatter(grad_value, "seq", scatter_dimension=0, tiled=True),
            lax.psum_scatter(grad_out, "seq", scatter_dimension=1, tiled=True),
            lax.psum_scatter(grad_gain2, "seq", scatter_dimension=0, tiled=True),
            lax.psum_scatter(grad_gate, "seq", scatter_dimension=0, tiled=True),
            lax.psum_scatter(grad_up, "seq", scatter_dimension=0, tiled=True),
            lax.psum_scatter(grad_down, "seq", scatter_dimension=1, tiled=True),
        )
        summed = (
            fresh
            if summed is None
            else tuple((older + newer for older, newer in zip(summed, fresh)))
        )
    return (
        jnp.stack(results),
        jnp.stack(input_grads),
        summed[0],
        summed[1],
        summed[2],
        summed[3],
        summed[4],
        summed[5],
        summed[6],
        summed[7],
        summed[8],
    )


MESH = pl.DeviceIdType.MESH
bf16 = jnp.bfloat16
f32 = jnp.float32
ZED = 4
VMEM_LIMIT = 60 * 1024 * 1024


def where_am_i():
    place = lax.axis_index("seq")
    return place % 2, (place // 2) % 2, place // 4, lax.axis_index("head")


def index_of(z, y, x):
    return (z * 2 + y) * 2 + x


def remote(src, dst, send, recv, place, head):
    return pltpu.make_async_remote_copy(
        src_ref=src, dst_ref=dst, send_sem=send, recv_sem=recv, device_id=(place, head),
        device_id_type=MESH,
    )


def arrived(dst, send, recv, place, head):
    remote(dst, dst, send, recv, place, head).wait_recv()


def params():
    return pltpu.CompilerParams(has_side_effects=True, vmem_limit_bytes=VMEM_LIMIT)


ANY = pl.BlockSpec(memory_space=pl.ANY)
VMEM = pl.BlockSpec(memory_space=pltpu.VMEM)
DMA = pltpu.SemaphoreType.DMA
ORDER = (0, 1, 3, 2)


def mix(a, b, over):
    return lax.dot_general(a, b, (over, ((), ())), preferred_element_type=f32)


CHUNK = 512
COLS = 256


def spread(got, q_t, k_t, va):
    count = got.shape[2]
    for b in range(got.shape[0]):
        q_t[:, b * count : (b + 1) * count] = got[b, 0:F, :]
        k_t[:, b * count : (b + 1) * count] = got[b, F : 2 * F, :]
        va[b * count : (b + 1) * count, 0:DV] = got[b, 2 * F :, :]
    va[:, DV:] = jnp.ones((va.shape[0], va.shape[1] - DV), bf16)


def lower(count):
    return lax.broadcasted_iota(jnp.int32, (count, count), 0) >= lax.broadcasted_iota(
        jnp.int32, (count, count), 1
    )


def attend_rows(qi, q_t, k_t, va, ratio, den, causal):
    qs = slice(qi * CHUNK, (qi + 1) * CHUNK)
    acc = jnp.zeros((CHUNK, va.shape[1]), f32)
    for kj in range(qi + 1):
        ks = slice(kj * CHUNK, (kj + 1) * CHUNK)
        s = mix(q_t[:, qs], k_t[:, ks], ((0,), (0,)))
        p = 1.0 + s * (0.25 + s * (1.0 / 32.0))
        if kj == qi:
            p = jnp.where(causal, p, 0.0)
        acc = acc + mix(p.astype(bf16), va[ks, :], ((1,), (0,)))
    ratio[qs, :] = acc[:, :DV] / acc[:, DV:]
    den[qs, :] = acc[:, DV:]


def column(gain):
    count = gain.shape[1]
    return jnp.transpose(jnp.broadcast_to(gain[...].astype(f32), (count, count)))


def front_kernel(
    wq, wk, wv, w_out, wg, wu, wd, g1, g2, cot, xin,
    wa1, wa2, wm, gg, got, ratio, den, heads_out, middle, near, xh,
    a1, a2, m, w1, w2, pack, q_t, k_t, va, ob, part, other,
    ls, zs, zr, us, ur, ps, pr, e1s, e1r, e2s, e2r, ws, wr, ds, dr,
):
    x, y, z, h = where_am_i()
    me = index_of(z, y, x)
    at_x, at_y = index_of(z, y, 1 - x), index_of(z, 1 - y, x)
    count = xin.shape[1]
    heads = 16 // xin.shape[0]
    late = []

    def when(true, do):
        if true is None:
            do()
        else:
            pl.when(true)(do)

    def go(copy, true=None):
        when(true, copy.start)
        late.append((true, copy))

    def rows(zz, yy, xx):
        return pl.ds(pl.multiple_of(index_of(zz, yy, xx) * 128, 128), 128)

    mine = rows(z, y, x)
    kept = [
        pltpu.make_async_copy(a1, w1.at[mine], ls.at[0]),
        pltpu.make_async_copy(a2, w2.at[mine], ls.at[1]),
        pltpu.make_async_copy(m.at[z], wm.at[mine], ls.at[2]),
        pltpu.make_async_copy(cot, gg.at[z], ls.at[6]),
    ]
    lanes = g1.shape[1]
    scale = column(g1)
    at = 0
    for w in (wq, wk, wv):
        for c in range(0, w.shape[1], lanes):
            a1[:, at + c : at + c + lanes] = (w[:, c : c + lanes].astype(f32) * scale).astype(bf16)
        at += w.shape[1]
    kept[0].start()
    kept[3].start()
    dest = (w1, w2, wm)
    UP, DOWN = 0, 1
    COT, NEAR = 2, 3

    def held(kind, zz):
        return (lambda: w1.at[rows(zz, y, x)], lambda: w2.at[rows(zz, y, x)],
                lambda: gg.at[zz, h], lambda: near.at[zz, h])[kind]()

    def origin(way, step):
        return (z + ZED - step) % ZED if way == UP else (z + step) % ZED

    def valid(way, step):
        return z >= step if way == UP else z <= ZED - 1 - step

    def pass_on(kind, way, step, src, true):
        there = index_of((z + 1) % ZED if way == UP else (z + ZED - 1) % ZED, y, x)
        block = held(kind, origin(way, step))
        go(remote(block if src is None else src, block, us.at[kind, way, step], ur.at[kind, way, step + 1], there, h), true)

    def offer(kind, src=None):
        pass_on(kind, UP, 0, src, z < ZED - 1)
        pass_on(kind, DOWN, 0, src, z > 0)

    def hop(kind, way, step):
        block = held(kind, origin(way, step))
        when(
            valid(way, step),
            lambda: arrived(block, us.at[kind, way, step], ur.at[kind, way, step], me, h),
        )
        if step < ZED - 1:
            more = z < ZED - 1 if way == UP else z > 0
            pass_on(kind, way, step, None, valid(way, step) & more)

    def across(kind, way, step):
        zz = origin(way, step)
        block = held(kind, zz)
        go(remote(block, block, ds.at[kind, way, step], dr.at[kind, way, step], me, 1 - h), valid(way, step))

    def across_done(kind, way, step):
        zz = origin(way, step)
        block = (gg if kind == COT else near).at[zz, 1 - h]
        when(
            valid(way, step),
            lambda: arrived(block, ds.at[kind, way, step], dr.at[kind, way, step], me, 1 - h),
        )

    def both(do, kind, step):
        do(kind, UP, step)
        do(kind, DOWN, step)

    partner = (z, z + 1 - 2 * (z % 2), ZED - 1 - z, (z + 2) % ZED)

    inner = (z > 0) & (z < ZED - 1)
    outer = (z == 0) | (z == ZED - 1)

    def line(d, true=None):
        zz = partner[d]
        copy = remote(m.at[zz], wm.at[mine], zs.at[d], zr.at[d], index_of(zz, y, x), h)
        go(copy, true)

    def slot_of(way, step):
        return step if way == UP else 3 + step if step else 0

    def plane_set(kind, slot, zz, true):
        block = dest[kind].at[rows(zz, y, x)]
        go(remote(block, block, ps.at[kind, slot, 0], pr.at[kind, slot, 0], at_x, h), true)
        go(remote(block, block, ps.at[kind, slot, 1], pr.at[kind, slot, 1], at_y, h), true)

    def onward_set(kind, slot, zz, true):
        w = dest[kind]
        half = w.shape[1] // 2
        from_x, from_y = rows(zz, y, 1 - x), rows(zz, 1 - y, x)

        def wait():
            arrived(w.at[from_x], ps.at[kind, slot, 0], pr.at[kind, slot, 0], me, h)
            arrived(w.at[from_y], ps.at[kind, slot, 1], pr.at[kind, slot, 1], me, h)

        when(true, wait)
        left = w.at[from_y, pl.ds(0, half)]
        right = w.at[from_x, pl.ds(half, half)]
        go(remote(left, left, ps.at[kind, slot, 2], pr.at[kind, slot, 2], at_x, h), true)
        go(remote(right, right, ps.at[kind, slot, 3], pr.at[kind, slot, 3], at_y, h), true)

    def corner_set(kind, slot, zz, true):
        w = dest[kind]
        half = w.shape[1] // 2
        far = rows(zz, 1 - y, 1 - x)

        def wait():
            arrived(w.at[far, pl.ds(0, half)], ps.at[kind, slot, 2], pr.at[kind, slot, 2], me, h)
            arrived(w.at[far, pl.ds(half, half)], ps.at[kind, slot, 3], pr.at[kind, slot, 3], me, h)

        when(true, wait)

    def plane(kind, way, step):
        if step == 0:
            kept[kind].wait()
        plane_set(kind, slot_of(way, step), origin(way, step), valid(way, step) if step else None)

    def onward(kind, way, step):
        onward_set(kind, slot_of(way, step), origin(way, step), valid(way, step) if step else None)

    def corner(kind):
        corner_set(kind, 0, z, None)
        for step in (1, 2, 3):
            for way in (UP, DOWN):
                corner_set(kind, slot_of(way, step), origin(way, step), valid(way, step))

    def m_plane(d):
        zz = partner[d]
        if d:
            arrived(wm.at[rows(zz, y, x)], zs.at[d], zr.at[d], me, h)
        else:
            kept[2].wait()
        plane_set(2, d, zz, None)

    def m_onward(d):
        onward_set(2, d, partner[d], None)

    offer(0, a1)
    plane(0, UP, 0)
    for c in range(0, w_out.shape[0], lanes):
        a2[:, c : c + lanes] = jnp.transpose(w_out[c : c + lanes, :].astype(f32)).astype(bf16)
    kept[1].start()
    for way in (UP, DOWN):
        hop(0, way, 1)
        plane(0, way, 1)
    units = wg.shape[1] // ZED
    room = m.shape[2] // 3
    scale = column(g2)
    for n in range(ZED):
        for part_at, w in ((0, wg), (room, wu)):
            for c in range(0, units, lanes):
                size = min(lanes, units - c)
                m[n, :, part_at + c : part_at + c + size] = (
                    w[:, n * units + c : n * units + c + size].astype(f32) * scale[:, 0:size]
                ).astype(bf16)
        for c in range(0, units, lanes):
            size = min(lanes, units - c)
            m[n, :, 2 * room + c : 2 * room + c + size] = jnp.transpose(
                wd[n * units + c : n * units + c + size, :].astype(f32)
            ).astype(bf16)
        for part_at in (0, room, 2 * room):
            m[n, :, part_at + units : part_at + room] = jnp.zeros((lanes, room - units), bf16)
    kept[2].start()
    onward(0, UP, 0)
    for way in (UP, DOWN):
        hop(0, way, 2)
        plane(0, way, 2)
    offer(1, a2)
    both(onward, 0, 1)
    for way in (UP, DOWN):
        hop(0, way, 3)
        plane(0, way, 3)
    both(onward, 0, 2)
    both(hop, 1, 1)
    plane(1, UP, 0)
    for mb in range(xin.shape[0]):

        def normed(turn, carry):
            row = pl.ds(pl.multiple_of(turn * 16, 16), 16)
            v = xin[mb, row, :].astype(f32)
            r = lax.rsqrt(jnp.mean(v * v, axis=-1, keepdims=True) + epsilon)
            xh[pl.ds(pl.multiple_of(mb * count + turn * 16, 16), 16), :] = (v * r).astype(bf16)
            return carry

        lax.fori_loop(0, count // 16, normed, 0)
    both(onward, 0, 3)
    both(hop, 1, 2)
    both(hop, 1, 3)
    line(1)
    line(2, inner)
    corner(0)
    out1 = pltpu.make_async_copy(w1, wa1, ls.at[3])
    out1.start()
    kq = mix(xh[...], w1[:, 0 : 2 * heads * F], ((1,), (0,)))
    qk = jnp.transpose(kq).astype(bf16)
    for mb in range(16 // heads):
        for k in range(heads):
            t = k + heads * mb
            cols = slice(mb * count, (mb + 1) * count)
            pack[t, 0:F, :] = qk[k * F : (k + 1) * F, cols]
            pack[t, F : 2 * F, :] = qk[(heads + k) * F : (heads + k + 1) * F, cols]
    for c in range(heads * DV // COLS):
        at = 2 * heads * F + c * COLS
        val = mix(xh[...], w1[:, at : at + COLS], ((1,), (0,))).astype(bf16)
        for mb in range(16 // heads):
            for i in range(COLS // DV):
                t = c * (COLS // DV) + i + heads * mb
                pack[t, 2 * F :, :] = val[mb * count : (mb + 1) * count, i * DV : (i + 1) * DV]
    keep = pltpu.make_async_copy(pack.at[me], got.at[me], ls.at[4])
    keep.start()
    for d in range(1, 16):
        there = (me + d) % 16
        go(remote(pack.at[there], got.at[me], e1s.at[d], e1r.at[d], there, h))
    line(2, outer)
    line(3, inner)
    both(plane, 1, 1)
    onward(1, UP, 0)
    both(plane, 1, 2)
    both(onward, 1, 1)
    both(plane, 1, 3)
    both(onward, 1, 2)
    keep.wait()
    for d in range(1, 16):
        arrived(got.at[(me + 16 - d) % 16], e1s.at[d], e1r.at[d], me, h)
    both(onward, 1, 3)
    spread(got, q_t, k_t, va)
    causal = lower(CHUNK)
    for qi in range(va.shape[0] // CHUNK):
        attend_rows(qi, q_t, k_t, va, ratio, den, causal)
    for b in range(16):
        ob[b, :, :] = ratio[b * count : (b + 1) * count, :].astype(bf16)

    def window(source):
        return heads_out.at[
            pl.ds(pl.multiple_of((source // heads) * count, count), count),
            pl.ds(pl.multiple_of((source % heads) * DV, DV), DV),
        ]

    keep = pltpu.make_async_copy(ob.at[me], window(me), ls.at[4])
    keep.start()
    for d in range(1, 16):
        there = (me + d) % 16
        go(remote(ob.at[there], window(me), e2s.at[d], e2r.at[d], there, h))
    line(3, outer)
    offer(COT, cot.at[h])
    m_plane(0)
    m_plane(1)
    corner(1)
    out2 = pltpu.make_async_copy(w2, wa2, ls.at[5])
    out2.start()
    keep.wait()
    for d in range(1, 16):
        arrived(window((me + 16 - d) % 16), e2s.at[d], e2r.at[d], me, h)
    wide = part.shape[1]
    for c in range(wide // COLS):
        cols = pl.ds(c * COLS, COLS)
        part[:, c * COLS : (c + 1) * COLS] = mix(
            heads_out[...], w2[c * COLS : (c + 1) * COLS, :], ((1,), (1,))
        )
        go(remote(part.at[:, cols], other.at[:, cols], ws.at[c], wr.at[c], me, 1 - h))
    m_onward(0)
    both(hop, COT, 1)
    m_plane(2)
    for c in range(wide // COLS):
        cols = pl.ds(c * COLS, COLS)
        arrived(other.at[:, cols], ws.at[c], wr.at[c], me, 1 - h)

    def one(mb):
        def body(turn, carry):
            row = pl.ds(pl.multiple_of(turn * 16, 16), 16)
            flat = pl.ds(pl.multiple_of(mb * count + turn * 16, 16), 16)
            mid = xin[mb, row, :].astype(f32) + (part[flat, :] + other[flat, :])
            middle[mb, row, :] = mid
            scale = lax.rsqrt(jnp.mean(mid * mid, axis=-1, keepdims=True) + epsilon)
            near[z, mb, row, :] = (mid * scale).astype(bf16)
            return carry

        lax.fori_loop(0, count // 16, body, 0)

    one(h)
    offer(NEAR)
    one(1 - h)
    m_onward(1)
    both(hop, COT, 2)
    m_plane(3)
    kept[3].wait()
    both(across, COT, 1)
    both(across, COT, 2)
    both(hop, NEAR, 1)
    both(across, NEAR, 1)
    m_onward(2)
    both(hop, COT, 3)
    both(across, COT, 3)
    both(hop, NEAR, 2)
    both(across, NEAR, 2)
    m_onward(3)
    both(hop, NEAR, 3)
    both(across, NEAR, 3)
    for d in range(4):
        corner_set(2, d, partner[d], None)
    for kind in (NEAR, COT):
        for step in (1, 2, 3):
            both(across_done, kind, step)
    out1.wait()
    out2.wait()
    for true, copy in late:
        when(true, copy.wait_send)


def front(wq, wk, wv, w_out, wg, wu, wd, g1, g2, cot, xin):
    mbs, count, wide = xin.shape
    depth = 16 * count
    wide1, wide2 = wq.shape[1] + wk.shape[1] + wv.shape[1], w_out.shape[0]
    wide3 = 3 * (-(-wg.shape[1] // ZED // 256) * 256)
    shape = jax.ShapeDtypeStruct
    return pl.pallas_call(
        front_kernel,
        out_shape=(
            shape((wide, wide1), bf16),
            shape((wide, wide2), bf16),
            shape((wide, wide3), bf16),
            shape((ZED,) + cot.shape, bf16),
            shape((16, 2 * F + DV, count), bf16),
            shape((depth, DV), f32),
            shape((depth, DV), f32),
            shape((mbs * count, wide2), bf16),
            shape(xin.shape, f32),
            shape((ZED,) + xin.shape, bf16),
            shape((mbs * count, wide), bf16),
        ),
        in_specs=[VMEM] * 9 + [ANY] + [VMEM],
        out_specs=(ANY,) * 4 + (VMEM,) * 7,
        scratch_shapes=[
            pltpu.VMEM((wq.shape[0], wide1), bf16),
            pltpu.VMEM((wq.shape[0], wide2), bf16),
            pltpu.VMEM((ZED, wq.shape[0], wide3), bf16),
            pltpu.VMEM((wide, wide1), bf16),
            pltpu.VMEM((wide, wide2), bf16),
            pltpu.VMEM((16, 2 * F + DV, count), bf16),
            pltpu.VMEM((F, depth), bf16),
            pltpu.VMEM((F, depth), bf16),
            pltpu.VMEM((depth, 2 * DV), bf16),
            pltpu.VMEM((16, count, DV), bf16),
            pltpu.VMEM((mbs * count, wide), f32),
            pltpu.VMEM((mbs * count, wide), f32),
            DMA((7,)), DMA((4,)), DMA((4,)), DMA((4, 2, 4)), DMA((4, 2, 4)), DMA((3, 7, 4)), DMA((3, 7, 4)),
            DMA((16,)), DMA((16,)), DMA((16,)), DMA((16,)),
            DMA((wide // COLS,)), DMA((wide // COLS,)), DMA((4, 2, 4)), DMA((4, 2, 4)),
        ],
        compiler_params=params(),
        name="front",
    )(wq, wk, wv, w_out, wg, wu, wd, g1, g2, cot, xin)


def attend_back_body(got, ratio, den, d_o, d_qk, d_v, q_t, k_t, va, da, dn_t):
    spread(got, q_t, k_t, va)
    depth = va.shape[0]
    lane = lax.broadcasted_iota(jnp.int32, (CHUNK, DV), 1)
    for qi in range(depth // CHUNK):
        qs = slice(qi * CHUNK, (qi + 1) * CHUNK)
        dn = d_o[qs, :].astype(f32) / den[qs, :]
        dd = -jnp.sum(dn * ratio[qs, :], axis=-1, keepdims=True)
        big = dd.astype(bf16).astype(f32)
        da[qs, 0:DV] = dn.astype(bf16)
        da[qs, DV:] = jnp.where(lane == 0, big, jnp.where(lane == 1, dd - big, 0.0)).astype(bf16)
        dn_t[:, qs] = jnp.transpose(dn).astype(bf16)
    causal = lower(CHUNK)
    for kj in range(depth // CHUNK):
        ks = slice(kj * CHUNK, (kj + 1) * CHUNK)
        acc_k = jnp.zeros((F, CHUNK), f32)
        acc_v = jnp.zeros((DV, CHUNK), f32)
        for qi in range(kj, depth // CHUNK):
            qs = slice(qi * CHUNK, (qi + 1) * CHUNK)
            s = mix(q_t[:, qs], k_t[:, ks], ((0,), (0,)))
            p = 1.0 + s * (0.25 + s * (1.0 / 32.0))
            d_s = mix(da[qs, :], va[ks, :], ((1,), (1,))) * (0.25 + s * (1.0 / 16.0))
            if kj == qi:
                p = jnp.where(causal, p, 0.0)
                d_s = jnp.where(causal, d_s, 0.0)
            d_s = d_s.astype(bf16)
            acc_v = acc_v + mix(dn_t[:, qs], p.astype(bf16), ((1,), (0,)))
            acc_k = acc_k + mix(q_t[:, qs], d_s, ((1,), (0,)))
            d_q = mix(k_t[:, ks], d_s, ((1,), (1,)))
            d_qk[0:F, qs] = d_q if kj == 0 else d_qk[0:F, qs] + d_q
        d_qk[F : 2 * F, ks] = acc_k
        d_v[ks, :] = jnp.transpose(acc_v)


FAR = (2, 1, 3, 0)


def chunk(turn):
    return pl.ds(pl.multiple_of(turn * 16, 16), 16)


class Scatter:
    def __init__(self, g, low_acc, high_acc, fin, out, r1x, r1y, r2x, r2y, s, q, go, planes=None, relay=None):
        self.planes, self.relay = planes, relay
        self.g, self.low_acc, self.high_acc, self.fin, self.out = g, low_acc, high_acc, fin, out
        self.r1x, self.r1y, self.r2x, self.r2y, self.s, self.q = r1x, r1y, r2x, r2y, s, q
        self.go = go
        self.x, self.y, self.z, self.h = where_am_i()
        self.me = index_of(self.z, self.y, self.x)
        self.at_x = index_of(self.z, self.y, 1 - self.x)
        self.at_y = index_of(self.z, 1 - self.y, self.x)
        self.half = r1x.shape[-1]
        self.low, self.high = pl.ds(0, self.half), pl.ds(self.half, self.half)

    def plane(self, d):
        return (self.z + d) % ZED if self.planes is None else self.planes[d]

    def first_copies(self, d):
        zz, x, y, g = self.plane(d), self.x, self.y, self.g
        return (
            remote(g.at[zz, :, 1 - x, :, self.low], self.r1x.at[d], self.s.at[d, 0], self.q.at[d, 0], self.at_x, self.h),
            remote(g.at[zz, 1 - y, :, :, self.high], self.r1y.at[d], self.s.at[d, 1], self.q.at[d, 1], self.at_y, self.h),
        )

    def first(self, d):
        for copy in self.first_copies(d):
            self.go(copy)

    def second_copies(self, d):
        return (
            remote(self.low_acc(d), self.r2y.at[d], self.s.at[d, 2], self.q.at[d, 2], self.at_y, self.h),
            remote(self.high_acc(d), self.r2x.at[d], self.s.at[d, 3], self.q.at[d, 3], self.at_x, self.h),
        )

    def second_sum(self, d):
        x, y, me, h, r1x, r1y = self.x, self.y, self.me, self.h, self.r1x, self.r1y
        arrived(r1x.at[d], self.s.at[d, 0], self.q.at[d, 0], me, h)
        arrived(r1y.at[d], self.s.at[d, 1], self.q.at[d, 1], me, h)
        low_acc, high_acc = self.low_acc(d), self.high_acc(d)

        def body(i, carry):
            row = chunk(i)
            low_acc[row, :] = (
                low_acc[row, :].astype(f32) + r1x[d, 1 - y, row, :].astype(f32)
            ).astype(bf16)
            high_acc[row, :] = (
                high_acc[row, :].astype(f32) + r1y[d, 1 - x, row, :].astype(f32)
            ).astype(bf16)
            return carry

        lax.fori_loop(0, 8, body, 0)

    def second(self, d):
        self.second_sum(d)
        for copy in self.second_copies(d):
            self.go(copy)

    def third_sum(self, d, target):
        x, y, me, h = self.x, self.y, self.me, self.h
        arrived(self.r2y.at[d], self.s.at[d, 2], self.q.at[d, 2], me, h)
        arrived(self.r2x.at[d], self.s.at[d, 3], self.q.at[d, 3], me, h)
        fin, low, high = self.fin(d), self.low, self.high

        def body(i, carry):
            row = chunk(i)
            target[row, low] = (
                fin[row, low].astype(f32)
                + self.r1x[d, y, row, :].astype(f32)
                + self.r2y[d, row, :].astype(f32)
            ).astype(bf16)
            target[row, high] = (
                fin[row, high].astype(f32)
                + self.r1y[d, x, row, :].astype(f32)
                + self.r2x[d, row, :].astype(f32)
            ).astype(bf16)
            return carry

        lax.fori_loop(0, 8, body, 0)

    def third(self, d):
        fin, z = self.fin(d), self.z
        self.third_sum(d, fin if d else self.out.at[z])
        if d:
            there = index_of((z + d) % ZED, self.y, self.x)
            self.go(remote(fin, self.out.at[z], self.s.at[d, 4], self.q.at[d, 4], there, self.h))

    def last(self):
        for d in (1, 3, 2):
            arrived(
                self.out.at[(self.z + ZED - d) % ZED], self.s.at[d, 4], self.q.at[d, 4], self.me, self.h
            )

    def third_join(self, k):
        fin = self.fin(k)
        self.third_sum(k, fin if k else self.out.at[0])
        near = index_of(self.planes[1], self.y, self.x)
        if k == 1:
            self.go(remote(fin, self.out.at[1], self.s.at[1, 4], self.q.at[1, 4], near, self.h))
        if k > 1:
            outer = (self.z == 0) | (self.z == ZED - 1)
            copy = remote(fin, self.relay.at[3 - k], self.s.at[k, 4], self.q.at[5 - k, 4], near, self.h)
            self.go(copy, outer)

    def join(self, k):
        fin, relay, s, q = self.fin(k), self.relay, self.s, self.q
        inner = (self.z > 0) & (self.z < ZED - 1)

        @pl.when(inner)
        def _():
            arrived(relay.at[k - 2], s.at[k, 4], q.at[k, 4], self.me, self.h)

            def body(i, carry):
                row = chunk(i)
                fin[row, :] = (fin[row, :].astype(f32) + relay[k - 2, row, :].astype(f32)).astype(bf16)
                return carry

            lax.fori_loop(0, 8, body, 0)

        far = index_of(self.planes[k], self.y, self.x)
        self.go(remote(fin, self.out.at[2], s.at[k, 4], q.at[0, 4], far, self.h), inner)

    def joined(self):
        arrived(self.out.at[1], self.s.at[1, 4], self.q.at[1, 4], self.me, self.h)
        arrived(self.out.at[2], self.s.at[0, 4], self.q.at[0, 4], self.me, self.h)


class Combine:
    def __init__(self, t, out, other, summed, landed, ls, s, q, go):
        self.t, self.out, self.other, self.summed, self.landed = t, out, other, summed, landed
        self.ls, self.s, self.q, self.go = ls, s, q, go
        self.x, self.y, self.z, self.h = where_am_i()
        self.me = index_of(self.z, self.y, self.x)

    def begin(self):
        t, h, other = self.t, self.h, self.other
        self.own = {}
        for d in FAR:
            zz = (self.z + d) % ZED
            self.own[d] = pltpu.make_async_copy(t.at[zz, h], self.summed.at[d], self.ls.at[d])
            self.own[d].start()
            self.go(remote(t.at[zz, 1 - h], other.at[d], self.s.at[d, 0], self.q.at[d, 0], self.me, 1 - h))

    def spread(self):
        summed, other = self.summed, self.other
        for d in FAR:
            zz = (self.z + d) % ZED
            self.own[d].wait()
            arrived(other.at[d], self.s.at[d, 0], self.q.at[d, 0], self.me, 1 - self.h)

            def add(turn, carry):
                row = chunk(turn)
                summed[d, row, :] = (
                    summed[d, row, :].astype(f32) + other[d, row, :].astype(f32)
                ).astype(bf16)
                return carry

            lax.fori_loop(0, 8, add, 0)
            if d:
                there = index_of(zz, self.y, self.x)
                self.go(remote(summed.at[d], self.landed.at[d], self.s.at[d, 1], self.q.at[d, 1], there, self.h))

    def total(self):
        summed, landed, out, h = self.summed, self.landed, self.out, self.h
        for d in (1, 3, 2):
            arrived(landed.at[d], self.s.at[d, 1], self.q.at[d, 1], self.me, h)

        def body(turn, carry):
            row = chunk(turn)
            acc = summed[0, row, :].astype(f32)
            for d in (1, 2, 3):
                acc = acc + landed[d, row, :].astype(f32)
            out[h, row, :] = acc.astype(bf16)
            return carry

        lax.fori_loop(0, 8, body, 0)
        self.go(remote(out.at[h], out.at[h], self.s.at[0, 1], self.q.at[0, 1], self.me, 1 - h))

    def done(self):
        arrived(self.out.at[1 - self.h], self.s.at[0, 1], self.q.at[0, 1], self.me, 1 - self.h)


class Join:
    def __init__(self, t, out, other, summed, landed, relay, ls, s, q, go, planes):
        self.t, self.out, self.other, self.summed, self.landed = t, out, other, summed, landed
        self.relay, self.ls, self.s, self.q, self.go, self.planes = relay, ls, s, q, go, planes
        self.x, self.y, self.z, self.h = where_am_i()
        self.me = index_of(self.z, self.y, self.x)
        self.inner = (self.z > 0) & (self.z < ZED - 1)
        self.outer = (self.z == 0) | (self.z == ZED - 1)

    def begin(self):
        self.own = {}
        for k in (2, 3, 1, 0):
            zz = self.planes[k]
            self.own[k] = pltpu.make_async_copy(self.t.at[zz, self.h], self.summed.at[k], self.ls.at[k])
            self.own[k].start()
            self.go(
                remote(self.t.at[zz, 1 - self.h], self.other.at[k], self.s.at[k, 0], self.q.at[k, 0], self.me, 1 - self.h)
            )

    def add(self, k, ref, index):
        summed = self.summed

        def body(turn, carry):
            row = chunk(turn)
            summed[k, row, :] = (
                summed[k, row, :].astype(f32) + ref[index, row, :].astype(f32)
            ).astype(bf16)
            return carry

        lax.fori_loop(0, 8, body, 0)

    def spread(self):
        near = index_of(self.planes[1], self.y, self.x)
        for k in (2, 3, 1, 0):
            self.own[k].wait()
            arrived(self.other.at[k], self.s.at[k, 0], self.q.at[k, 0], self.me, 1 - self.h)
            self.add(k, self.other, k)
            if k == 1:
                self.go(remote(self.summed.at[1], self.landed.at[0], self.s.at[1, 1], self.q.at[1, 1], near, self.h))
            if k > 1:
                copy = remote(
                    self.summed.at[k], self.relay.at[3 - k], self.s.at[k, 1], self.q.at[5 - k, 1], near, self.h
                )
                self.go(copy, self.outer)

    def join(self, k):
        @pl.when(self.inner)
        def _():
            arrived(self.relay.at[k - 2], self.s.at[k, 1], self.q.at[k, 1], self.me, self.h)
            self.add(k, self.relay, k - 2)

        far = index_of(self.planes[k], self.y, self.x)
        copy = remote(self.summed.at[k], self.landed.at[1], self.s.at[k, 1], self.q.at[0, 1], far, self.h)
        self.go(copy, self.inner)

    def total(self):
        summed, landed, out, h = self.summed, self.landed, self.out, self.h
        arrived(landed.at[0], self.s.at[1, 1], self.q.at[1, 1], self.me, h)
        arrived(landed.at[1], self.s.at[0, 1], self.q.at[0, 1], self.me, h)

        def body(turn, carry):
            row = chunk(turn)
            out[h, row, :] = (
                summed[0, row, :].astype(f32)
                + landed[0, row, :].astype(f32)
                + landed[1, row, :].astype(f32)
            ).astype(bf16)
            return carry

        lax.fori_loop(0, 8, body, 0)
        self.go(remote(out.at[h], out.at[h], self.s.at[4, 0], self.q.at[4, 0], self.me, 1 - h))

    def done(self):
        arrived(self.out.at[1 - self.h], self.s.at[4, 0], self.q.at[4, 0], self.me, 1 - self.h)


def back_kernel(
    near, gg, dg, du, hid, t, wo, wm, mid, cot, got, ratio, den,
    zm, d_mid, d_att, home, tb,
    g, r1x, r1y, r2x, r2y, e2, other, summed, landed, w2, pack, d_o, d_qk, d_v,
    q_t, k_t, va, da, dn_t, pack2, nbuf, gbuf, turned, stage,
    ls, fs, bs, gs, gq, cs, cq, e1s, e1r, e2s, e2r,
):
    x, y, z, h = where_am_i()
    me = index_of(z, y, x)
    count = mid.shape[1]
    heads = 16 // mid.shape[0]
    room = dg.shape[1]
    late = []

    def go(copy):
        copy.start()
        late.append(copy)

    def fetch(i):
        cols = pl.ds(pl.multiple_of(((z + ZED - 1 - i) % ZED) * 512, 512), 512)
        return (
            pltpu.make_async_copy(near.at[:, cols], nbuf.at[i % 2], fs.at[i % 2, 0]),
            pltpu.make_async_copy(gg.at[:, cols], gbuf.at[i % 2], fs.at[i % 2, 1]),
        )

    for copy in fetch(0):
        copy.start()
    combine = Combine(t, e2, other, summed, landed, ls, cs, cq, go)
    scatter = Scatter(
        g,
        lambda d: g.at[(z + d) % ZED, 1 - y, x, :, pl.ds(0, g.shape[-1] // 2)],
        lambda d: g.at[(z + d) % ZED, y, 1 - x, :, pl.ds(g.shape[-1] // 2, g.shape[-1] // 2)],
        lambda d: g.at[(z + d) % ZED, y, x],
        zm, r1x, r1y, r2x, r2y, gs, gq, go,
    )
    combine.begin()
    weight = pltpu.make_async_copy(wo, w2, ls.at[4])
    weight.start()
    combine.spread()

    def block(i, carry):
        d = ZED - 1 - i
        zz = (z + d) % ZED

        @pl.when(i < ZED - 1)
        def _():
            for copy in fetch(i + 1):
                copy.start()

        for copy in fetch(i):
            copy.wait()
        for buf, terms in ((nbuf, (dg, du)), (gbuf, (hid,))):
            turned[...] = jnp.transpose(buf[i % 2])
            for term in terms:
                base = {id(dg): 0, id(du): room, id(hid): 2 * room}[id(term)]

                def piece(c, carry):
                    src = pl.ds(pl.multiple_of(c * COLS, COLS), COLS)
                    dst = pl.ds(pl.multiple_of(base + c * COLS, COLS), COLS)
                    res = mix(turned[...], term[:, src], ((1,), (0,))).astype(bf16)
                    for n in range(4):
                        g[zz, n // 2, n % 2, :, dst] = res[n * 128 : (n + 1) * 128, :]
                    return carry

                lax.fori_loop(0, room // COLS, piece, 0)
        @pl.when(i < ZED - 1)
        def _():
            for copy in scatter.first_copies(d):
                copy.start()

        @pl.when((i > 0) & (i < ZED - 1))
        def _():
            scatter.second_sum(d + 1)
            for copy in scatter.second_copies(d + 1):
                copy.start()

        return carry

    lax.fori_loop(0, ZED, block, 0)
    for d in (1, 2, 3):
        late.extend(scatter.first_copies(d))
    for d in (2, 3):
        late.extend(scatter.second_copies(d))
    half = near.shape[1] // 2
    shards = []
    for r in range(2):
        at = pl.ds(r * half, half)
        shards.append(
            (
                pltpu.make_async_copy(wm.at[at, pl.ds(2 * room, 512)], nbuf.at[r], fs.at[r, 0]),
                pltpu.make_async_copy(
                    wm.at[at, pl.ds(2 * room + 512, room - 512)],
                    gbuf.at[r, :, pl.ds(0, room - 512)],
                    fs.at[r, 1],
                ),
            )
        )
        for copy in shards[r]:
            copy.start()
    weight.wait()
    scatter.third(3)
    combine.total()
    combine.done()

    for mb in range(mid.shape[0]):

        def body(turn, carry):
            row = chunk(turn)
            m = mid[mb, row, :]
            scale = lax.rsqrt(jnp.mean(m * m, axis=-1, keepdims=True) + epsilon)
            hat = m * scale
            e = e2[mb, row, :].astype(f32)
            d_m = cot[mb, row, :].astype(f32) + scale * (
                e - hat * jnp.mean(e * hat, axis=-1, keepdims=True)
            )
            d_mid[mb, row, :] = d_m
            d_att[pl.ds(pl.multiple_of(mb * count + turn * 16, 16), 16), :] = d_m.astype(bf16)
            return carry

        lax.fori_loop(0, count // 16, body, 0)
    for c in range(heads * DV // COLS):
        val = mix(d_att[...], w2[:, c * COLS : (c + 1) * COLS], ((1,), (0,))).astype(bf16)
        for mb in range(16 // heads):
            for i in range(COLS // DV):
                pack[c * (COLS // DV) + i + heads * mb, :, :] = val[
                    mb * count : (mb + 1) * count, i * DV : (i + 1) * DV
                ]

    def window(source):
        return d_o.at[pl.ds(pl.multiple_of(source * count, count), count)]

    own = pltpu.make_async_copy(pack.at[me], window(me), ls.at[5])
    own.start()
    for d in range(1, 16):
        there = (me + d) % 16
        go(remote(pack.at[there], window(me), e1s.at[d], e1r.at[d], there, h))
    scatter.second(1)
    scatter.first(0)
    scatter.third(2)
    stored = {}
    for n in range(2 * half // COLS):
        r, c = n // (half // COLS), n % (half // COLS)
        if c == 0:
            for copy in shards[r]:
                copy.wait()
        if n > 1:
            stored[n - 2].wait()
        at = slice(c * COLS, (c + 1) * COLS)
        stage[n % 2, :, :] = (
            mix(hid[:, 0:512], nbuf[r, at, :], ((1,), (1,)))
            + mix(hid[:, 512:room], gbuf[r, at, 0 : room - 512], ((1,), (1,)))
        ).astype(bf16)
        stored[n] = pltpu.make_async_copy(
            stage.at[n % 2], tb.at[:, pl.ds(n * COLS, COLS)], bs.at[n % 2]
        )
        stored[n].start()
    own.wait()
    for d in range(1, 16):
        arrived(window((me + 16 - d) % 16), e1s.at[d], e1r.at[d], me, h)
    attend_back_body(got, ratio, den, d_o, d_qk, d_v, q_t, k_t, va, da, dn_t)
    for b in range(16):
        pack2[b, 0 : 2 * F, :] = d_qk[:, b * count : (b + 1) * count].astype(bf16)
        pack2[b, 2 * F :, :] = d_v[b * count : (b + 1) * count, :].astype(bf16)
    own = pltpu.make_async_copy(pack2.at[me], home.at[me], ls.at[5])
    own.start()
    for d in range(1, 16):
        there = (me + d) % 16
        go(remote(pack2.at[there], home.at[me], e2s.at[d], e2r.at[d], there, h))
    stored[2 * half // COLS - 2].wait()
    stored[2 * half // COLS - 1].wait()
    scatter.third(1)
    scatter.second(0)
    scatter.third(0)
    own.wait()
    for d in range(1, 16):
        arrived(home.at[(me + 16 - d) % 16], e2s.at[d], e2r.at[d], me, h)
    scatter.last()
    for copy in late:
        copy.wait_send()


def scatter_room(wide):
    return [
        pltpu.VMEM((4, 2, 128, wide // 2), bf16),
        pltpu.VMEM((4, 2, 128, wide // 2), bf16),
        pltpu.VMEM((4, 128, wide // 2), bf16),
        pltpu.VMEM((4, 128, wide // 2), bf16),
    ]


def back(near, gg, dg, du, hid, t, wo, wm, mid, cot, got, ratio, den):
    mbs, count, wide = cot.shape
    depth = 16 * count
    shape = jax.ShapeDtypeStruct
    cols = 3 * dg.shape[1]
    line = pltpu.VMEM((ZED, count, wide), bf16)
    return pl.pallas_call(
        back_kernel,
        out_shape=(
            shape((ZED, 128, cols), bf16),
            shape(cot.shape, f32),
            shape((mbs * count, wide), bf16),
            shape((16, 2 * F + DV, count), bf16),
            shape(near.shape, bf16),
        ),
        in_specs=[ANY] * 2 + [VMEM] * 3 + [ANY] * 3 + [VMEM] * 5,
        out_specs=(VMEM,) * 4 + (ANY,),
        scratch_shapes=[pltpu.VMEM((ZED, 2, 2, 128, cols), bf16)] + scatter_room(cols) + [
            pltpu.VMEM(cot.shape, bf16), line, line, line,
            pltpu.VMEM(wo.shape, bf16),
            pltpu.VMEM((16, count, DV), bf16),
            pltpu.VMEM((depth, DV), bf16),
            pltpu.VMEM((2 * F, depth), f32),
            pltpu.VMEM((depth, DV), f32),
            pltpu.VMEM((F, depth), bf16),
            pltpu.VMEM((F, depth), bf16),
            pltpu.VMEM((depth, 2 * DV), bf16),
            pltpu.VMEM((depth, 2 * DV), bf16),
            pltpu.VMEM((DV, depth), bf16),
            pltpu.VMEM((16, 2 * F + DV, count), bf16),
            pltpu.VMEM((2, near.shape[0], 512), bf16),
            pltpu.VMEM((2, near.shape[0], 512), bf16),
            pltpu.VMEM((512, near.shape[0]), bf16),
            pltpu.VMEM((2, near.shape[0], COLS), bf16),
            DMA((6,)), DMA((2, 2)), DMA((2,)), DMA((4, 5)), DMA((4, 5)), DMA((4, 2)), DMA((4, 2)),
            DMA((16,)), DMA((16,)), DMA((16,)), DMA((16,)),
        ],
        compiler_params=params(),
        name="back",
    )(near, gg, dg, du, hid, t, wo, wm, mid, cot, got, ratio, den)


def end_kernel(
    t, home, xh, d_att, heads_out, wa1, d_mid, xin, mid,
    za, d_in, outputs,
    g, r1x, r1y, r2x, r2y, relay, branch, other, summed, landed, relayed, w1, dqk_t, dqkv, part, swap,
    ls, gs, gq, cs, cq, ws, wr,
):
    x, y, z, h = where_am_i()
    me = index_of(z, y, x)
    mbs, count, wide = xin.shape
    heads = 16 // mbs
    qk, vv = 2 * heads * F, heads * DV
    late = []

    def go(copy, true=None):
        if true is None:
            copy.start()
        else:
            pl.when(true)(copy.start)
        late.append((true, copy))

    planes = (z, z + 1 - 2 * (z % 2), ZED - 1 - z, (z + 2) % ZED)
    combine = Join(t, branch, other, summed, landed, relayed, ls, cs, cq, go, planes)
    scatter = Scatter(
        g,
        lambda k: g.at[planes[k], 1 - y, x, :, pl.ds(0, g.shape[-1] // 2)],
        lambda k: g.at[planes[k], y, 1 - x, :, pl.ds(g.shape[-1] // 2, g.shape[-1] // 2)],
        lambda k: g.at[planes[k], y, x],
        za, r1x, r1y, r2x, r2y, gs, gq, go, planes, relay,
    )
    combine.begin()
    weight = pltpu.make_async_copy(wa1, w1, ls.at[4])
    weight.start()
    for mb in range(mbs):
        cols = slice(mb * count, (mb + 1) * count)
        for k in range(heads):
            block = home.at[k + heads * mb]
            dqk_t[k * F : (k + 1) * F, cols] = block[0:F, :].astype(f32)
            dqk_t[(heads + k) * F : (heads + k + 1) * F, cols] = block[F : 2 * F, :].astype(f32)
            dqkv[cols, qk + k * DV : qk + (k + 1) * DV] = block[2 * F :, :]
    dqkv[:, 0:qk] = jnp.transpose(dqk_t[...]).astype(bf16)

    def terms(k):
        zz = planes[k]

        def body(n, carry):
            at = pl.ds(pl.multiple_of((zz * 4 + n) * 128, 128), 128)
            g[zz, n // 2, n % 2, :, 0 : qk + vv] = mix(xh[:, at], dqkv[...], ((0,), (0,))).astype(bf16)
            g[zz, n // 2, n % 2, :, qk + vv :] = mix(d_att[:, at], heads_out[...], ((0,), (0,))).astype(bf16)
            return carry

        lax.fori_loop(0, 4, body, 0)

    terms(2)
    scatter.first(2)
    combine.spread()
    terms(3)
    scatter.first(3)
    scatter.second(2)
    terms(1)
    scatter.first(1)
    weight.wait()
    for c in range(wide // COLS):
        cols = pl.ds(c * COLS, COLS)
        part[:, c * COLS : (c + 1) * COLS] = mix(dqkv[...], w1[c * COLS : (c + 1) * COLS, :], ((1,), (1,)))
        go(remote(part.at[:, cols], swap.at[:, cols], ws.at[c], wr.at[c], me, 1 - h))
    scatter.second(3)
    combine.join(3)
    terms(0)
    scatter.third_join(2)
    combine.join(2)
    for c in range(wide // COLS):
        cols = pl.ds(c * COLS, COLS)
        arrived(swap.at[:, cols], ws.at[c], wr.at[c], me, 1 - h)
    for mb in range(mbs):

        def body(turn, carry):
            row = chunk(turn)
            flat = pl.ds(pl.multiple_of(mb * count + turn * 16, 16), 16)
            v = xin[mb, row, :].astype(f32)
            scale = lax.rsqrt(jnp.mean(v * v, axis=-1, keepdims=True) + epsilon)
            hat = v * scale
            e = part[flat, :] + swap[flat, :]
            d_in[mb, row, :] = (
                d_mid[mb, row, :] + scale * (e - hat * jnp.mean(e * hat, axis=-1, keepdims=True))
            ).astype(bf16)
            return carry

        lax.fori_loop(0, count // 16, body, 0)
    scatter.second(1)
    scatter.first(0)
    scatter.third_join(3)
    scatter.join(3)
    scatter.third_join(1)
    scatter.join(2)
    combine.total()
    scatter.second(0)
    combine.done()
    for mb in range(mbs):

        def body(turn, carry):
            row = chunk(turn)
            outputs[mb, row, :] = (mid[mb, row, :] + branch[mb, row, :].astype(f32)).astype(bf16)
            return carry

        lax.fori_loop(0, count // 16, body, 0)
    scatter.third_join(0)
    scatter.joined()
    for true, copy in late:
        if true is None:
            copy.wait_send()
        else:
            pl.when(true)(copy.wait_send)


def end(t, home, xh, d_att, heads_out, wa1, d_mid, xin, mid):
    mbs, count, wide = xin.shape
    shape = jax.ShapeDtypeStruct
    cols = wa1.shape[1] + heads_out.shape[1]
    line = pltpu.VMEM((ZED, count, wide), bf16)
    return pl.pallas_call(
        end_kernel,
        out_shape=(shape((3, 128, cols), bf16), shape(xin.shape, bf16), shape(xin.shape, bf16)),
        in_specs=[ANY] + [VMEM] * 4 + [ANY] + [VMEM] * 3,
        out_specs=(VMEM,) * 3,
        scratch_shapes=[pltpu.VMEM((ZED, 2, 2, 128, cols), bf16)] + scatter_room(cols) + [
            pltpu.VMEM((2, 128, cols), bf16),
            pltpu.VMEM(xin.shape, bf16), line, line,
            pltpu.VMEM((2, count, wide), bf16),
            pltpu.VMEM((2, count, wide), bf16),
            pltpu.VMEM(wa1.shape, bf16),
            pltpu.VMEM((mbs * count, mbs * count), f32),
            pltpu.VMEM((mbs * count, wa1.shape[1]), bf16),
            pltpu.VMEM((mbs * count, wide), f32),
            pltpu.VMEM((mbs * count, wide), f32),
            DMA((6,)), DMA((4, 5)), DMA((4, 5)), DMA((5, 2)), DMA((5, 2)),
            DMA((wide // COLS,)), DMA((wide // COLS,)),
        ],
        compiler_params=params(),
        name="end",
    )(t, home, xh, d_att, heads_out, wa1, d_mid, xin, mid)


def finish_kernel(
    zm, za, wq, wk, wv, wg, wu, g1, g2, o_q, o_k, o_v, o_out, o_g, o_u, o_d, gains
):
    units = wg.shape[1] // ZED
    room = zm.shape[2] // 3
    nq, nv = wq.shape[1], wv.shape[1]
    lanes = g1.shape[1]
    scale1, scale2 = column(g1), column(g2)

    def total(cols):
        acc = za[0, :, cols].astype(f32)
        for n in range(1, za.shape[0]):
            acc = acc + za[n, :, cols].astype(f32)
        return acc

    first = jnp.zeros((zm.shape[1], lanes), f32)
    at = 0
    for w, out in ((wq, o_q), (wk, o_k), (wv, o_v)):
        for c in range(w.shape[1] // lanes):
            cols = slice(c * lanes, (c + 1) * lanes)
            value = total(slice(at + c * lanes, at + (c + 1) * lanes))
            out[:, cols] = value * scale1
            first = first + value * w[:, cols].astype(f32)
        at += w.shape[1]
    for c in range(nv // lanes):
        o_out[c * lanes : (c + 1) * lanes, :] = jnp.transpose(
            total(slice(at + c * lanes, at + (c + 1) * lanes))
        )
    second = jnp.zeros((zm.shape[1], lanes), f32)
    for n in range(ZED):
        for base, w, out in ((0, wg, o_g), (room, wu, o_u)):
            for c in range(0, units, lanes):
                size = min(lanes, units - c)
                cols = slice(n * units + c, n * units + c + size)
                value = zm[n, :, base + c : base + c + size].astype(f32)
                out[:, cols] = value * scale2[:, 0:size]
                prod = value * w[:, cols].astype(f32)
                if size == lanes:
                    second = second + prod
                else:
                    second = second + jnp.concatenate(
                        [prod, jnp.zeros((prod.shape[0], lanes - size), f32)], axis=1
                    )
        for c in range(0, units, lanes):
            size = min(lanes, units - c)
            value = jnp.transpose(zm[n, :, 2 * room + c : 2 * room + c + lanes].astype(f32))
            o_d[n * units + c : n * units + c + size, :] = value[0:size, :]
    gains[0:1, :] = jnp.sum(jnp.transpose(first), axis=0, keepdims=True)
    gains[1:2, :] = jnp.sum(jnp.transpose(second), axis=0, keepdims=True)


def finish(zm, za, wq, wk, wv, wg, wu, g1, g2, w_out, w_down):
    shape = lambda w: jax.ShapeDtypeStruct(w.shape, f32)
    return pl.pallas_call(
        finish_kernel,
        out_shape=(
            shape(wq), shape(wk), shape(wv), shape(w_out), shape(wg), shape(wu), shape(w_down),
            jax.ShapeDtypeStruct((2, 128), f32),
        ),
        in_specs=[VMEM] * 9,
        out_specs=(VMEM,) * 8,
        compiler_params=pltpu.CompilerParams(vmem_limit_bytes=VMEM_LIMIT),
        name="finish",
    )(zm, za, wq, wk, wv, wg, wu, g1, g2)


def fast(
    inputs, norm_gain1, w_query, w_key, w_value, w_out, norm_gain2, w_gate, w_up, w_down, cotangent
):
    mbs, count, wide = inputs.shape
    rows = w_query.shape[0]
    gain1, gain2 = norm_gain1.reshape(1, rows), norm_gain2.reshape(1, rows)
    wa1, w_o, wm, gg, got, ratio, den, heads_out, middle, near, xh1 = front(
        w_query, w_key, w_value, w_out, w_gate, w_up, w_down, gain1, gain2, cotangent, inputs
    )
    room = wm.shape[1] // 3
    w_g, w_u, w_d = wm[:, :room], wm[:, room : 2 * room], wm[:, 2 * room :]
    many = ZED * mbs * count
    n2 = near.reshape(many, wide)
    up_g = gg.reshape(many, wide)
    gate = mix(n2, w_g, ((1,), (0,)))
    up = mix(n2, w_u, ((1,), (0,)))
    d_hidden = mix(up_g, w_d, ((1,), (0,)))
    sig = jax.nn.sigmoid(gate)
    silu = gate * sig
    hidden = (silu * up).astype(bf16)
    d_gate = (d_hidden * up * sig * (1.0 + gate * (1.0 - sig))).astype(bf16)
    d_up = (d_hidden * silu).astype(bf16)
    d_n2 = (mix(d_gate, w_g, ((1,), (1,))) + mix(d_up, w_u, ((1,), (1,)))).astype(bf16)
    lines = (ZED, mbs, count, wide)
    zm, d_mid, d_att, home, branch = back(
        n2, up_g, d_gate, d_up, hidden, d_n2.reshape(lines), w_o, wm, middle, cotangent, got, ratio, den
    )
    za, input_grad, outputs = end(
        branch.reshape(lines), home, xh1, d_att, heads_out, wa1, d_mid, inputs, middle
    )
    o_q, o_k, o_v, o_out, o_g, o_u, o_d, gains = finish(
        zm, za, w_query, w_key, w_value, w_gate, w_up,
        gain1, gain2, w_out, w_down,
    )
    gains = lax.psum(gains, "head")
    return (outputs, input_grad, gains[0], o_q, o_k, o_v, o_out, gains[1], o_g, o_u, o_d)


def solution(mesh):
    return jax.shard_map(
        fast if mesh.shape["seq"] == 16 else local,
        mesh=mesh,
        in_specs=(
            P(None, "seq", None),
            P("seq"),
            P("seq", "head"),
            P("seq", "head"),
            P("seq", "head"),
            P("head", "seq"),
            P("seq"),
            P("seq", "head"),
            P("seq", "head"),
            P("head", "seq"),
            P(None, "seq", None),
        ),
        out_specs=(
            P(None, "seq", None),
            P(None, "seq", None),
            P("seq"),
            P("seq", "head"),
            P("seq", "head"),
            P("seq", "head"),
            P("head", "seq"),
            P("seq"),
            P("seq", "head"),
            P("seq", "head"),
            P("head", "seq"),
        ),
        check_vma=False,
    )
```

```python
import jax
import jax.numpy as jnp
from jax import lax
from jax.experimental import pallas as pl
from jax.experimental.pallas import tpu as pltpu
from jax.sharding import PartitionSpec as P

F = 16
DV = 128


epsilon = 1e-05
highest = lax.Precision.HIGHEST


def entering(part, axis, combine, identity, reverse):
    count = lax.axis_size(axis)
    place = lax.axis_index(axis)
    ahead = count - 1 - place if reverse else place
    gathered = jax.tree.map(lambda a: lax.all_gather(a, axis), part)
    state = jax.tree.map(lambda a, e: jnp.zeros_like(a) + jnp.asarray(e, a.dtype), part, identity)

    def one(turn, state):
        source = count - 1 - turn if reverse else turn
        return combine(
            state, jax.tree.map(lambda a: lax.dynamic_index_in_dim(a, source, 0, False), gathered)
        )

    return lax.fori_loop(0, ahead, one, state)


def rms_apply(values, gain):
    scale = lax.rsqrt(jnp.mean(values * values, axis=-1, keepdims=True) + epsilon)
    return values * scale * gain


def feature_map(projected):
    count = projected.shape[0]
    pieces = projected.reshape(count, -1, F)
    square = (pieces[:, :, :, None] * pieces[:, :, None, :]).reshape(count, pieces.shape[1], F * F)
    return jnp.concatenate(
        [jnp.ones_like(pieces[:, :, :1]), pieces * F ** (-0.25), square * (2.0 * F) ** (-0.5)],
        axis=-1,
    )


def swiglu(gate, up_part):
    return jax.nn.silu(gate) * up_part


def round_trip(values):
    return lax.optimization_barrier(values.astype(jnp.bfloat16)).astype(jnp.float32)


def add_pair(earlier, later):
    return (earlier[0] + later[0], earlier[1] + later[1])


def block_pass(tokens, upstream, gathered):
    gain_one, query_w, key_w, value_w, out_w, gain_two, gate_w, up_w, down_w = gathered
    f32 = jnp.float32
    bf16 = jnp.bfloat16
    stream = tokens.astype(f32)
    count = stream.shape[0]
    normed_f, norm_one_pull = jax.vjp(rms_apply, stream, gain_one.astype(f32))
    normed = normed_f.astype(bf16)
    queries = jnp.dot(normed, query_w, preferred_element_type=f32)
    keys_all = jnp.dot(normed, key_w, preferred_element_type=f32)
    values = jnp.dot(normed, value_w, preferred_element_type=f32).astype(bf16)
    query_feat_f, query_pull = jax.vjp(feature_map, queries)
    key_feat_f, key_pull = jax.vjp(feature_map, keys_all)
    query_feat = jnp.transpose(query_feat_f.astype(bf16), (1, 0, 2))
    key_feat = jnp.transpose(key_feat_f.astype(bf16), (1, 0, 2))
    value_heads = jnp.transpose(values.reshape(count, -1, DV), (1, 0, 2))
    causal = (jnp.arange(count)[:, None] >= jnp.arange(count)[None, :]).astype(f32)
    scores = jnp.einsum("htf,hsf->hts", query_feat, key_feat, preferred_element_type=f32) * causal
    weighted = scores.astype(bf16)
    num_local = jnp.einsum("hts,hsd->htd", weighted, value_heads, preferred_element_type=f32)
    den_local = jnp.sum(weighted.astype(f32), axis=-1)
    states = jnp.einsum("hsf,hsd->hfd", key_feat, value_heads, preferred_element_type=f32)
    totals = jnp.sum(key_feat.astype(f32), axis=1)
    state_before, total_before = entering(
        (states, totals), "seq", add_pair, (jnp.zeros_like(states), jnp.zeros_like(totals)), False
    )
    query_wide = query_feat.astype(f32)
    numer = num_local + jnp.einsum("htf,hfd->htd", query_wide, state_before, precision=highest)
    denom = den_local + jnp.einsum("htf,hf->ht", query_wide, total_before, precision=highest)
    ratio = numer / denom[..., None]
    heads_out = jnp.transpose(ratio, (1, 0, 2)).reshape(count, -1).astype(bf16)
    attended = lax.psum(jnp.dot(heads_out, out_w, preferred_element_type=f32), "head")
    middle = stream + attended
    normed_two_f, norm_two_pull = jax.vjp(rms_apply, middle, gain_two.astype(f32))
    normed_two = normed_two_f.astype(bf16)
    gate = jnp.dot(normed_two, gate_w, preferred_element_type=f32)
    up_part = jnp.dot(normed_two, up_w, preferred_element_type=f32)
    active, active_pull = jax.vjp(swiglu, gate, up_part)
    hidden = active.astype(bf16)
    branch = lax.psum(
        jnp.dot(hidden, down_w, preferred_element_type=f32).astype(jnp.bfloat16), "head"
    ).astype(jnp.float32)
    result = (middle + branch).astype(bf16)
    grad_down = jnp.dot(hidden.T, upstream, preferred_element_type=f32)
    d_hidden = jnp.dot(upstream, down_w.T, preferred_element_type=f32)
    d_gate_f, d_up_f = active_pull(d_hidden)
    d_gate = d_gate_f.astype(bf16)
    d_up = d_up_f.astype(bf16)
    grad_gate = jnp.dot(normed_two.T, d_gate, preferred_element_type=f32)
    grad_up = jnp.dot(normed_two.T, d_up, preferred_element_type=f32)
    d_normed_two = lax.psum(
        jnp.dot(d_gate, gate_w.T, preferred_element_type=f32)
        + jnp.dot(d_up, up_w.T, preferred_element_type=f32),
        "head",
    )
    d_middle_norm, grad_gain2 = norm_two_pull(d_normed_two)
    d_middle = upstream.astype(f32) + d_middle_norm
    d_attended = d_middle.astype(bf16)
    grad_out = jnp.dot(heads_out.T, d_attended, preferred_element_type=f32)
    d_heads = jnp.transpose(
        jnp.dot(d_attended, out_w.T, preferred_element_type=f32).reshape(count, -1, DV), (1, 0, 2)
    )
    d_numer = (d_heads / denom[..., None]).astype(bf16)
    d_denom = -jnp.sum(d_heads * ratio, axis=-1) / denom
    d_numer_wide = d_numer.astype(f32)
    d_before = jnp.einsum("htf,htd->hfd", query_wide, d_numer_wide, precision=highest)
    d_total_before = jnp.einsum("htf,ht->hf", query_wide, d_denom, precision=highest)
    d_state, d_total = entering(
        (d_before, d_total_before),
        "seq",
        add_pair,
        (jnp.zeros_like(d_before), jnp.zeros_like(d_total_before)),
        True,
    )
    d_scores = (
        (
            jnp.einsum("htd,hsd->hts", d_numer, value_heads, preferred_element_type=f32)
            + d_denom[..., None]
        )
        * causal
    ).astype(bf16)
    d_values = jnp.einsum(
        "hts,htd->hsd", weighted, d_numer, preferred_element_type=f32
    ) + jnp.einsum("hsf,hfd->hsd", key_feat.astype(f32), d_state, precision=highest)
    d_query_feat = (
        jnp.einsum("hts,hsf->htf", d_scores, key_feat, preferred_element_type=f32)
        + jnp.einsum("htd,hfd->htf", d_numer_wide, state_before, precision=highest)
        + d_denom[..., None] * total_before[:, None, :]
    )
    d_key_feat = (
        jnp.einsum("hts,htf->hsf", d_scores, query_feat, preferred_element_type=f32)
        + jnp.einsum("hsd,hfd->hsf", value_heads.astype(f32), d_state, precision=highest)
        + d_total[:, None, :]
    )
    d_queries = query_pull(jnp.transpose(round_trip(d_query_feat), (1, 0, 2)))[0].astype(bf16)
    d_keys = key_pull(jnp.transpose(round_trip(d_key_feat), (1, 0, 2)))[0].astype(bf16)
    d_values_flat = jnp.transpose(d_values, (1, 0, 2)).reshape(count, -1).astype(bf16)
    grad_query = jnp.dot(normed.T, d_queries, preferred_element_type=f32)
    grad_key = jnp.dot(normed.T, d_keys, preferred_element_type=f32)
    grad_value = jnp.dot(normed.T, d_values_flat, preferred_element_type=f32)
    d_normed_part = (
        jnp.dot(d_queries, query_w.T, preferred_element_type=f32)
        + jnp.dot(d_keys, key_w.T, preferred_element_type=f32)
        + jnp.dot(d_values_flat, value_w.T, preferred_element_type=f32)
    )
    d_normed = lax.psum(d_normed_part.astype(jnp.bfloat16), "head").astype(jnp.float32)
    d_stream_norm, grad_gain1 = norm_one_pull(d_normed)
    input_grad = (d_middle + d_stream_norm).astype(bf16)
    return (
        result,
        input_grad,
        grad_gain1,
        grad_query,
        grad_key,
        grad_value,
        grad_out,
        grad_gain2,
        grad_gate,
        grad_up,
        grad_down,
    )


def local(
    inputs, norm_gain1, w_query, w_key, w_value, w_out, norm_gain2, w_gate, w_up, w_down, cotangent
):
    micro = inputs.shape[0]
    summed = None
    results = []
    input_grads = []
    for step_index in range(micro):
        gathered = (
            lax.all_gather(norm_gain1, "seq", axis=0, tiled=True),
            lax.all_gather(w_query, "seq", axis=0, tiled=True),
            lax.all_gather(w_key, "seq", axis=0, tiled=True),
            lax.all_gather(w_value, "seq", axis=0, tiled=True),
            lax.all_gather(w_out, "seq", axis=1, tiled=True),
            lax.all_gather(norm_gain2, "seq", axis=0, tiled=True),
            lax.all_gather(w_gate, "seq", axis=0, tiled=True),
            lax.all_gather(w_up, "seq", axis=0, tiled=True),
            lax.all_gather(w_down, "seq", axis=1, tiled=True),
        )
        (
            result,
            input_grad,
            grad_gain1,
            grad_query,
            grad_key,
            grad_value,
            grad_out,
            grad_gain2,
            grad_gate,
            grad_up,
            grad_down,
        ) = block_pass(inputs[step_index], cotangent[step_index], gathered)
        results.append(result)
        input_grads.append(input_grad)
        fresh = (
            lax.psum_scatter(grad_gain1, "seq", scatter_dimension=0, tiled=True),
            lax.psum_scatter(grad_query, "seq", scatter_dimension=0, tiled=True),
            lax.psum_scatter(grad_key, "seq", scatter_dimension=0, tiled=True),
            lax.psum_scatter(grad_value, "seq", scatter_dimension=0, tiled=True),
            lax.psum_scatter(grad_out, "seq", scatter_dimension=1, tiled=True),
            lax.psum_scatter(grad_gain2, "seq", scatter_dimension=0, tiled=True),
            lax.psum_scatter(grad_gate, "seq", scatter_dimension=0, tiled=True),
            lax.psum_scatter(grad_up, "seq", scatter_dimension=0, tiled=True),
            lax.psum_scatter(grad_down, "seq", scatter_dimension=1, tiled=True),
        )
        summed = (
            fresh
            if summed is None
            else tuple((older + newer for older, newer in zip(summed, fresh)))
        )
    return (
        jnp.stack(results),
        jnp.stack(input_grads),
        summed[0],
        summed[1],
        summed[2],
        summed[3],
        summed[4],
        summed[5],
        summed[6],
        summed[7],
        summed[8],
    )


MESH = pl.DeviceIdType.MESH
bf16 = jnp.bfloat16
f32 = jnp.float32
ZED = 4
VMEM_LIMIT = 60 * 1024 * 1024


def where_am_i():
    place = lax.axis_index("seq")
    return place % 2, (place // 2) % 2, place // 4, lax.axis_index("head")


def index_of(z, y, x):
    return (z * 2 + y) * 2 + x


def remote(src, dst, send, recv, place, head):
    return pltpu.make_async_remote_copy(
        src_ref=src, dst_ref=dst, send_sem=send, recv_sem=recv, device_id=(place, head),
        device_id_type=MESH,
    )


def arrived(dst, send, recv, place, head):
    remote(dst, dst, send, recv, place, head).wait_recv()


def params():
    return pltpu.CompilerParams(has_side_effects=True, vmem_limit_bytes=VMEM_LIMIT)


ANY = pl.BlockSpec(memory_space=pl.ANY)
VMEM = pl.BlockSpec(memory_space=pltpu.VMEM)
DMA = pltpu.SemaphoreType.DMA
ORDER = (0, 1, 3, 2)


def mix(a, b, over):
    return lax.dot_general(a, b, (over, ((), ())), preferred_element_type=f32)


CHUNK = 512
COLS = 256


def spread(got, q_t, k_t, va):
    count = got.shape[2]
    for b in range(got.shape[0]):
        q_t[:, b * count : (b + 1) * count] = got[b, 0:F, :]
        k_t[:, b * count : (b + 1) * count] = got[b, F : 2 * F, :]
        va[b * count : (b + 1) * count, 0:DV] = got[b, 2 * F :, :]
    va[:, DV:] = jnp.ones((va.shape[0], va.shape[1] - DV), bf16)


def lower(count):
    return lax.broadcasted_iota(jnp.int32, (count, count), 0) >= lax.broadcasted_iota(
        jnp.int32, (count, count), 1
    )


def attend_rows(qi, q_t, k_t, va, ratio, den, causal):
    qs = slice(qi * CHUNK, (qi + 1) * CHUNK)
    acc = jnp.zeros((CHUNK, va.shape[1]), f32)
    for kj in range(qi + 1):
        ks = slice(kj * CHUNK, (kj + 1) * CHUNK)
        s = mix(q_t[:, qs], k_t[:, ks], ((0,), (0,)))
        p = 1.0 + s * (0.25 + s * (1.0 / 32.0))
        if kj == qi:
            p = jnp.where(causal, p, 0.0)
        acc = acc + mix(p.astype(bf16), va[ks, :], ((1,), (0,)))
    ratio[qs, :] = acc[:, :DV] / acc[:, DV:]
    den[qs, :] = acc[:, DV:]


def column(gain):
    count = gain.shape[1]
    return jnp.transpose(jnp.broadcast_to(gain[...].astype(f32), (count, count)))


def front_kernel(
    wq, wk, wv, w_out, wg, wu, wd, g1, g2, cot, xin,
    wa1, wa2, wm, gg, got_out, ratio_out, den_out, heads_store, middle_out, near, xh_out,
    got, ratio, den, heads_out, middle, xh, fresh, a1, a2, m, w1, w2, pack, q_t, k_t, va, ob, part, other,
    os, ls, zs, zr, us, ur, ps, pr, e1s, e1r, e2s, e2r, ws, wr, ds, dr,
):
    x, y, z, h = where_am_i()
    me = index_of(z, y, x)
    at_x, at_y = index_of(z, y, 1 - x), index_of(z, 1 - y, x)
    count = xin.shape[1]
    heads = 16 // xin.shape[0]
    late = []
    stored = []

    def store(src, dst):
        copy = pltpu.make_async_copy(src, dst, os.at[len(stored)])
        copy.start()
        stored.append(copy)

    def when(true, do):
        if true is None:
            do()
        else:
            pl.when(true)(do)

    def go(copy, true=None):
        when(true, copy.start)
        late.append((true, copy))

    def rows(zz, yy, xx):
        return pl.ds(pl.multiple_of(index_of(zz, yy, xx) * 128, 128), 128)

    mine = rows(z, y, x)
    kept = [
        pltpu.make_async_copy(a1, w1.at[mine], ls.at[0]),
        pltpu.make_async_copy(a2, w2.at[mine], ls.at[1]),
        pltpu.make_async_copy(m.at[z], wm.at[mine], ls.at[2]),
        pltpu.make_async_copy(cot, gg.at[z], ls.at[6]),
    ]
    lanes = g1.shape[1]
    scale = column(g1)
    at = 0
    for w in (wq, wk, wv):
        for c in range(0, w.shape[1], lanes):
            a1[:, at + c : at + c + lanes] = (w[:, c : c + lanes].astype(f32) * scale).astype(bf16)
        at += w.shape[1]
    kept[0].start()
    kept[3].start()
    dest = (w1, w2, wm)
    UP, DOWN = 0, 1
    COT, NEAR = 2, 3

    def held(kind, zz):
        return (lambda: w1.at[rows(zz, y, x)], lambda: w2.at[rows(zz, y, x)],
                lambda: gg.at[zz, h], lambda: near.at[zz, h])[kind]()

    def origin(way, step):
        return (z + ZED - step) % ZED if way == UP else (z + step) % ZED

    def valid(way, step):
        return z >= step if way == UP else z <= ZED - 1 - step

    def pass_on(kind, way, step, src, true):
        there = index_of((z + 1) % ZED if way == UP else (z + ZED - 1) % ZED, y, x)
        block = held(kind, origin(way, step))
        go(remote(block if src is None else src, block, us.at[kind, way, step], ur.at[kind, way, step + 1], there, h), true)

    def offer(kind, src=None):
        pass_on(kind, UP, 0, src, z < ZED - 1)
        pass_on(kind, DOWN, 0, src, z > 0)

    def hop(kind, way, step):
        block = held(kind, origin(way, step))
        when(
            valid(way, step),
            lambda: arrived(block, us.at[kind, way, step], ur.at[kind, way, step], me, h),
        )
        if step < ZED - 1:
            more = z < ZED - 1 if way == UP else z > 0
            pass_on(kind, way, step, None, valid(way, step) & more)

    def across(kind, way, step):
        zz = origin(way, step)
        block = held(kind, zz)
        go(remote(block, block, ds.at[kind, way, step], dr.at[kind, way, step], me, 1 - h), valid(way, step))

    def across_done(kind, way, step):
        zz = origin(way, step)
        block = (gg if kind == COT else near).at[zz, 1 - h]
        when(
            valid(way, step),
            lambda: arrived(block, ds.at[kind, way, step], dr.at[kind, way, step], me, 1 - h),
        )

    def both(do, kind, step):
        do(kind, UP, step)
        do(kind, DOWN, step)

    partner = (z, z + 1 - 2 * (z % 2), ZED - 1 - z, (z + 2) % ZED)

    inner = (z > 0) & (z < ZED - 1)
    outer = (z == 0) | (z == ZED - 1)

    def line(d, true=None):
        zz = partner[d]
        copy = remote(m.at[zz], wm.at[mine], zs.at[d], zr.at[d], index_of(zz, y, x), h)
        go(copy, true)

    def slot_of(way, step):
        return step if way == UP else 3 + step if step else 0

    def plane_set(kind, slot, zz, true):
        block = dest[kind].at[rows(zz, y, x)]
        go(remote(block, block, ps.at[kind, slot, 0], pr.at[kind, slot, 0], at_x, h), true)
        go(remote(block, block, ps.at[kind, slot, 1], pr.at[kind, slot, 1], at_y, h), true)

    def onward_set(kind, slot, zz, true):
        w = dest[kind]
        half = w.shape[1] // 2
        from_x, from_y = rows(zz, y, 1 - x), rows(zz, 1 - y, x)

        def wait():
            arrived(w.at[from_x], ps.at[kind, slot, 0], pr.at[kind, slot, 0], me, h)
            arrived(w.at[from_y], ps.at[kind, slot, 1], pr.at[kind, slot, 1], me, h)

        when(true, wait)
        left = w.at[from_y, pl.ds(0, half)]
        right = w.at[from_x, pl.ds(half, half)]
        go(remote(left, left, ps.at[kind, slot, 2], pr.at[kind, slot, 2], at_x, h), true)
        go(remote(right, right, ps.at[kind, slot, 3], pr.at[kind, slot, 3], at_y, h), true)

    def corner_set(kind, slot, zz, true):
        w = dest[kind]
        half = w.shape[1] // 2
        far = rows(zz, 1 - y, 1 - x)

        def wait():
            arrived(w.at[far, pl.ds(0, half)], ps.at[kind, slot, 2], pr.at[kind, slot, 2], me, h)
            arrived(w.at[far, pl.ds(half, half)], ps.at[kind, slot, 3], pr.at[kind, slot, 3], me, h)

        when(true, wait)

    def plane(kind, way, step):
        if step == 0:
            kept[kind].wait()
        plane_set(kind, slot_of(way, step), origin(way, step), valid(way, step) if step else None)

    def onward(kind, way, step):
        onward_set(kind, slot_of(way, step), origin(way, step), valid(way, step) if step else None)

    def corner(kind):
        corner_set(kind, 0, z, None)
        for step in (1, 2, 3):
            for way in (UP, DOWN):
                corner_set(kind, slot_of(way, step), origin(way, step), valid(way, step))

    def m_plane(d):
        zz = partner[d]
        if d:
            arrived(wm.at[rows(zz, y, x)], zs.at[d], zr.at[d], me, h)
        else:
            kept[2].wait()
        plane_set(2, d, zz, None)

    def m_onward(d):
        onward_set(2, d, partner[d], None)

    offer(0, a1)
    plane(0, UP, 0)
    for c in range(0, w_out.shape[0], lanes):
        a2[:, c : c + lanes] = jnp.transpose(w_out[c : c + lanes, :].astype(f32)).astype(bf16)
    kept[1].start()
    for way in (UP, DOWN):
        hop(0, way, 1)
        plane(0, way, 1)
    units = wg.shape[1] // ZED
    room = m.shape[2] // 3
    scale = column(g2)
    for n in range(ZED):
        for part_at, w in ((0, wg), (room, wu)):
            for c in range(0, units, lanes):
                size = min(lanes, units - c)
                m[n, :, part_at + c : part_at + c + size] = (
                    w[:, n * units + c : n * units + c + size].astype(f32) * scale[:, 0:size]
                ).astype(bf16)
        for c in range(0, units, lanes):
            size = min(lanes, units - c)
            m[n, :, 2 * room + c : 2 * room + c + size] = jnp.transpose(
                wd[n * units + c : n * units + c + size, :].astype(f32)
            ).astype(bf16)
        for part_at in (0, room, 2 * room):
            m[n, :, part_at + units : part_at + room] = jnp.zeros((lanes, room - units), bf16)
    kept[2].start()
    onward(0, UP, 0)
    for way in (UP, DOWN):
        hop(0, way, 2)
        plane(0, way, 2)
    offer(1, a2)
    both(onward, 0, 1)
    for way in (UP, DOWN):
        hop(0, way, 3)
        plane(0, way, 3)
    both(onward, 0, 2)
    both(hop, 1, 1)
    plane(1, UP, 0)
    for mb in range(xin.shape[0]):

        def normed(turn, carry):
            row = pl.ds(pl.multiple_of(turn * 16, 16), 16)
            v = xin[mb, row, :].astype(f32)
            r = lax.rsqrt(jnp.mean(v * v, axis=-1, keepdims=True) + epsilon)
            xh[pl.ds(pl.multiple_of(mb * count + turn * 16, 16), 16), :] = (v * r).astype(bf16)
            return carry

        lax.fori_loop(0, count // 16, normed, 0)
    store(xh, xh_out)
    both(onward, 0, 3)
    both(hop, 1, 2)
    both(hop, 1, 3)
    line(1)
    line(2, inner)
    corner(0)
    out1 = pltpu.make_async_copy(w1, wa1, ls.at[3])
    out1.start()
    kq = mix(xh[...], w1[:, 0 : 2 * heads * F], ((1,), (0,)))
    qk = jnp.transpose(kq).astype(bf16)
    for mb in range(16 // heads):
        for k in range(heads):
            t = k + heads * mb
            cols = slice(mb * count, (mb + 1) * count)
            pack[t, 0:F, :] = qk[k * F : (k + 1) * F, cols]
            pack[t, F : 2 * F, :] = qk[(heads + k) * F : (heads + k + 1) * F, cols]
    for c in range(heads * DV // COLS):
        at = 2 * heads * F + c * COLS
        val = mix(xh[...], w1[:, at : at + COLS], ((1,), (0,))).astype(bf16)
        for mb in range(16 // heads):
            for i in range(COLS // DV):
                t = c * (COLS // DV) + i + heads * mb
                pack[t, 2 * F :, :] = val[mb * count : (mb + 1) * count, i * DV : (i + 1) * DV]
    keep = pltpu.make_async_copy(pack.at[me], got.at[me], ls.at[4])
    keep.start()
    for d in range(1, 16):
        there = (me + d) % 16
        go(remote(pack.at[there], got.at[me], e1s.at[d], e1r.at[d], there, h))
    line(2, outer)
    line(3, inner)
    both(plane, 1, 1)
    onward(1, UP, 0)
    both(plane, 1, 2)
    both(onward, 1, 1)
    both(plane, 1, 3)
    both(onward, 1, 2)
    keep.wait()
    for d in range(1, 16):
        arrived(got.at[(me + 16 - d) % 16], e1s.at[d], e1r.at[d], me, h)
    both(onward, 1, 3)
    store(got, got_out)
    spread(got, q_t, k_t, va)
    causal = lower(CHUNK)
    for qi in range(va.shape[0] // CHUNK):
        attend_rows(qi, q_t, k_t, va, ratio, den, causal)
    for b in range(16):
        ob[b, :, :] = ratio[b * count : (b + 1) * count, :].astype(bf16)

    store(ratio, ratio_out)
    store(den, den_out)

    def window(source):
        return heads_out.at[
            pl.ds(pl.multiple_of((source // heads) * count, count), count),
            pl.ds(pl.multiple_of((source % heads) * DV, DV), DV),
        ]

    keep = pltpu.make_async_copy(ob.at[me], window(me), ls.at[4])
    keep.start()
    for d in range(1, 16):
        there = (me + d) % 16
        go(remote(ob.at[there], window(me), e2s.at[d], e2r.at[d], there, h))
    line(3, outer)
    offer(COT, cot.at[h])
    m_plane(0)
    m_plane(1)
    corner(1)
    out2 = pltpu.make_async_copy(w2, wa2, ls.at[5])
    out2.start()
    keep.wait()
    for d in range(1, 16):
        arrived(window((me + 16 - d) % 16), e2s.at[d], e2r.at[d], me, h)
    store(heads_out, heads_store)
    wide = part.shape[1]
    for c in range(wide // COLS):
        cols = pl.ds(c * COLS, COLS)
        part[:, c * COLS : (c + 1) * COLS] = mix(
            heads_out[...], w2[c * COLS : (c + 1) * COLS, :], ((1,), (1,))
        )
        go(remote(part.at[:, cols], other.at[:, cols], ws.at[c], wr.at[c], me, 1 - h))
    m_onward(0)
    both(hop, COT, 1)
    m_plane(2)
    for c in range(wide // COLS):
        cols = pl.ds(c * COLS, COLS)
        arrived(other.at[:, cols], ws.at[c], wr.at[c], me, 1 - h)

    def one(mb):
        def body(turn, carry):
            row = pl.ds(pl.multiple_of(turn * 16, 16), 16)
            flat = pl.ds(pl.multiple_of(mb * count + turn * 16, 16), 16)
            mid = xin[mb, row, :].astype(f32) + (part[flat, :] + other[flat, :])
            middle[mb, row, :] = mid
            scale = lax.rsqrt(jnp.mean(mid * mid, axis=-1, keepdims=True) + epsilon)
            fresh[mb, row, :] = (mid * scale).astype(bf16)
            return carry

        lax.fori_loop(0, count // 16, body, 0)

    one(h)
    offer(NEAR, fresh.at[h])
    one(1 - h)
    store(middle, middle_out)
    store(fresh, near.at[z])
    m_onward(1)
    both(hop, COT, 2)
    m_plane(3)
    kept[3].wait()
    both(across, COT, 1)
    both(across, COT, 2)
    both(hop, NEAR, 1)
    both(across, NEAR, 1)
    m_onward(2)
    both(hop, COT, 3)
    both(across, COT, 3)
    both(hop, NEAR, 2)
    both(across, NEAR, 2)
    m_onward(3)
    both(hop, NEAR, 3)
    both(across, NEAR, 3)
    for d in range(4):
        corner_set(2, d, partner[d], None)
    for kind in (NEAR, COT):
        for step in (1, 2, 3):
            both(across_done, kind, step)
    out1.wait()
    out2.wait()
    for copy in stored:
        copy.wait()
    for true, copy in late:
        when(true, copy.wait_send)


def front(wq, wk, wv, w_out, wg, wu, wd, g1, g2, cot, xin):
    mbs, count, wide = xin.shape
    depth = 16 * count
    wide1, wide2 = wq.shape[1] + wk.shape[1] + wv.shape[1], w_out.shape[0]
    wide3 = 3 * (-(-wg.shape[1] // ZED // 256) * 256)
    shape = jax.ShapeDtypeStruct
    return pl.pallas_call(
        front_kernel,
        out_shape=(
            shape((wide, wide1), bf16),
            shape((wide, wide2), bf16),
            shape((wide, wide3), bf16),
            shape((ZED,) + cot.shape, bf16),
            shape((16, 2 * F + DV, count), bf16),
            shape((depth, DV), f32),
            shape((depth, DV), f32),
            shape((mbs * count, wide2), bf16),
            shape(xin.shape, f32),
            shape((ZED,) + xin.shape, bf16),
            shape((mbs * count, wide), bf16),
        ),
        in_specs=[VMEM] * 9 + [ANY] + [VMEM],
        out_specs=(ANY,) * 11,
        scratch_shapes=[
            pltpu.VMEM((16, 2 * F + DV, count), bf16),
            pltpu.VMEM((depth, DV), f32),
            pltpu.VMEM((depth, DV), f32),
            pltpu.VMEM((mbs * count, wide2), bf16),
            pltpu.VMEM(xin.shape, f32),
            pltpu.VMEM((mbs * count, wide), bf16),
            pltpu.VMEM(xin.shape, bf16),
            pltpu.VMEM((wq.shape[0], wide1), bf16),
            pltpu.VMEM((wq.shape[0], wide2), bf16),
            pltpu.VMEM((ZED, wq.shape[0], wide3), bf16),
            pltpu.VMEM((wide, wide1), bf16),
            pltpu.VMEM((wide, wide2), bf16),
            pltpu.VMEM((16, 2 * F + DV, count), bf16),
            pltpu.VMEM((F, depth), bf16),
            pltpu.VMEM((F, depth), bf16),
            pltpu.VMEM((depth, 2 * DV), bf16),
            pltpu.VMEM((16, count, DV), bf16),
            pltpu.VMEM((mbs * count, wide), f32),
            pltpu.VMEM((mbs * count, wide), f32),
            DMA((8,)), DMA((7,)), DMA((4,)), DMA((4,)), DMA((4, 2, 4)), DMA((4, 2, 4)), DMA((3, 7, 4)), DMA((3, 7, 4)),
            DMA((16,)), DMA((16,)), DMA((16,)), DMA((16,)),
            DMA((wide // COLS,)), DMA((wide // COLS,)), DMA((4, 2, 4)), DMA((4, 2, 4)),
        ],
        compiler_params=params(),
        name="front",
    )(wq, wk, wv, w_out, wg, wu, wd, g1, g2, cot, xin)


def attend_back_body(got, ratio, den, d_o, d_qk, d_v, q_t, k_t, va, da, dn_t):
    spread(got, q_t, k_t, va)
    depth = va.shape[0]
    lane = lax.broadcasted_iota(jnp.int32, (CHUNK, DV), 1)
    for qi in range(depth // CHUNK):
        qs = slice(qi * CHUNK, (qi + 1) * CHUNK)
        dn = d_o[qs, :].astype(f32) / den[qs, :]
        dd = -jnp.sum(dn * ratio[qs, :], axis=-1, keepdims=True)
        big = dd.astype(bf16).astype(f32)
        da[qs, 0:DV] = dn.astype(bf16)
        da[qs, DV:] = jnp.where(lane == 0, big, jnp.where(lane == 1, dd - big, 0.0)).astype(bf16)
        dn_t[:, qs] = jnp.transpose(dn).astype(bf16)
    causal = lower(CHUNK)
    for kj in range(depth // CHUNK):
        ks = slice(kj * CHUNK, (kj + 1) * CHUNK)
        acc_k = jnp.zeros((F, CHUNK), f32)
        acc_v = jnp.zeros((DV, CHUNK), f32)
        for qi in range(kj, depth // CHUNK):
            qs = slice(qi * CHUNK, (qi + 1) * CHUNK)
            s = mix(q_t[:, qs], k_t[:, ks], ((0,), (0,)))
            p = 1.0 + s * (0.25 + s * (1.0 / 32.0))
            d_s = mix(da[qs, :], va[ks, :], ((1,), (1,))) * (0.25 + s * (1.0 / 16.0))
            if kj == qi:
                p = jnp.where(causal, p, 0.0)
                d_s = jnp.where(causal, d_s, 0.0)
            d_s = d_s.astype(bf16)
            acc_v = acc_v + mix(dn_t[:, qs], p.astype(bf16), ((1,), (0,)))
            acc_k = acc_k + mix(q_t[:, qs], d_s, ((1,), (0,)))
            d_q = mix(k_t[:, ks], d_s, ((1,), (1,)))
            d_qk[0:F, qs] = d_q if kj == 0 else d_qk[0:F, qs] + d_q
        d_qk[F : 2 * F, ks] = acc_k
        d_v[ks, :] = jnp.transpose(acc_v)


def chunk(turn):
    return pl.ds(pl.multiple_of(turn * 16, 16), 16)


class Scatter:
    def __init__(self, g, low_acc, high_acc, fin, out, r1x, r1y, r2x, r2y, s, q, go, planes=None, relay=None):
        self.planes, self.relay = planes, relay
        self.g, self.low_acc, self.high_acc, self.fin, self.out = g, low_acc, high_acc, fin, out
        self.r1x, self.r1y, self.r2x, self.r2y, self.s, self.q = r1x, r1y, r2x, r2y, s, q
        self.go = go
        self.x, self.y, self.z, self.h = where_am_i()
        self.me = index_of(self.z, self.y, self.x)
        self.at_x = index_of(self.z, self.y, 1 - self.x)
        self.at_y = index_of(self.z, 1 - self.y, self.x)
        self.half = r1x.shape[-1]
        self.low, self.high = pl.ds(0, self.half), pl.ds(self.half, self.half)

    def plane(self, d):
        return (self.z + d) % ZED if self.planes is None else self.planes[d]

    def first_copies(self, d):
        zz, x, y, g = self.plane(d), self.x, self.y, self.g
        return (
            remote(g.at[zz, :, 1 - x, :, self.low], self.r1x.at[d], self.s.at[d, 0], self.q.at[d, 0], self.at_x, self.h),
            remote(g.at[zz, 1 - y, :, :, self.high], self.r1y.at[d], self.s.at[d, 1], self.q.at[d, 1], self.at_y, self.h),
        )

    def first(self, d):
        for copy in self.first_copies(d):
            self.go(copy)

    def second_copies(self, d):
        return (
            remote(self.low_acc(d), self.r2y.at[d], self.s.at[d, 2], self.q.at[d, 2], self.at_y, self.h),
            remote(self.high_acc(d), self.r2x.at[d], self.s.at[d, 3], self.q.at[d, 3], self.at_x, self.h),
        )

    def second_sum(self, d):
        x, y, me, h, r1x, r1y = self.x, self.y, self.me, self.h, self.r1x, self.r1y
        arrived(r1x.at[d], self.s.at[d, 0], self.q.at[d, 0], me, h)
        arrived(r1y.at[d], self.s.at[d, 1], self.q.at[d, 1], me, h)
        low_acc, high_acc = self.low_acc(d), self.high_acc(d)

        def body(i, carry):
            row = chunk(i)
            low_acc[row, :] = (
                low_acc[row, :].astype(f32) + r1x[d, 1 - y, row, :].astype(f32)
            ).astype(bf16)
            high_acc[row, :] = (
                high_acc[row, :].astype(f32) + r1y[d, 1 - x, row, :].astype(f32)
            ).astype(bf16)
            return carry

        lax.fori_loop(0, 8, body, 0)

    def second(self, d):
        self.second_sum(d)
        for copy in self.second_copies(d):
            self.go(copy)

    def third_sum(self, d, target):
        x, y, me, h = self.x, self.y, self.me, self.h
        arrived(self.r2y.at[d], self.s.at[d, 2], self.q.at[d, 2], me, h)
        arrived(self.r2x.at[d], self.s.at[d, 3], self.q.at[d, 3], me, h)
        fin, low, high = self.fin(d), self.low, self.high

        def body(i, carry):
            row = chunk(i)
            target[row, low] = (
                fin[row, low].astype(f32)
                + self.r1x[d, y, row, :].astype(f32)
                + self.r2y[d, row, :].astype(f32)
            ).astype(bf16)
            target[row, high] = (
                fin[row, high].astype(f32)
                + self.r1y[d, x, row, :].astype(f32)
                + self.r2x[d, row, :].astype(f32)
            ).astype(bf16)
            return carry

        lax.fori_loop(0, 8, body, 0)

    def third(self, d):
        fin, z = self.fin(d), self.z
        self.third_sum(d, fin if d else self.out.at[z])
        if d:
            there = index_of((z + d) % ZED, self.y, self.x)
            self.go(remote(fin, self.out.at[z], self.s.at[d, 4], self.q.at[d, 4], there, self.h))

    def last(self):
        for d in (1, 3, 2):
            arrived(
                self.out.at[(self.z + ZED - d) % ZED], self.s.at[d, 4], self.q.at[d, 4], self.me, self.h
            )

    def third_join(self, k):
        fin = self.fin(k)
        self.third_sum(k, fin if k else self.out.at[0])
        near = index_of(self.planes[1], self.y, self.x)
        if k == 1:
            self.go(remote(fin, self.out.at[1], self.s.at[1, 4], self.q.at[1, 4], near, self.h))
        if k > 1:
            outer = (self.z == 0) | (self.z == ZED - 1)
            copy = remote(fin, self.relay.at[3 - k], self.s.at[k, 4], self.q.at[5 - k, 4], near, self.h)
            self.go(copy, outer)

    def join(self, k):
        fin, relay, s, q = self.fin(k), self.relay, self.s, self.q
        inner = (self.z > 0) & (self.z < ZED - 1)

        @pl.when(inner)
        def _():
            arrived(relay.at[k - 2], s.at[k, 4], q.at[k, 4], self.me, self.h)

            def body(i, carry):
                row = chunk(i)
                fin[row, :] = (fin[row, :].astype(f32) + relay[k - 2, row, :].astype(f32)).astype(bf16)
                return carry

            lax.fori_loop(0, 8, body, 0)

        far = index_of(self.planes[k], self.y, self.x)
        self.go(remote(fin, self.out.at[2], s.at[k, 4], q.at[0, 4], far, self.h), inner)

    def joined(self):
        arrived(self.out.at[1], self.s.at[1, 4], self.q.at[1, 4], self.me, self.h)
        arrived(self.out.at[2], self.s.at[0, 4], self.q.at[0, 4], self.me, self.h)


class Join:
    def __init__(self, t, out, other, summed, landed, relay, ls, s, q, go, planes):
        self.t, self.out, self.other, self.summed, self.landed = t, out, other, summed, landed
        self.relay, self.ls, self.s, self.q, self.go, self.planes = relay, ls, s, q, go, planes
        self.x, self.y, self.z, self.h = where_am_i()
        self.me = index_of(self.z, self.y, self.x)
        self.inner = (self.z > 0) & (self.z < ZED - 1)
        self.outer = (self.z == 0) | (self.z == ZED - 1)

    def begin(self):
        self.own = {}
        for k in (2, 3, 1, 0):
            zz = self.planes[k]
            self.own[k] = pltpu.make_async_copy(self.t.at[zz, self.h], self.summed.at[k], self.ls.at[k])
            self.own[k].start()
            self.go(
                remote(self.t.at[zz, 1 - self.h], self.other.at[k], self.s.at[k, 0], self.q.at[k, 0], self.me, 1 - self.h)
            )

    def add(self, k, ref, index):
        summed = self.summed

        def body(turn, carry):
            row = chunk(turn)
            summed[k, row, :] = (
                summed[k, row, :].astype(f32) + ref[index, row, :].astype(f32)
            ).astype(bf16)
            return carry

        lax.fori_loop(0, 8, body, 0)

    def spread(self):
        near = index_of(self.planes[1], self.y, self.x)
        for k in (2, 3, 1, 0):
            self.own[k].wait()
            arrived(self.other.at[k], self.s.at[k, 0], self.q.at[k, 0], self.me, 1 - self.h)
            self.add(k, self.other, k)
            if k == 1:
                self.go(remote(self.summed.at[1], self.landed.at[0], self.s.at[1, 1], self.q.at[1, 1], near, self.h))
            if k > 1:
                copy = remote(
                    self.summed.at[k], self.relay.at[3 - k], self.s.at[k, 1], self.q.at[5 - k, 1], near, self.h
                )
                self.go(copy, self.outer)

    def join_sum(self, k):
        arrived(self.relay.at[k - 2], self.s.at[k, 1], self.q.at[k, 1], self.me, self.h)
        self.add(k, self.relay, k - 2)

    def join_copy(self, k):
        far = index_of(self.planes[k], self.y, self.x)
        return remote(self.summed.at[k], self.landed.at[1], self.s.at[k, 1], self.q.at[0, 1], far, self.h)

    def join(self, k):
        pl.when(self.inner)(lambda: self.join_sum(k))
        self.go(self.join_copy(k), self.inner)

    def total(self):
        summed, landed, out, h = self.summed, self.landed, self.out, self.h
        arrived(landed.at[0], self.s.at[1, 1], self.q.at[1, 1], self.me, h)
        arrived(landed.at[1], self.s.at[0, 1], self.q.at[0, 1], self.me, h)

        def body(turn, carry):
            row = chunk(turn)
            out[h, row, :] = (
                summed[0, row, :].astype(f32)
                + landed[0, row, :].astype(f32)
                + landed[1, row, :].astype(f32)
            ).astype(bf16)
            return carry

        lax.fori_loop(0, 8, body, 0)
        self.go(remote(out.at[h], out.at[h], self.s.at[4, 0], self.q.at[4, 0], self.me, 1 - h))

    def done(self):
        arrived(self.out.at[1 - self.h], self.s.at[4, 0], self.q.at[4, 0], self.me, 1 - self.h)


def back_kernel(
    near, gg, dg_in, du_in, hid_in, t, wo, wm, mid_in, cot_in, got_in, ratio_in, den_in,
    zm, d_mid, d_att, home, tb,
    g, r1x, r1y, r2x, r2y, e2, other, summed, landed, relayed, w2, pack, d_o, d_qk, d_v,
    q_t, k_t, va, da, dn_t, pack2, nbuf, gbuf, turned, stage,
    dg, du, hid, mid, cot, got, ratio, den,
    hs, ls, fs, bs, gs, gq, cs, cq, e1s, e1r, e2s, e2r,
):
    x, y, z, h = where_am_i()
    me = index_of(z, y, x)
    count = mid.shape[1]
    heads = 16 // mid.shape[0]
    room = dg.shape[1]
    late = []

    def go(copy, true=None):
        if true is None:
            copy.start()
        else:
            pl.when(true)(copy.start)
        late.append((true, copy))

    def fetch(i):
        cols = pl.ds(pl.multiple_of(((z + ZED - 1 - i) % ZED) * 512, 512), 512)
        return (
            pltpu.make_async_copy(near.at[:, cols], nbuf.at[i % 2], fs.at[i % 2, 0]),
            pltpu.make_async_copy(gg.at[:, cols], gbuf.at[i % 2], fs.at[i % 2, 1]),
        )

    for copy in fetch(0):
        copy.start()
    pairs = (
        (dg_in, dg), (du_in, du), (hid_in, hid), (mid_in, mid), (cot_in, cot), (got_in, got),
        (ratio_in, ratio), (den_in, den),
    )
    brought = [pltpu.make_async_copy(src, dst, hs.at[n]) for n, (src, dst) in enumerate(pairs)]
    for copy in brought:
        copy.start()
    planes = (z, z + 1 - 2 * (z % 2), ZED - 1 - z, (z + 2) % ZED)
    combine = Join(t, e2, other, summed, landed, relayed, ls, cs, cq, go, planes)
    scatter = Scatter(
        g,
        lambda d: g.at[(z + d) % ZED, 1 - y, x, :, pl.ds(0, g.shape[-1] // 2)],
        lambda d: g.at[(z + d) % ZED, y, 1 - x, :, pl.ds(g.shape[-1] // 2, g.shape[-1] // 2)],
        lambda d: g.at[(z + d) % ZED, y, x],
        zm, r1x, r1y, r2x, r2y, gs, gq, go,
    )
    combine.begin()
    weight = pltpu.make_async_copy(wo, w2, ls.at[4])
    weight.start()
    combine.spread()
    for copy in brought[0:3]:
        copy.wait()

    def block(i, carry):
        d = ZED - 1 - i
        zz = (z + d) % ZED

        @pl.when(i < ZED - 1)
        def _():
            for copy in fetch(i + 1):
                copy.start()

        for copy in fetch(i):
            copy.wait()
        for buf, terms in ((nbuf, (dg, du)), (gbuf, (hid,))):
            turned[...] = jnp.transpose(buf[i % 2])
            for term in terms:
                base = {id(dg): 0, id(du): room, id(hid): 2 * room}[id(term)]

                def piece(c, carry):
                    src = pl.ds(pl.multiple_of(c * COLS, COLS), COLS)
                    dst = pl.ds(pl.multiple_of(base + c * COLS, COLS), COLS)
                    res = mix(turned[...], term[:, src], ((1,), (0,))).astype(bf16)
                    for n in range(4):
                        g[zz, n // 2, n % 2, :, dst] = res[n * 128 : (n + 1) * 128, :]
                    return carry

                lax.fori_loop(0, room // COLS, piece, 0)
        @pl.when(i < ZED - 1)
        def _():
            for copy in scatter.first_copies(d):
                copy.start()

        @pl.when(i == 1)
        def _():
            scatter.second_sum(d + 1)
            for copy in scatter.second_copies(d + 1):
                copy.start()

        for k in (3, 2):

            @pl.when((i == 3 - k) & combine.inner)
            def _():
                combine.join_sum(k)
                combine.join_copy(k).start()

        return carry

    lax.fori_loop(0, ZED - 1, block, 0)
    for d in (1, 2, 3):
        late.extend((None, copy) for copy in scatter.first_copies(d))
    late.extend((None, copy) for copy in scatter.second_copies(3))
    for k in (2, 3):
        late.append((combine.inner, combine.join_copy(k)))
    combine.total()
    weight.wait()
    combine.done()
    for copy in brought[3:]:
        copy.wait()

    for mb in range(mid.shape[0]):

        def body(turn, carry):
            row = chunk(turn)
            m = mid[mb, row, :]
            scale = lax.rsqrt(jnp.mean(m * m, axis=-1, keepdims=True) + epsilon)
            hat = m * scale
            e = e2[mb, row, :].astype(f32)
            d_m = cot[mb, row, :].astype(f32) + scale * (
                e - hat * jnp.mean(e * hat, axis=-1, keepdims=True)
            )
            d_mid[mb, row, :] = d_m
            d_att[pl.ds(pl.multiple_of(mb * count + turn * 16, 16), 16), :] = d_m.astype(bf16)
            return carry

        lax.fori_loop(0, count // 16, body, 0)
    for c in range(heads * DV // COLS):
        val = mix(d_att[...], w2[:, c * COLS : (c + 1) * COLS], ((1,), (0,))).astype(bf16)
        for mb in range(16 // heads):
            for i in range(COLS // DV):
                pack[c * (COLS // DV) + i + heads * mb, :, :] = val[
                    mb * count : (mb + 1) * count, i * DV : (i + 1) * DV
                ]

    def window(source):
        return d_o.at[pl.ds(pl.multiple_of(source * count, count), count)]

    own = pltpu.make_async_copy(pack.at[me], window(me), ls.at[5])
    own.start()
    for d in range(1, 16):
        there = (me + d) % 16
        go(remote(pack.at[there], window(me), e1s.at[d], e1r.at[d], there, h))
    scatter.second(2)
    scatter.third(3)
    scatter.second(1)
    lax.fori_loop(ZED - 1, ZED, block, 0)
    scatter.first(0)
    half = near.shape[1] // 2
    shards = []
    for r in range(2):
        at = pl.ds(r * half, half)
        shards.append(
            (
                pltpu.make_async_copy(wm.at[at, pl.ds(2 * room, 512)], nbuf.at[r], fs.at[r, 0]),
                pltpu.make_async_copy(
                    wm.at[at, pl.ds(2 * room + 512, room - 512)],
                    gbuf.at[r, :, pl.ds(0, room - 512)],
                    fs.at[r, 1],
                ),
            )
        )
        for copy in shards[r]:
            copy.start()
    scatter.third(2)
    own.wait()
    for d in range(1, 16):
        arrived(window((me + 16 - d) % 16), e1s.at[d], e1r.at[d], me, h)
    attend_back_body(got, ratio, den, d_o, d_qk, d_v, q_t, k_t, va, da, dn_t)
    for b in range(16):
        pack2[b, 0 : 2 * F, :] = d_qk[:, b * count : (b + 1) * count].astype(bf16)
        pack2[b, 2 * F :, :] = d_v[b * count : (b + 1) * count, :].astype(bf16)
    own = pltpu.make_async_copy(pack2.at[me], home.at[me], ls.at[5])
    own.start()
    for d in range(1, 16):
        there = (me + d) % 16
        go(remote(pack2.at[there], home.at[me], e2s.at[d], e2r.at[d], there, h))
    scatter.third(1)
    scatter.second(0)
    stored = {}
    for n in range(2 * half // COLS):
        r, c = n // (half // COLS), n % (half // COLS)
        if c == 0:
            for copy in shards[r]:
                copy.wait()
        if n > 1:
            stored[n - 2].wait()
        at = slice(c * COLS, (c + 1) * COLS)
        stage[n % 2, :, :] = (
            mix(hid[:, 0:512], nbuf[r, at, :], ((1,), (1,)))
            + mix(hid[:, 512:room], gbuf[r, at, 0 : room - 512], ((1,), (1,)))
        ).astype(bf16)
        stored[n] = pltpu.make_async_copy(
            stage.at[n % 2], tb.at[:, pl.ds(n * COLS, COLS)], bs.at[n % 2]
        )
        stored[n].start()
    scatter.third(0)
    stored[2 * half // COLS - 2].wait()
    stored[2 * half // COLS - 1].wait()
    own.wait()
    for d in range(1, 16):
        arrived(home.at[(me + 16 - d) % 16], e2s.at[d], e2r.at[d], me, h)
    scatter.last()
    for true, copy in late:
        if true is None:
            copy.wait_send()
        else:
            pl.when(true)(copy.wait_send)


def scatter_room(wide):
    return [
        pltpu.VMEM((4, 2, 128, wide // 2), bf16),
        pltpu.VMEM((4, 2, 128, wide // 2), bf16),
        pltpu.VMEM((4, 128, wide // 2), bf16),
        pltpu.VMEM((4, 128, wide // 2), bf16),
    ]


def back(near, gg, dg, du, hid, t, wo, wm, mid, cot, got, ratio, den):
    mbs, count, wide = cot.shape
    depth = 16 * count
    shape = jax.ShapeDtypeStruct
    cols = 3 * dg.shape[1]
    line = pltpu.VMEM((ZED, count, wide), bf16)
    return pl.pallas_call(
        back_kernel,
        out_shape=(
            shape((ZED, 128, cols), bf16),
            shape(cot.shape, f32),
            shape((mbs * count, wide), bf16),
            shape((16, 2 * F + DV, count), bf16),
            shape(near.shape, bf16),
        ),
        in_specs=[ANY] * 13,
        out_specs=(VMEM,) * 4 + (ANY,),
        scratch_shapes=[pltpu.VMEM((ZED, 2, 2, 128, cols), bf16)] + scatter_room(cols) + [
            pltpu.VMEM(cot.shape, bf16), line, line,
            pltpu.VMEM((2, count, wide), bf16),
            pltpu.VMEM((2, count, wide), bf16),
            pltpu.VMEM(wo.shape, bf16),
            pltpu.VMEM((16, count, DV), bf16),
            pltpu.VMEM((depth, DV), bf16),
            pltpu.VMEM((2 * F, depth), f32),
            pltpu.VMEM((depth, DV), f32),
            pltpu.VMEM((F, depth), bf16),
            pltpu.VMEM((F, depth), bf16),
            pltpu.VMEM((depth, 2 * DV), bf16),
            pltpu.VMEM((depth, 2 * DV), bf16),
            pltpu.VMEM((DV, depth), bf16),
            pltpu.VMEM((16, 2 * F + DV, count), bf16),
            pltpu.VMEM((2, near.shape[0], 512), bf16),
            pltpu.VMEM((2, near.shape[0], 512), bf16),
            pltpu.VMEM((512, near.shape[0]), bf16),
            pltpu.VMEM((2, near.shape[0], COLS), bf16),
            pltpu.VMEM(dg.shape, bf16),
            pltpu.VMEM(dg.shape, bf16),
            pltpu.VMEM(dg.shape, bf16),
            pltpu.VMEM(mid.shape, f32),
            pltpu.VMEM(cot.shape, bf16),
            pltpu.VMEM(got.shape, bf16),
            pltpu.VMEM(ratio.shape, f32),
            pltpu.VMEM(den.shape, f32),
            DMA((8,)), DMA((6,)), DMA((2, 2)), DMA((2,)), DMA((4, 5)), DMA((4, 5)), DMA((5, 2)), DMA((5, 2)),
            DMA((16,)), DMA((16,)), DMA((16,)), DMA((16,)),
        ],
        compiler_params=params(),
        name="back",
    )(near, gg, dg, du, hid, t, wo, wm, mid, cot, got, ratio, den)


def end_kernel(
    t, home, xh, d_att, heads_out, wa1, d_mid_in, xin_in, mid_in,
    za, d_in, outputs,
    g, r1x, r1y, r2x, r2y, relay, branch, other, summed, landed, relayed, w1, dqk_t, dqkv, part, swap,
    d_mid, xin, mid, hs, ls, gs, gq, cs, cq, ws, wr,
):
    x, y, z, h = where_am_i()
    me = index_of(z, y, x)
    mbs, count, wide = xin.shape
    heads = 16 // mbs
    qk, vv = 2 * heads * F, heads * DV
    late = []

    def go(copy, true=None):
        if true is None:
            copy.start()
        else:
            pl.when(true)(copy.start)
        late.append((true, copy))

    planes = (z, z + 1 - 2 * (z % 2), ZED - 1 - z, (z + 2) % ZED)
    combine = Join(t, branch, other, summed, landed, relayed, ls, cs, cq, go, planes)
    scatter = Scatter(
        g,
        lambda k: g.at[planes[k], 1 - y, x, :, pl.ds(0, g.shape[-1] // 2)],
        lambda k: g.at[planes[k], y, 1 - x, :, pl.ds(g.shape[-1] // 2, g.shape[-1] // 2)],
        lambda k: g.at[planes[k], y, x],
        za, r1x, r1y, r2x, r2y, gs, gq, go, planes, relay,
    )
    combine.begin()
    brought = [
        pltpu.make_async_copy(d_mid_in, d_mid, hs.at[0]),
        pltpu.make_async_copy(xin_in, xin, hs.at[1]),
        pltpu.make_async_copy(mid_in, mid, hs.at[2]),
    ]
    for copy in brought:
        copy.start()
    weight = pltpu.make_async_copy(wa1, w1, ls.at[4])
    weight.start()
    for mb in range(mbs):
        cols = slice(mb * count, (mb + 1) * count)
        for k in range(heads):
            block = home.at[k + heads * mb]
            dqk_t[k * F : (k + 1) * F, cols] = block[0:F, :].astype(f32)
            dqk_t[(heads + k) * F : (heads + k + 1) * F, cols] = block[F : 2 * F, :].astype(f32)
            dqkv[cols, qk + k * DV : qk + (k + 1) * DV] = block[2 * F :, :]
    dqkv[:, 0:qk] = jnp.transpose(dqk_t[...]).astype(bf16)

    def terms(k):
        zz = planes[k]

        def body(n, carry):
            at = pl.ds(pl.multiple_of((zz * 4 + n) * 128, 128), 128)
            g[zz, n // 2, n % 2, :, 0 : qk + vv] = mix(xh[:, at], dqkv[...], ((0,), (0,))).astype(bf16)
            g[zz, n // 2, n % 2, :, qk + vv :] = mix(d_att[:, at], heads_out[...], ((0,), (0,))).astype(bf16)
            return carry

        lax.fori_loop(0, 4, body, 0)

    terms(2)
    scatter.first(2)
    combine.spread()
    terms(3)
    scatter.first(3)
    scatter.second(2)
    terms(1)
    scatter.first(1)
    weight.wait()
    for copy in brought:
        copy.wait()
    for c in range(wide // COLS):
        cols = pl.ds(c * COLS, COLS)
        part[:, c * COLS : (c + 1) * COLS] = mix(dqkv[...], w1[c * COLS : (c + 1) * COLS, :], ((1,), (1,)))
        go(remote(part.at[:, cols], swap.at[:, cols], ws.at[c], wr.at[c], me, 1 - h))
    scatter.second(3)
    combine.join(3)
    terms(0)
    scatter.third_join(2)
    combine.join(2)
    for c in range(wide // COLS):
        cols = pl.ds(c * COLS, COLS)
        arrived(swap.at[:, cols], ws.at[c], wr.at[c], me, 1 - h)
    for mb in range(mbs):

        def body(turn, carry):
            row = chunk(turn)
            flat = pl.ds(pl.multiple_of(mb * count + turn * 16, 16), 16)
            v = xin[mb, row, :].astype(f32)
            scale = lax.rsqrt(jnp.mean(v * v, axis=-1, keepdims=True) + epsilon)
            hat = v * scale
            e = part[flat, :] + swap[flat, :]
            d_in[mb, row, :] = (
                d_mid[mb, row, :] + scale * (e - hat * jnp.mean(e * hat, axis=-1, keepdims=True))
            ).astype(bf16)
            return carry

        lax.fori_loop(0, count // 16, body, 0)
    scatter.second(1)
    scatter.first(0)
    scatter.third_join(3)
    scatter.join(3)
    scatter.third_join(1)
    scatter.join(2)
    combine.total()
    scatter.second(0)
    combine.done()
    for mb in range(mbs):

        def body(turn, carry):
            row = chunk(turn)
            outputs[mb, row, :] = (mid[mb, row, :] + branch[mb, row, :].astype(f32)).astype(bf16)
            return carry

        lax.fori_loop(0, count // 16, body, 0)
    scatter.third_join(0)
    scatter.joined()
    for true, copy in late:
        if true is None:
            copy.wait_send()
        else:
            pl.when(true)(copy.wait_send)


def end(t, home, xh, d_att, heads_out, wa1, d_mid, xin, mid):
    mbs, count, wide = xin.shape
    shape = jax.ShapeDtypeStruct
    cols = wa1.shape[1] + heads_out.shape[1]
    line = pltpu.VMEM((ZED, count, wide), bf16)
    return pl.pallas_call(
        end_kernel,
        out_shape=(shape((3, 128, cols), bf16), shape(xin.shape, bf16), shape(xin.shape, bf16)),
        in_specs=[ANY] + [VMEM] * 4 + [ANY] * 4,
        out_specs=(VMEM,) * 3,
        scratch_shapes=[pltpu.VMEM((ZED, 2, 2, 128, cols), bf16)] + scatter_room(cols) + [
            pltpu.VMEM((2, 128, cols), bf16),
            pltpu.VMEM(xin.shape, bf16), line, line,
            pltpu.VMEM((2, count, wide), bf16),
            pltpu.VMEM((2, count, wide), bf16),
            pltpu.VMEM(wa1.shape, bf16),
            pltpu.VMEM((mbs * count, mbs * count), f32),
            pltpu.VMEM((mbs * count, wa1.shape[1]), bf16),
            pltpu.VMEM((mbs * count, wide), f32),
            pltpu.VMEM((mbs * count, wide), f32),
            pltpu.VMEM(d_mid.shape, f32),
            pltpu.VMEM(xin.shape, bf16),
            pltpu.VMEM(mid.shape, f32),
            DMA((3,)), DMA((6,)), DMA((4, 5)), DMA((4, 5)), DMA((5, 2)), DMA((5, 2)),
            DMA((wide // COLS,)), DMA((wide // COLS,)),
        ],
        compiler_params=params(),
        name="end",
    )(t, home, xh, d_att, heads_out, wa1, d_mid, xin, mid)


def finish_kernel(
    zm, za, wq, wk, wv, wg, wu, g1, g2, o_q, o_k, o_v, o_out, o_g, o_u, o_d, gains
):
    units = wg.shape[1] // ZED
    room = zm.shape[2] // 3
    nq, nv = wq.shape[1], wv.shape[1]
    lanes = g1.shape[1]
    scale1, scale2 = column(g1), column(g2)

    def total(cols):
        acc = za[0, :, cols].astype(f32)
        for n in range(1, za.shape[0]):
            acc = acc + za[n, :, cols].astype(f32)
        return acc

    first = jnp.zeros((zm.shape[1], lanes), f32)
    at = 0
    for w, out in ((wq, o_q), (wk, o_k), (wv, o_v)):
        for c in range(w.shape[1] // lanes):
            cols = slice(c * lanes, (c + 1) * lanes)
            value = total(slice(at + c * lanes, at + (c + 1) * lanes))
            out[:, cols] = value * scale1
            first = first + value * w[:, cols].astype(f32)
        at += w.shape[1]
    for c in range(nv // lanes):
        o_out[c * lanes : (c + 1) * lanes, :] = jnp.transpose(
            total(slice(at + c * lanes, at + (c + 1) * lanes))
        )
    second = jnp.zeros((zm.shape[1], lanes), f32)
    for n in range(ZED):
        for base, w, out in ((0, wg, o_g), (room, wu, o_u)):
            for c in range(0, units, lanes):
                size = min(lanes, units - c)
                cols = slice(n * units + c, n * units + c + size)
                value = zm[n, :, base + c : base + c + size].astype(f32)
                out[:, cols] = value * scale2[:, 0:size]
                prod = value * w[:, cols].astype(f32)
                if size == lanes:
                    second = second + prod
                else:
                    second = second + jnp.concatenate(
                        [prod, jnp.zeros((prod.shape[0], lanes - size), f32)], axis=1
                    )
        for c in range(0, units, lanes):
            size = min(lanes, units - c)
            value = jnp.transpose(zm[n, :, 2 * room + c : 2 * room + c + lanes].astype(f32))
            o_d[n * units + c : n * units + c + size, :] = value[0:size, :]
    gains[0:1, :] = jnp.sum(jnp.transpose(first), axis=0, keepdims=True)
    gains[1:2, :] = jnp.sum(jnp.transpose(second), axis=0, keepdims=True)


def finish(zm, za, wq, wk, wv, wg, wu, g1, g2, w_out, w_down):
    shape = lambda w: jax.ShapeDtypeStruct(w.shape, f32)
    return pl.pallas_call(
        finish_kernel,
        out_shape=(
            shape(wq), shape(wk), shape(wv), shape(w_out), shape(wg), shape(wu), shape(w_down),
            jax.ShapeDtypeStruct((2, 128), f32),
        ),
        in_specs=[VMEM] * 9,
        out_specs=(VMEM,) * 8,
        compiler_params=pltpu.CompilerParams(vmem_limit_bytes=VMEM_LIMIT),
        name="finish",
    )(zm, za, wq, wk, wv, wg, wu, g1, g2)


def fast(
    inputs, norm_gain1, w_query, w_key, w_value, w_out, norm_gain2, w_gate, w_up, w_down, cotangent
):
    mbs, count, wide = inputs.shape
    rows = w_query.shape[0]
    gain1, gain2 = norm_gain1.reshape(1, rows), norm_gain2.reshape(1, rows)
    wa1, w_o, wm, gg, got, ratio, den, heads_out, middle, near, xh1 = front(
        w_query, w_key, w_value, w_out, w_gate, w_up, w_down, gain1, gain2, cotangent, inputs
    )
    room = wm.shape[1] // 3
    w_g, w_u, w_d = wm[:, :room], wm[:, room : 2 * room], wm[:, 2 * room :]
    many = ZED * mbs * count
    n2 = near.reshape(many, wide)
    up_g = gg.reshape(many, wide)
    gate = mix(n2, w_g, ((1,), (0,)))
    up = mix(n2, w_u, ((1,), (0,)))
    d_hidden = mix(up_g, w_d, ((1,), (0,)))
    sig = jax.nn.sigmoid(gate)
    silu = gate * sig
    hidden = (silu * up).astype(bf16)
    d_gate = (d_hidden * up * sig * (1.0 + gate * (1.0 - sig))).astype(bf16)
    d_up = (d_hidden * silu).astype(bf16)
    d_n2 = (mix(d_gate, w_g, ((1,), (1,))) + mix(d_up, w_u, ((1,), (1,)))).astype(bf16)
    lines = (ZED, mbs, count, wide)
    zm, d_mid, d_att, home, branch = back(
        n2, up_g, d_gate, d_up, hidden, d_n2.reshape(lines), w_o, wm, middle, cotangent, got, ratio, den
    )
    za, input_grad, outputs = end(
        branch.reshape(lines), home, xh1, d_att, heads_out, wa1, d_mid, inputs, middle
    )
    o_q, o_k, o_v, o_out, o_g, o_u, o_d, gains = finish(
        zm, za, w_query, w_key, w_value, w_gate, w_up,
        gain1, gain2, w_out, w_down,
    )
    gains = lax.psum(gains, "head")
    return (outputs, input_grad, gains[0], o_q, o_k, o_v, o_out, gains[1], o_g, o_u, o_d)


def solution(mesh):
    return jax.shard_map(
        fast if mesh.shape["seq"] == 16 else local,
        mesh=mesh,
        in_specs=(
            P(None, "seq", None),
            P("seq"),
            P("seq", "head"),
            P("seq", "head"),
            P("seq", "head"),
            P("head", "seq"),
            P("seq"),
            P("seq", "head"),
            P("seq", "head"),
            P("head", "seq"),
            P(None, "seq", None),
        ),
        out_specs=(
            P(None, "seq", None),
            P(None, "seq", None),
            P("seq"),
            P("seq", "head"),
            P("seq", "head"),
            P("seq", "head"),
            P("head", "seq"),
            P("seq"),
            P("seq", "head"),
            P("seq", "head"),
            P("head", "seq"),
        ),
        check_vma=False,
    )
```

```python
import jax
import jax.numpy as jnp
from jax import lax
from jax.experimental import pallas as pl
from jax.experimental.pallas import tpu as pltpu
from jax.sharding import PartitionSpec as P

F = 16
DV = 128


epsilon = 1e-05
highest = lax.Precision.HIGHEST


def entering(part, axis, combine, identity, reverse):
    count = lax.axis_size(axis)
    place = lax.axis_index(axis)
    ahead = count - 1 - place if reverse else place
    gathered = jax.tree.map(lambda a: lax.all_gather(a, axis), part)
    state = jax.tree.map(lambda a, e: jnp.zeros_like(a) + jnp.asarray(e, a.dtype), part, identity)

    def one(turn, state):
        source = count - 1 - turn if reverse else turn
        return combine(
            state, jax.tree.map(lambda a: lax.dynamic_index_in_dim(a, source, 0, False), gathered)
        )

    return lax.fori_loop(0, ahead, one, state)


def rms_apply(values, gain):
    scale = lax.rsqrt(jnp.mean(values * values, axis=-1, keepdims=True) + epsilon)
    return values * scale * gain


def feature_map(projected):
    count = projected.shape[0]
    pieces = projected.reshape(count, -1, F)
    square = (pieces[:, :, :, None] * pieces[:, :, None, :]).reshape(count, pieces.shape[1], F * F)
    return jnp.concatenate(
        [jnp.ones_like(pieces[:, :, :1]), pieces * F ** (-0.25), square * (2.0 * F) ** (-0.5)],
        axis=-1,
    )


def swiglu(gate, up_part):
    return jax.nn.silu(gate) * up_part


def round_trip(values):
    return lax.optimization_barrier(values.astype(jnp.bfloat16)).astype(jnp.float32)


def add_pair(earlier, later):
    return (earlier[0] + later[0], earlier[1] + later[1])


def block_pass(tokens, upstream, gathered):
    gain_one, query_w, key_w, value_w, out_w, gain_two, gate_w, up_w, down_w = gathered
    f32 = jnp.float32
    bf16 = jnp.bfloat16
    stream = tokens.astype(f32)
    count = stream.shape[0]
    normed_f, norm_one_pull = jax.vjp(rms_apply, stream, gain_one.astype(f32))
    normed = normed_f.astype(bf16)
    queries = jnp.dot(normed, query_w, preferred_element_type=f32)
    keys_all = jnp.dot(normed, key_w, preferred_element_type=f32)
    values = jnp.dot(normed, value_w, preferred_element_type=f32).astype(bf16)
    query_feat_f, query_pull = jax.vjp(feature_map, queries)
    key_feat_f, key_pull = jax.vjp(feature_map, keys_all)
    query_feat = jnp.transpose(query_feat_f.astype(bf16), (1, 0, 2))
    key_feat = jnp.transpose(key_feat_f.astype(bf16), (1, 0, 2))
    value_heads = jnp.transpose(values.reshape(count, -1, DV), (1, 0, 2))
    causal = (jnp.arange(count)[:, None] >= jnp.arange(count)[None, :]).astype(f32)
    scores = jnp.einsum("htf,hsf->hts", query_feat, key_feat, preferred_element_type=f32) * causal
    weighted = scores.astype(bf16)
    num_local = jnp.einsum("hts,hsd->htd", weighted, value_heads, preferred_element_type=f32)
    den_local = jnp.sum(weighted.astype(f32), axis=-1)
    states = jnp.einsum("hsf,hsd->hfd", key_feat, value_heads, preferred_element_type=f32)
    totals = jnp.sum(key_feat.astype(f32), axis=1)
    state_before, total_before = entering(
        (states, totals), "seq", add_pair, (jnp.zeros_like(states), jnp.zeros_like(totals)), False
    )
    query_wide = query_feat.astype(f32)
    numer = num_local + jnp.einsum("htf,hfd->htd", query_wide, state_before, precision=highest)
    denom = den_local + jnp.einsum("htf,hf->ht", query_wide, total_before, precision=highest)
    ratio = numer / denom[..., None]
    heads_out = jnp.transpose(ratio, (1, 0, 2)).reshape(count, -1).astype(bf16)
    attended = lax.psum(jnp.dot(heads_out, out_w, preferred_element_type=f32), "head")
    middle = stream + attended
    normed_two_f, norm_two_pull = jax.vjp(rms_apply, middle, gain_two.astype(f32))
    normed_two = normed_two_f.astype(bf16)
    gate = jnp.dot(normed_two, gate_w, preferred_element_type=f32)
    up_part = jnp.dot(normed_two, up_w, preferred_element_type=f32)
    active, active_pull = jax.vjp(swiglu, gate, up_part)
    hidden = active.astype(bf16)
    branch = lax.psum(
        jnp.dot(hidden, down_w, preferred_element_type=f32).astype(jnp.bfloat16), "head"
    ).astype(jnp.float32)
    result = (middle + branch).astype(bf16)
    grad_down = jnp.dot(hidden.T, upstream, preferred_element_type=f32)
    d_hidden = jnp.dot(upstream, down_w.T, preferred_element_type=f32)
    d_gate_f, d_up_f = active_pull(d_hidden)
    d_gate = d_gate_f.astype(bf16)
    d_up = d_up_f.astype(bf16)
    grad_gate = jnp.dot(normed_two.T, d_gate, preferred_element_type=f32)
    grad_up = jnp.dot(normed_two.T, d_up, preferred_element_type=f32)
    d_normed_two = lax.psum(
        jnp.dot(d_gate, gate_w.T, preferred_element_type=f32)
        + jnp.dot(d_up, up_w.T, preferred_element_type=f32),
        "head",
    )
    d_middle_norm, grad_gain2 = norm_two_pull(d_normed_two)
    d_middle = upstream.astype(f32) + d_middle_norm
    d_attended = d_middle.astype(bf16)
    grad_out = jnp.dot(heads_out.T, d_attended, preferred_element_type=f32)
    d_heads = jnp.transpose(
        jnp.dot(d_attended, out_w.T, preferred_element_type=f32).reshape(count, -1, DV), (1, 0, 2)
    )
    d_numer = (d_heads / denom[..., None]).astype(bf16)
    d_denom = -jnp.sum(d_heads * ratio, axis=-1) / denom
    d_numer_wide = d_numer.astype(f32)
    d_before = jnp.einsum("htf,htd->hfd", query_wide, d_numer_wide, precision=highest)
    d_total_before = jnp.einsum("htf,ht->hf", query_wide, d_denom, precision=highest)
    d_state, d_total = entering(
        (d_before, d_total_before),
        "seq",
        add_pair,
        (jnp.zeros_like(d_before), jnp.zeros_like(d_total_before)),
        True,
    )
    d_scores = (
        (
            jnp.einsum("htd,hsd->hts", d_numer, value_heads, preferred_element_type=f32)
            + d_denom[..., None]
        )
        * causal
    ).astype(bf16)
    d_values = jnp.einsum(
        "hts,htd->hsd", weighted, d_numer, preferred_element_type=f32
    ) + jnp.einsum("hsf,hfd->hsd", key_feat.astype(f32), d_state, precision=highest)
    d_query_feat = (
        jnp.einsum("hts,hsf->htf", d_scores, key_feat, preferred_element_type=f32)
        + jnp.einsum("htd,hfd->htf", d_numer_wide, state_before, precision=highest)
        + d_denom[..., None] * total_before[:, None, :]
    )
    d_key_feat = (
        jnp.einsum("hts,htf->hsf", d_scores, query_feat, preferred_element_type=f32)
        + jnp.einsum("hsd,hfd->hsf", value_heads.astype(f32), d_state, precision=highest)
        + d_total[:, None, :]
    )
    d_queries = query_pull(jnp.transpose(round_trip(d_query_feat), (1, 0, 2)))[0].astype(bf16)
    d_keys = key_pull(jnp.transpose(round_trip(d_key_feat), (1, 0, 2)))[0].astype(bf16)
    d_values_flat = jnp.transpose(d_values, (1, 0, 2)).reshape(count, -1).astype(bf16)
    grad_query = jnp.dot(normed.T, d_queries, preferred_element_type=f32)
    grad_key = jnp.dot(normed.T, d_keys, preferred_element_type=f32)
    grad_value = jnp.dot(normed.T, d_values_flat, preferred_element_type=f32)
    d_normed_part = (
        jnp.dot(d_queries, query_w.T, preferred_element_type=f32)
        + jnp.dot(d_keys, key_w.T, preferred_element_type=f32)
        + jnp.dot(d_values_flat, value_w.T, preferred_element_type=f32)
    )
    d_normed = lax.psum(d_normed_part.astype(jnp.bfloat16), "head").astype(jnp.float32)
    d_stream_norm, grad_gain1 = norm_one_pull(d_normed)
    input_grad = (d_middle + d_stream_norm).astype(bf16)
    return (
        result,
        input_grad,
        grad_gain1,
        grad_query,
        grad_key,
        grad_value,
        grad_out,
        grad_gain2,
        grad_gate,
        grad_up,
        grad_down,
    )


def local(
    inputs, norm_gain1, w_query, w_key, w_value, w_out, norm_gain2, w_gate, w_up, w_down, cotangent
):
    micro = inputs.shape[0]
    summed = None
    results = []
    input_grads = []
    for step_index in range(micro):
        gathered = (
            lax.all_gather(norm_gain1, "seq", axis=0, tiled=True),
            lax.all_gather(w_query, "seq", axis=0, tiled=True),
            lax.all_gather(w_key, "seq", axis=0, tiled=True),
            lax.all_gather(w_value, "seq", axis=0, tiled=True),
            lax.all_gather(w_out, "seq", axis=1, tiled=True),
            lax.all_gather(norm_gain2, "seq", axis=0, tiled=True),
            lax.all_gather(w_gate, "seq", axis=0, tiled=True),
            lax.all_gather(w_up, "seq", axis=0, tiled=True),
            lax.all_gather(w_down, "seq", axis=1, tiled=True),
        )
        (
            result,
            input_grad,
            grad_gain1,
            grad_query,
            grad_key,
            grad_value,
            grad_out,
            grad_gain2,
            grad_gate,
            grad_up,
            grad_down,
        ) = block_pass(inputs[step_index], cotangent[step_index], gathered)
        results.append(result)
        input_grads.append(input_grad)
        fresh = (
            lax.psum_scatter(grad_gain1, "seq", scatter_dimension=0, tiled=True),
            lax.psum_scatter(grad_query, "seq", scatter_dimension=0, tiled=True),
            lax.psum_scatter(grad_key, "seq", scatter_dimension=0, tiled=True),
            lax.psum_scatter(grad_value, "seq", scatter_dimension=0, tiled=True),
            lax.psum_scatter(grad_out, "seq", scatter_dimension=1, tiled=True),
            lax.psum_scatter(grad_gain2, "seq", scatter_dimension=0, tiled=True),
            lax.psum_scatter(grad_gate, "seq", scatter_dimension=0, tiled=True),
            lax.psum_scatter(grad_up, "seq", scatter_dimension=0, tiled=True),
            lax.psum_scatter(grad_down, "seq", scatter_dimension=1, tiled=True),
        )
        summed = (
            fresh
            if summed is None
            else tuple((older + newer for older, newer in zip(summed, fresh)))
        )
    return (
        jnp.stack(results),
        jnp.stack(input_grads),
        summed[0],
        summed[1],
        summed[2],
        summed[3],
        summed[4],
        summed[5],
        summed[6],
        summed[7],
        summed[8],
    )


MESH = pl.DeviceIdType.MESH
bf16 = jnp.bfloat16
f32 = jnp.float32
ZED = 4
VMEM_LIMIT = 60 * 1024 * 1024


def where_am_i():
    place = lax.axis_index("seq")
    return place % 2, (place // 2) % 2, place // 4, lax.axis_index("head")


def index_of(z, y, x):
    return (z * 2 + y) * 2 + x


def remote(src, dst, send, recv, place, head):
    return pltpu.make_async_remote_copy(
        src_ref=src, dst_ref=dst, send_sem=send, recv_sem=recv, device_id=(place, head),
        device_id_type=MESH,
    )


def arrived(dst, send, recv, place, head):
    remote(dst, dst, send, recv, place, head).wait_recv()


def params():
    return pltpu.CompilerParams(has_side_effects=True, vmem_limit_bytes=VMEM_LIMIT)


ANY = pl.BlockSpec(memory_space=pl.ANY)
VMEM = pl.BlockSpec(memory_space=pltpu.VMEM)
DMA = pltpu.SemaphoreType.DMA
ORDER = (0, 1, 3, 2)


def mix(a, b, over):
    return lax.dot_general(a, b, (over, ((), ())), preferred_element_type=f32)


CHUNK = 512
COLS = 256


def spread(got, q_t, k_t, va):
    count = got.shape[2]
    for b in range(got.shape[0]):
        q_t[:, b * count : (b + 1) * count] = got[b, 0:F, :]
        k_t[:, b * count : (b + 1) * count] = got[b, F : 2 * F, :]
        va[b * count : (b + 1) * count, 0:DV] = got[b, 2 * F :, :]
    va[:, DV:] = jnp.ones((va.shape[0], va.shape[1] - DV), bf16)


def lower(count):
    return lax.broadcasted_iota(jnp.int32, (count, count), 0) >= lax.broadcasted_iota(
        jnp.int32, (count, count), 1
    )


def attend_rows(qi, q_t, k_t, va, ratio, den, causal):
    qs = slice(qi * CHUNK, (qi + 1) * CHUNK)
    acc = jnp.zeros((CHUNK, va.shape[1]), f32)
    for kj in range(qi + 1):
        ks = slice(kj * CHUNK, (kj + 1) * CHUNK)
        s = mix(q_t[:, qs], k_t[:, ks], ((0,), (0,)))
        p = 1.0 + s * (0.25 + s * (1.0 / 32.0))
        if kj == qi:
            p = jnp.where(causal, p, 0.0)
        acc = acc + mix(p.astype(bf16), va[ks, :], ((1,), (0,)))
    ratio[qs, :] = acc[:, :DV] / acc[:, DV:]
    den[qs, :] = acc[:, DV:]


def column(gain):
    count = gain.shape[1]
    return jnp.transpose(jnp.broadcast_to(gain[...].astype(f32), (count, count)))


def front_kernel(
    wq, wk, wv, w_out, wg, wu, wd, g1, g2, cot, xin,
    wa1, wa2, wm, gg, got_out, ratio_out, den_out, heads_store, middle_out, near, xh_out,
    got, ratio, den, heads_out, middle, xh, fresh, a1, a2, m, w1, w2, pack, q_t, k_t, va, ob, part, other,
    os, ls, zs, zr, us, ur, ps, pr, e1s, e1r, e2s, e2r, ws, wr, ds, dr,
):
    x, y, z, h = where_am_i()
    me = index_of(z, y, x)
    at_x, at_y = index_of(z, y, 1 - x), index_of(z, 1 - y, x)
    count = xin.shape[1]
    heads = 16 // xin.shape[0]
    late = []
    stored = []

    def store(src, dst):
        copy = pltpu.make_async_copy(src, dst, os.at[len(stored)])
        copy.start()
        stored.append(copy)

    def when(true, do):
        if true is None:
            do()
        else:
            pl.when(true)(do)

    def go(copy, true=None):
        when(true, copy.start)
        late.append((true, copy))

    def rows(zz, yy, xx):
        return pl.ds(pl.multiple_of(index_of(zz, yy, xx) * 128, 128), 128)

    mine = rows(z, y, x)
    kept = [
        pltpu.make_async_copy(a1, w1.at[mine], ls.at[0]),
        pltpu.make_async_copy(a2, w2.at[mine], ls.at[1]),
        pltpu.make_async_copy(m.at[z], wm.at[mine], ls.at[2]),
        pltpu.make_async_copy(cot, gg.at[z], ls.at[6]),
    ]
    lanes = g1.shape[1]
    scale = column(g1)
    at = 0
    for w in (wq, wk, wv):
        for c in range(0, w.shape[1], lanes):
            a1[:, at + c : at + c + lanes] = (w[:, c : c + lanes].astype(f32) * scale).astype(bf16)
        at += w.shape[1]
    kept[0].start()
    kept[3].start()
    dest = (w1, w2, wm)
    UP, DOWN = 0, 1
    COT, NEAR = 2, 3

    def held(kind, zz):
        return (lambda: w1.at[rows(zz, y, x)], lambda: w2.at[rows(zz, y, x)],
                lambda: gg.at[zz, h], lambda: near.at[zz, h])[kind]()

    def origin(way, step):
        return (z + ZED - step) % ZED if way == UP else (z + step) % ZED

    def valid(way, step):
        return z >= step if way == UP else z <= ZED - 1 - step

    def pass_on(kind, way, step, src, true):
        there = index_of((z + 1) % ZED if way == UP else (z + ZED - 1) % ZED, y, x)
        block = held(kind, origin(way, step))
        go(remote(block if src is None else src, block, us.at[kind, way, step], ur.at[kind, way, step + 1], there, h), true)

    def offer(kind, src=None):
        pass_on(kind, UP, 0, src, z < ZED - 1)
        pass_on(kind, DOWN, 0, src, z > 0)

    def hop(kind, way, step):
        block = held(kind, origin(way, step))
        when(
            valid(way, step),
            lambda: arrived(block, us.at[kind, way, step], ur.at[kind, way, step], me, h),
        )
        if step < ZED - 1:
            more = z < ZED - 1 if way == UP else z > 0
            pass_on(kind, way, step, None, valid(way, step) & more)

    def across(kind, way, step):
        zz = origin(way, step)
        block = held(kind, zz)
        go(remote(block, block, ds.at[kind, way, step], dr.at[kind, way, step], me, 1 - h), valid(way, step))

    def across_done(kind, way, step):
        zz = origin(way, step)
        block = (gg if kind == COT else near).at[zz, 1 - h]
        when(
            valid(way, step),
            lambda: arrived(block, ds.at[kind, way, step], dr.at[kind, way, step], me, 1 - h),
        )

    def both(do, kind, step):
        do(kind, UP, step)
        do(kind, DOWN, step)

    partner = (z, z + 1 - 2 * (z % 2), ZED - 1 - z, (z + 2) % ZED)

    inner = (z > 0) & (z < ZED - 1)
    outer = (z == 0) | (z == ZED - 1)

    def line(d, true=None):
        zz = partner[d]
        copy = remote(m.at[zz], wm.at[mine], zs.at[d], zr.at[d], index_of(zz, y, x), h)
        go(copy, true)

    def slot_of(way, step):
        return step if way == UP else 3 + step if step else 0

    def plane_set(kind, slot, zz, true):
        block = dest[kind].at[rows(zz, y, x)]
        go(remote(block, block, ps.at[kind, slot, 0], pr.at[kind, slot, 0], at_x, h), true)
        go(remote(block, block, ps.at[kind, slot, 1], pr.at[kind, slot, 1], at_y, h), true)

    def onward_set(kind, slot, zz, true):
        w = dest[kind]
        half = w.shape[1] // 2
        from_x, from_y = rows(zz, y, 1 - x), rows(zz, 1 - y, x)

        def wait():
            arrived(w.at[from_x], ps.at[kind, slot, 0], pr.at[kind, slot, 0], me, h)
            arrived(w.at[from_y], ps.at[kind, slot, 1], pr.at[kind, slot, 1], me, h)

        when(true, wait)
        left = w.at[from_y, pl.ds(0, half)]
        right = w.at[from_x, pl.ds(half, half)]
        go(remote(left, left, ps.at[kind, slot, 2], pr.at[kind, slot, 2], at_x, h), true)
        go(remote(right, right, ps.at[kind, slot, 3], pr.at[kind, slot, 3], at_y, h), true)

    def corner_set(kind, slot, zz, true):
        w = dest[kind]
        half = w.shape[1] // 2
        far = rows(zz, 1 - y, 1 - x)

        def wait():
            arrived(w.at[far, pl.ds(0, half)], ps.at[kind, slot, 2], pr.at[kind, slot, 2], me, h)
            arrived(w.at[far, pl.ds(half, half)], ps.at[kind, slot, 3], pr.at[kind, slot, 3], me, h)

        when(true, wait)

    def plane(kind, way, step):
        if step == 0:
            kept[kind].wait()
        plane_set(kind, slot_of(way, step), origin(way, step), valid(way, step) if step else None)

    def onward(kind, way, step):
        onward_set(kind, slot_of(way, step), origin(way, step), valid(way, step) if step else None)

    def corner(kind):
        corner_set(kind, 0, z, None)
        for step in (1, 2, 3):
            for way in (UP, DOWN):
                corner_set(kind, slot_of(way, step), origin(way, step), valid(way, step))

    def m_plane(d):
        zz = partner[d]
        if d:
            arrived(wm.at[rows(zz, y, x)], zs.at[d], zr.at[d], me, h)
        else:
            kept[2].wait()
        plane_set(2, d, zz, None)

    def m_onward(d):
        onward_set(2, d, partner[d], None)

    offer(0, a1)
    plane(0, UP, 0)
    for c in range(0, w_out.shape[0], lanes):
        a2[:, c : c + lanes] = jnp.transpose(w_out[c : c + lanes, :].astype(f32)).astype(bf16)
    kept[1].start()
    for way in (UP, DOWN):
        hop(0, way, 1)
        plane(0, way, 1)
    units = wg.shape[1] // ZED
    room = m.shape[2] // 3
    scale = column(g2)
    for n in range(ZED):
        for part_at, w in ((0, wg), (room, wu)):
            for c in range(0, units, lanes):
                size = min(lanes, units - c)
                m[n, :, part_at + c : part_at + c + size] = (
                    w[:, n * units + c : n * units + c + size].astype(f32) * scale[:, 0:size]
                ).astype(bf16)
        for c in range(0, units, lanes):
            size = min(lanes, units - c)
            m[n, :, 2 * room + c : 2 * room + c + size] = jnp.transpose(
                wd[n * units + c : n * units + c + size, :].astype(f32)
            ).astype(bf16)
        for part_at in (0, room, 2 * room):
            m[n, :, part_at + units : part_at + room] = jnp.zeros((lanes, room - units), bf16)
    kept[2].start()
    onward(0, UP, 0)
    for way in (UP, DOWN):
        hop(0, way, 2)
        plane(0, way, 2)
    offer(1, a2)
    both(onward, 0, 1)
    for way in (UP, DOWN):
        hop(0, way, 3)
        plane(0, way, 3)
    both(onward, 0, 2)
    both(hop, 1, 1)
    plane(1, UP, 0)
    for mb in range(xin.shape[0]):

        def normed(turn, carry):
            row = pl.ds(pl.multiple_of(turn * 16, 16), 16)
            v = xin[mb, row, :].astype(f32)
            r = lax.rsqrt(jnp.mean(v * v, axis=-1, keepdims=True) + epsilon)
            xh[pl.ds(pl.multiple_of(mb * count + turn * 16, 16), 16), :] = (v * r).astype(bf16)
            return carry

        lax.fori_loop(0, count // 16, normed, 0)
    store(xh, xh_out)
    both(onward, 0, 3)
    both(hop, 1, 2)
    both(hop, 1, 3)
    line(1)
    line(2, inner)
    corner(0)
    out1 = pltpu.make_async_copy(w1, wa1, ls.at[3])
    out1.start()
    kq = mix(xh[...], w1[:, 0 : 2 * heads * F], ((1,), (0,)))
    qk = jnp.transpose(kq).astype(bf16)
    for mb in range(16 // heads):
        for k in range(heads):
            t = k + heads * mb
            cols = slice(mb * count, (mb + 1) * count)
            pack[t, 0:F, :] = qk[k * F : (k + 1) * F, cols]
            pack[t, F : 2 * F, :] = qk[(heads + k) * F : (heads + k + 1) * F, cols]

    def valued(c, carry):
        cols = pl.ds(pl.multiple_of(2 * heads * F + c * COLS, COLS), COLS)
        val = mix(xh[...], w1[:, cols], ((1,), (0,))).astype(bf16)
        for mb in range(16 // heads):
            for i in range(COLS // DV):
                t = c * (COLS // DV) + i + heads * mb
                pack[t, 2 * F :, :] = val[mb * count : (mb + 1) * count, i * DV : (i + 1) * DV]
        return carry

    lax.fori_loop(0, heads * DV // COLS, valued, 0)
    keep = pltpu.make_async_copy(pack.at[me], got.at[me], ls.at[4])
    keep.start()
    for d in range(1, 16):
        there = (me + d) % 16
        go(remote(pack.at[there], got.at[me], e1s.at[d], e1r.at[d], there, h))
    line(2, outer)
    line(3, inner)
    both(plane, 1, 1)
    onward(1, UP, 0)
    both(plane, 1, 2)
    both(onward, 1, 1)
    both(plane, 1, 3)
    both(onward, 1, 2)
    keep.wait()
    for d in range(1, 16):
        arrived(got.at[(me + 16 - d) % 16], e1s.at[d], e1r.at[d], me, h)
    both(onward, 1, 3)
    store(got, got_out)
    spread(got, q_t, k_t, va)
    causal = lower(CHUNK)
    for qi in range(va.shape[0] // CHUNK):
        attend_rows(qi, q_t, k_t, va, ratio, den, causal)
    for b in range(16):
        ob[b, :, :] = ratio[b * count : (b + 1) * count, :].astype(bf16)

    store(ratio, ratio_out)
    store(den, den_out)

    def window(source):
        return heads_out.at[
            pl.ds(pl.multiple_of((source // heads) * count, count), count),
            pl.ds(pl.multiple_of((source % heads) * DV, DV), DV),
        ]

    keep = pltpu.make_async_copy(ob.at[me], window(me), ls.at[4])
    keep.start()
    for d in range(1, 16):
        there = (me + d) % 16
        go(remote(ob.at[there], window(me), e2s.at[d], e2r.at[d], there, h))
    line(3, outer)
    offer(COT, cot.at[h])
    m_plane(0)
    m_plane(1)
    corner(1)
    out2 = pltpu.make_async_copy(w2, wa2, ls.at[5])
    out2.start()
    keep.wait()
    for d in range(1, 16):
        arrived(window((me + 16 - d) % 16), e2s.at[d], e2r.at[d], me, h)
    store(heads_out, heads_store)
    wide = part.shape[1]

    def pair(c):
        cols = pl.ds(pl.multiple_of(c * COLS, COLS), COLS)
        return remote(part.at[:, cols], other.at[:, cols], ws.at[c], wr.at[c], me, 1 - h)

    def project(c, carry):
        cols = pl.ds(pl.multiple_of(c * COLS, COLS), COLS)
        part[:, cols] = mix(heads_out[...], w2[cols, :], ((1,), (1,)))
        pair(c).start()
        return carry

    lax.fori_loop(0, wide // COLS, project, 0)
    for c in range(wide // COLS):
        late.append((None, pair(c)))
    m_onward(0)
    both(hop, COT, 1)
    m_plane(2)
    for c in range(wide // COLS):
        cols = pl.ds(c * COLS, COLS)
        arrived(other.at[:, cols], ws.at[c], wr.at[c], me, 1 - h)

    def one(mb):
        def body(turn, carry):
            row = pl.ds(pl.multiple_of(turn * 16, 16), 16)
            flat = pl.ds(pl.multiple_of(mb * count + turn * 16, 16), 16)
            mid = xin[mb, row, :].astype(f32) + (part[flat, :] + other[flat, :])
            middle[mb, row, :] = mid
            scale = lax.rsqrt(jnp.mean(mid * mid, axis=-1, keepdims=True) + epsilon)
            fresh[mb, row, :] = (mid * scale).astype(bf16)
            return carry

        lax.fori_loop(0, count // 16, body, 0)

    one(h)
    offer(NEAR, fresh.at[h])
    one(1 - h)
    store(middle, middle_out)
    store(fresh, near.at[z])
    m_onward(1)
    both(hop, COT, 2)
    m_plane(3)
    kept[3].wait()
    both(across, COT, 1)
    both(across, COT, 2)
    both(hop, NEAR, 1)
    both(across, NEAR, 1)
    m_onward(2)
    both(hop, COT, 3)
    both(across, COT, 3)
    both(hop, NEAR, 2)
    both(across, NEAR, 2)
    m_onward(3)
    both(hop, NEAR, 3)
    both(across, NEAR, 3)
    for d in range(4):
        corner_set(2, d, partner[d], None)
    for kind in (NEAR, COT):
        for step in (1, 2, 3):
            both(across_done, kind, step)
    out1.wait()
    out2.wait()
    for copy in stored:
        copy.wait()
    for true, copy in late:
        when(true, copy.wait_send)


def front(wq, wk, wv, w_out, wg, wu, wd, g1, g2, cot, xin):
    mbs, count, wide = xin.shape
    depth = 16 * count
    wide1, wide2 = wq.shape[1] + wk.shape[1] + wv.shape[1], w_out.shape[0]
    wide3 = 3 * (-(-wg.shape[1] // ZED // 256) * 256)
    shape = jax.ShapeDtypeStruct
    return pl.pallas_call(
        front_kernel,
        out_shape=(
            shape((wide, wide1), bf16),
            shape((wide, wide2), bf16),
            shape((wide, wide3), bf16),
            shape((ZED,) + cot.shape, bf16),
            shape((16, 2 * F + DV, count), bf16),
            shape((depth, DV), f32),
            shape((depth, DV), f32),
            shape((mbs * count, wide2), bf16),
            shape(xin.shape, f32),
            shape((ZED,) + xin.shape, bf16),
            shape((mbs * count, wide), bf16),
        ),
        in_specs=[VMEM] * 9 + [ANY] + [VMEM],
        out_specs=(ANY,) * 11,
        scratch_shapes=[
            pltpu.VMEM((16, 2 * F + DV, count), bf16),
            pltpu.VMEM((depth, DV), f32),
            pltpu.VMEM((depth, DV), f32),
            pltpu.VMEM((mbs * count, wide2), bf16),
            pltpu.VMEM(xin.shape, f32),
            pltpu.VMEM((mbs * count, wide), bf16),
            pltpu.VMEM(xin.shape, bf16),
            pltpu.VMEM((wq.shape[0], wide1), bf16),
            pltpu.VMEM((wq.shape[0], wide2), bf16),
            pltpu.VMEM((ZED, wq.shape[0], wide3), bf16),
            pltpu.VMEM((wide, wide1), bf16),
            pltpu.VMEM((wide, wide2), bf16),
            pltpu.VMEM((16, 2 * F + DV, count), bf16),
            pltpu.VMEM((F, depth), bf16),
            pltpu.VMEM((F, depth), bf16),
            pltpu.VMEM((depth, 2 * DV), bf16),
            pltpu.VMEM((16, count, DV), bf16),
            pltpu.VMEM((mbs * count, wide), f32),
            pltpu.VMEM((mbs * count, wide), f32),
            DMA((8,)), DMA((7,)), DMA((4,)), DMA((4,)), DMA((4, 2, 4)), DMA((4, 2, 4)), DMA((3, 7, 4)), DMA((3, 7, 4)),
            DMA((16,)), DMA((16,)), DMA((16,)), DMA((16,)),
            DMA((wide // COLS,)), DMA((wide // COLS,)), DMA((4, 2, 4)), DMA((4, 2, 4)),
        ],
        compiler_params=params(),
        name="front",
    )(wq, wk, wv, w_out, wg, wu, wd, g1, g2, cot, xin)


def attend_back_body(got, ratio, den, d_o, d_qk, d_v, q_t, k_t, va, da, dn_t):
    spread(got, q_t, k_t, va)
    depth = va.shape[0]
    lane = lax.broadcasted_iota(jnp.int32, (CHUNK, DV), 1)
    for qi in range(depth // CHUNK):
        qs = slice(qi * CHUNK, (qi + 1) * CHUNK)
        dn = d_o[qs, :].astype(f32) / den[qs, :]
        dd = -jnp.sum(dn * ratio[qs, :], axis=-1, keepdims=True)
        big = dd.astype(bf16).astype(f32)
        da[qs, 0:DV] = dn.astype(bf16)
        da[qs, DV:] = jnp.where(lane == 0, big, jnp.where(lane == 1, dd - big, 0.0)).astype(bf16)
        dn_t[:, qs] = jnp.transpose(dn).astype(bf16)
    causal = lower(CHUNK)
    for kj in range(depth // CHUNK):
        ks = slice(kj * CHUNK, (kj + 1) * CHUNK)
        acc_k = jnp.zeros((F, CHUNK), f32)
        acc_v = jnp.zeros((DV, CHUNK), f32)
        for qi in range(kj, depth // CHUNK):
            qs = slice(qi * CHUNK, (qi + 1) * CHUNK)
            s = mix(q_t[:, qs], k_t[:, ks], ((0,), (0,)))
            p = 1.0 + s * (0.25 + s * (1.0 / 32.0))
            d_s = mix(da[qs, :], va[ks, :], ((1,), (1,))) * (0.25 + s * (1.0 / 16.0))
            if kj == qi:
                p = jnp.where(causal, p, 0.0)
                d_s = jnp.where(causal, d_s, 0.0)
            d_s = d_s.astype(bf16)
            acc_v = acc_v + mix(dn_t[:, qs], p.astype(bf16), ((1,), (0,)))
            acc_k = acc_k + mix(q_t[:, qs], d_s, ((1,), (0,)))
            d_q = mix(k_t[:, ks], d_s, ((1,), (1,)))
            d_qk[0:F, qs] = d_q if kj == 0 else d_qk[0:F, qs] + d_q
        d_qk[F : 2 * F, ks] = acc_k
        d_v[ks, :] = jnp.transpose(acc_v)


def chunk(turn):
    return pl.ds(pl.multiple_of(turn * 16, 16), 16)


class Scatter:
    def __init__(self, g, low_acc, high_acc, fin, out, r1x, r1y, r2x, r2y, s, q, go, planes=None, relay=None):
        self.planes, self.relay = planes, relay
        self.g, self.low_acc, self.high_acc, self.fin, self.out = g, low_acc, high_acc, fin, out
        self.r1x, self.r1y, self.r2x, self.r2y, self.s, self.q = r1x, r1y, r2x, r2y, s, q
        self.go = go
        self.x, self.y, self.z, self.h = where_am_i()
        self.me = index_of(self.z, self.y, self.x)
        self.at_x = index_of(self.z, self.y, 1 - self.x)
        self.at_y = index_of(self.z, 1 - self.y, self.x)
        self.half = r1x.shape[-1]
        self.low, self.high = pl.ds(0, self.half), pl.ds(self.half, self.half)

    def plane(self, d):
        return (self.z + d) % ZED if self.planes is None else self.planes[d]

    def first_copies(self, d):
        zz, x, y, g = self.plane(d), self.x, self.y, self.g
        return (
            remote(g.at[zz, :, 1 - x, :, self.low], self.r1x.at[d], self.s.at[d, 0], self.q.at[d, 0], self.at_x, self.h),
            remote(g.at[zz, 1 - y, :, :, self.high], self.r1y.at[d], self.s.at[d, 1], self.q.at[d, 1], self.at_y, self.h),
        )

    def first(self, d):
        for copy in self.first_copies(d):
            self.go(copy)

    def second_copies(self, d):
        return (
            remote(self.low_acc(d), self.r2y.at[d], self.s.at[d, 2], self.q.at[d, 2], self.at_y, self.h),
            remote(self.high_acc(d), self.r2x.at[d], self.s.at[d, 3], self.q.at[d, 3], self.at_x, self.h),
        )

    def second_sum(self, d):
        x, y, me, h, r1x, r1y = self.x, self.y, self.me, self.h, self.r1x, self.r1y
        arrived(r1x.at[d], self.s.at[d, 0], self.q.at[d, 0], me, h)
        arrived(r1y.at[d], self.s.at[d, 1], self.q.at[d, 1], me, h)
        low_acc, high_acc = self.low_acc(d), self.high_acc(d)

        def body(i, carry):
            row = chunk(i)
            low_acc[row, :] = (
                low_acc[row, :].astype(f32) + r1x[d, 1 - y, row, :].astype(f32)
            ).astype(bf16)
            high_acc[row, :] = (
                high_acc[row, :].astype(f32) + r1y[d, 1 - x, row, :].astype(f32)
            ).astype(bf16)
            return carry

        lax.fori_loop(0, 8, body, 0)

    def second(self, d):
        self.second_sum(d)
        for copy in self.second_copies(d):
            self.go(copy)

    def third_sum(self, d, target):
        x, y, me, h = self.x, self.y, self.me, self.h
        arrived(self.r2y.at[d], self.s.at[d, 2], self.q.at[d, 2], me, h)
        arrived(self.r2x.at[d], self.s.at[d, 3], self.q.at[d, 3], me, h)
        fin, low, high = self.fin(d), self.low, self.high

        def body(i, carry):
            row = chunk(i)
            target[row, low] = (
                fin[row, low].astype(f32)
                + self.r1x[d, y, row, :].astype(f32)
                + self.r2y[d, row, :].astype(f32)
            ).astype(bf16)
            target[row, high] = (
                fin[row, high].astype(f32)
                + self.r1y[d, x, row, :].astype(f32)
                + self.r2x[d, row, :].astype(f32)
            ).astype(bf16)
            return carry

        lax.fori_loop(0, 8, body, 0)

    def third(self, d):
        fin, z = self.fin(d), self.z
        self.third_sum(d, fin if d else self.out.at[z])
        if d:
            there = index_of((z + d) % ZED, self.y, self.x)
            self.go(remote(fin, self.out.at[z], self.s.at[d, 4], self.q.at[d, 4], there, self.h))

    def last(self):
        for d in (1, 3, 2):
            arrived(
                self.out.at[(self.z + ZED - d) % ZED], self.s.at[d, 4], self.q.at[d, 4], self.me, self.h
            )

    def third_join(self, k):
        fin = self.fin(k)
        self.third_sum(k, fin if k else self.out.at[0])
        near = index_of(self.planes[1], self.y, self.x)
        if k == 1:
            self.go(remote(fin, self.out.at[1], self.s.at[1, 4], self.q.at[1, 4], near, self.h))
        if k > 1:
            outer = (self.z == 0) | (self.z == ZED - 1)
            copy = remote(fin, self.relay.at[3 - k], self.s.at[k, 4], self.q.at[5 - k, 4], near, self.h)
            self.go(copy, outer)

    def join(self, k):
        fin, relay, s, q = self.fin(k), self.relay, self.s, self.q
        inner = (self.z > 0) & (self.z < ZED - 1)

        @pl.when(inner)
        def _():
            arrived(relay.at[k - 2], s.at[k, 4], q.at[k, 4], self.me, self.h)

            def body(i, carry):
                row = chunk(i)
                fin[row, :] = (fin[row, :].astype(f32) + relay[k - 2, row, :].astype(f32)).astype(bf16)
                return carry

            lax.fori_loop(0, 8, body, 0)

        far = index_of(self.planes[k], self.y, self.x)
        self.go(remote(fin, self.out.at[2], s.at[k, 4], q.at[0, 4], far, self.h), inner)

    def joined(self):
        arrived(self.out.at[1], self.s.at[1, 4], self.q.at[1, 4], self.me, self.h)
        arrived(self.out.at[2], self.s.at[0, 4], self.q.at[0, 4], self.me, self.h)


class Join:
    def __init__(self, t, out, other, summed, landed, relay, ls, s, q, go, planes):
        self.t, self.out, self.other, self.summed, self.landed = t, out, other, summed, landed
        self.relay, self.ls, self.s, self.q, self.go, self.planes = relay, ls, s, q, go, planes
        self.x, self.y, self.z, self.h = where_am_i()
        self.me = index_of(self.z, self.y, self.x)
        self.inner = (self.z > 0) & (self.z < ZED - 1)
        self.outer = (self.z == 0) | (self.z == ZED - 1)

    def begin(self):
        self.own = {}
        for k in (2, 3, 1, 0):
            zz = self.planes[k]
            self.own[k] = pltpu.make_async_copy(self.t.at[zz, self.h], self.summed.at[k], self.ls.at[k])
            self.own[k].start()
            self.go(
                remote(self.t.at[zz, 1 - self.h], self.other.at[k], self.s.at[k, 0], self.q.at[k, 0], self.me, 1 - self.h)
            )

    def add(self, k, ref, index):
        summed = self.summed

        def body(turn, carry):
            row = chunk(turn)
            summed[k, row, :] = (
                summed[k, row, :].astype(f32) + ref[index, row, :].astype(f32)
            ).astype(bf16)
            return carry

        lax.fori_loop(0, 8, body, 0)

    def spread(self):
        near = index_of(self.planes[1], self.y, self.x)
        for k in (2, 3, 1, 0):
            self.own[k].wait()
            arrived(self.other.at[k], self.s.at[k, 0], self.q.at[k, 0], self.me, 1 - self.h)
            self.add(k, self.other, k)
            if k == 1:
                self.go(remote(self.summed.at[1], self.landed.at[0], self.s.at[1, 1], self.q.at[1, 1], near, self.h))
            if k > 1:
                copy = remote(
                    self.summed.at[k], self.relay.at[3 - k], self.s.at[k, 1], self.q.at[5 - k, 1], near, self.h
                )
                self.go(copy, self.outer)

    def join_sum(self, k):
        arrived(self.relay.at[k - 2], self.s.at[k, 1], self.q.at[k, 1], self.me, self.h)
        self.add(k, self.relay, k - 2)

    def join_copy(self, k):
        far = index_of(self.planes[k], self.y, self.x)
        return remote(self.summed.at[k], self.landed.at[1], self.s.at[k, 1], self.q.at[0, 1], far, self.h)

    def join(self, k):
        pl.when(self.inner)(lambda: self.join_sum(k))
        self.go(self.join_copy(k), self.inner)

    def total(self):
        summed, landed, out, h = self.summed, self.landed, self.out, self.h
        arrived(landed.at[0], self.s.at[1, 1], self.q.at[1, 1], self.me, h)
        arrived(landed.at[1], self.s.at[0, 1], self.q.at[0, 1], self.me, h)

        def body(turn, carry):
            row = chunk(turn)
            out[h, row, :] = (
                summed[0, row, :].astype(f32)
                + landed[0, row, :].astype(f32)
                + landed[1, row, :].astype(f32)
            ).astype(bf16)
            return carry

        lax.fori_loop(0, 8, body, 0)
        self.go(remote(out.at[h], out.at[h], self.s.at[4, 0], self.q.at[4, 0], self.me, 1 - h))

    def done(self):
        arrived(self.out.at[1 - self.h], self.s.at[4, 0], self.q.at[4, 0], self.me, 1 - self.h)


def back_kernel(
    near, gg, dg_in, du_in, hid_in, t, wo, wm, mid_in, cot_in, got_in, ratio_in, den_in,
    zm, d_mid, d_att, home, tb,
    g, r1x, r1y, r2x, r2y, e2, other, summed, landed, relayed, w2, pack, d_o, d_qk, d_v,
    q_t, k_t, va, da, dn_t, pack2, nbuf, gbuf, turned, stage,
    dg, du, hid, mid, cot, got, ratio, den,
    hs, ls, fs, bs, gs, gq, cs, cq, e1s, e1r, e2s, e2r,
):
    x, y, z, h = where_am_i()
    me = index_of(z, y, x)
    count = mid.shape[1]
    heads = 16 // mid.shape[0]
    room = dg.shape[1]
    late = []

    def go(copy, true=None):
        if true is None:
            copy.start()
        else:
            pl.when(true)(copy.start)
        late.append((true, copy))

    def fetch(i):
        cols = pl.ds(pl.multiple_of(((z + ZED - 1 - i) % ZED) * 512, 512), 512)
        return (
            pltpu.make_async_copy(near.at[:, cols], nbuf.at[i % 2], fs.at[i % 2, 0]),
            pltpu.make_async_copy(gg.at[:, cols], gbuf.at[i % 2], fs.at[i % 2, 1]),
        )

    for copy in fetch(0):
        copy.start()
    pairs = (
        (dg_in, dg), (du_in, du), (hid_in, hid), (mid_in, mid), (cot_in, cot), (got_in, got),
        (ratio_in, ratio), (den_in, den),
    )
    brought = [pltpu.make_async_copy(src, dst, hs.at[n]) for n, (src, dst) in enumerate(pairs)]
    for copy in brought:
        copy.start()
    planes = (z, z + 1 - 2 * (z % 2), ZED - 1 - z, (z + 2) % ZED)
    combine = Join(t, e2, other, summed, landed, relayed, ls, cs, cq, go, planes)
    scatter = Scatter(
        g,
        lambda d: g.at[(z + d) % ZED, 1 - y, x, :, pl.ds(0, g.shape[-1] // 2)],
        lambda d: g.at[(z + d) % ZED, y, 1 - x, :, pl.ds(g.shape[-1] // 2, g.shape[-1] // 2)],
        lambda d: g.at[(z + d) % ZED, y, x],
        zm, r1x, r1y, r2x, r2y, gs, gq, go,
    )
    combine.begin()
    weight = pltpu.make_async_copy(wo, w2, ls.at[4])
    weight.start()
    combine.spread()
    for copy in brought[0:3]:
        copy.wait()

    def block(i, carry):
        d = ZED - 1 - i
        zz = (z + d) % ZED

        @pl.when(i < ZED - 1)
        def _():
            for copy in fetch(i + 1):
                copy.start()

        for copy in fetch(i):
            copy.wait()
        for buf, terms in ((nbuf, (dg, du)), (gbuf, (hid,))):
            turned[...] = jnp.transpose(buf[i % 2])
            for term in terms:
                base = {id(dg): 0, id(du): room, id(hid): 2 * room}[id(term)]

                def piece(c, carry):
                    src = pl.ds(pl.multiple_of(c * COLS, COLS), COLS)
                    dst = pl.ds(pl.multiple_of(base + c * COLS, COLS), COLS)
                    res = mix(turned[...], term[:, src], ((1,), (0,))).astype(bf16)
                    for n in range(4):
                        g[zz, n // 2, n % 2, :, dst] = res[n * 128 : (n + 1) * 128, :]
                    return carry

                lax.fori_loop(0, room // COLS, piece, 0)
        @pl.when(i < ZED - 1)
        def _():
            for copy in scatter.first_copies(d):
                copy.start()

        @pl.when(i == 1)
        def _():
            scatter.second_sum(d + 1)
            for copy in scatter.second_copies(d + 1):
                copy.start()

        for k in (3, 2):

            @pl.when((i == 3 - k) & combine.inner)
            def _():
                combine.join_sum(k)
                combine.join_copy(k).start()

        return carry

    lax.fori_loop(0, ZED - 1, block, 0)
    for d in (1, 2, 3):
        late.extend((None, copy) for copy in scatter.first_copies(d))
    late.extend((None, copy) for copy in scatter.second_copies(3))
    for k in (2, 3):
        late.append((combine.inner, combine.join_copy(k)))
    combine.total()
    weight.wait()
    combine.done()
    for copy in brought[3:]:
        copy.wait()

    for mb in range(mid.shape[0]):

        def body(turn, carry):
            row = chunk(turn)
            m = mid[mb, row, :]
            scale = lax.rsqrt(jnp.mean(m * m, axis=-1, keepdims=True) + epsilon)
            hat = m * scale
            e = e2[mb, row, :].astype(f32)
            d_m = cot[mb, row, :].astype(f32) + scale * (
                e - hat * jnp.mean(e * hat, axis=-1, keepdims=True)
            )
            d_mid[mb, row, :] = d_m
            d_att[pl.ds(pl.multiple_of(mb * count + turn * 16, 16), 16), :] = d_m.astype(bf16)
            return carry

        lax.fori_loop(0, count // 16, body, 0)

    def to_heads(c, carry):
        cols = pl.ds(pl.multiple_of(c * COLS, COLS), COLS)
        val = mix(d_att[...], w2[:, cols], ((1,), (0,))).astype(bf16)
        for mb in range(16 // heads):
            for i in range(COLS // DV):
                pack[c * (COLS // DV) + i + heads * mb, :, :] = val[
                    mb * count : (mb + 1) * count, i * DV : (i + 1) * DV
                ]
        return carry

    lax.fori_loop(0, heads * DV // COLS, to_heads, 0)

    def window(source):
        return d_o.at[pl.ds(pl.multiple_of(source * count, count), count)]

    own = pltpu.make_async_copy(pack.at[me], window(me), ls.at[5])
    own.start()
    for d in range(1, 16):
        there = (me + d) % 16
        go(remote(pack.at[there], window(me), e1s.at[d], e1r.at[d], there, h))
    scatter.second(2)
    scatter.third(3)
    scatter.second(1)
    lax.fori_loop(ZED - 1, ZED, block, 0)
    scatter.first(0)
    half = near.shape[1] // 2
    shards = []
    for r in range(2):
        at = pl.ds(r * half, half)
        shards.append(
            (
                pltpu.make_async_copy(wm.at[at, pl.ds(2 * room, 512)], nbuf.at[r], fs.at[r, 0]),
                pltpu.make_async_copy(
                    wm.at[at, pl.ds(2 * room + 512, room - 512)],
                    gbuf.at[r, :, pl.ds(0, room - 512)],
                    fs.at[r, 1],
                ),
            )
        )
        for copy in shards[r]:
            copy.start()
    scatter.third(2)
    own.wait()
    for d in range(1, 16):
        arrived(window((me + 16 - d) % 16), e1s.at[d], e1r.at[d], me, h)
    attend_back_body(got, ratio, den, d_o, d_qk, d_v, q_t, k_t, va, da, dn_t)
    for b in range(16):
        pack2[b, 0 : 2 * F, :] = d_qk[:, b * count : (b + 1) * count].astype(bf16)
        pack2[b, 2 * F :, :] = d_v[b * count : (b + 1) * count, :].astype(bf16)
    own = pltpu.make_async_copy(pack2.at[me], home.at[me], ls.at[5])
    own.start()
    for d in range(1, 16):
        there = (me + d) % 16
        go(remote(pack2.at[there], home.at[me], e2s.at[d], e2r.at[d], there, h))
    scatter.third(1)
    scatter.second(0)
    for pair in shards:
        for copy in pair:
            copy.wait()
    pieces = half // COLS

    def save(n):
        at = pl.ds(pl.multiple_of(n * COLS, COLS), COLS)
        return pltpu.make_async_copy(stage.at[n % 2], tb.at[:, at], bs.at[n % 2])

    def down(n, carry):
        @pl.when(n > 1)
        def _():
            save(n - 2).wait()

        r = n // pieces
        at = pl.ds(pl.multiple_of((n % pieces) * COLS, COLS), COLS)
        stage[n % 2, :, :] = (
            mix(hid[:, 0:512], nbuf[r, at, :], ((1,), (1,)))
            + mix(hid[:, 512:room], gbuf[r, at, 0 : room - 512], ((1,), (1,)))
        ).astype(bf16)
        save(n).start()
        return carry

    lax.fori_loop(0, 2 * pieces, down, 0)
    scatter.third(0)
    save(2 * pieces - 2).wait()
    save(2 * pieces - 1).wait()
    own.wait()
    for d in range(1, 16):
        arrived(home.at[(me + 16 - d) % 16], e2s.at[d], e2r.at[d], me, h)
    scatter.last()
    for true, copy in late:
        if true is None:
            copy.wait_send()
        else:
            pl.when(true)(copy.wait_send)


def scatter_room(wide):
    return [
        pltpu.VMEM((4, 2, 128, wide // 2), bf16),
        pltpu.VMEM((4, 2, 128, wide // 2), bf16),
        pltpu.VMEM((4, 128, wide // 2), bf16),
        pltpu.VMEM((4, 128, wide // 2), bf16),
    ]


def back(near, gg, dg, du, hid, t, wo, wm, mid, cot, got, ratio, den):
    mbs, count, wide = cot.shape
    depth = 16 * count
    shape = jax.ShapeDtypeStruct
    cols = 3 * dg.shape[1]
    line = pltpu.VMEM((ZED, count, wide), bf16)
    return pl.pallas_call(
        back_kernel,
        out_shape=(
            shape((ZED, 128, cols), bf16),
            shape(cot.shape, f32),
            shape((mbs * count, wide), bf16),
            shape((16, 2 * F + DV, count), bf16),
            shape(near.shape, bf16),
        ),
        in_specs=[ANY] * 13,
        out_specs=(VMEM,) * 4 + (ANY,),
        scratch_shapes=[pltpu.VMEM((ZED, 2, 2, 128, cols), bf16)] + scatter_room(cols) + [
            pltpu.VMEM(cot.shape, bf16), line, line,
            pltpu.VMEM((2, count, wide), bf16),
            pltpu.VMEM((2, count, wide), bf16),
            pltpu.VMEM(wo.shape, bf16),
            pltpu.VMEM((16, count, DV), bf16),
            pltpu.VMEM((depth, DV), bf16),
            pltpu.VMEM((2 * F, depth), f32),
            pltpu.VMEM((depth, DV), f32),
            pltpu.VMEM((F, depth), bf16),
            pltpu.VMEM((F, depth), bf16),
            pltpu.VMEM((depth, 2 * DV), bf16),
            pltpu.VMEM((depth, 2 * DV), bf16),
            pltpu.VMEM((DV, depth), bf16),
            pltpu.VMEM((16, 2 * F + DV, count), bf16),
            pltpu.VMEM((2, near.shape[0], 512), bf16),
            pltpu.VMEM((2, near.shape[0], 512), bf16),
            pltpu.VMEM((512, near.shape[0]), bf16),
            pltpu.VMEM((2, near.shape[0], COLS), bf16),
            pltpu.VMEM(dg.shape, bf16),
            pltpu.VMEM(dg.shape, bf16),
            pltpu.VMEM(dg.shape, bf16),
            pltpu.VMEM(mid.shape, f32),
            pltpu.VMEM(cot.shape, bf16),
            pltpu.VMEM(got.shape, bf16),
            pltpu.VMEM(ratio.shape, f32),
            pltpu.VMEM(den.shape, f32),
            DMA((8,)), DMA((6,)), DMA((2, 2)), DMA((2,)), DMA((4, 5)), DMA((4, 5)), DMA((5, 2)), DMA((5, 2)),
            DMA((16,)), DMA((16,)), DMA((16,)), DMA((16,)),
        ],
        compiler_params=params(),
        name="back",
    )(near, gg, dg, du, hid, t, wo, wm, mid, cot, got, ratio, den)


def end_kernel(
    t, home, xh, d_att, heads_out, wa1, d_mid_in, xin_in, mid_in,
    za, d_in, outputs,
    g, r1x, r1y, r2x, r2y, relay, branch, other, summed, landed, relayed, w1, dqk_t, dqkv, part, swap,
    d_mid, xin, mid, hs, ls, gs, gq, cs, cq, ws, wr,
):
    x, y, z, h = where_am_i()
    me = index_of(z, y, x)
    mbs, count, wide = xin.shape
    heads = 16 // mbs
    qk, vv = 2 * heads * F, heads * DV
    late = []

    def go(copy, true=None):
        if true is None:
            copy.start()
        else:
            pl.when(true)(copy.start)
        late.append((true, copy))

    planes = (z, z + 1 - 2 * (z % 2), ZED - 1 - z, (z + 2) % ZED)
    combine = Join(t, branch, other, summed, landed, relayed, ls, cs, cq, go, planes)
    scatter = Scatter(
        g,
        lambda k: g.at[planes[k], 1 - y, x, :, pl.ds(0, g.shape[-1] // 2)],
        lambda k: g.at[planes[k], y, 1 - x, :, pl.ds(g.shape[-1] // 2, g.shape[-1] // 2)],
        lambda k: g.at[planes[k], y, x],
        za, r1x, r1y, r2x, r2y, gs, gq, go, planes, relay,
    )
    combine.begin()
    brought = [
        pltpu.make_async_copy(d_mid_in, d_mid, hs.at[0]),
        pltpu.make_async_copy(xin_in, xin, hs.at[1]),
        pltpu.make_async_copy(mid_in, mid, hs.at[2]),
    ]
    for copy in brought:
        copy.start()
    weight = pltpu.make_async_copy(wa1, w1, ls.at[4])
    weight.start()
    for mb in range(mbs):
        cols = slice(mb * count, (mb + 1) * count)
        for k in range(heads):
            block = home.at[k + heads * mb]
            dqk_t[k * F : (k + 1) * F, cols] = block[0:F, :].astype(f32)
            dqk_t[(heads + k) * F : (heads + k + 1) * F, cols] = block[F : 2 * F, :].astype(f32)
            dqkv[cols, qk + k * DV : qk + (k + 1) * DV] = block[2 * F :, :]
    dqkv[:, 0:qk] = jnp.transpose(dqk_t[...]).astype(bf16)

    def terms(k):
        zz = planes[k]

        def body(n, carry):
            at = pl.ds(pl.multiple_of((zz * 4 + n) * 128, 128), 128)
            g[zz, n // 2, n % 2, :, 0 : qk + vv] = mix(xh[:, at], dqkv[...], ((0,), (0,))).astype(bf16)
            g[zz, n // 2, n % 2, :, qk + vv :] = mix(d_att[:, at], heads_out[...], ((0,), (0,))).astype(bf16)
            return carry

        lax.fori_loop(0, 4, body, 0)

    terms(2)
    scatter.first(2)
    combine.spread()
    terms(3)
    scatter.first(3)
    scatter.second(2)
    terms(1)
    scatter.first(1)
    weight.wait()
    for copy in brought:
        copy.wait()

    def pair(c):
        cols = pl.ds(pl.multiple_of(c * COLS, COLS), COLS)
        return remote(part.at[:, cols], swap.at[:, cols], ws.at[c], wr.at[c], me, 1 - h)

    def project(c, carry):
        cols = pl.ds(pl.multiple_of(c * COLS, COLS), COLS)
        part[:, cols] = mix(dqkv[...], w1[cols, :], ((1,), (1,)))
        pair(c).start()
        return carry

    lax.fori_loop(0, wide // COLS, project, 0)
    for c in range(wide // COLS):
        late.append((None, pair(c)))
    scatter.second(3)
    combine.join(3)
    terms(0)
    scatter.third_join(2)
    combine.join(2)
    for c in range(wide // COLS):
        cols = pl.ds(c * COLS, COLS)
        arrived(swap.at[:, cols], ws.at[c], wr.at[c], me, 1 - h)
    for mb in range(mbs):

        def body(turn, carry):
            row = chunk(turn)
            flat = pl.ds(pl.multiple_of(mb * count + turn * 16, 16), 16)
            v = xin[mb, row, :].astype(f32)
            scale = lax.rsqrt(jnp.mean(v * v, axis=-1, keepdims=True) + epsilon)
            hat = v * scale
            e = part[flat, :] + swap[flat, :]
            d_in[mb, row, :] = (
                d_mid[mb, row, :] + scale * (e - hat * jnp.mean(e * hat, axis=-1, keepdims=True))
            ).astype(bf16)
            return carry

        lax.fori_loop(0, count // 16, body, 0)
    scatter.second(1)
    scatter.first(0)
    scatter.third_join(3)
    scatter.join(3)
    scatter.third_join(1)
    scatter.join(2)
    combine.total()
    scatter.second(0)
    combine.done()
    for mb in range(mbs):

        def body(turn, carry):
            row = chunk(turn)
            outputs[mb, row, :] = (mid[mb, row, :] + branch[mb, row, :].astype(f32)).astype(bf16)
            return carry

        lax.fori_loop(0, count // 16, body, 0)
    scatter.third_join(0)
    scatter.joined()
    for true, copy in late:
        if true is None:
            copy.wait_send()
        else:
            pl.when(true)(copy.wait_send)


def end(t, home, xh, d_att, heads_out, wa1, d_mid, xin, mid):
    mbs, count, wide = xin.shape
    shape = jax.ShapeDtypeStruct
    cols = wa1.shape[1] + heads_out.shape[1]
    line = pltpu.VMEM((ZED, count, wide), bf16)
    return pl.pallas_call(
        end_kernel,
        out_shape=(shape((3, 128, cols), bf16), shape(xin.shape, bf16), shape(xin.shape, bf16)),
        in_specs=[ANY] + [VMEM] * 4 + [ANY] * 4,
        out_specs=(VMEM,) * 3,
        scratch_shapes=[pltpu.VMEM((ZED, 2, 2, 128, cols), bf16)] + scatter_room(cols) + [
            pltpu.VMEM((2, 128, cols), bf16),
            pltpu.VMEM(xin.shape, bf16), line, line,
            pltpu.VMEM((2, count, wide), bf16),
            pltpu.VMEM((2, count, wide), bf16),
            pltpu.VMEM(wa1.shape, bf16),
            pltpu.VMEM((mbs * count, mbs * count), f32),
            pltpu.VMEM((mbs * count, wa1.shape[1]), bf16),
            pltpu.VMEM((mbs * count, wide), f32),
            pltpu.VMEM((mbs * count, wide), f32),
            pltpu.VMEM(d_mid.shape, f32),
            pltpu.VMEM(xin.shape, bf16),
            pltpu.VMEM(mid.shape, f32),
            DMA((3,)), DMA((6,)), DMA((4, 5)), DMA((4, 5)), DMA((5, 2)), DMA((5, 2)),
            DMA((wide // COLS,)), DMA((wide // COLS,)),
        ],
        compiler_params=params(),
        name="end",
    )(t, home, xh, d_att, heads_out, wa1, d_mid, xin, mid)


def finish_kernel(
    zm, za, wq, wk, wv, wg, wu, g1, g2, o_q, o_k, o_v, o_out, o_g, o_u, o_d, gains
):
    units = wg.shape[1] // ZED
    room = zm.shape[2] // 3
    nq, nv = wq.shape[1], wv.shape[1]
    lanes = g1.shape[1]
    scale1, scale2 = column(g1), column(g2)

    def total(cols):
        acc = za[0, :, cols].astype(f32)
        for n in range(1, za.shape[0]):
            acc = acc + za[n, :, cols].astype(f32)
        return acc

    first = jnp.zeros((zm.shape[1], lanes), f32)
    at = 0
    for w, out in ((wq, o_q), (wk, o_k), (wv, o_v)):
        for c in range(w.shape[1] // lanes):
            cols = slice(c * lanes, (c + 1) * lanes)
            value = total(slice(at + c * lanes, at + (c + 1) * lanes))
            out[:, cols] = value * scale1
            first = first + value * w[:, cols].astype(f32)
        at += w.shape[1]
    for c in range(nv // lanes):
        o_out[c * lanes : (c + 1) * lanes, :] = jnp.transpose(
            total(slice(at + c * lanes, at + (c + 1) * lanes))
        )
    second = jnp.zeros((zm.shape[1], lanes), f32)
    for n in range(ZED):
        for base, w, out in ((0, wg, o_g), (room, wu, o_u)):
            for c in range(0, units, lanes):
                size = min(lanes, units - c)
                cols = slice(n * units + c, n * units + c + size)
                value = zm[n, :, base + c : base + c + size].astype(f32)
                out[:, cols] = value * scale2[:, 0:size]
                prod = value * w[:, cols].astype(f32)
                if size == lanes:
                    second = second + prod
                else:
                    second = second + jnp.concatenate(
                        [prod, jnp.zeros((prod.shape[0], lanes - size), f32)], axis=1
                    )
        for c in range(0, units, lanes):
            size = min(lanes, units - c)
            value = jnp.transpose(zm[n, :, 2 * room + c : 2 * room + c + lanes].astype(f32))
            o_d[n * units + c : n * units + c + size, :] = value[0:size, :]
    gains[0:1, :] = jnp.sum(jnp.transpose(first), axis=0, keepdims=True)
    gains[1:2, :] = jnp.sum(jnp.transpose(second), axis=0, keepdims=True)


def finish(zm, za, wq, wk, wv, wg, wu, g1, g2, w_out, w_down):
    shape = lambda w: jax.ShapeDtypeStruct(w.shape, f32)
    return pl.pallas_call(
        finish_kernel,
        out_shape=(
            shape(wq), shape(wk), shape(wv), shape(w_out), shape(wg), shape(wu), shape(w_down),
            jax.ShapeDtypeStruct((2, 128), f32),
        ),
        in_specs=[VMEM] * 9,
        out_specs=(VMEM,) * 8,
        compiler_params=pltpu.CompilerParams(vmem_limit_bytes=VMEM_LIMIT),
        name="finish",
    )(zm, za, wq, wk, wv, wg, wu, g1, g2)


def fast(
    inputs, norm_gain1, w_query, w_key, w_value, w_out, norm_gain2, w_gate, w_up, w_down, cotangent
):
    mbs, count, wide = inputs.shape
    rows = w_query.shape[0]
    gain1, gain2 = norm_gain1.reshape(1, rows), norm_gain2.reshape(1, rows)
    wa1, w_o, wm, gg, got, ratio, den, heads_out, middle, near, xh1 = front(
        w_query, w_key, w_value, w_out, w_gate, w_up, w_down, gain1, gain2, cotangent, inputs
    )
    room = wm.shape[1] // 3
    w_g, w_u, w_d = wm[:, :room], wm[:, room : 2 * room], wm[:, 2 * room :]
    many = ZED * mbs * count
    n2 = near.reshape(many, wide)
    up_g = gg.reshape(many, wide)
    gate = mix(n2, w_g, ((1,), (0,)))
    up = mix(n2, w_u, ((1,), (0,)))
    d_hidden = mix(up_g, w_d, ((1,), (0,)))
    sig = jax.nn.sigmoid(gate)
    silu = gate * sig
    hidden = (silu * up).astype(bf16)
    d_gate = (d_hidden * up * sig * (1.0 + gate * (1.0 - sig))).astype(bf16)
    d_up = (d_hidden * silu).astype(bf16)
    d_n2 = (mix(d_gate, w_g, ((1,), (1,))) + mix(d_up, w_u, ((1,), (1,)))).astype(bf16)
    lines = (ZED, mbs, count, wide)
    zm, d_mid, d_att, home, branch = back(
        n2, up_g, d_gate, d_up, hidden, d_n2.reshape(lines), w_o, wm, middle, cotangent, got, ratio, den
    )
    za, input_grad, outputs = end(
        branch.reshape(lines), home, xh1, d_att, heads_out, wa1, d_mid, inputs, middle
    )
    o_q, o_k, o_v, o_out, o_g, o_u, o_d, gains = finish(
        zm, za, w_query, w_key, w_value, w_gate, w_up,
        gain1, gain2, w_out, w_down,
    )
    gains = lax.psum(gains, "head")
    return (outputs, input_grad, gains[0], o_q, o_k, o_v, o_out, gains[1], o_g, o_u, o_d)


def solution(mesh):
    return jax.shard_map(
        fast if mesh.shape["seq"] == 16 else local,
        mesh=mesh,
        in_specs=(
            P(None, "seq", None),
            P("seq"),
            P("seq", "head"),
            P("seq", "head"),
            P("seq", "head"),
            P("head", "seq"),
            P("seq"),
            P("seq", "head"),
            P("seq", "head"),
            P("head", "seq"),
            P(None, "seq", None),
        ),
        out_specs=(
            P(None, "seq", None),
            P(None, "seq", None),
            P("seq"),
            P("seq", "head"),
            P("seq", "head"),
            P("seq", "head"),
            P("head", "seq"),
            P("seq"),
            P("seq", "head"),
            P("seq", "head"),
            P("head", "seq"),
        ),
        check_vma=False,
    )
```

```python
import jax
import jax.numpy as jnp
from jax import lax
from jax.experimental import pallas as pl
from jax.experimental.pallas import tpu as pltpu
from jax.sharding import PartitionSpec as P

F = 16
DV = 128


epsilon = 1e-05
highest = lax.Precision.HIGHEST


def entering(part, axis, combine, identity, reverse):
    count = lax.axis_size(axis)
    place = lax.axis_index(axis)
    ahead = count - 1 - place if reverse else place
    gathered = jax.tree.map(lambda a: lax.all_gather(a, axis), part)
    state = jax.tree.map(lambda a, e: jnp.zeros_like(a) + jnp.asarray(e, a.dtype), part, identity)

    def one(turn, state):
        source = count - 1 - turn if reverse else turn
        return combine(
            state, jax.tree.map(lambda a: lax.dynamic_index_in_dim(a, source, 0, False), gathered)
        )

    return lax.fori_loop(0, ahead, one, state)


def rms_apply(values, gain):
    scale = lax.rsqrt(jnp.mean(values * values, axis=-1, keepdims=True) + epsilon)
    return values * scale * gain


def feature_map(projected):
    count = projected.shape[0]
    pieces = projected.reshape(count, -1, F)
    square = (pieces[:, :, :, None] * pieces[:, :, None, :]).reshape(count, pieces.shape[1], F * F)
    return jnp.concatenate(
        [jnp.ones_like(pieces[:, :, :1]), pieces * F ** (-0.25), square * (2.0 * F) ** (-0.5)],
        axis=-1,
    )


def swiglu(gate, up_part):
    return jax.nn.silu(gate) * up_part


def round_trip(values):
    return lax.optimization_barrier(values.astype(jnp.bfloat16)).astype(jnp.float32)


def add_pair(earlier, later):
    return (earlier[0] + later[0], earlier[1] + later[1])


def block_pass(tokens, upstream, gathered):
    gain_one, query_w, key_w, value_w, out_w, gain_two, gate_w, up_w, down_w = gathered
    f32 = jnp.float32
    bf16 = jnp.bfloat16
    stream = tokens.astype(f32)
    count = stream.shape[0]
    normed_f, norm_one_pull = jax.vjp(rms_apply, stream, gain_one.astype(f32))
    normed = normed_f.astype(bf16)
    queries = jnp.dot(normed, query_w, preferred_element_type=f32)
    keys_all = jnp.dot(normed, key_w, preferred_element_type=f32)
    values = jnp.dot(normed, value_w, preferred_element_type=f32).astype(bf16)
    query_feat_f, query_pull = jax.vjp(feature_map, queries)
    key_feat_f, key_pull = jax.vjp(feature_map, keys_all)
    query_feat = jnp.transpose(query_feat_f.astype(bf16), (1, 0, 2))
    key_feat = jnp.transpose(key_feat_f.astype(bf16), (1, 0, 2))
    value_heads = jnp.transpose(values.reshape(count, -1, DV), (1, 0, 2))
    causal = (jnp.arange(count)[:, None] >= jnp.arange(count)[None, :]).astype(f32)
    scores = jnp.einsum("htf,hsf->hts", query_feat, key_feat, preferred_element_type=f32) * causal
    weighted = scores.astype(bf16)
    num_local = jnp.einsum("hts,hsd->htd", weighted, value_heads, preferred_element_type=f32)
    den_local = jnp.sum(weighted.astype(f32), axis=-1)
    states = jnp.einsum("hsf,hsd->hfd", key_feat, value_heads, preferred_element_type=f32)
    totals = jnp.sum(key_feat.astype(f32), axis=1)
    state_before, total_before = entering(
        (states, totals), "seq", add_pair, (jnp.zeros_like(states), jnp.zeros_like(totals)), False
    )
    query_wide = query_feat.astype(f32)
    numer = num_local + jnp.einsum("htf,hfd->htd", query_wide, state_before, precision=highest)
    denom = den_local + jnp.einsum("htf,hf->ht", query_wide, total_before, precision=highest)
    ratio = numer / denom[..., None]
    heads_out = jnp.transpose(ratio, (1, 0, 2)).reshape(count, -1).astype(bf16)
    attended = lax.psum(jnp.dot(heads_out, out_w, preferred_element_type=f32), "head")
    middle = stream + attended
    normed_two_f, norm_two_pull = jax.vjp(rms_apply, middle, gain_two.astype(f32))
    normed_two = normed_two_f.astype(bf16)
    gate = jnp.dot(normed_two, gate_w, preferred_element_type=f32)
    up_part = jnp.dot(normed_two, up_w, preferred_element_type=f32)
    active, active_pull = jax.vjp(swiglu, gate, up_part)
    hidden = active.astype(bf16)
    branch = lax.psum(
        jnp.dot(hidden, down_w, preferred_element_type=f32).astype(jnp.bfloat16), "head"
    ).astype(jnp.float32)
    result = (middle + branch).astype(bf16)
    grad_down = jnp.dot(hidden.T, upstream, preferred_element_type=f32)
    d_hidden = jnp.dot(upstream, down_w.T, preferred_element_type=f32)
    d_gate_f, d_up_f = active_pull(d_hidden)
    d_gate = d_gate_f.astype(bf16)
    d_up = d_up_f.astype(bf16)
    grad_gate = jnp.dot(normed_two.T, d_gate, preferred_element_type=f32)
    grad_up = jnp.dot(normed_two.T, d_up, preferred_element_type=f32)
    d_normed_two = lax.psum(
        jnp.dot(d_gate, gate_w.T, preferred_element_type=f32)
        + jnp.dot(d_up, up_w.T, preferred_element_type=f32),
        "head",
    )
    d_middle_norm, grad_gain2 = norm_two_pull(d_normed_two)
    d_middle = upstream.astype(f32) + d_middle_norm
    d_attended = d_middle.astype(bf16)
    grad_out = jnp.dot(heads_out.T, d_attended, preferred_element_type=f32)
    d_heads = jnp.transpose(
        jnp.dot(d_attended, out_w.T, preferred_element_type=f32).reshape(count, -1, DV), (1, 0, 2)
    )
    d_numer = (d_heads / denom[..., None]).astype(bf16)
    d_denom = -jnp.sum(d_heads * ratio, axis=-1) / denom
    d_numer_wide = d_numer.astype(f32)
    d_before = jnp.einsum("htf,htd->hfd", query_wide, d_numer_wide, precision=highest)
    d_total_before = jnp.einsum("htf,ht->hf", query_wide, d_denom, precision=highest)
    d_state, d_total = entering(
        (d_before, d_total_before),
        "seq",
        add_pair,
        (jnp.zeros_like(d_before), jnp.zeros_like(d_total_before)),
        True,
    )
    d_scores = (
        (
            jnp.einsum("htd,hsd->hts", d_numer, value_heads, preferred_element_type=f32)
            + d_denom[..., None]
        )
        * causal
    ).astype(bf16)
    d_values = jnp.einsum(
        "hts,htd->hsd", weighted, d_numer, preferred_element_type=f32
    ) + jnp.einsum("hsf,hfd->hsd", key_feat.astype(f32), d_state, precision=highest)
    d_query_feat = (
        jnp.einsum("hts,hsf->htf", d_scores, key_feat, preferred_element_type=f32)
        + jnp.einsum("htd,hfd->htf", d_numer_wide, state_before, precision=highest)
        + d_denom[..., None] * total_before[:, None, :]
    )
    d_key_feat = (
        jnp.einsum("hts,htf->hsf", d_scores, query_feat, preferred_element_type=f32)
        + jnp.einsum("hsd,hfd->hsf", value_heads.astype(f32), d_state, precision=highest)
        + d_total[:, None, :]
    )
    d_queries = query_pull(jnp.transpose(round_trip(d_query_feat), (1, 0, 2)))[0].astype(bf16)
    d_keys = key_pull(jnp.transpose(round_trip(d_key_feat), (1, 0, 2)))[0].astype(bf16)
    d_values_flat = jnp.transpose(d_values, (1, 0, 2)).reshape(count, -1).astype(bf16)
    grad_query = jnp.dot(normed.T, d_queries, preferred_element_type=f32)
    grad_key = jnp.dot(normed.T, d_keys, preferred_element_type=f32)
    grad_value = jnp.dot(normed.T, d_values_flat, preferred_element_type=f32)
    d_normed_part = (
        jnp.dot(d_queries, query_w.T, preferred_element_type=f32)
        + jnp.dot(d_keys, key_w.T, preferred_element_type=f32)
        + jnp.dot(d_values_flat, value_w.T, preferred_element_type=f32)
    )
    d_normed = lax.psum(d_normed_part.astype(jnp.bfloat16), "head").astype(jnp.float32)
    d_stream_norm, grad_gain1 = norm_one_pull(d_normed)
    input_grad = (d_middle + d_stream_norm).astype(bf16)
    return (
        result,
        input_grad,
        grad_gain1,
        grad_query,
        grad_key,
        grad_value,
        grad_out,
        grad_gain2,
        grad_gate,
        grad_up,
        grad_down,
    )


def local(
    inputs, norm_gain1, w_query, w_key, w_value, w_out, norm_gain2, w_gate, w_up, w_down, cotangent
):
    micro = inputs.shape[0]
    summed = None
    results = []
    input_grads = []
    for step_index in range(micro):
        gathered = (
            lax.all_gather(norm_gain1, "seq", axis=0, tiled=True),
            lax.all_gather(w_query, "seq", axis=0, tiled=True),
            lax.all_gather(w_key, "seq", axis=0, tiled=True),
            lax.all_gather(w_value, "seq", axis=0, tiled=True),
            lax.all_gather(w_out, "seq", axis=1, tiled=True),
            lax.all_gather(norm_gain2, "seq", axis=0, tiled=True),
            lax.all_gather(w_gate, "seq", axis=0, tiled=True),
            lax.all_gather(w_up, "seq", axis=0, tiled=True),
            lax.all_gather(w_down, "seq", axis=1, tiled=True),
        )
        (
            result,
            input_grad,
            grad_gain1,
            grad_query,
            grad_key,
            grad_value,
            grad_out,
            grad_gain2,
            grad_gate,
            grad_up,
            grad_down,
        ) = block_pass(inputs[step_index], cotangent[step_index], gathered)
        results.append(result)
        input_grads.append(input_grad)
        fresh = (
            lax.psum_scatter(grad_gain1, "seq", scatter_dimension=0, tiled=True),
            lax.psum_scatter(grad_query, "seq", scatter_dimension=0, tiled=True),
            lax.psum_scatter(grad_key, "seq", scatter_dimension=0, tiled=True),
            lax.psum_scatter(grad_value, "seq", scatter_dimension=0, tiled=True),
            lax.psum_scatter(grad_out, "seq", scatter_dimension=1, tiled=True),
            lax.psum_scatter(grad_gain2, "seq", scatter_dimension=0, tiled=True),
            lax.psum_scatter(grad_gate, "seq", scatter_dimension=0, tiled=True),
            lax.psum_scatter(grad_up, "seq", scatter_dimension=0, tiled=True),
            lax.psum_scatter(grad_down, "seq", scatter_dimension=1, tiled=True),
        )
        summed = (
            fresh
            if summed is None
            else tuple((older + newer for older, newer in zip(summed, fresh)))
        )
    return (
        jnp.stack(results),
        jnp.stack(input_grads),
        summed[0],
        summed[1],
        summed[2],
        summed[3],
        summed[4],
        summed[5],
        summed[6],
        summed[7],
        summed[8],
    )


MESH = pl.DeviceIdType.MESH
bf16 = jnp.bfloat16
f32 = jnp.float32
ZED = 4
VMEM_LIMIT = 60 * 1024 * 1024


def where_am_i():
    place = lax.axis_index("seq")
    return place % 2, (place // 2) % 2, place // 4, lax.axis_index("head")


def index_of(z, y, x):
    return (z * 2 + y) * 2 + x


def remote(src, dst, send, recv, place, head):
    return pltpu.make_async_remote_copy(
        src_ref=src, dst_ref=dst, send_sem=send, recv_sem=recv, device_id=(place, head),
        device_id_type=MESH,
    )


def arrived(dst, send, recv, place, head):
    remote(dst, dst, send, recv, place, head).wait_recv()


def params():
    return pltpu.CompilerParams(has_side_effects=True, vmem_limit_bytes=VMEM_LIMIT)


ANY = pl.BlockSpec(memory_space=pl.ANY)
VMEM = pl.BlockSpec(memory_space=pltpu.VMEM)
DMA = pltpu.SemaphoreType.DMA
ORDER = (0, 1, 3, 2)


def mix(a, b, over):
    return lax.dot_general(a, b, (over, ((), ())), preferred_element_type=f32)


CHUNK = 512
COLS = 256


def spread(got, q_t, k_t, va):
    count = got.shape[2]
    for b in range(got.shape[0]):
        q_t[:, b * count : (b + 1) * count] = got[b, 0:F, :]
        k_t[:, b * count : (b + 1) * count] = got[b, F : 2 * F, :]
        va[b * count : (b + 1) * count, 0:DV] = got[b, 2 * F :, :]
    va[:, DV:] = jnp.ones((va.shape[0], va.shape[1] - DV), bf16)


def lower(count):
    return lax.broadcasted_iota(jnp.int32, (count, count), 0) >= lax.broadcasted_iota(
        jnp.int32, (count, count), 1
    )


def attend_rows(qi, q_t, k_t, va, ratio, den, causal):
    qs = slice(qi * CHUNK, (qi + 1) * CHUNK)
    acc = jnp.zeros((CHUNK, va.shape[1]), f32)
    for kj in range(qi + 1):
        ks = slice(kj * CHUNK, (kj + 1) * CHUNK)
        s = mix(q_t[:, qs], k_t[:, ks], ((0,), (0,)))
        p = 1.0 + s * (0.25 + s * (1.0 / 32.0))
        if kj == qi:
            p = jnp.where(causal, p, 0.0)
        acc = acc + mix(p.astype(bf16), va[ks, :], ((1,), (0,)))
    ratio[qs, :] = acc[:, :DV] / acc[:, DV:]
    den[qs, :] = acc[:, DV:]


def column(gain):
    count = gain.shape[1]
    return jnp.transpose(jnp.broadcast_to(gain[...].astype(f32), (count, count)))


def front_kernel(
    wq, wk, wv, w_out, wg, wu, wd, g1, g2, cot, xin,
    wa1, wa2, wm, gg, got_out, ratio_out, den_out, heads_store, middle_out, near, xh_out,
    got, ratio, den, heads_out, middle, xh, fresh, a1, a2, m, w1, w2, pack, q_t, k_t, va, ob, part, other,
    os, ls, zs, zr, us, ur, ps, pr, e1s, e1r, e2s, e2r, ws, wr, ds, dr,
):
    x, y, z, h = where_am_i()
    me = index_of(z, y, x)
    at_x, at_y = index_of(z, y, 1 - x), index_of(z, 1 - y, x)
    count = xin.shape[1]
    heads = 16 // xin.shape[0]
    late = []
    stored = []

    def store(src, dst):
        copy = pltpu.make_async_copy(src, dst, os.at[len(stored)])
        copy.start()
        stored.append(copy)

    def when(true, do):
        if true is None:
            do()
        else:
            pl.when(true)(do)

    def go(copy, true=None):
        when(true, copy.start)
        late.append((true, copy))

    def rows(zz, yy, xx):
        return pl.ds(pl.multiple_of(index_of(zz, yy, xx) * 128, 128), 128)

    mine = rows(z, y, x)
    kept = [
        pltpu.make_async_copy(a1, w1.at[mine], ls.at[0]),
        pltpu.make_async_copy(a2, w2.at[mine], ls.at[1]),
        pltpu.make_async_copy(m.at[z], wm.at[mine], ls.at[2]),
        pltpu.make_async_copy(cot, gg.at[z], ls.at[6]),
    ]
    lanes = g1.shape[1]
    scale = column(g1)
    at = 0
    for w in (wq, wk, wv):
        for c in range(0, w.shape[1], lanes):
            a1[:, at + c : at + c + lanes] = (w[:, c : c + lanes].astype(f32) * scale).astype(bf16)
        at += w.shape[1]
    kept[0].start()
    kept[3].start()
    dest = (w1, w2, wm)
    UP, DOWN = 0, 1
    COT, NEAR = 2, 3

    def held(kind, zz):
        return (lambda: w1.at[rows(zz, y, x)], lambda: w2.at[rows(zz, y, x)],
                lambda: gg.at[zz, h], lambda: near.at[zz, h])[kind]()

    def origin(way, step):
        return (z + ZED - step) % ZED if way == UP else (z + step) % ZED

    def valid(way, step):
        return z >= step if way == UP else z <= ZED - 1 - step

    def pass_on(kind, way, step, src, true):
        there = index_of((z + 1) % ZED if way == UP else (z + ZED - 1) % ZED, y, x)
        block = held(kind, origin(way, step))
        go(remote(block if src is None else src, block, us.at[kind, way, step], ur.at[kind, way, step + 1], there, h), true)

    def offer(kind, src=None):
        pass_on(kind, UP, 0, src, z < ZED - 1)
        pass_on(kind, DOWN, 0, src, z > 0)

    def hop(kind, way, step):
        block = held(kind, origin(way, step))
        when(
            valid(way, step),
            lambda: arrived(block, us.at[kind, way, step], ur.at[kind, way, step], me, h),
        )
        if step < ZED - 1:
            more = z < ZED - 1 if way == UP else z > 0
            pass_on(kind, way, step, None, valid(way, step) & more)

    def across(kind, way, step):
        zz = origin(way, step)
        block = held(kind, zz)
        go(remote(block, block, ds.at[kind, way, step], dr.at[kind, way, step], me, 1 - h), valid(way, step))

    def across_done(kind, way, step):
        zz = origin(way, step)
        block = (gg if kind == COT else near).at[zz, 1 - h]
        when(
            valid(way, step),
            lambda: arrived(block, ds.at[kind, way, step], dr.at[kind, way, step], me, 1 - h),
        )

    def both(do, kind, step):
        do(kind, UP, step)
        do(kind, DOWN, step)

    partner = (z, z + 1 - 2 * (z % 2), ZED - 1 - z, (z + 2) % ZED)

    inner = (z > 0) & (z < ZED - 1)
    outer = (z == 0) | (z == ZED - 1)

    def line(d, true=None):
        zz = partner[d]
        copy = remote(m.at[zz], wm.at[mine], zs.at[d], zr.at[d], index_of(zz, y, x), h)
        go(copy, true)

    def slot_of(way, step):
        return step if way == UP else 3 + step if step else 0

    def plane_set(kind, slot, zz, true):
        block = dest[kind].at[rows(zz, y, x)]
        go(remote(block, block, ps.at[kind, slot, 0], pr.at[kind, slot, 0], at_x, h), true)
        go(remote(block, block, ps.at[kind, slot, 1], pr.at[kind, slot, 1], at_y, h), true)

    def onward_set(kind, slot, zz, true):
        w = dest[kind]
        half = w.shape[1] // 2
        from_x, from_y = rows(zz, y, 1 - x), rows(zz, 1 - y, x)

        def wait():
            arrived(w.at[from_x], ps.at[kind, slot, 0], pr.at[kind, slot, 0], me, h)
            arrived(w.at[from_y], ps.at[kind, slot, 1], pr.at[kind, slot, 1], me, h)

        when(true, wait)
        left = w.at[from_y, pl.ds(0, half)]
        right = w.at[from_x, pl.ds(half, half)]
        go(remote(left, left, ps.at[kind, slot, 2], pr.at[kind, slot, 2], at_x, h), true)
        go(remote(right, right, ps.at[kind, slot, 3], pr.at[kind, slot, 3], at_y, h), true)

    def corner_set(kind, slot, zz, true):
        w = dest[kind]
        half = w.shape[1] // 2
        far = rows(zz, 1 - y, 1 - x)

        def wait():
            arrived(w.at[far, pl.ds(0, half)], ps.at[kind, slot, 2], pr.at[kind, slot, 2], me, h)
            arrived(w.at[far, pl.ds(half, half)], ps.at[kind, slot, 3], pr.at[kind, slot, 3], me, h)

        when(true, wait)

    def plane(kind, way, step):
        if step == 0:
            kept[kind].wait()
        plane_set(kind, slot_of(way, step), origin(way, step), valid(way, step) if step else None)

    def onward(kind, way, step):
        onward_set(kind, slot_of(way, step), origin(way, step), valid(way, step) if step else None)

    def corner(kind):
        corner_set(kind, 0, z, None)
        for step in (1, 2, 3):
            for way in (UP, DOWN):
                corner_set(kind, slot_of(way, step), origin(way, step), valid(way, step))

    def m_plane(d):
        zz = partner[d]
        if d:
            arrived(wm.at[rows(zz, y, x)], zs.at[d], zr.at[d], me, h)
        else:
            kept[2].wait()
        plane_set(2, d, zz, None)

    def m_onward(d):
        onward_set(2, d, partner[d], None)

    offer(0, a1)
    plane(0, UP, 0)
    for c in range(0, w_out.shape[0], lanes):
        a2[:, c : c + lanes] = jnp.transpose(w_out[c : c + lanes, :].astype(f32)).astype(bf16)
    kept[1].start()
    for way in (UP, DOWN):
        hop(0, way, 1)
        plane(0, way, 1)
    units = wg.shape[1] // ZED
    room = m.shape[2] // 3
    scale = column(g2)
    for n in range(ZED):
        for part_at, w in ((0, wg), (room, wu)):
            for c in range(0, units, lanes):
                size = min(lanes, units - c)
                m[n, :, part_at + c : part_at + c + size] = (
                    w[:, n * units + c : n * units + c + size].astype(f32) * scale[:, 0:size]
                ).astype(bf16)
        for c in range(0, units, lanes):
            size = min(lanes, units - c)
            m[n, :, 2 * room + c : 2 * room + c + size] = jnp.transpose(
                wd[n * units + c : n * units + c + size, :].astype(f32)
            ).astype(bf16)
        for part_at in (0, room, 2 * room):
            m[n, :, part_at + units : part_at + room] = jnp.zeros((lanes, room - units), bf16)
    kept[2].start()
    onward(0, UP, 0)
    for way in (UP, DOWN):
        hop(0, way, 2)
        plane(0, way, 2)
    offer(1, a2)
    both(onward, 0, 1)
    for way in (UP, DOWN):
        hop(0, way, 3)
        plane(0, way, 3)
    both(onward, 0, 2)
    both(hop, 1, 1)
    plane(1, UP, 0)
    for mb in range(xin.shape[0]):

        def normed(turn, carry):
            row = pl.ds(pl.multiple_of(turn * 16, 16), 16)
            v = xin[mb, row, :].astype(f32)
            r = lax.rsqrt(jnp.mean(v * v, axis=-1, keepdims=True) + epsilon)
            xh[pl.ds(pl.multiple_of(mb * count + turn * 16, 16), 16), :] = (v * r).astype(bf16)
            return carry

        lax.fori_loop(0, count // 16, normed, 0)
    store(xh, xh_out)
    both(onward, 0, 3)
    both(hop, 1, 2)
    both(hop, 1, 3)
    line(1)
    line(2, inner)
    corner(0)
    out1 = pltpu.make_async_copy(w1, wa1, ls.at[3])
    out1.start()
    kq = mix(xh[...], w1[:, 0 : 2 * heads * F], ((1,), (0,)))
    qk = jnp.transpose(kq).astype(bf16)
    for mb in range(16 // heads):
        for k in range(heads):
            t = k + heads * mb
            cols = slice(mb * count, (mb + 1) * count)
            pack[t, 0:F, :] = qk[k * F : (k + 1) * F, cols]
            pack[t, F : 2 * F, :] = qk[(heads + k) * F : (heads + k + 1) * F, cols]

    def valued(c, carry):
        cols = pl.ds(pl.multiple_of(2 * heads * F + c * COLS, COLS), COLS)
        val = mix(xh[...], w1[:, cols], ((1,), (0,))).astype(bf16)
        for mb in range(16 // heads):
            for i in range(COLS // DV):
                t = c * (COLS // DV) + i + heads * mb
                pack[t, 2 * F :, :] = val[mb * count : (mb + 1) * count, i * DV : (i + 1) * DV]
        return carry

    lax.fori_loop(0, heads * DV // COLS, valued, 0)
    keep = pltpu.make_async_copy(pack.at[me], got.at[me], ls.at[4])
    keep.start()
    for d in range(1, 16):
        there = (me + d) % 16
        go(remote(pack.at[there], got.at[me], e1s.at[d], e1r.at[d], there, h))
    line(2, outer)
    line(3, inner)
    both(plane, 1, 1)
    onward(1, UP, 0)
    both(plane, 1, 2)
    both(onward, 1, 1)
    both(plane, 1, 3)
    both(onward, 1, 2)
    keep.wait()
    for d in range(1, 16):
        arrived(got.at[(me + 16 - d) % 16], e1s.at[d], e1r.at[d], me, h)
    both(onward, 1, 3)
    store(got, got_out)
    spread(got, q_t, k_t, va)
    causal = lower(CHUNK)
    for qi in range(va.shape[0] // CHUNK):
        attend_rows(qi, q_t, k_t, va, ratio, den, causal)
    for b in range(16):
        ob[b, :, :] = ratio[b * count : (b + 1) * count, :].astype(bf16)

    store(ratio, ratio_out)
    store(den, den_out)

    def window(source):
        return heads_out.at[
            pl.ds(pl.multiple_of((source // heads) * count, count), count),
            pl.ds(pl.multiple_of((source % heads) * DV, DV), DV),
        ]

    keep = pltpu.make_async_copy(ob.at[me], window(me), ls.at[4])
    keep.start()
    for d in range(1, 16):
        there = (me + d) % 16
        go(remote(ob.at[there], window(me), e2s.at[d], e2r.at[d], there, h))
    line(3, outer)
    offer(COT, cot.at[h])
    m_plane(0)
    m_plane(1)
    corner(1)
    out2 = pltpu.make_async_copy(w2, wa2, ls.at[5])
    out2.start()
    keep.wait()
    for d in range(1, 16):
        arrived(window((me + 16 - d) % 16), e2s.at[d], e2r.at[d], me, h)
    store(heads_out, heads_store)
    wide = part.shape[1]

    def pair(c):
        cols = pl.ds(pl.multiple_of(c * COLS, COLS), COLS)
        return remote(part.at[:, cols], other.at[:, cols], ws.at[c], wr.at[c], me, 1 - h)

    def project(c, carry):
        cols = pl.ds(pl.multiple_of(c * COLS, COLS), COLS)
        part[:, cols] = mix(heads_out[...], w2[cols, :], ((1,), (1,)))
        pair(c).start()
        return carry

    lax.fori_loop(0, wide // COLS, project, 0)
    for c in range(wide // COLS):
        late.append((None, pair(c)))
    m_onward(0)
    both(hop, COT, 1)
    m_plane(2)
    for c in range(wide // COLS):
        cols = pl.ds(c * COLS, COLS)
        arrived(other.at[:, cols], ws.at[c], wr.at[c], me, 1 - h)

    def one(mb):
        def body(turn, carry):
            row = pl.ds(pl.multiple_of(turn * 16, 16), 16)
            flat = pl.ds(pl.multiple_of(mb * count + turn * 16, 16), 16)
            mid = xin[mb, row, :].astype(f32) + (part[flat, :] + other[flat, :])
            middle[mb, row, :] = mid
            scale = lax.rsqrt(jnp.mean(mid * mid, axis=-1, keepdims=True) + epsilon)
            fresh[mb, row, :] = (mid * scale).astype(bf16)
            return carry

        lax.fori_loop(0, count // 16, body, 0)

    one(h)
    offer(NEAR, fresh.at[h])
    one(1 - h)
    store(middle, middle_out)
    store(fresh, near.at[z])
    m_onward(1)
    both(hop, COT, 2)
    m_plane(3)
    kept[3].wait()
    both(across, COT, 1)
    both(across, COT, 2)
    both(hop, NEAR, 1)
    both(across, NEAR, 1)
    m_onward(2)
    both(hop, COT, 3)
    both(across, COT, 3)
    both(hop, NEAR, 2)
    both(across, NEAR, 2)
    m_onward(3)
    both(hop, NEAR, 3)
    both(across, NEAR, 3)
    for d in range(4):
        corner_set(2, d, partner[d], None)
    for kind in (NEAR, COT):
        for step in (1, 2, 3):
            both(across_done, kind, step)
    out1.wait()
    out2.wait()
    for copy in stored:
        copy.wait()
    for true, copy in late:
        when(true, copy.wait_send)


def front(wq, wk, wv, w_out, wg, wu, wd, g1, g2, cot, xin):
    mbs, count, wide = xin.shape
    depth = 16 * count
    wide1, wide2 = wq.shape[1] + wk.shape[1] + wv.shape[1], w_out.shape[0]
    wide3 = 3 * (-(-wg.shape[1] // ZED // 256) * 256)
    shape = jax.ShapeDtypeStruct
    return pl.pallas_call(
        front_kernel,
        out_shape=(
            shape((wide, wide1), bf16),
            shape((wide, wide2), bf16),
            shape((wide, wide3), bf16),
            shape((ZED,) + cot.shape, bf16),
            shape((16, 2 * F + DV, count), bf16),
            shape((depth, DV), f32),
            shape((depth, DV), f32),
            shape((mbs * count, wide2), bf16),
            shape(xin.shape, f32),
            shape((ZED,) + xin.shape, bf16),
            shape((mbs * count, wide), bf16),
        ),
        in_specs=[VMEM] * 9 + [ANY] + [VMEM],
        out_specs=(ANY,) * 11,
        scratch_shapes=[
            pltpu.VMEM((16, 2 * F + DV, count), bf16),
            pltpu.VMEM((depth, DV), f32),
            pltpu.VMEM((depth, DV), f32),
            pltpu.VMEM((mbs * count, wide2), bf16),
            pltpu.VMEM(xin.shape, f32),
            pltpu.VMEM((mbs * count, wide), bf16),
            pltpu.VMEM(xin.shape, bf16),
            pltpu.VMEM((wq.shape[0], wide1), bf16),
            pltpu.VMEM((wq.shape[0], wide2), bf16),
            pltpu.VMEM((ZED, wq.shape[0], wide3), bf16),
            pltpu.VMEM((wide, wide1), bf16),
            pltpu.VMEM((wide, wide2), bf16),
            pltpu.VMEM((16, 2 * F + DV, count), bf16),
            pltpu.VMEM((F, depth), bf16),
            pltpu.VMEM((F, depth), bf16),
            pltpu.VMEM((depth, 2 * DV), bf16),
            pltpu.VMEM((16, count, DV), bf16),
            pltpu.VMEM((mbs * count, wide), f32),
            pltpu.VMEM((mbs * count, wide), f32),
            DMA((8,)), DMA((7,)), DMA((4,)), DMA((4,)), DMA((4, 2, 4)), DMA((4, 2, 4)), DMA((3, 7, 4)), DMA((3, 7, 4)),
            DMA((16,)), DMA((16,)), DMA((16,)), DMA((16,)),
            DMA((wide // COLS,)), DMA((wide // COLS,)), DMA((4, 2, 4)), DMA((4, 2, 4)),
        ],
        compiler_params=params(),
        name="front",
    )(wq, wk, wv, w_out, wg, wu, wd, g1, g2, cot, xin)


def attend_back_body(got, ratio, den, d_o, d_qk, d_v, q_t, k_t, va, da, dn_t):
    spread(got, q_t, k_t, va)
    depth = va.shape[0]
    lane = lax.broadcasted_iota(jnp.int32, (CHUNK, DV), 1)
    for qi in range(depth // CHUNK):
        qs = slice(qi * CHUNK, (qi + 1) * CHUNK)
        dn = d_o[qs, :].astype(f32) / den[qs, :]
        dd = -jnp.sum(dn * ratio[qs, :], axis=-1, keepdims=True)
        big = dd.astype(bf16).astype(f32)
        da[qs, 0:DV] = dn.astype(bf16)
        da[qs, DV:] = jnp.where(lane == 0, big, jnp.where(lane == 1, dd - big, 0.0)).astype(bf16)
        dn_t[:, qs] = jnp.transpose(dn).astype(bf16)
    causal = lower(CHUNK)
    for kj in range(depth // CHUNK):
        ks = slice(kj * CHUNK, (kj + 1) * CHUNK)
        acc_k = jnp.zeros((F, CHUNK), f32)
        acc_v = jnp.zeros((DV, CHUNK), f32)
        for qi in range(kj, depth // CHUNK):
            qs = slice(qi * CHUNK, (qi + 1) * CHUNK)
            s = mix(q_t[:, qs], k_t[:, ks], ((0,), (0,)))
            p = 1.0 + s * (0.25 + s * (1.0 / 32.0))
            d_s = mix(da[qs, :], va[ks, :], ((1,), (1,))) * (0.25 + s * (1.0 / 16.0))
            if kj == qi:
                p = jnp.where(causal, p, 0.0)
                d_s = jnp.where(causal, d_s, 0.0)
            d_s = d_s.astype(bf16)
            acc_v = acc_v + mix(dn_t[:, qs], p.astype(bf16), ((1,), (0,)))
            acc_k = acc_k + mix(q_t[:, qs], d_s, ((1,), (0,)))
            d_q = mix(k_t[:, ks], d_s, ((1,), (1,)))
            d_qk[0:F, qs] = d_q if kj == 0 else d_qk[0:F, qs] + d_q
        d_qk[F : 2 * F, ks] = acc_k
        d_v[ks, :] = jnp.transpose(acc_v)


def chunk(turn):
    return pl.ds(pl.multiple_of(turn * 16, 16), 16)


class Scatter:
    def __init__(self, g, low_acc, high_acc, fin, out, r1x, r1y, r2x, r2y, s, q, go, planes=None, relay=None):
        self.planes, self.relay = planes, relay
        self.g, self.low_acc, self.high_acc, self.fin, self.out = g, low_acc, high_acc, fin, out
        self.r1x, self.r1y, self.r2x, self.r2y, self.s, self.q = r1x, r1y, r2x, r2y, s, q
        self.go = go
        self.x, self.y, self.z, self.h = where_am_i()
        self.me = index_of(self.z, self.y, self.x)
        self.at_x = index_of(self.z, self.y, 1 - self.x)
        self.at_y = index_of(self.z, 1 - self.y, self.x)
        self.half = r1x.shape[-1]
        self.low, self.high = pl.ds(0, self.half), pl.ds(self.half, self.half)

    def plane(self, d):
        return (self.z + d) % ZED if self.planes is None else self.planes[d]

    def first_copies(self, d):
        zz, x, y, g = self.plane(d), self.x, self.y, self.g
        return (
            remote(g.at[zz, :, 1 - x, :, self.low], self.r1x.at[d], self.s.at[d, 0], self.q.at[d, 0], self.at_x, self.h),
            remote(g.at[zz, 1 - y, :, :, self.high], self.r1y.at[d], self.s.at[d, 1], self.q.at[d, 1], self.at_y, self.h),
        )

    def first(self, d):
        for copy in self.first_copies(d):
            self.go(copy)

    def second_copies(self, d):
        return (
            remote(self.low_acc(d), self.r2y.at[d], self.s.at[d, 2], self.q.at[d, 2], self.at_y, self.h),
            remote(self.high_acc(d), self.r2x.at[d], self.s.at[d, 3], self.q.at[d, 3], self.at_x, self.h),
        )

    def second_sum(self, d):
        x, y, me, h, r1x, r1y = self.x, self.y, self.me, self.h, self.r1x, self.r1y
        arrived(r1x.at[d], self.s.at[d, 0], self.q.at[d, 0], me, h)
        arrived(r1y.at[d], self.s.at[d, 1], self.q.at[d, 1], me, h)
        low_acc, high_acc = self.low_acc(d), self.high_acc(d)

        def body(i, carry):
            row = chunk(i)
            low_acc[row, :] = (
                low_acc[row, :].astype(f32) + r1x[d, 1 - y, row, :].astype(f32)
            ).astype(bf16)
            high_acc[row, :] = (
                high_acc[row, :].astype(f32) + r1y[d, 1 - x, row, :].astype(f32)
            ).astype(bf16)
            return carry

        lax.fori_loop(0, 8, body, 0)

    def second(self, d):
        self.second_sum(d)
        for copy in self.second_copies(d):
            self.go(copy)

    def third_sum(self, d, target):
        x, y, me, h = self.x, self.y, self.me, self.h
        arrived(self.r2y.at[d], self.s.at[d, 2], self.q.at[d, 2], me, h)
        arrived(self.r2x.at[d], self.s.at[d, 3], self.q.at[d, 3], me, h)
        fin, low, high = self.fin(d), self.low, self.high

        def body(i, carry):
            row = chunk(i)
            target[row, low] = (
                fin[row, low].astype(f32)
                + self.r1x[d, y, row, :].astype(f32)
                + self.r2y[d, row, :].astype(f32)
            ).astype(bf16)
            target[row, high] = (
                fin[row, high].astype(f32)
                + self.r1y[d, x, row, :].astype(f32)
                + self.r2x[d, row, :].astype(f32)
            ).astype(bf16)
            return carry

        lax.fori_loop(0, 8, body, 0)

    def third(self, d):
        fin, z = self.fin(d), self.z
        self.third_sum(d, fin if d else self.out.at[z])
        if d:
            there = index_of((z + d) % ZED, self.y, self.x)
            self.go(remote(fin, self.out.at[z], self.s.at[d, 4], self.q.at[d, 4], there, self.h))

    def last(self, ds):
        for d in ds:
            arrived(
                self.out.at[(self.z + ZED - d) % ZED], self.s.at[d, 4], self.q.at[d, 4], self.me, self.h
            )

    def third_join(self, k):
        fin = self.fin(k)
        self.third_sum(k, fin if k else self.out.at[0])
        near = index_of(self.planes[1], self.y, self.x)
        if k == 1:
            self.go(remote(fin, self.out.at[1], self.s.at[1, 4], self.q.at[1, 4], near, self.h))
        if k > 1:
            outer = (self.z == 0) | (self.z == ZED - 1)
            copy = remote(fin, self.relay.at[3 - k], self.s.at[k, 4], self.q.at[5 - k, 4], near, self.h)
            self.go(copy, outer)

    def join(self, k):
        fin, relay, s, q = self.fin(k), self.relay, self.s, self.q
        inner = (self.z > 0) & (self.z < ZED - 1)

        @pl.when(inner)
        def _():
            arrived(relay.at[k - 2], s.at[k, 4], q.at[k, 4], self.me, self.h)

            def body(i, carry):
                row = chunk(i)
                fin[row, :] = (fin[row, :].astype(f32) + relay[k - 2, row, :].astype(f32)).astype(bf16)
                return carry

            lax.fori_loop(0, 8, body, 0)

        far = index_of(self.planes[k], self.y, self.x)
        self.go(remote(fin, self.out.at[2], s.at[k, 4], q.at[0, 4], far, self.h), inner)

    def joined(self):
        arrived(self.out.at[1], self.s.at[1, 4], self.q.at[1, 4], self.me, self.h)
        arrived(self.out.at[2], self.s.at[0, 4], self.q.at[0, 4], self.me, self.h)


class Join:
    def __init__(self, t, out, other, summed, landed, relay, ls, s, q, go, planes):
        self.t, self.out, self.other, self.summed, self.landed = t, out, other, summed, landed
        self.relay, self.ls, self.s, self.q, self.go, self.planes = relay, ls, s, q, go, planes
        self.x, self.y, self.z, self.h = where_am_i()
        self.me = index_of(self.z, self.y, self.x)
        self.inner = (self.z > 0) & (self.z < ZED - 1)
        self.outer = (self.z == 0) | (self.z == ZED - 1)

    def begin(self):
        self.own = {}
        for k in (2, 3, 1, 0):
            zz = self.planes[k]
            self.own[k] = pltpu.make_async_copy(self.t.at[zz, self.h], self.summed.at[k], self.ls.at[k])
            self.own[k].start()
            self.go(
                remote(self.t.at[zz, 1 - self.h], self.other.at[k], self.s.at[k, 0], self.q.at[k, 0], self.me, 1 - self.h)
            )

    def add(self, k, ref, index):
        summed = self.summed

        def body(turn, carry):
            row = chunk(turn)
            summed[k, row, :] = (
                summed[k, row, :].astype(f32) + ref[index, row, :].astype(f32)
            ).astype(bf16)
            return carry

        lax.fori_loop(0, 8, body, 0)

    def spread(self):
        near = index_of(self.planes[1], self.y, self.x)
        for k in (2, 3, 1, 0):
            self.own[k].wait()
            arrived(self.other.at[k], self.s.at[k, 0], self.q.at[k, 0], self.me, 1 - self.h)
            self.add(k, self.other, k)
            if k == 1:
                self.go(remote(self.summed.at[1], self.landed.at[0], self.s.at[1, 1], self.q.at[1, 1], near, self.h))
            if k > 1:
                copy = remote(
                    self.summed.at[k], self.relay.at[3 - k], self.s.at[k, 1], self.q.at[5 - k, 1], near, self.h
                )
                self.go(copy, self.outer)

    def join_sum(self, k):
        arrived(self.relay.at[k - 2], self.s.at[k, 1], self.q.at[k, 1], self.me, self.h)
        self.add(k, self.relay, k - 2)

    def join_copy(self, k):
        far = index_of(self.planes[k], self.y, self.x)
        return remote(self.summed.at[k], self.landed.at[1], self.s.at[k, 1], self.q.at[0, 1], far, self.h)

    def join(self, k):
        pl.when(self.inner)(lambda: self.join_sum(k))
        self.go(self.join_copy(k), self.inner)

    def total(self):
        summed, landed, out, h = self.summed, self.landed, self.out, self.h
        arrived(landed.at[0], self.s.at[1, 1], self.q.at[1, 1], self.me, h)
        arrived(landed.at[1], self.s.at[0, 1], self.q.at[0, 1], self.me, h)

        def body(turn, carry):
            row = chunk(turn)
            out[h, row, :] = (
                summed[0, row, :].astype(f32)
                + landed[0, row, :].astype(f32)
                + landed[1, row, :].astype(f32)
            ).astype(bf16)
            return carry

        lax.fori_loop(0, 8, body, 0)
        self.go(remote(out.at[h], out.at[h], self.s.at[4, 0], self.q.at[4, 0], self.me, 1 - h))

    def done(self):
        arrived(self.out.at[1 - self.h], self.s.at[4, 0], self.q.at[4, 0], self.me, 1 - self.h)


def back_kernel(
    near, gg, dg_in, du_in, hid_in, t, wo, wm, mid_in, cot_in, got_in, ratio_in, den_in,
    zm, d_mid, d_att, home, tb, rest,
    g, r1x, r1y, r2x, r2y, e2, other, summed, landed, relayed, w2, pack, d_o, d_qk, d_v,
    q_t, k_t, va, da, dn_t, pack2, nbuf, gbuf, turned, stage,
    dg, du, hid, mid, cot, got, ratio, den,
    hs, ls, fs, bs, gs, gq, cs, cq, e1s, e1r, e2s, e2r,
):
    x, y, z, h = where_am_i()
    me = index_of(z, y, x)
    count = mid.shape[1]
    heads = 16 // mid.shape[0]
    room = dg.shape[1]
    late = []

    def go(copy, true=None):
        if true is None:
            copy.start()
        else:
            pl.when(true)(copy.start)
        late.append((true, copy))

    def fetch(i):
        cols = pl.ds(pl.multiple_of(((z + ZED - 1 - i) % ZED) * 512, 512), 512)
        return (
            pltpu.make_async_copy(near.at[:, cols], nbuf.at[i % 2], fs.at[i % 2, 0]),
            pltpu.make_async_copy(gg.at[:, cols], gbuf.at[i % 2], fs.at[i % 2, 1]),
        )

    for copy in fetch(0):
        copy.start()
    pairs = (
        (dg_in, dg), (du_in, du), (hid_in, hid), (mid_in, mid), (cot_in, cot), (got_in, got),
        (ratio_in, ratio), (den_in, den),
    )
    brought = [pltpu.make_async_copy(src, dst, hs.at[n]) for n, (src, dst) in enumerate(pairs)]
    for copy in brought:
        copy.start()
    planes = (z, z + 1 - 2 * (z % 2), ZED - 1 - z, (z + 2) % ZED)
    combine = Join(t, e2, other, summed, landed, relayed, ls, cs, cq, go, planes)
    scatter = Scatter(
        g,
        lambda d: g.at[(z + d) % ZED, 1 - y, x, :, pl.ds(0, g.shape[-1] // 2)],
        lambda d: g.at[(z + d) % ZED, y, 1 - x, :, pl.ds(g.shape[-1] // 2, g.shape[-1] // 2)],
        lambda d: g.at[(z + d) % ZED, y, x],
        zm, r1x, r1y, r2x, r2y, gs, gq, go,
    )
    combine.begin()
    weight = pltpu.make_async_copy(wo, w2, ls.at[4])
    weight.start()
    combine.spread()
    for copy in brought[0:3]:
        copy.wait()

    def block(i, carry):
        d = ZED - 1 - i
        zz = (z + d) % ZED

        @pl.when(i < ZED - 1)
        def _():
            for copy in fetch(i + 1):
                copy.start()

        for copy in fetch(i):
            copy.wait()
        for buf, terms in ((nbuf, (dg, du)), (gbuf, (hid,))):
            turned[...] = jnp.transpose(buf[i % 2])
            for term in terms:
                base = {id(dg): 0, id(du): room, id(hid): 2 * room}[id(term)]

                def piece(c, carry):
                    src = pl.ds(pl.multiple_of(c * COLS, COLS), COLS)
                    dst = pl.ds(pl.multiple_of(base + c * COLS, COLS), COLS)
                    res = mix(turned[...], term[:, src], ((1,), (0,))).astype(bf16)
                    for n in range(4):
                        g[zz, n // 2, n % 2, :, dst] = res[n * 128 : (n + 1) * 128, :]
                    return carry

                lax.fori_loop(0, room // COLS, piece, 0)
        @pl.when(i < ZED - 1)
        def _():
            for copy in scatter.first_copies(d):
                copy.start()

        @pl.when(i == 1)
        def _():
            scatter.second_sum(d + 1)
            for copy in scatter.second_copies(d + 1):
                copy.start()

        for k in (3, 2):

            @pl.when((i == 3 - k) & combine.inner)
            def _():
                combine.join_sum(k)
                combine.join_copy(k).start()

        return carry

    lax.fori_loop(0, ZED - 1, block, 0)
    for d in (1, 2, 3):
        late.extend((None, copy) for copy in scatter.first_copies(d))
    late.extend((None, copy) for copy in scatter.second_copies(3))
    for k in (2, 3):
        late.append((combine.inner, combine.join_copy(k)))
    combine.total()
    weight.wait()
    combine.done()
    for copy in brought[3:]:
        copy.wait()

    for mb in range(mid.shape[0]):

        def body(turn, carry):
            row = chunk(turn)
            m = mid[mb, row, :]
            scale = lax.rsqrt(jnp.mean(m * m, axis=-1, keepdims=True) + epsilon)
            hat = m * scale
            e = e2[mb, row, :].astype(f32)
            d_m = cot[mb, row, :].astype(f32) + scale * (
                e - hat * jnp.mean(e * hat, axis=-1, keepdims=True)
            )
            d_mid[mb, row, :] = d_m
            d_att[pl.ds(pl.multiple_of(mb * count + turn * 16, 16), 16), :] = d_m.astype(bf16)
            return carry

        lax.fori_loop(0, count // 16, body, 0)

    def to_heads(c, carry):
        cols = pl.ds(pl.multiple_of(c * COLS, COLS), COLS)
        val = mix(d_att[...], w2[:, cols], ((1,), (0,))).astype(bf16)
        for mb in range(16 // heads):
            for i in range(COLS // DV):
                pack[c * (COLS // DV) + i + heads * mb, :, :] = val[
                    mb * count : (mb + 1) * count, i * DV : (i + 1) * DV
                ]
        return carry

    lax.fori_loop(0, heads * DV // COLS, to_heads, 0)

    def window(source):
        return d_o.at[pl.ds(pl.multiple_of(source * count, count), count)]

    own = pltpu.make_async_copy(pack.at[me], window(me), ls.at[5])
    own.start()
    for d in range(1, 16):
        there = (me + d) % 16
        go(remote(pack.at[there], window(me), e1s.at[d], e1r.at[d], there, h))
    scatter.second(2)
    scatter.third(3)
    scatter.second(1)
    lax.fori_loop(ZED - 1, ZED, block, 0)
    scatter.first(0)
    half = near.shape[1] // 2
    shards = []
    for r in range(2):
        at = pl.ds(r * half, half)
        shards.append(
            (
                pltpu.make_async_copy(wm.at[at, pl.ds(2 * room, 512)], nbuf.at[r], fs.at[r, 0]),
                pltpu.make_async_copy(
                    wm.at[at, pl.ds(2 * room + 512, room - 512)],
                    gbuf.at[r, :, pl.ds(0, room - 512)],
                    fs.at[r, 1],
                ),
            )
        )
        for copy in shards[r]:
            copy.start()
    scatter.third_sum(2, scatter.fin(2))
    resting = pltpu.make_async_copy(scatter.fin(2), rest, ls.at[6])
    resting.start()
    zm[(z + 2) % ZED] = jnp.zeros(zm.shape[1:], bf16)
    own.wait()
    for d in range(1, 16):
        arrived(window((me + 16 - d) % 16), e1s.at[d], e1r.at[d], me, h)
    attend_back_body(got, ratio, den, d_o, d_qk, d_v, q_t, k_t, va, da, dn_t)
    for b in range(16):
        pack2[b, 0 : 2 * F, :] = d_qk[:, b * count : (b + 1) * count].astype(bf16)
        pack2[b, 2 * F :, :] = d_v[b * count : (b + 1) * count, :].astype(bf16)
    own = pltpu.make_async_copy(pack2.at[me], home.at[me], ls.at[5])
    own.start()
    for d in range(1, 16):
        there = (me + d) % 16
        go(remote(pack2.at[there], home.at[me], e2s.at[d], e2r.at[d], there, h))
    scatter.third(1)
    scatter.second(0)
    for pair in shards:
        for copy in pair:
            copy.wait()
    pieces = half // COLS

    def save(n):
        at = pl.ds(pl.multiple_of(n * COLS, COLS), COLS)
        return pltpu.make_async_copy(stage.at[n % 2], tb.at[:, at], bs.at[n % 2])

    def down(n, carry):
        @pl.when(n > 1)
        def _():
            save(n - 2).wait()

        r = n // pieces
        at = pl.ds(pl.multiple_of((n % pieces) * COLS, COLS), COLS)
        stage[n % 2, :, :] = (
            mix(hid[:, 0:512], nbuf[r, at, :], ((1,), (1,)))
            + mix(hid[:, 512:room], gbuf[r, at, 0 : room - 512], ((1,), (1,)))
        ).astype(bf16)
        save(n).start()
        return carry

    lax.fori_loop(0, 2 * pieces, down, 0)
    scatter.third(0)
    save(2 * pieces - 2).wait()
    save(2 * pieces - 1).wait()
    own.wait()
    for d in range(1, 16):
        arrived(home.at[(me + 16 - d) % 16], e2s.at[d], e2r.at[d], me, h)
    scatter.last((1, 3))
    resting.wait()
    for true, copy in late:
        if true is None:
            copy.wait_send()
        else:
            pl.when(true)(copy.wait_send)


def scatter_room(wide):
    return [
        pltpu.VMEM((4, 2, 128, wide // 2), bf16),
        pltpu.VMEM((4, 2, 128, wide // 2), bf16),
        pltpu.VMEM((4, 128, wide // 2), bf16),
        pltpu.VMEM((4, 128, wide // 2), bf16),
    ]


def back(near, gg, dg, du, hid, t, wo, wm, mid, cot, got, ratio, den):
    mbs, count, wide = cot.shape
    depth = 16 * count
    shape = jax.ShapeDtypeStruct
    cols = 3 * dg.shape[1]
    line = pltpu.VMEM((ZED, count, wide), bf16)
    return pl.pallas_call(
        back_kernel,
        out_shape=(
            shape((ZED, 128, cols), bf16),
            shape(cot.shape, f32),
            shape((mbs * count, wide), bf16),
            shape((16, 2 * F + DV, count), bf16),
            shape(near.shape, bf16),
            shape((128, cols), bf16),
        ),
        in_specs=[ANY] * 13,
        out_specs=(VMEM,) * 4 + (ANY,) * 2,
        scratch_shapes=[pltpu.VMEM((ZED, 2, 2, 128, cols), bf16)] + scatter_room(cols) + [
            pltpu.VMEM(cot.shape, bf16), line, line,
            pltpu.VMEM((2, count, wide), bf16),
            pltpu.VMEM((2, count, wide), bf16),
            pltpu.VMEM(wo.shape, bf16),
            pltpu.VMEM((16, count, DV), bf16),
            pltpu.VMEM((depth, DV), bf16),
            pltpu.VMEM((2 * F, depth), f32),
            pltpu.VMEM((depth, DV), f32),
            pltpu.VMEM((F, depth), bf16),
            pltpu.VMEM((F, depth), bf16),
            pltpu.VMEM((depth, 2 * DV), bf16),
            pltpu.VMEM((depth, 2 * DV), bf16),
            pltpu.VMEM((DV, depth), bf16),
            pltpu.VMEM((16, 2 * F + DV, count), bf16),
            pltpu.VMEM((2, near.shape[0], 512), bf16),
            pltpu.VMEM((2, near.shape[0], 512), bf16),
            pltpu.VMEM((512, near.shape[0]), bf16),
            pltpu.VMEM((2, near.shape[0], COLS), bf16),
            pltpu.VMEM(dg.shape, bf16),
            pltpu.VMEM(dg.shape, bf16),
            pltpu.VMEM(dg.shape, bf16),
            pltpu.VMEM(mid.shape, f32),
            pltpu.VMEM(cot.shape, bf16),
            pltpu.VMEM(got.shape, bf16),
            pltpu.VMEM(ratio.shape, f32),
            pltpu.VMEM(den.shape, f32),
            DMA((8,)), DMA((7,)), DMA((2, 2)), DMA((2,)), DMA((4, 5)), DMA((4, 5)), DMA((5, 2)), DMA((5, 2)),
            DMA((16,)), DMA((16,)), DMA((16,)), DMA((16,)),
        ],
        compiler_params=params(),
        name="back",
    )(near, gg, dg, du, hid, t, wo, wm, mid, cot, got, ratio, den)


def end_kernel(
    t, home, xh, d_att, heads_out, wa1, d_mid_in, xin_in, mid_in, rest,
    za, d_in, outputs, zr,
    g, r1x, r1y, r2x, r2y, relay, branch, other, summed, landed, relayed, w1, dqk_t, dqkv, part, swap,
    d_mid, xin, mid, hs, ts, ls, gs, gq, cs, cq, ws, wr,
):
    x, y, z, h = where_am_i()
    me = index_of(z, y, x)
    mbs, count, wide = xin.shape
    heads = 16 // mbs
    qk, vv = 2 * heads * F, heads * DV
    late = []

    def go(copy, true=None):
        if true is None:
            copy.start()
        else:
            pl.when(true)(copy.start)
        late.append((true, copy))

    planes = (z, z + 1 - 2 * (z % 2), ZED - 1 - z, (z + 2) % ZED)
    combine = Join(t, branch, other, summed, landed, relayed, ls, cs, cq, go, planes)
    scatter = Scatter(
        g,
        lambda k: g.at[planes[k], 1 - y, x, :, pl.ds(0, g.shape[-1] // 2)],
        lambda k: g.at[planes[k], y, 1 - x, :, pl.ds(g.shape[-1] // 2, g.shape[-1] // 2)],
        lambda k: g.at[planes[k], y, x],
        za, r1x, r1y, r2x, r2y, gs, gq, go, planes, relay,
    )
    there = index_of((z + 2) % ZED, y, x)
    go(remote(rest, zr, ts.at[0], ts.at[1], there, h))
    combine.begin()
    brought = [
        pltpu.make_async_copy(d_mid_in, d_mid, hs.at[0]),
        pltpu.make_async_copy(xin_in, xin, hs.at[1]),
        pltpu.make_async_copy(mid_in, mid, hs.at[2]),
    ]
    for copy in brought:
        copy.start()
    weight = pltpu.make_async_copy(wa1, w1, ls.at[4])
    weight.start()
    for mb in range(mbs):
        cols = slice(mb * count, (mb + 1) * count)
        for k in range(heads):
            block = home.at[k + heads * mb]
            dqk_t[k * F : (k + 1) * F, cols] = block[0:F, :].astype(f32)
            dqk_t[(heads + k) * F : (heads + k + 1) * F, cols] = block[F : 2 * F, :].astype(f32)
            dqkv[cols, qk + k * DV : qk + (k + 1) * DV] = block[2 * F :, :]
    dqkv[:, 0:qk] = jnp.transpose(dqk_t[...]).astype(bf16)

    def terms(k):
        zz = planes[k]

        def body(n, carry):
            at = pl.ds(pl.multiple_of((zz * 4 + n) * 128, 128), 128)
            g[zz, n // 2, n % 2, :, 0 : qk + vv] = mix(xh[:, at], dqkv[...], ((0,), (0,))).astype(bf16)
            g[zz, n // 2, n % 2, :, qk + vv :] = mix(d_att[:, at], heads_out[...], ((0,), (0,))).astype(bf16)
            return carry

        lax.fori_loop(0, 4, body, 0)

    terms(2)
    scatter.first(2)
    combine.spread()
    terms(3)
    scatter.first(3)
    scatter.second(2)
    terms(1)
    scatter.first(1)
    weight.wait()
    for copy in brought:
        copy.wait()

    def pair(c):
        cols = pl.ds(pl.multiple_of(c * COLS, COLS), COLS)
        return remote(part.at[:, cols], swap.at[:, cols], ws.at[c], wr.at[c], me, 1 - h)

    def project(c, carry):
        cols = pl.ds(pl.multiple_of(c * COLS, COLS), COLS)
        part[:, cols] = mix(dqkv[...], w1[cols, :], ((1,), (1,)))
        pair(c).start()
        return carry

    lax.fori_loop(0, wide // COLS, project, 0)
    for c in range(wide // COLS):
        late.append((None, pair(c)))
    scatter.second(3)
    combine.join(3)
    terms(0)
    scatter.third_join(2)
    combine.join(2)
    for c in range(wide // COLS):
        cols = pl.ds(c * COLS, COLS)
        arrived(swap.at[:, cols], ws.at[c], wr.at[c], me, 1 - h)
    for mb in range(mbs):

        def body(turn, carry):
            row = chunk(turn)
            flat = pl.ds(pl.multiple_of(mb * count + turn * 16, 16), 16)
            v = xin[mb, row, :].astype(f32)
            scale = lax.rsqrt(jnp.mean(v * v, axis=-1, keepdims=True) + epsilon)
            hat = v * scale
            e = part[flat, :] + swap[flat, :]
            d_in[mb, row, :] = (
                d_mid[mb, row, :] + scale * (e - hat * jnp.mean(e * hat, axis=-1, keepdims=True))
            ).astype(bf16)
            return carry

        lax.fori_loop(0, count // 16, body, 0)
    scatter.second(1)
    scatter.first(0)
    scatter.third_join(3)
    scatter.join(3)
    scatter.third_join(1)
    scatter.join(2)
    combine.total()
    scatter.second(0)
    combine.done()
    for mb in range(mbs):

        def body(turn, carry):
            row = chunk(turn)
            outputs[mb, row, :] = (mid[mb, row, :] + branch[mb, row, :].astype(f32)).astype(bf16)
            return carry

        lax.fori_loop(0, count // 16, body, 0)
    scatter.third_join(0)
    scatter.joined()
    arrived(zr, ts.at[0], ts.at[1], there, h)
    for true, copy in late:
        if true is None:
            copy.wait_send()
        else:
            pl.when(true)(copy.wait_send)


def end(t, home, xh, d_att, heads_out, wa1, d_mid, xin, mid, rest):
    mbs, count, wide = xin.shape
    shape = jax.ShapeDtypeStruct
    cols = wa1.shape[1] + heads_out.shape[1]
    line = pltpu.VMEM((ZED, count, wide), bf16)
    return pl.pallas_call(
        end_kernel,
        out_shape=(shape((3, 128, cols), bf16), shape(xin.shape, bf16), shape(xin.shape, bf16), shape(rest.shape, bf16)),
        in_specs=[ANY] + [VMEM] * 4 + [ANY] * 5,
        out_specs=(VMEM,) * 3 + (ANY,),
        scratch_shapes=[pltpu.VMEM((ZED, 2, 2, 128, cols), bf16)] + scatter_room(cols) + [
            pltpu.VMEM((2, 128, cols), bf16),
            pltpu.VMEM(xin.shape, bf16), line, line,
            pltpu.VMEM((2, count, wide), bf16),
            pltpu.VMEM((2, count, wide), bf16),
            pltpu.VMEM(wa1.shape, bf16),
            pltpu.VMEM((mbs * count, mbs * count), f32),
            pltpu.VMEM((mbs * count, wa1.shape[1]), bf16),
            pltpu.VMEM((mbs * count, wide), f32),
            pltpu.VMEM((mbs * count, wide), f32),
            pltpu.VMEM(d_mid.shape, f32),
            pltpu.VMEM(xin.shape, bf16),
            pltpu.VMEM(mid.shape, f32),
            DMA((3,)), DMA((2,)), DMA((6,)), DMA((4, 5)), DMA((4, 5)), DMA((5, 2)), DMA((5, 2)),
            DMA((wide // COLS,)), DMA((wide // COLS,)),
        ],
        compiler_params=params(),
        name="end",
    )(t, home, xh, d_att, heads_out, wa1, d_mid, xin, mid, rest)


def finish_kernel(
    zm, zr, za, wq, wk, wv, wg, wu, g1, g2, o_q, o_k, o_v, o_out, o_g, o_u, o_d, gains
):
    units = wg.shape[1] // ZED
    hole = (lax.axis_index("seq") // 4 + 2) % ZED

    def quarter(n, cols):
        return jnp.where(hole == n, zr[:, cols].astype(f32), zm[n, :, cols].astype(f32))

    room = zm.shape[2] // 3
    nq, nv = wq.shape[1], wv.shape[1]
    lanes = g1.shape[1]
    scale1, scale2 = column(g1), column(g2)

    def total(cols):
        acc = za[0, :, cols].astype(f32)
        for n in range(1, za.shape[0]):
            acc = acc + za[n, :, cols].astype(f32)
        return acc

    first = jnp.zeros((zm.shape[1], lanes), f32)
    at = 0
    for w, out in ((wq, o_q), (wk, o_k), (wv, o_v)):
        for c in range(w.shape[1] // lanes):
            cols = slice(c * lanes, (c + 1) * lanes)
            value = total(slice(at + c * lanes, at + (c + 1) * lanes))
            out[:, cols] = value * scale1
            first = first + value * w[:, cols].astype(f32)
        at += w.shape[1]
    for c in range(nv // lanes):
        o_out[c * lanes : (c + 1) * lanes, :] = jnp.transpose(
            total(slice(at + c * lanes, at + (c + 1) * lanes))
        )
    second = jnp.zeros((zm.shape[1], lanes), f32)
    for n in range(ZED):
        for base, w, out in ((0, wg, o_g), (room, wu, o_u)):
            for c in range(0, units, lanes):
                size = min(lanes, units - c)
                cols = slice(n * units + c, n * units + c + size)
                value = quarter(n, slice(base + c, base + c + size))
                out[:, cols] = value * scale2[:, 0:size]
                prod = value * w[:, cols].astype(f32)
                if size == lanes:
                    second = second + prod
                else:
                    second = second + jnp.concatenate(
                        [prod, jnp.zeros((prod.shape[0], lanes - size), f32)], axis=1
                    )
        for c in range(0, units, lanes):
            size = min(lanes, units - c)
            value = jnp.transpose(quarter(n, slice(2 * room + c, 2 * room + c + lanes)))
            o_d[n * units + c : n * units + c + size, :] = value[0:size, :]
    gains[0:1, :] = jnp.sum(jnp.transpose(first), axis=0, keepdims=True)
    gains[1:2, :] = jnp.sum(jnp.transpose(second), axis=0, keepdims=True)


def finish(zm, zr, za, wq, wk, wv, wg, wu, g1, g2, w_out, w_down):
    shape = lambda w: jax.ShapeDtypeStruct(w.shape, f32)
    return pl.pallas_call(
        finish_kernel,
        out_shape=(
            shape(wq), shape(wk), shape(wv), shape(w_out), shape(wg), shape(wu), shape(w_down),
            jax.ShapeDtypeStruct((2, 128), f32),
        ),
        in_specs=[VMEM] * 10,
        out_specs=(VMEM,) * 8,
        compiler_params=pltpu.CompilerParams(vmem_limit_bytes=VMEM_LIMIT),
        name="finish",
    )(zm, zr, za, wq, wk, wv, wg, wu, g1, g2)


def fast(
    inputs, norm_gain1, w_query, w_key, w_value, w_out, norm_gain2, w_gate, w_up, w_down, cotangent
):
    mbs, count, wide = inputs.shape
    rows = w_query.shape[0]
    gain1, gain2 = norm_gain1.reshape(1, rows), norm_gain2.reshape(1, rows)
    wa1, w_o, wm, gg, got, ratio, den, heads_out, middle, near, xh1 = front(
        w_query, w_key, w_value, w_out, w_gate, w_up, w_down, gain1, gain2, cotangent, inputs
    )
    room = wm.shape[1] // 3
    w_g, w_u, w_d = wm[:, :room], wm[:, room : 2 * room], wm[:, 2 * room :]
    many = ZED * mbs * count
    n2 = near.reshape(many, wide)
    up_g = gg.reshape(many, wide)
    gate = mix(n2, w_g, ((1,), (0,)))
    up = mix(n2, w_u, ((1,), (0,)))
    d_hidden = mix(up_g, w_d, ((1,), (0,)))
    sig = jax.nn.sigmoid(gate)
    silu = gate * sig
    hidden = (silu * up).astype(bf16)
    d_gate = (d_hidden * up * sig * (1.0 + gate * (1.0 - sig))).astype(bf16)
    d_up = (d_hidden * silu).astype(bf16)
    d_n2 = (mix(d_gate, w_g, ((1,), (1,))) + mix(d_up, w_u, ((1,), (1,)))).astype(bf16)
    lines = (ZED, mbs, count, wide)
    zm, d_mid, d_att, home, branch, rest = back(
        n2, up_g, d_gate, d_up, hidden, d_n2.reshape(lines), w_o, wm, middle, cotangent, got, ratio, den
    )
    za, input_grad, outputs, zr = end(
        branch.reshape(lines), home, xh1, d_att, heads_out, wa1, d_mid, inputs, middle, rest
    )
    o_q, o_k, o_v, o_out, o_g, o_u, o_d, gains = finish(
        zm, zr, za, w_query, w_key, w_value, w_gate, w_up,
        gain1, gain2, w_out, w_down,
    )
    gains = lax.psum(gains, "head")
    return (outputs, input_grad, gains[0], o_q, o_k, o_v, o_out, gains[1], o_g, o_u, o_d)


def solution(mesh):
    return jax.shard_map(
        fast if mesh.shape["seq"] == 16 else local,
        mesh=mesh,
        in_specs=(
            P(None, "seq", None),
            P("seq"),
            P("seq", "head"),
            P("seq", "head"),
            P("seq", "head"),
            P("head", "seq"),
            P("seq"),
            P("seq", "head"),
            P("seq", "head"),
            P("head", "seq"),
            P(None, "seq", None),
        ),
        out_specs=(
            P(None, "seq", None),
            P(None, "seq", None),
            P("seq"),
            P("seq", "head"),
            P("seq", "head"),
            P("seq", "head"),
            P("head", "seq"),
            P("seq"),
            P("seq", "head"),
            P("seq", "head"),
            P("head", "seq"),
        ),
        check_vma=False,
    )
```
